32 devices in a mesh: dp: 8 (over z, x), zero: 4 (over y, core).
Axes of the slice: x: 2, y: 2, z: 4, core: 2. Of those that a mesh axis runs over, the one named last changes fastest.
Arguments:
- tokens: bfloat16 [64, 1024, 768], P('zero', 'dp'), may hold values from -6 to 6
- loss_sensitivity: bfloat16 [32, 1024, 768], P(('dp', 'zero')), may hold values from -6 to 6
- lengths: int32 [64], replicated, may hold values from 0 to 1024, as said below
- holder_sequence_list: int32 [64], replicated, may hold values from 0 to 63, as said below
- master: float32 [3768320], P('zero')
- moment_one: float32 [3768320], P('zero'), may hold values from -18 to 18
- moment_two: float32 [3768320], P('zero'), may hold values from 1 to 1000
- adam_rates: float32 [2], replicated, may hold values from 0.05 to 0.2
- iteration_tally: int32 [1], replicated, may hold values from 1 to 8
Outputs:
- tokens_out: bfloat16 [64, 1024, 768], P('zero', 'dp')
- grad_tokens: bfloat16 [64, 1024, 768], P('zero', 'dp')
- new_master: float32 [3768320], replicated
- grads: float32 [3768320], P('zero')
- moment_one_out: float32 [3768320], P('zero')
- moment_two_out: float32 [3768320], P('zero')
The draws below stay inside these ranges and needn't reach their ends.
Inputs may be any that keep to these rules, and one draw needn't show every extreme that they name: A permutation of the sequences. Slot i lies on the device whose index along dp+zero is i // 2, and holder_sequence_list[i] is one of the 64 / 4 sequences of that device's zero index (sequences z * 64 / 4 onward for zero index z). The two sequences of slots 2j and 2j + 1 have lengths summing to exactly 1024; in some pack one of them has 1024 tokens and the other none.
All inputs are finite; a program needn't handle non-finite values.
Results may differ from the reference program's by a relative error of at most 0.002.
The reference program's roundings to bfloat16 on the way count: a program that leaves them out, or rounds other values in their place, can miss the bound.
Values may be sent and summed in bfloat16 or wider, within the bound.
No kernel may reach another device: no remote copies, remote signals or barrier semaphores. Data moves between devices by JAX's collectives and lax.ppermute only.
A program may use at most 256 MiB of HBM per device.

```python
import math
from functools import partial
import jax
import jax.numpy as jnp
from jax import lax

D = 768
HEADS = 24
HEADDIM = 64
STATE = 128
CONV = 4
SPAN = 256
LMAX = 1024
SEQ_DEV = 2
INNER = 1536
XBC = 1792
PROJ = 3352
NSEQ = 64
RAW_PARAMS = 3765632
PARAMS = 3768320
N_DP = 8
N_ZERO = 4


def dealt_slots(key):
    base = jax.random.fold_in(key, 17)
    key_list = jax.random.split(base, 3)
    group_seqs = NSEQ // N_ZERO
    group_keys = jax.random.split(key_list[0], N_ZERO)

    def one_perm(group_key):
        return jax.random.permutation(group_key, group_seqs).astype(jnp.int32)
    perms = jax.vmap(one_perm)(group_keys)
    offsets = (jnp.arange(N_ZERO, dtype=jnp.int32) * group_seqs)[:, None]
    grouped = (perms + offsets).reshape(N_ZERO, N_DP, SEQ_DEV)
    order = jnp.transpose(grouped, (1, 0, 2)).reshape(NSEQ)
    packs = NSEQ // 2
    first = jax.random.randint(key_list[1], (packs,), 1, LMAX, dtype=jnp.int32)
    forced = jax.random.randint(key_list[2], (), 0, packs, dtype=jnp.int32)
    first = jnp.where(jnp.arange(packs, dtype=jnp.int32) == forced, 0, first)
    composed = jnp.stack([first, LMAX - first], axis=1).reshape(NSEQ)
    seq_lengths = jnp.zeros((NSEQ,), jnp.int32).at[order].set(composed)
    return (order, seq_lengths)


def draw_holder_sequence_list(key, part):
    return dealt_slots(key)[0]


def draw_lengths(key, part):
    return dealt_slots(key)[1]


def with_gap(piece, gap_key):
    amount = piece.shape[0]
    slot = (amount + 127) // 128 * 128
    return jnp.concatenate([piece, jax.random.normal(gap_key, (slot - amount,), jnp.float32) * 0.05])


def draw_master(key, part):
    key_list = jax.random.split(key, 10)
    gap_keys = jax.random.split(jax.random.fold_in(key, 29), 9)
    norm_gain = jax.random.uniform(key_list[0], (D,), jnp.float32, 0.5, 1.5)
    input_weight = jax.random.normal(key_list[1], (D * PROJ,), jnp.float32) * D ** (-0.5)
    dt_bias = jax.random.uniform(key_list[4], (HEADS,), jnp.float32, -7.5, -3.0)
    conv_w = jax.random.normal(key_list[2], (CONV * XBC,), jnp.float32) * 0.5
    conv_b = jax.random.normal(key_list[3], (XBC,), jnp.float32) * 0.5
    a_log = jax.random.uniform(key_list[5], (HEADS,), jnp.float32, 0.0, 0.7)
    d_skip = jax.random.uniform(key_list[6], (HEADS,), jnp.float32, 0.5, 1.5)
    gated_gain = jax.random.uniform(key_list[7], (INNER,), jnp.float32, 0.5, 1.5)
    emitting_matrix = jax.random.normal(key_list[8], (INNER * D,), jnp.float32) * INNER ** (-0.5)
    pieces = [norm_gain, input_weight, conv_w, conv_b, dt_bias, a_log, d_skip, gated_gain, emitting_matrix]
    laid = [with_gap(pieces[index], gap_keys[index]) for index in range(9)]
    unused = jax.random.normal(key_list[9], (PARAMS - RAW_PARAMS,), jnp.float32) * 0.05
    return jnp.concatenate(laid + [unused])


def shard_levels(rng, shape, shards, low, high):
    level = 1.0
    for dim, shards_of in shards:
        draws = jax.random.uniform(jax.random.fold_in(jax.random.fold_in(rng, 6), dim), (shards_of,), jnp.float32, low / len(shards), high / len(shards))
        level = level * jnp.repeat(jnp.exp(draws), shape[dim] // shards_of).reshape((-1,) + (1,) * (len(shape) - 1 - dim))
    return level


def bell_draw(own_key, extent, spread, bound, cuts=(), kind=jnp.bfloat16):
    result = jax.random.normal(own_key, extent, jnp.float32) * spread
    if len(cuts) > 0:
        result = shard_levels(own_key, extent, cuts, -0.22, 0.18) * result
    return jnp.clip(result, min=-bound, max=bound).astype(kind)


def setup_inputs(seed: int = 0) -> dict:
    splits = jax.random.split(jax.random.key(seed), 10)
    return {
        "tokens": bell_draw(splits[0], (NSEQ, LMAX, D), 1.0, 6.0, ((0, 4), (1, 8))),
        "loss_sensitivity": bell_draw(splits[1], (NSEQ // 2, LMAX, D), 1.0, 6.0, ((0, 32),)),
        "lengths": draw_lengths(jax.random.fold_in(splits[9], 71), 0),
        "holder_sequence_list": draw_holder_sequence_list(jax.random.fold_in(splits[9], 71), 0),
        "master": draw_master(jax.random.fold_in(splits[9], 71), 0),
        "moment_one": bell_draw(splits[5], (PARAMS,), 3.0, 18.0, ((0, 4),), jnp.float32),
        "moment_two": jnp.clip(jnp.exp(math.log(1000.0) - 6.9077553 * jax.random.uniform(splits[6], (PARAMS,), jnp.float32) ** shard_levels(splits[6], (PARAMS,), ((0, 4),), -0.2, 0.2)), 1.0, 1000.0),
        "adam_rates": jnp.clip(jax.random.uniform(splits[7], (2,), jnp.float32, 0.05, 0.2), 0.05, 0.2),
        "iteration_tally": jax.random.randint(splits[8], (1,), 1, 9).astype(jnp.int32),
    }


@jax.custom_vjp
def low(v):
    return lax.optimization_barrier(v.astype(jnp.bfloat16)).astype(jnp.float32)

@jax.custom_vjp
def low_back(v):
    return v

def low_keep(v):
    return (low(v), None)

def low_pass(kept, grad):
    return (grad,)

def back_keep(v):
    return (v, None)

def back_low(kept, grad):
    return (low(grad),)
low.defvjp(low_keep, low_pass)
low_back.defvjp(back_keep, back_low)
EXACT_MATMUL = lax.Precision.HIGHEST
EPS_NORM = 1e-05
BETA_ONE = 0.9
BETA_TWO = 0.95
EPS_ADAM = 1e-08

def padded_slot(amount):
    return (amount + 127) // 128 * 128

def unpack(linear_coefficient_list):
    piece_sizes = [D, D * PROJ, CONV * XBC, XBC, HEADS, HEADS, HEADS, INNER, INNER * D]
    pieces = []
    offset = 0
    for amount in piece_sizes:
        pieces.append(linear_coefficient_list[offset:offset + amount])
        offset = offset + padded_slot(amount)
    norm_gain, input_weight_t, conv_w, conv_b, dt_bias, a_log, d_skip, gated_gain, emitting_matrix = pieces
    return (norm_gain, input_weight_t.reshape(PROJ, D).T, conv_w.reshape(CONV, XBC), conv_b, dt_bias, a_log, d_skip, gated_gain, emitting_matrix.reshape(INNER, D))

def pre_norm(values, gain):
    return values * lax.rsqrt(lax.optimization_barrier(jnp.mean(values * values, axis=-1, keepdims=True)) + EPS_NORM) * gain

def causal_conv(conv_in, conv_w, conv_b):
    seq_len = conv_in.shape[1]
    padded = jnp.pad(conv_in, ((0, 0), (CONV - 1, 0), (0, 0)))
    summed = conv_b + jnp.zeros_like(conv_in)
    for offset in range(CONV):
        summed = summed + conv_w[offset] * padded[:, offset:offset + seq_len]
    return summed

def span_scan(x_heads, dt_pos, decay_rate, b_rows, c_rows):
    batch_size, seq_len, head_count, head_width = x_heads.shape
    block_count = seq_len // SPAN

    def split_blocks(values):
        shaped = values.reshape((batch_size, block_count, SPAN) + values.shape[2:])
        return jnp.moveaxis(shaped, 1, 0)
    causal = jnp.arange(SPAN)[:, None] >= jnp.arange(SPAN)[None, :]

    def advance(carried, block_in):
        x_blk, dt_blk, b_blk, c_blk = block_in
        dt_cols = jnp.swapaxes(dt_blk, 1, 2)
        cum_blk = jnp.cumsum(dt_cols * decay_rate[None, :, None], axis=2)
        differ = cum_blk[:, :, :, None] - cum_blk[:, :, None, :]
        weights_in = jnp.exp(jnp.where(causal, differ, -jnp.inf))
        gram_blk = jnp.einsum('stn,srn->str', c_blk, b_blk, precision=EXACT_MATMUL)
        mixing = gram_blk[:, None] * weights_in * dt_cols[:, :, None, :]
        inside = jnp.einsum('shtr,srhp->sthp', mixing, x_blk, precision=EXACT_MATMUL)
        from_state = jnp.einsum('stn,shpn->sthp', c_blk, carried, precision=EXACT_MATMUL)
        from_state = from_state * jnp.swapaxes(jnp.exp(cum_blk), 1, 2)[..., None]
        cum_end = cum_blk[:, :, -1]
        carry_weight = jnp.exp(cum_end[:, :, None] - cum_blk) * dt_cols
        added_state = jnp.einsum('srn,shr,srhp->shpn', b_blk, carry_weight, x_blk, precision=EXACT_MATMUL)
        carried = carried * jnp.exp(cum_end)[:, :, None, None] + added_state
        return (carried, inside + from_state)
    initial = jnp.zeros((batch_size, head_count, head_width, b_rows.shape[-1]), jnp.float32)
    final_state, outputs = lax.scan(jax.checkpoint(advance), initial, (split_blocks(x_heads), split_blocks(dt_pos), split_blocks(b_rows), split_blocks(c_rows)))
    return jnp.moveaxis(outputs, 0, 1).reshape(batch_size, seq_len, head_count, head_width)

def mixer_branch(input_projection, conv_w, conv_b, dt_bias, a_log, d_skip, gated_gain):
    batch_size, seq_len = (input_projection.shape[0], input_projection.shape[1])
    gate_z = input_projection[..., :INNER]
    conv_in = input_projection[..., INNER:INNER + XBC]
    dt_raw = input_projection[..., INNER + XBC:]
    conv_out = jax.nn.silu(causal_conv(conv_in, conv_w, conv_b))
    x_heads = conv_out[..., :INNER].reshape(batch_size, seq_len, HEADS, HEADDIM)
    b_rows = conv_out[..., INNER:INNER + STATE]
    c_rows = conv_out[..., INNER + STATE:]
    dt_pos = jax.nn.softplus(dt_raw + dt_bias)
    decay_rate = -jnp.exp(a_log)
    scanned = span_scan(x_heads, dt_pos, decay_rate, b_rows, c_rows) + d_skip[:, None] * x_heads
    gated_out = scanned.reshape(batch_size, seq_len, INNER) * jax.nn.silu(gate_z)
    return gated_out * lax.rsqrt(lax.optimization_barrier(jnp.mean(gated_out * gated_out, axis=-1, keepdims=True)) + EPS_NORM) * gated_gain

def forward(tokens_f, linear_coefficient_list, live_mask):
    rounded = low(linear_coefficient_list)
    norm_gain, input_weight, conv_w, conv_b, dt_bias, a_log, d_skip, gated_gain, emitting_matrix = unpack(rounded)
    group_size = math.gcd(NSEQ, max(1, 4096 // LMAX))
    tok_groups = tokens_f.reshape(NSEQ // group_size, group_size, LMAX, D)
    mask_groups = live_mask.reshape(NSEQ // group_size, group_size, LMAX)

    def one_group(pair_in):
        block_tokens, block_mask = pair_in
        normalized = low(pre_norm(block_tokens, norm_gain))
        input_projection = low_back(jnp.einsum('mgv,vb->mgb', normalized, input_weight, precision=EXACT_MATMUL))
        mixer_output = low(mixer_branch(input_projection, conv_w, conv_b, dt_bias, a_log, d_skip, gated_gain))
        mixer_path = low_back(jnp.einsum('ocr,rb->ocb', mixer_output, emitting_matrix, precision=EXACT_MATMUL))
        return block_tokens + block_mask[..., None] * mixer_path
    outputs = lax.map(jax.checkpoint(one_group), (tok_groups, mask_groups))
    return outputs.reshape(NSEQ, LMAX, D)

def adam_update(weights, first_moment, second_moment, gradient, adam_rates, iteration_tally):
    steps_f = iteration_tally[0].astype(jnp.float32)
    first_next = BETA_ONE * first_moment + (1.0 - BETA_ONE) * gradient
    second_next = BETA_TWO * second_moment + (1.0 - BETA_TWO) * gradient * gradient
    first_hat = first_next / (1.0 - jnp.power(BETA_ONE, steps_f))
    second_hat = second_next / (1.0 - jnp.power(BETA_TWO, steps_f))
    updated = weights - adam_rates[0] * (first_hat / (jnp.sqrt(second_hat) + EPS_ADAM) + adam_rates[1] * weights)
    return (updated, first_next, second_next)

def reference(tokens, loss_sensitivity, lengths, holder_sequence_list, master, moment_one, moment_two, adam_rates, iteration_tally):
    positions = jnp.arange(LMAX, dtype=jnp.int32)
    live_mask = (positions[None, :] < lengths[:, None]).astype(jnp.float32)
    slot_of = jnp.zeros((NSEQ,), jnp.int32).at[holder_sequence_list].set(jnp.arange(NSEQ, dtype=jnp.int32))
    partner = holder_sequence_list[jnp.maximum(slot_of - 1, 0)]
    start = jnp.where(slot_of % 2 == 1, lengths[partner], 0).astype(jnp.int32)
    pack_of = (slot_of // 2).astype(jnp.int32)
    rows = jnp.minimum(start[:, None] + positions[None, :], LMAX - 1).astype(jnp.int32)
    cot_seq = loss_sensitivity[pack_of[:, None], rows].astype(jnp.float32) * live_mask[..., None]
    tokens_f = tokens.astype(jnp.float32)
    outputs, reverse_derivative_map = jax.vjp(partial(forward, live_mask=live_mask), tokens_f, master)
    grad_tokens, gradient = reverse_derivative_map(cot_seq * live_mask[..., None])
    new_master, first_next, second_next = adam_update(master, moment_one, moment_two, gradient, adam_rates, iteration_tally)
    return (outputs.astype(jnp.bfloat16), grad_tokens.astype(jnp.bfloat16), new_master, gradient, first_next, second_next)
```

```python
import jax
import jax.numpy as jnp
from jax import lax
from jax.experimental import pallas as pl
from jax.experimental.pallas import tpu as pltpu
from jax.sharding import PartitionSpec as P

D = 768
HEADS = 24
HEADDIM = 64
STATE = 128
CONV = 4
INNER = 1536
XBC = 1792
PROJ = 3352
Q = 128
LATE = PROJ - INNER
WINDOW = 1024
PAIRS = HEADS // 2
EPS_NORM = 1e-05
NEG = -1e30
F32 = jnp.float32
BF16 = jnp.bfloat16


def dot(a, b):
    return lax.dot_general(a, b, (((1,), (0,)), ((), ())), preferred_element_type=F32)


def dot_nt(a, b):
    return lax.dot_general(a, b, (((1,), (1,)), ((), ())), preferred_element_type=F32)


def split2(v):
    hi = v.astype(BF16)
    return hi, (v - hi.astype(F32)).astype(BF16)


def split3(v):
    hi = v.astype(BF16)
    rest = v - hi.astype(F32)
    mid = rest.astype(BF16)
    return hi, mid, (rest - mid.astype(F32)).astype(BF16)


def wide_left(v):
    hi, lo = split2(v)
    return jnp.concatenate([hi, lo, hi], axis=1)


def tall_right(v):
    hi, lo = split2(v)
    return jnp.concatenate([hi, hi, lo], axis=0)


def exact_left(v):
    return jnp.concatenate(split3(v), axis=1)


def sigmoid(v):
    return 1.0 / (1.0 + jnp.exp(-v))


def softplus(v):
    return jnp.maximum(v, 0.0) + jnp.log1p(jnp.exp(-jnp.abs(v)))


def iota(shape, dim):
    return lax.broadcasted_iota(jnp.int32, shape, dim)


def expand(v, e_ref):
    hi, lo = split2(v)
    return dot(jnp.concatenate([hi, lo], axis=1), e_ref[...])


def head_sum(v, et_ref):
    hi, lo = split2(v)
    return dot(hi, et_ref[...]) + dot(lo, et_ref[...])


def chunk_masks(t0, bound):
    rows = t0 + iota((Q, 1), 0)
    rr = t0 + iota((Q, Q), 0)
    cc = t0 + iota((Q, Q), 1)
    return rows, rr, cc


def conv_rows(ext_ref, w_ref, b_ref, rows, bound):
    total = b_ref[...] + w_ref[3:4, :] * ext_ref[8 : 8 + Q, :]
    for back in (1, 2, 3):
        ok = jnp.logical_or(rows - back >= bound, rows < bound).astype(F32)
        total = total + w_ref[3 - back : 4 - back, :] * (ext_ref[8 - back : 8 - back + Q, :] * ok)
    return total


def decay_parts(dt_raw, dtb_ref, alog_ref, rr, cc):
    dt_in = dt_raw + dtb_ref[...]
    dt_pos = softplus(dt_in)
    rate = -jnp.exp(alog_ref[...])
    step = dt_pos * rate
    tri = (cc <= rr).astype(F32).astype(BF16)
    s_hi, s_mid, s_lo = split3(step)
    cum = dot(tri, s_hi) + dot(tri, s_mid) + dot(tri, s_lo)
    return dt_in, dt_pos, rate, cum


def forward_kernel(
    bound_ref, z_ref, proj_ref, gm_ref, e_ref, et_ref, convw_ref, convb_ref, dtb_ref, alog_ref,
    skip_ref, gain_ref,
    pair_ref, dy_ref, through_ref, state_ref, ggain_ref,
    ext_ref, dt_ref, carry_ref, xd_ref, acc_ref, cumt_ref,
):
    step = pl.program_id(0)
    bound = bound_ref[0]
    t0 = step * Q

    @pl.when(step == 0)
    def _():
        ext_ref[0:8, :] = jnp.zeros((8, XBC), F32)
        carry_ref[...] = jnp.zeros_like(carry_ref)
        dt_ref[...] = jnp.zeros_like(dt_ref)
        ggain_ref[...] = jnp.zeros_like(ggain_ref)

    rows, rr, cc = chunk_masks(t0, bound)
    ext_ref[8 : 8 + Q, :] = proj_ref[:, :XBC]
    pre = conv_rows(ext_ref, convw_ref, convb_ref, rows, bound)
    ext_ref[0:8, :] = ext_ref[Q : Q + 8, :]
    conv_out = pre * sigmoid(pre)
    x = conv_out[:, :INNER]
    b_rows = conv_out[:, INNER : INNER + STATE]
    c_rows = conv_out[:, INNER + STATE :]
    dt_ref[:, 0:HEADS] = proj_ref[:, XBC:LATE]
    _, dt_pos, _, cum = decay_parts(dt_ref[...], dtb_ref, alog_ref, rr, cc)
    cum_end = cum[Q - 1 : Q, :]
    keep = jnp.logical_or(rows < bound, bound < t0).astype(F32)
    in_last = jnp.logical_or(rows >= bound, bound > t0 + Q - 1).astype(F32)
    whole = jnp.logical_or(bound < t0, bound > t0 + Q - 1).astype(F32)
    from_start = jnp.exp(cum) * keep
    to_end = jnp.exp(cum_end - cum) * in_last
    carry_scale = jnp.exp(cum_end) * whole
    allowed = jnp.logical_and(cc <= rr, (cc >= bound) == (rr >= bound))
    cumt_ref[...] = cum.T

    state = carry_ref[...]
    state_ref[0] = state
    xd = x * expand(dt_pos, e_ref)
    xd_ref[...] = xd
    acc = dot(wide_left(c_rows), tall_right(state)) * expand(from_start, e_ref)
    acc_ref[...] = acc + skip_ref[...] * x
    b_t = b_rows.T
    scale_all = expand(jnp.broadcast_to(carry_scale, (Q, Q)), e_ref)
    carry_ref[...] = state * scale_all + dot(
        wide_left(b_t), tall_right(xd * expand(to_end, e_ref))
    )
    gram = dot(wide_left(c_rows), tall_right(b_t))
    first = iota((Q, Q), 1) < HEADDIM
    for pair in range(PAIRS):
        parts = []
        for head in (2 * pair, 2 * pair + 1):
            differ = cum[:, head : head + 1] - cumt_ref[head : head + 1, :]
            parts.append(gram * jnp.exp(jnp.where(allowed, differ, NEG)))
        left = jnp.concatenate(split2(jnp.concatenate(parts, axis=1)), axis=0)
        lanes = slice(pair * 128, pair * 128 + 128)
        xp = xd_ref[:, lanes]
        diag = jnp.concatenate([jnp.where(first, xp, 0.0), jnp.where(first, 0.0, xp)], axis=0)
        out = dot(left, jnp.concatenate(split2(diag), axis=1))
        acc_ref[:, lanes] += out[:Q, :128] + (out[:Q, 128:] + out[Q:, :128])
    scanned = acc_ref[...]
    z = z_ref[...]
    sig_z = sigmoid(z)
    silu_z = z * sig_z
    gated = scanned * silu_z
    ginv = lax.rsqrt(jnp.mean(gated * gated, axis=1, keepdims=True) + EPS_NORM)
    mhat = gated * ginv
    pair_ref[1] = (mhat * gain_ref[...]).astype(BF16)
    gm = gm_ref[...]
    ggain_ref[...] += jnp.sum(mhat * gm, axis=0, keepdims=True)
    gmg = gm * gain_ref[...]
    ggated = ginv * (gmg - mhat * jnp.mean(mhat * gmg, axis=1, keepdims=True))
    dy = ggated * silu_z
    dy_ref[...] = dy
    pair_ref[0] = (ggated * scanned * (sig_z * (1.0 + z * (1.0 - sig_z)))).astype(BF16)
    through_ref[...] = head_sum(dy * (scanned - skip_ref[...] * x), et_ref)


def const_spec(shape):
    return pl.BlockSpec(shape, lambda *_: (0,) * len(shape))


def run_forward(z, proj, gm, bound, e2, et, params):
    n = proj.shape[0]
    steps = n // Q
    return pl.pallas_call(
        forward_kernel,
        grid=(steps,),
        in_specs=[
            pl.BlockSpec(memory_space=pltpu.SMEM),
            pl.BlockSpec((Q, INNER), lambda i: (i, 0)),
            pl.BlockSpec((Q, LATE), lambda i: (i, 0)),
            pl.BlockSpec((Q, INNER), lambda i: (i, 0)),
            const_spec((256, INNER)), const_spec((INNER, 128)),
            const_spec((8, XBC)), const_spec((1, XBC)), const_spec((1, 128)),
            const_spec((1, 128)), const_spec((1, INNER)), const_spec((1, INNER)),
        ],
        out_specs=[
            pl.BlockSpec((2, Q, INNER), lambda i: (0, i, 0)),
            pl.BlockSpec((Q, INNER), lambda i: (i, 0)),
            pl.BlockSpec((Q, 128), lambda i: (i, 0)),
            pl.BlockSpec((1, STATE, INNER), lambda i: (i, 0, 0)),
            const_spec((1, INNER)),
        ],
        out_shape=[
            jax.ShapeDtypeStruct((2, n, INNER), BF16),
            jax.ShapeDtypeStruct((n, INNER), F32),
            jax.ShapeDtypeStruct((n, 128), F32),
            jax.ShapeDtypeStruct((steps, STATE, INNER), F32),
            jax.ShapeDtypeStruct((1, INNER), F32),
        ],
        scratch_shapes=[
            pltpu.VMEM((Q + 8, XBC), F32),
            pltpu.VMEM((Q, 128), F32),
            pltpu.VMEM((STATE, INNER), F32),
            pltpu.VMEM((Q, INNER), F32),
            pltpu.VMEM((Q, INNER), F32),
            pltpu.VMEM((128, Q), F32),
        ],
        compiler_params=pltpu.CompilerParams(
            dimension_semantics=("arbitrary",), vmem_limit_bytes=48 * 2**20),
        cost_estimate=pl.CostEstimate(
            flops=30 * 10**9, bytes_accessed=40 * 2**20, transcendentals=10**7),
    )(bound, z, proj, gm, e2, et, *params)


def backward_kernel(
    bound_ref, proj_ref, before_ref, dy_ref, through_ref, state_ref,
    e_ref, et_ref, convw_ref, convb_ref, dtb_ref, alog_ref, skip_ref,
    gp_ref, window_ref, small_ref,
    gskip_ref, gsmall_ref, ext_ref, dt_ref, lam_ref, dsum_ref, xd_ref, g_ref, gnext_ref, cumt_ref,
):
    step = pl.program_id(0)
    steps = pl.num_programs(0)
    bound = bound_ref[0]
    t0 = (steps - 1 - step) * Q

    @pl.when(step == 0)
    def _():
        lam_ref[...] = jnp.zeros_like(lam_ref)
        dsum_ref[...] = jnp.zeros_like(dsum_ref)
        dt_ref[...] = jnp.zeros_like(dt_ref)
        gnext_ref[Q : Q + 8, :] = jnp.zeros((8, XBC), F32)
        gskip_ref[...] = jnp.zeros_like(gskip_ref)
        small_ref[...] = jnp.zeros_like(small_ref)
        gsmall_ref[...] = jnp.zeros_like(gsmall_ref)

    rows, rr, cc = chunk_masks(t0, bound)
    dy = dy_ref[...]
    first_chunk = (t0 > 0).astype(F32)
    ext_ref[0:8, :] = before_ref[:, :XBC] * first_chunk
    ext_ref[8 : 8 + Q, :] = proj_ref[:, :XBC]
    pre = conv_rows(ext_ref, convw_ref, convb_ref, rows, bound)
    sig_pre = sigmoid(pre)
    conv_out = pre * sig_pre
    x = conv_out[:, :INNER]
    b_rows = conv_out[:, INNER : INNER + STATE]
    c_rows = conv_out[:, INNER + STATE :]
    dt_ref[:, 0:HEADS] = proj_ref[:, XBC:LATE]
    dt_in, dt_pos, rate, cum = decay_parts(dt_ref[...], dtb_ref, alog_ref, rr, cc)
    cum_end = cum[Q - 1 : Q, :]
    keep = jnp.logical_or(rows < bound, bound < t0).astype(F32)
    in_last = jnp.logical_or(rows >= bound, bound > t0 + Q - 1).astype(F32)
    whole = jnp.logical_or(bound < t0, bound > t0 + Q - 1).astype(F32)
    from_start = jnp.exp(cum) * keep
    to_end = jnp.exp(cum_end - cum) * in_last
    carry_scale = jnp.exp(cum_end) * whole
    allowed_t = jnp.logical_and(rr <= cc, (cc >= bound) == (rr >= bound))
    cumt_ref[...] = cum.T
    c_t = c_rows.T
    gram_t = dot(wide_left(b_rows), tall_right(c_t))
    dt_all = expand(dt_pos, e_ref)
    end_all = expand(to_end, e_ref)
    xd = x * dt_all
    xd_ref[...] = xd
    skip = skip_ref[...]
    gskip_ref[...] += jnp.sum(dy * x, axis=0, keepdims=True)
    lam = lam_ref[...]
    lam_hi, lam_lo = split2(lam)
    g_ref[...] = (
        dot(wide_left(b_rows), jnp.concatenate([lam_hi, lam_hi, lam_lo], axis=0)) * end_all
    )
    xw_hi, xw_lo = split2(xd * end_all)
    grad_b = dot_nt(xw_hi, lam_hi) + (dot_nt(xw_hi, lam_lo) + dot_nt(xw_lo, lam_hi))
    state = state_ref[0]
    st_hi, st_lo = split2(state)
    dye = dy * expand(from_start, e_ref)
    dye_hi, dye_lo = split2(dye)
    grad_c = dot_nt(dye_hi, st_hi) + (dot_nt(dye_hi, st_lo) + dot_nt(dye_lo, st_hi))
    scale_all = expand(jnp.broadcast_to(carry_scale, (Q, Q)), e_ref)
    lam_new = lam * scale_all + dot(
        wide_left(c_t), jnp.concatenate([dye_hi, dye_hi, dye_lo], axis=0)
    )
    lam_ref[...] = lam_new
    ended = dsum_ref[0:1, :]
    first = iota((Q, Q), 1) < HEADDIM
    first_row = iota((Q, Q), 0) < HEADDIM
    gram_grad = jnp.zeros((Q, Q), F32)
    for pair in range(PAIRS):
        lanes = slice(pair * 128, pair * 128 + 128)
        weights = []
        for head in (2 * pair, 2 * pair + 1):
            differ = cumt_ref[head : head + 1, :] - cum[:, head : head + 1]
            weights.append(jnp.exp(jnp.where(allowed_t, differ, NEG)))
        left = jnp.concatenate([gram_t * weights[0], gram_t * weights[1]], axis=1)
        left = jnp.concatenate(split2(left), axis=0)
        dyp = dy_ref[:, lanes]
        diag = jnp.concatenate([jnp.where(first, dyp, 0.0), jnp.where(first, 0.0, dyp)], axis=0)
        out = dot(left, jnp.concatenate(split2(diag), axis=1))
        g_ref[:, lanes] += out[:Q, :128] + (out[:Q, 128:] + out[Q:, :128])
        dyt = dyp.T
        right = jnp.concatenate(
            [jnp.where(first_row, dyt, 0.0), jnp.where(first_row, 0.0, dyt)], axis=1)
        outer = dot(wide_left(xd_ref[:, lanes]), tall_right(right))
        gram_grad = gram_grad + (outer[:, :128] * weights[0] + outer[:, 128:] * weights[1])
    g = g_ref[...]
    grad_x = dt_all * g + skip * dy
    direct = head_sum(x * g, et_ref)
    balance = through_ref[...] - dt_pos * direct
    keep_t = allowed_t.astype(F32).astype(BF16)
    b_hi, b_mid, b_lo = split3(balance)
    grad_step = dot(keep_t, b_hi) + dot(keep_t, b_mid) + dot(keep_t, b_lo) + in_last * ended
    dsum_ref[...] = head_sum(
        jnp.broadcast_to(jnp.sum(lam_new * state, axis=0, keepdims=True), (8, INNER)), et_ref)
    grad_dt = (direct + rate * grad_step) * sigmoid(dt_in)
    gsmall_ref[0:1, :] += jnp.sum(grad_dt, axis=0, keepdims=True)
    gsmall_ref[1:2, :] += rate * jnp.sum(dt_pos * grad_step, axis=0, keepdims=True)
    gp_ref[:, XBC:LATE] = grad_dt[:, 0:HEADS].astype(BF16)
    grad_c = grad_c + dot(wide_left(gram_grad.T), tall_right(b_rows))
    grad_b = grad_b + dot(wide_left(gram_grad), tall_right(c_rows))
    slope = sig_pre * (1.0 + pre * (1.0 - sig_pre))
    gnext_ref[0:Q, :INNER] = grad_x * slope[:, :INNER]
    gnext_ref[0:Q, INNER : INNER + STATE] = grad_b * slope[:, INNER : INNER + STATE]
    gnext_ref[0:Q, INNER + STATE :] = grad_c * slope[:, INNER + STATE :]
    gcp = gnext_ref[0:Q, :]
    small_ref[4:5, :] += jnp.sum(gcp, axis=0, keepdims=True)
    small_ref[3:4, :] += jnp.sum(gcp * ext_ref[8 : 8 + Q, :], axis=0, keepdims=True)
    total = convw_ref[3:4, :] * gcp
    for back in (1, 2, 3):
        ok = jnp.logical_or(rows - back >= bound, rows < bound).astype(F32)
        small_ref[3 - back : 4 - back, :] += jnp.sum(
            gcp * (ext_ref[8 - back : 8 - back + Q, :] * ok), axis=0, keepdims=True)
        okn = jnp.logical_or(rows >= bound, rows + back < bound).astype(F32)
        total = total + convw_ref[3 - back : 4 - back, :] * (gnext_ref[back : back + Q, :] * okn)
    total = total.astype(BF16)
    gp_ref[:, :XBC] = total
    window_ref[0] = total[:, :WINDOW]
    window_ref[1] = total[:, XBC - WINDOW :]
    gnext_ref[Q : Q + 8, :] = gnext_ref[0:8, :]

    @pl.when(step == steps - 1)
    def _():
        skips = head_sum(jnp.broadcast_to(gskip_ref[...], (8, INNER)), et_ref)
        small_ref[6:7, D : D + 128] = gsmall_ref[0:1, :]
        small_ref[6:7, D + 128 : D + 256] = gsmall_ref[1:2, :]
        small_ref[6:7, D + 256 : D + 384] = skips[0:1, :]


def run_backward(proj, dy, through, states, bound, e2, et, params):
    n = proj.shape[0]
    steps = n // Q

    def rev(i):
        return (steps - 1 - i, 0)

    return pl.pallas_call(
        backward_kernel,
        grid=(steps,),
        in_specs=[
            pl.BlockSpec(memory_space=pltpu.SMEM),
            pl.BlockSpec((Q, LATE), rev),
            pl.BlockSpec((8, LATE), lambda i: (jnp.maximum((steps - 1 - i) * (Q // 8) - 1, 0), 0)),
            pl.BlockSpec((Q, INNER), rev),
            pl.BlockSpec((Q, 128), rev),
            pl.BlockSpec((1, STATE, INNER), lambda i: (steps - 1 - i, 0, 0)),
            const_spec((256, INNER)), const_spec((INNER, 128)),
            const_spec((8, XBC)), const_spec((1, XBC)), const_spec((1, 128)),
            const_spec((1, 128)), const_spec((1, INNER)),
        ],
        out_specs=[
            pl.BlockSpec((Q, LATE), rev),
            pl.BlockSpec((2, Q, WINDOW), lambda i: (0, steps - 1 - i, 0)),
            const_spec((8, XBC)),
        ],
        out_shape=[
            jax.ShapeDtypeStruct((n, LATE), BF16),
            jax.ShapeDtypeStruct((2, n, WINDOW), BF16),
            jax.ShapeDtypeStruct((8, XBC), F32),
        ],
        scratch_shapes=[
            pltpu.VMEM((1, INNER), F32),
            pltpu.VMEM((8, 128), F32),
            pltpu.VMEM((Q + 8, XBC), F32),
            pltpu.VMEM((Q, 128), F32),
            pltpu.VMEM((STATE, INNER), F32),
            pltpu.VMEM((8, 128), F32),
            pltpu.VMEM((Q, INNER), F32),
            pltpu.VMEM((Q, INNER), F32),
            pltpu.VMEM((Q + 8, XBC), F32),
            pltpu.VMEM((128, Q), F32),
        ],
        compiler_params=pltpu.CompilerParams(
            dimension_semantics=("arbitrary",), vmem_limit_bytes=48 * 2**20),
        cost_estimate=pl.CostEstimate(
            flops=50 * 10**9, bytes_accessed=50 * 2**20, transcendentals=2 * 10**7),
    )(bound, proj, proj, dy, through, states, e2, et, *params[:5])


BETA_ONE = 0.9
BETA_TWO = 0.95
EPS_ADAM = 1e-08
LANES = 128
NORM_ROWS = D // LANES
IN_ROWS = PROJ * D // LANES
CONVW_ROWS = CONV * XBC // LANES
CONVB_ROWS = XBC // LANES
GAIN_ROWS = INNER // LANES
OUT_ROWS = INNER * D // LANES
DT_ROWS = HEADS * D // LANES
SMALL_ROWS = DT_ROWS + CONVW_ROWS + CONVB_ROWS + 3 + GAIN_ROWS
OUT_START = NORM_ROWS + IN_ROWS + SMALL_ROWS - DT_ROWS
LATE_START = NORM_ROWS + INNER * NORM_ROWS
LEAD = 896
STAGE_ROWS = 16264
ADAM_BLOCKS = 10
F16_TOP = 30000.0


PREP_STEPS = 7
IN_BLOCK = 512
OUT_BLOCK = 256
SMALL_START = NORM_ROWS + IN_ROWS


def prepare_kernel(
    flat_ref,
    in_ref, out_ref, norm_ref, convw_ref, convb_ref, dtb_ref, alog_ref, skip_ref, gain_ref,
    e_ref, et_ref,
    stage_ref,
):
    step = pl.program_id(0)

    @pl.when(step == 0)
    def _():
        rows = flat_ref[0:16, :].astype(F32)
        for lane in range(NORM_ROWS):
            norm_ref[:, lane * LANES : lane * LANES + LANES] = rows[lane : lane + 1, :]
        low = SMALL_START // 16 * 16
        stage_ref[0:112, :] = flat_ref[low : low + 112, :].astype(F32)
        at = SMALL_START - low
        convw_ref[...] = jnp.zeros_like(convw_ref)
        for tap in range(CONV):
            for lane in range(CONVB_ROWS):
                convw_ref[tap : tap + 1, lane * LANES : lane * LANES + LANES] = stage_ref[
                    at : at + 1, :]
                at += 1
        for lane in range(CONVB_ROWS):
            convb_ref[:, lane * LANES : lane * LANES + LANES] = stage_ref[at : at + 1, :]
            at += 1
        heads = iota((1, LANES), 1) < HEADS
        dtb_ref[...] = jnp.where(heads, stage_ref[at : at + 1, :], 0.0)
        alog_ref[...] = jnp.where(heads, stage_ref[at + 1 : at + 2, :], 0.0)
        skips = jnp.where(heads, stage_ref[at + 2 : at + 3, :], 0.0)
        at += 3
        for lane in range(GAIN_ROWS):
            gain_ref[:, lane * LANES : lane * LANES + LANES] = stage_ref[at : at + 1, :]
            at += 1
        one = (iota((128, INNER), 1) // HEADDIM == iota((128, INNER), 0)).astype(F32).astype(BF16)
        e_ref[0:128, :] = one
        e_ref[128:256, :] = one
        et_ref[...] = (
            iota((INNER, 128), 0) // HEADDIM == iota((INNER, 128), 1)).astype(F32).astype(BF16)
        skip_ref[...] = dot(jnp.broadcast_to(skips, (16, LANES)).astype(BF16), one)[0:1, :]

    def block(start, offset, rows, dest_ref):
        size = rows * NORM_ROWS + 16
        at = pl.multiple_of(start + step * (rows * NORM_ROWS), 16)
        stage_ref[0:size, :] = flat_ref[pl.ds(at, size), :].astype(F32)
        for lane in range(NORM_ROWS):
            dest_ref[:, lane * LANES : lane * LANES + LANES] = stage_ref[
                pl.ds(offset + lane, rows, stride=NORM_ROWS), :].astype(BF16)

    block(0, NORM_ROWS, IN_BLOCK, in_ref)

    @pl.when(step < INNER // OUT_BLOCK)
    def _():
        low = OUT_START // 16 * 16
        block(low, OUT_START - low, OUT_BLOCK, out_ref)


def run_prepare(flat):
    vector = lambda n: jax.ShapeDtypeStruct((1, n), F32)
    return pl.pallas_call(
        prepare_kernel,
        grid=(PREP_STEPS,),
        in_specs=[const_spec(flat.shape)],
        out_specs=[
            pl.BlockSpec((IN_BLOCK, D), lambda i: (i, 0)),
            pl.BlockSpec((OUT_BLOCK, D), lambda i: (jnp.minimum(i, INNER // OUT_BLOCK - 1), 0)),
            const_spec((1, D)), const_spec((8, XBC)), const_spec((1, XBC)), const_spec((1, 128)),
            const_spec((1, 128)), const_spec((1, INNER)), const_spec((1, INNER)),
            const_spec((256, INNER)), const_spec((INNER, 128)),
        ],
        out_shape=[
            jax.ShapeDtypeStruct((PROJ, D), BF16), jax.ShapeDtypeStruct((INNER, D), BF16),
            vector(D), jax.ShapeDtypeStruct((8, XBC), F32), vector(XBC), vector(128), vector(128),
            vector(INNER), vector(INNER),
            jax.ShapeDtypeStruct((256, INNER), BF16), jax.ShapeDtypeStruct((INNER, 128), BF16),
        ],
        scratch_shapes=[pltpu.VMEM((IN_BLOCK * NORM_ROWS + 16, LANES), F32)],
        compiler_params=pltpu.CompilerParams(
            dimension_semantics=("arbitrary",), vmem_limit_bytes=40 * 2**20),
        cost_estimate=pl.CostEstimate(
            flops=10**9, bytes_accessed=16 * 2**20, transcendentals=0),
    )(flat)


def adam_kernel(
    who_ref, rate_ref, early_ref, early_other_ref, late_ref, late_other_ref, small_ref,
    weight_ref, first_ref, second_ref,
    grad_ref, first_out_ref, second_out_ref, ratio_ref,
    stage_ref,
):
    step = pl.program_id(0)
    upper = who_ref[0]
    mine = who_ref[1]
    block = weight_ref.shape[0]
    half = 2 * block * ADAM_BLOCKS

    @pl.when(step == 0)
    def _():
        early_at = LEAD + jnp.where(upper == 1, OUT_START - half, NORM_ROWS)
        window = LATE_START + (XBC - WINDOW) * NORM_ROWS
        late_at = LEAD + jnp.where(upper == 1, window - half, LATE_START)
        for source_ref, at, which in (
            (late_ref, late_at, mine), (late_other_ref, late_at, 1 - mine),
            (early_ref, early_at, mine), (early_other_ref, early_at, 1 - mine),
        ):
            size = source_ref.shape[0]
            start = at + which * (size * NORM_ROWS)
            for lane in range(NORM_ROWS):
                stage_ref[pl.ds(start + lane, size, stride=NORM_ROWS), :] = source_ref[
                    :, lane * LANES : lane * LANES + LANES]

        @pl.when(upper == 0)
        def _():
            for lane in range(NORM_ROWS):
                stage_ref[LEAD + lane : LEAD + lane + 1, :] = small_ref[
                    6:7, lane * LANES : lane * LANES + LANES]

        @pl.when(upper == 1)
        def _():
            at = LEAD + OUT_START - half - SMALL_ROWS
            for lane in range(NORM_ROWS):
                stage_ref[pl.ds(at + lane, HEADS, stride=NORM_ROWS), :] = small_ref[
                    8 : 8 + HEADS, lane * LANES : lane * LANES + LANES]
            at += DT_ROWS
            places = [(k, j) for k in range(CONV + 1) for j in range(CONVB_ROWS)]
            places += [(6, NORM_ROWS + j) for j in range(3)]
            places += [(5, j) for j in range(GAIN_ROWS)]
            for number, (line, lane) in enumerate(places):
                stage_ref[at + number : at + number + 1, :] = small_ref[
                    line : line + 1, lane * LANES : lane * LANES + LANES]
            at = LEAD + OUT_START + OUT_ROWS - half
            stage_ref[at : LEAD + half, :] = jnp.zeros((LEAD + half - at, LANES), F32)

    @pl.when(step > 0)
    def _():
        at = LEAD + mine * (half // 2) + (step - 1) * block
        grad = stage_ref[pl.ds(pl.multiple_of(at, 8), block), :]
        grad_ref[...] = grad
        first = BETA_ONE * first_ref[...] + (1.0 - BETA_ONE) * grad
        second = BETA_TWO * second_ref[...] + (1.0 - BETA_TWO) * grad * grad
        first_out_ref[...] = first
        second_out_ref[...] = second
        ratio_ref[...] = (first * rate_ref[0]) / (jnp.sqrt(second * rate_ref[1]) + EPS_ADAM)


def run_adam(who, rates, early, early_other, late, late_other, small, weight, first, second):
    rows = weight.shape[0]
    block = rows // ADAM_BLOCKS

    def at(i):
        return (jnp.maximum(i - 1, 0), 0)

    spec = pl.BlockSpec((block, LANES), at)
    out = jax.ShapeDtypeStruct((rows, LANES), F32)
    return pl.pallas_call(
        adam_kernel,
        grid=(ADAM_BLOCKS + 1,),
        in_specs=[
            pl.BlockSpec(memory_space=pltpu.SMEM), pl.BlockSpec(memory_space=pltpu.SMEM),
            const_spec(early.shape), const_spec(early.shape),
            const_spec(late.shape), const_spec(late.shape), const_spec(small.shape),
            spec, spec, spec,
        ],
        out_specs=[spec, spec, spec, spec],
        out_shape=[out, out, out, out],
        scratch_shapes=[pltpu.VMEM((STAGE_ROWS, LANES), F32)],
        compiler_params=pltpu.CompilerParams(
            dimension_semantics=("arbitrary",), vmem_limit_bytes=48 * 2**20),
        cost_estimate=pl.CostEstimate(
            flops=10**8, bytes_accessed=36 * 2**20, transcendentals=10**6),
    )(who, rates, early, early_other, late, late_other, small, weight, first, second)


def swap(values, axis, bit):
    size = lax.axis_size(axis)
    return lax.ppermute(values, axis, [(i, i ^ bit) for i in range(size)])


def top_block(values):
    return jnp.broadcast_to(jnp.max(jnp.abs(values)), (8, LANES))


def to_wire(values, top):
    return (values * (F16_TOP / jnp.maximum(top[0, 0], 1e-30))).astype(jnp.float16)


def from_wire(values, top):
    return values.astype(F32) * (top[0, 0] * (1.0 / F16_TOP))


def halve(values, top, axis, bit):
    side = (lax.axis_index(axis) // bit) % 2
    keep = lax.dynamic_index_in_dim(values, side, 0, keepdims=False)
    send = lax.dynamic_index_in_dim(values, 1 - side, 0, keepdims=False)
    got = swap(to_wire(send, top), axis, bit)
    got_top = swap(top, axis, bit)
    return keep + from_wire(got, got_top), top + got_top


def data_bits():
    return [1 << k for k in range(lax.axis_size("dp").bit_length() - 1)]


def halve_data(values, top, bit):
    rows = values.shape[0] // 2
    return halve(values.reshape(2, rows, D), top, "dp", bit)


def double_data(wire, bit):
    side = (lax.axis_index("dp") // bit) % 2
    got = swap(wire, "dp", bit)
    return jnp.where(side == 0, jnp.concatenate([wire, got]), jnp.concatenate([got, wire]))


def dot_tn(a, b):
    return lax.dot_general(a, b, (((0,), (0,)), ((), ())), preferred_element_type=F32)


def pick_rows(index, rows):
    chosen = index[:, None] == jnp.arange(rows.shape[0], dtype=jnp.int32)[None, :]
    return dot(chosen.astype(BF16), rows).astype(BF16)


def on_device(
    tokens, loss_sensitivity, lengths, holder_sequence_list, master, moment_one, moment_two,
    adam_rates, iteration_tally,
):
    group_devices = lax.axis_size("zero")
    data_devices = lax.axis_size("dp")
    zero_index = lax.axis_index("zero")
    dp_index = lax.axis_index("dp")
    seq_len = loss_sensitivity.shape[1]
    group_seqs = tokens.shape[0]
    span = tokens.shape[1]
    slots = group_seqs // data_devices
    shard_rows = master.shape[0] // LANES
    tie = lax.optimization_barrier

    own = master.reshape(shard_rows, LANES)
    flat = lax.all_gather(own.astype(BF16), "zero", axis=0, tiled=True)

    arranged = holder_sequence_list.reshape(data_devices, group_devices, slots)
    group_order = lax.dynamic_index_in_dim(arranged, zero_index, 1, keepdims=False).reshape(-1)
    local_ids = group_order - zero_index * group_seqs
    dealt = tokens.at[local_ids].get(mode="promise_in_bounds")
    local_tok = lax.all_to_all(dealt, "dp", split_axis=0, concat_axis=0, tiled=True)
    my_seqs = lax.dynamic_slice_in_dim(group_order, dp_index * slots, slots)
    bound = lengths[my_seqs[0]]
    positions = jnp.arange(seq_len, dtype=jnp.int32)

    in_w, out_w, norm_gain, *params, e2, et = run_prepare(flat)
    cot = loss_sensitivity[0]
    gm = dot_nt(cot, out_w)
    local_tok, in_w, gm = tie((local_tok, in_w, gm))
    own_late, _ = tie((own, flat[:8]))
    whole_master = lax.all_gather(own_late, "zero", axis=0, tiled=True)

    def place(slot, at):
        return (at // span) * (slots * span) + slot * span + at % span

    source = jnp.where(positions < bound, place(0, positions), place(1, positions - bound))
    packed = pick_rows(source, local_tok.reshape(slots * seq_len, D))
    blocks = jnp.arange(data_devices, dtype=jnp.int32)[:, None, None] * span
    within = blocks + jnp.arange(span, dtype=jnp.int32)[None, None, :]
    within = within + jnp.arange(slots, dtype=jnp.int32)[None, :, None] * bound
    unpack_rows = jnp.minimum(within, seq_len - 1).reshape(-1)

    def spread(rows):
        return pick_rows(unpack_rows, rows).reshape(data_devices * slots, span, D)

    def send_back(picked):
        return lax.all_to_all(picked, "dp", split_axis=0, concat_axis=0, tiled=True)

    restore = jnp.zeros_like(local_ids).at[local_ids].set(
        jnp.arange(group_seqs, dtype=jnp.int32))
    mine = lax.dynamic_slice_in_dim(lengths, zero_index * group_seqs, group_seqs)
    at = dp_index * span + jnp.arange(span, dtype=jnp.int32)
    live = (at[None, :] < mine[:, None])[:, :, None]

    bound_arr = bound.reshape(1)
    tok = packed.astype(F32)
    rinv = lax.rsqrt(jnp.mean(tok * tok, axis=1, keepdims=True) + EPS_NORM)
    nhat = tok * rinv
    normed = (nhat * norm_gain).astype(BF16)
    proj_z = dot_nt(normed, in_w[:INNER])
    proj = dot_nt(normed, in_w[INNER:])
    pair, dy, through, states, ggain = run_forward(proj_z, proj, gm, bound_arr, e2, et, params)
    result = (tok + dot(pair[1], out_w)).astype(BF16)
    picked = spread(result)
    picked, pair = tie((picked, pair))
    back_out = send_back(picked)
    early = lax.dot_general(
        pair, jnp.stack([normed, cot]), (((1,), (1,)), ((0,), (0,))), preferred_element_type=F32)
    early = jnp.swapaxes(early.reshape(2, 2, INNER // 2, D), 0, 1)
    early, early_top = halve(early, top_block(early), "zero", 1)
    part_normed = dot(pair[0], in_w[:INNER])
    early, early_top, part_normed, dy = tie((early, early_top, part_normed, dy))
    early, early_top = halve(early, early_top, "zero", 2)
    gp, window, small8 = run_backward(proj, dy, through, states, bound_arr, e2, et, params)
    gp, window, back_out, early, early_top, whole_master = tie(
        (gp, window, back_out, early, early_top, whole_master))

    bits = data_bits()
    late = lax.dot_general(
        window, jnp.stack([normed, normed]), (((1,), (1,)), ((0,), (0,))),
        preferred_element_type=F32)
    late, gp = tie((late, gp))
    late = jnp.swapaxes(late.reshape(2, 2, WINDOW // 2, D), 0, 1)
    late, late_top = halve(late, top_block(late), "zero", 1)
    early, early_top = halve_data(early, early_top, bits[0])
    grad_normed = part_normed + dot(gp, in_w[INNER:])
    late, late_top, early, early_top, grad_normed = tie(
        (late, late_top, early, early_top, grad_normed))
    late, late_top = halve(late, late_top, "zero", 2)
    for bit in bits[1:-1]:
        early, early_top = halve_data(early, early_top, bit)
    gng = grad_normed * norm_gain
    grad_norm_gain = jnp.sum(nhat * grad_normed, axis=0, keepdims=True)
    grad_tok = cot.astype(F32) + rinv * (gng - nhat * jnp.mean(nhat * gng, axis=1, keepdims=True))
    grad_tok = grad_tok.astype(BF16)
    small8 = small8 + jnp.pad(ggain, ((5, 2), (0, XBC - INNER)))
    small8 = small8 + jnp.pad(grad_norm_gain, ((6, 1), (0, XBC - D)))
    small = jnp.concatenate([
        small8, jnp.pad(dot_tn(gp[:, XBC:], normed), ((0, 0), (0, XBC - D)))])
    late, late_top, early, early_top, small, grad_tok = tie(
        (late, late_top, early, early_top, small, grad_tok))
    late, late_top = halve_data(late, late_top, bits[0])
    early, early_top = halve_data(early, early_top, bits[-1])
    early = to_wire(early, early_top)
    small = small + swap(small, "dp", bits[0])
    picked_grad = spread(grad_tok)
    late, late_top, early, small, picked_grad = tie((late, late_top, early, small, picked_grad))
    for bit in bits[1:-1]:
        late, late_top = halve_data(late, late_top, bit)
        small = small + swap(small, "dp", bit)
        early = double_data(early, bits[-1]) if bit == bits[1] else early
    back_rows = back_out.at[restore].get(mode="promise_in_bounds")
    late, late_top, early, small, back_rows = tie((late, late_top, early, small, back_rows))
    late, late_top = halve_data(late, late_top, bits[-1])
    late = to_wire(late, late_top)
    for bit in reversed(bits[1:-1]):
        early = double_data(early, bit)
    small = small + swap(small, "dp", bits[-1])
    tokens_out = jnp.where(live, back_rows, tokens)
    late, early, small, tokens_out = tie((late, early, small, tokens_out))
    late = double_data(late, bits[-1])
    early = from_wire(double_data(early, bits[0]), early_top)
    small = small + swap(small, "zero", 1)
    late, early, small = tie((late, early, small))
    for bit in reversed(bits[1:-1]):
        late = double_data(late, bit)
    early_other = swap(early, "zero", 1)
    small = small + swap(small, "zero", 2)
    late, early_other, small = tie((late, early_other, small))
    late = from_wire(double_data(late, bits[0]), late_top)
    late, picked_grad = tie((late, picked_grad))
    late_other = swap(late, "zero", 1)
    back_grad = send_back(picked_grad)
    grad_tokens = jnp.where(
        live, back_grad.at[restore].get(mode="promise_in_bounds"), jnp.zeros((), BF16))

    steps_f = iteration_tally[0].astype(F32)
    rates = jnp.stack([
        1.0 / (1.0 - jnp.power(BETA_ONE, steps_f)), 1.0 / (1.0 - jnp.power(BETA_TWO, steps_f))])
    who = jnp.stack([zero_index // 2, zero_index % 2]).astype(jnp.int32)
    grad_shard, first_next, second_next, ratio = run_adam(
        who, rates, early, early_other, late, late_other, small,
        own, moment_one.reshape(shard_rows, LANES), moment_two.reshape(shard_rows, LANES))
    ratios = lax.all_gather(ratio.astype(jnp.float16), "zero", axis=0, tiled=True).astype(F32)
    new_master = whole_master - adam_rates[0] * (ratios + adam_rates[1] * whole_master)
    return (
        tokens_out, grad_tokens, new_master.reshape(-1), grad_shard.reshape(-1),
        first_next.reshape(-1), second_next.reshape(-1))


def solution(mesh):
    return jax.shard_map(
        on_device,
        mesh=mesh,
        in_specs=(
            P("zero", "dp", None), P(("dp", "zero"), None, None), P(), P(),
            P("zero"), P("zero"), P("zero"), P(), P(),
        ),
        out_specs=(
            P("zero", "dp", None), P("zero", "dp", None), P(), P("zero"), P("zero"), P("zero"),
        ),
        check_vma=False,
    )
```

```python
import jax
import jax.numpy as jnp
from jax import lax
from jax.experimental import pallas as pl
from jax.experimental.pallas import tpu as pltpu
from jax.sharding import PartitionSpec as P

D = 768
HEADS = 24
HEADDIM = 64
STATE = 128
CONV = 4
INNER = 1536
XBC = 1792
PROJ = 3352
Q = 128
LATE = PROJ - INNER
WINDOW = 1024
PAIRS = HEADS // 2
EPS_NORM = 1e-05
NEG = -1e30
F32 = jnp.float32
BF16 = jnp.bfloat16


def dot(a, b):
    return lax.dot_general(a, b, (((1,), (0,)), ((), ())), preferred_element_type=F32)


def dot_nt(a, b):
    return lax.dot_general(a, b, (((1,), (1,)), ((), ())), preferred_element_type=F32)


def split2(v):
    hi = v.astype(BF16)
    return hi, (v - hi.astype(F32)).astype(BF16)


def split3(v):
    hi = v.astype(BF16)
    rest = v - hi.astype(F32)
    mid = rest.astype(BF16)
    return hi, mid, (rest - mid.astype(F32)).astype(BF16)


def wide_left(v):
    hi, lo = split2(v)
    return jnp.concatenate([hi, lo, hi], axis=1)


def tall_right(v):
    hi, lo = split2(v)
    return jnp.concatenate([hi, hi, lo], axis=0)


def exact_left(v):
    return jnp.concatenate(split3(v), axis=1)


def sigmoid(v):
    return 1.0 / (1.0 + jnp.exp(-v))


def softplus(v):
    return jnp.maximum(v, 0.0) + jnp.log1p(jnp.exp(-jnp.abs(v)))


def iota(shape, dim):
    return lax.broadcasted_iota(jnp.int32, shape, dim)


def expand(v, e_ref):
    hi, lo = split2(v)
    return dot(jnp.concatenate([hi, lo], axis=1), e_ref[...])


def head_sum(v, et_ref):
    hi, lo = split2(v)
    return dot(hi, et_ref[...]) + dot(lo, et_ref[...])


def chunk_masks(t0, bound):
    rows = t0 + iota((Q, 1), 0)
    rr = t0 + iota((Q, Q), 0)
    cc = t0 + iota((Q, Q), 1)
    return rows, rr, cc


def conv_rows(ext_ref, w_ref, b_ref, rows, bound):
    total = b_ref[...] + w_ref[3:4, :] * ext_ref[8 : 8 + Q, :]
    for back in (1, 2, 3):
        ok = jnp.logical_or(rows - back >= bound, rows < bound).astype(F32)
        total = total + w_ref[3 - back : 4 - back, :] * (ext_ref[8 - back : 8 - back + Q, :] * ok)
    return total


def decay_parts(dt_raw, dtb_ref, alog_ref, rr, cc):
    dt_in = dt_raw + dtb_ref[...]
    dt_pos = softplus(dt_in)
    rate = -jnp.exp(alog_ref[...])
    step = dt_pos * rate
    tri = (cc <= rr).astype(F32).astype(BF16)
    s_hi, s_mid, s_lo = split3(step)
    cum = dot(tri, s_hi) + dot(tri, s_mid) + dot(tri, s_lo)
    return dt_in, dt_pos, rate, cum


def forward_kernel(
    bound_ref, z_ref, proj_ref, gm_ref, e_ref, et_ref, convw_ref, convb_ref, dtb_ref, alog_ref,
    skip_ref, gain_ref,
    pair_ref, dy_ref, through_ref, state_ref, ggain_ref, zmax_ref,
    ext_ref, dt_ref, carry_ref, xd_ref, acc_ref, cumt_ref,
):
    step = pl.program_id(0)
    bound = bound_ref[0]
    t0 = step * Q

    @pl.when(step == 0)
    def _():
        ext_ref[0:8, :] = jnp.zeros((8, XBC), F32)
        carry_ref[...] = jnp.zeros_like(carry_ref)
        dt_ref[...] = jnp.zeros_like(dt_ref)
        ggain_ref[...] = jnp.zeros_like(ggain_ref)
        zmax_ref[...] = jnp.zeros_like(zmax_ref)

    rows, rr, cc = chunk_masks(t0, bound)
    ext_ref[8 : 8 + Q, :] = proj_ref[:, :XBC]
    pre = conv_rows(ext_ref, convw_ref, convb_ref, rows, bound)
    ext_ref[0:8, :] = ext_ref[Q : Q + 8, :]
    conv_out = pre * sigmoid(pre)
    x = conv_out[:, :INNER]
    b_rows = conv_out[:, INNER : INNER + STATE]
    c_rows = conv_out[:, INNER + STATE :]
    dt_ref[:, 0:HEADS] = proj_ref[:, XBC:LATE]
    _, dt_pos, _, cum = decay_parts(dt_ref[...], dtb_ref, alog_ref, rr, cc)
    cum_end = cum[Q - 1 : Q, :]
    keep = jnp.logical_or(rows < bound, bound < t0).astype(F32)
    in_last = jnp.logical_or(rows >= bound, bound > t0 + Q - 1).astype(F32)
    whole = jnp.logical_or(bound < t0, bound > t0 + Q - 1).astype(F32)
    from_start = jnp.exp(cum) * keep
    to_end = jnp.exp(cum_end - cum) * in_last
    carry_scale = jnp.exp(cum_end) * whole
    allowed = jnp.logical_and(cc <= rr, (cc >= bound) == (rr >= bound))
    cumt_ref[...] = cum.T

    state = carry_ref[...]
    state_ref[0] = state
    xd = x * expand(dt_pos, e_ref)
    xd_ref[...] = xd
    acc = dot(wide_left(c_rows), tall_right(state)) * expand(from_start, e_ref)
    acc_ref[...] = acc + skip_ref[...] * x
    b_t = b_rows.T
    scale_all = expand(jnp.broadcast_to(carry_scale, (Q, Q)), e_ref)
    carry_ref[...] = state * scale_all + dot(
        wide_left(b_t), tall_right(xd * expand(to_end, e_ref))
    )
    gram = dot(wide_left(c_rows), tall_right(b_t))
    first = iota((Q, Q), 1) < HEADDIM
    for pair in range(PAIRS):
        parts = []
        for head in (2 * pair, 2 * pair + 1):
            differ = cum[:, head : head + 1] - cumt_ref[head : head + 1, :]
            parts.append(gram * jnp.exp(jnp.where(allowed, differ, NEG)))
        left = jnp.concatenate(split2(jnp.concatenate(parts, axis=1)), axis=0)
        lanes = slice(pair * 128, pair * 128 + 128)
        xp = xd_ref[:, lanes]
        diag = jnp.concatenate([jnp.where(first, xp, 0.0), jnp.where(first, 0.0, xp)], axis=0)
        out = dot(left, jnp.concatenate(split2(diag), axis=1))
        acc_ref[:, lanes] += out[:Q, :128] + (out[:Q, 128:] + out[Q:, :128])
    scanned = acc_ref[...]
    z = z_ref[...]
    sig_z = sigmoid(z)
    silu_z = z * sig_z
    gated = scanned * silu_z
    ginv = lax.rsqrt(jnp.mean(gated * gated, axis=1, keepdims=True) + EPS_NORM)
    mhat = gated * ginv
    pair_ref[1] = (mhat * gain_ref[...]).astype(BF16)
    gm = gm_ref[...]
    ggain_ref[...] += jnp.sum(mhat * gm, axis=0, keepdims=True)
    gmg = gm * gain_ref[...]
    ggated = ginv * (gmg - mhat * jnp.mean(mhat * gmg, axis=1, keepdims=True))
    dy = ggated * silu_z
    dy_ref[...] = dy
    grad_z = ggated * scanned * (sig_z * (1.0 + z * (1.0 - sig_z)))
    zmax_ref[...] = jnp.maximum(zmax_ref[...], jnp.max(jnp.abs(grad_z), axis=0, keepdims=True))
    pair_ref[0] = grad_z.astype(BF16)
    through_ref[...] = head_sum(dy * (scanned - skip_ref[...] * x), et_ref)


def const_spec(shape):
    return pl.BlockSpec(shape, lambda *_: (0,) * len(shape))


def run_forward(z, proj, gm, bound, e2, et, params):
    n = proj.shape[0]
    steps = n // Q
    return pl.pallas_call(
        forward_kernel,
        grid=(steps,),
        in_specs=[
            pl.BlockSpec(memory_space=pltpu.SMEM),
            pl.BlockSpec((Q, INNER), lambda i: (i, 0)),
            pl.BlockSpec((Q, LATE), lambda i: (i, 0)),
            pl.BlockSpec((Q, INNER), lambda i: (i, 0)),
            const_spec((256, INNER)), const_spec((INNER, 128)),
            const_spec((8, XBC)), const_spec((1, XBC)), const_spec((1, 128)),
            const_spec((1, 128)), const_spec((1, INNER)), const_spec((1, INNER)),
        ],
        out_specs=[
            pl.BlockSpec((2, Q, INNER), lambda i: (0, i, 0)),
            pl.BlockSpec((Q, INNER), lambda i: (i, 0)),
            pl.BlockSpec((Q, 128), lambda i: (i, 0)),
            pl.BlockSpec((1, STATE, INNER), lambda i: (i, 0, 0)),
            const_spec((1, INNER)), const_spec((1, INNER)),
        ],
        out_shape=[
            jax.ShapeDtypeStruct((2, n, INNER), BF16),
            jax.ShapeDtypeStruct((n, INNER), F32),
            jax.ShapeDtypeStruct((n, 128), F32),
            jax.ShapeDtypeStruct((steps, STATE, INNER), F32),
            jax.ShapeDtypeStruct((1, INNER), F32),
            jax.ShapeDtypeStruct((1, INNER), F32),
        ],
        scratch_shapes=[
            pltpu.VMEM((Q + 8, XBC), F32),
            pltpu.VMEM((Q, 128), F32),
            pltpu.VMEM((STATE, INNER), F32),
            pltpu.VMEM((Q, INNER), F32),
            pltpu.VMEM((Q, INNER), F32),
            pltpu.VMEM((128, Q), F32),
        ],
        compiler_params=pltpu.CompilerParams(
            dimension_semantics=("arbitrary",), vmem_limit_bytes=48 * 2**20),
        cost_estimate=pl.CostEstimate(
            flops=30 * 10**9, bytes_accessed=40 * 2**20, transcendentals=10**7),
    )(bound, z, proj, gm, e2, et, *params)


def backward_kernel(
    bound_ref, proj_ref, before_ref, dy_ref, through_ref, state_ref,
    e_ref, et_ref, convw_ref, convb_ref, dtb_ref, alog_ref, skip_ref,
    gp_ref, window_ref, small_ref,
    gskip_ref, gsmall_ref, ext_ref, dt_ref, lam_ref, dsum_ref, xd_ref, g_ref, gnext_ref, cumt_ref,
):
    step = pl.program_id(0)
    steps = pl.num_programs(0)
    bound = bound_ref[0]
    t0 = (steps - 1 - step) * Q

    @pl.when(step == 0)
    def _():
        lam_ref[...] = jnp.zeros_like(lam_ref)
        dsum_ref[...] = jnp.zeros_like(dsum_ref)
        dt_ref[...] = jnp.zeros_like(dt_ref)
        gnext_ref[Q : Q + 8, :] = jnp.zeros((8, XBC), F32)
        gskip_ref[...] = jnp.zeros_like(gskip_ref)
        small_ref[...] = jnp.zeros_like(small_ref)
        gsmall_ref[...] = jnp.zeros_like(gsmall_ref)

    rows, rr, cc = chunk_masks(t0, bound)
    dy = dy_ref[...]
    first_chunk = (t0 > 0).astype(F32)
    ext_ref[0:8, :] = before_ref[:, :XBC] * first_chunk
    ext_ref[8 : 8 + Q, :] = proj_ref[:, :XBC]
    pre = conv_rows(ext_ref, convw_ref, convb_ref, rows, bound)
    sig_pre = sigmoid(pre)
    conv_out = pre * sig_pre
    x = conv_out[:, :INNER]
    b_rows = conv_out[:, INNER : INNER + STATE]
    c_rows = conv_out[:, INNER + STATE :]
    dt_ref[:, 0:HEADS] = proj_ref[:, XBC:LATE]
    dt_in, dt_pos, rate, cum = decay_parts(dt_ref[...], dtb_ref, alog_ref, rr, cc)
    cum_end = cum[Q - 1 : Q, :]
    keep = jnp.logical_or(rows < bound, bound < t0).astype(F32)
    in_last = jnp.logical_or(rows >= bound, bound > t0 + Q - 1).astype(F32)
    whole = jnp.logical_or(bound < t0, bound > t0 + Q - 1).astype(F32)
    from_start = jnp.exp(cum) * keep
    to_end = jnp.exp(cum_end - cum) * in_last
    carry_scale = jnp.exp(cum_end) * whole
    allowed_t = jnp.logical_and(rr <= cc, (cc >= bound) == (rr >= bound))
    cumt_ref[...] = cum.T
    c_t = c_rows.T
    gram_t = dot(wide_left(b_rows), tall_right(c_t))
    dt_all = expand(dt_pos, e_ref)
    end_all = expand(to_end, e_ref)
    xd = x * dt_all
    xd_ref[...] = xd
    skip = skip_ref[...]
    gskip_ref[...] += jnp.sum(dy * x, axis=0, keepdims=True)
    lam = lam_ref[...]
    lam_hi, lam_lo = split2(lam)
    g_ref[...] = (
        dot(wide_left(b_rows), jnp.concatenate([lam_hi, lam_hi, lam_lo], axis=0)) * end_all
    )
    xw_hi, xw_lo = split2(xd * end_all)
    grad_b = dot_nt(xw_hi, lam_hi) + (dot_nt(xw_hi, lam_lo) + dot_nt(xw_lo, lam_hi))
    state = state_ref[0]
    st_hi, st_lo = split2(state)
    dye = dy * expand(from_start, e_ref)
    dye_hi, dye_lo = split2(dye)
    grad_c = dot_nt(dye_hi, st_hi) + (dot_nt(dye_hi, st_lo) + dot_nt(dye_lo, st_hi))
    scale_all = expand(jnp.broadcast_to(carry_scale, (Q, Q)), e_ref)
    lam_new = lam * scale_all + dot(
        wide_left(c_t), jnp.concatenate([dye_hi, dye_hi, dye_lo], axis=0)
    )
    lam_ref[...] = lam_new
    ended = dsum_ref[0:1, :]
    first = iota((Q, Q), 1) < HEADDIM
    first_row = iota((Q, Q), 0) < HEADDIM
    gram_grad = jnp.zeros((Q, Q), F32)
    for pair in range(PAIRS):
        lanes = slice(pair * 128, pair * 128 + 128)
        weights = []
        for head in (2 * pair, 2 * pair + 1):
            differ = cumt_ref[head : head + 1, :] - cum[:, head : head + 1]
            weights.append(jnp.exp(jnp.where(allowed_t, differ, NEG)))
        left = jnp.concatenate([gram_t * weights[0], gram_t * weights[1]], axis=1)
        left = jnp.concatenate(split2(left), axis=0)
        dyp = dy_ref[:, lanes]
        diag = jnp.concatenate([jnp.where(first, dyp, 0.0), jnp.where(first, 0.0, dyp)], axis=0)
        out = dot(left, jnp.concatenate(split2(diag), axis=1))
        g_ref[:, lanes] += out[:Q, :128] + (out[:Q, 128:] + out[Q:, :128])
        dyt = dyp.T
        right = jnp.concatenate(
            [jnp.where(first_row, dyt, 0.0), jnp.where(first_row, 0.0, dyt)], axis=1)
        outer = dot(wide_left(xd_ref[:, lanes]), tall_right(right))
        gram_grad = gram_grad + (outer[:, :128] * weights[0] + outer[:, 128:] * weights[1])
    g = g_ref[...]
    grad_x = dt_all * g + skip * dy
    direct = head_sum(x * g, et_ref)
    balance = through_ref[...] - dt_pos * direct
    keep_t = allowed_t.astype(F32).astype(BF16)
    b_hi, b_mid, b_lo = split3(balance)
    grad_step = dot(keep_t, b_hi) + dot(keep_t, b_mid) + dot(keep_t, b_lo) + in_last * ended
    dsum_ref[...] = head_sum(
        jnp.broadcast_to(jnp.sum(lam_new * state, axis=0, keepdims=True), (8, INNER)), et_ref)
    grad_dt = (direct + rate * grad_step) * sigmoid(dt_in)
    gsmall_ref[0:1, :] += jnp.sum(grad_dt, axis=0, keepdims=True)
    gsmall_ref[1:2, :] += rate * jnp.sum(dt_pos * grad_step, axis=0, keepdims=True)
    gp_ref[:, XBC:LATE] = grad_dt[:, 0:HEADS].astype(BF16)
    grad_c = grad_c + dot(wide_left(gram_grad.T), tall_right(b_rows))
    grad_b = grad_b + dot(wide_left(gram_grad), tall_right(c_rows))
    slope = sig_pre * (1.0 + pre * (1.0 - sig_pre))
    gnext_ref[0:Q, :INNER] = grad_x * slope[:, :INNER]
    gnext_ref[0:Q, INNER : INNER + STATE] = grad_b * slope[:, INNER : INNER + STATE]
    gnext_ref[0:Q, INNER + STATE :] = grad_c * slope[:, INNER + STATE :]
    gcp = gnext_ref[0:Q, :]
    small_ref[4:5, :] += jnp.sum(gcp, axis=0, keepdims=True)
    small_ref[3:4, :] += jnp.sum(gcp * ext_ref[8 : 8 + Q, :], axis=0, keepdims=True)
    total = convw_ref[3:4, :] * gcp
    for back in (1, 2, 3):
        ok = jnp.logical_or(rows - back >= bound, rows < bound).astype(F32)
        small_ref[3 - back : 4 - back, :] += jnp.sum(
            gcp * (ext_ref[8 - back : 8 - back + Q, :] * ok), axis=0, keepdims=True)
        okn = jnp.logical_or(rows >= bound, rows + back < bound).astype(F32)
        total = total + convw_ref[3 - back : 4 - back, :] * (gnext_ref[back : back + Q, :] * okn)
    small_ref[7:8, :] = jnp.maximum(
        small_ref[7:8, :], jnp.max(jnp.abs(total), axis=0, keepdims=True))
    total = total.astype(BF16)
    gp_ref[:, :XBC] = total
    window_ref[0] = total[:, :WINDOW]
    window_ref[1] = total[:, XBC - WINDOW :]
    gnext_ref[Q : Q + 8, :] = gnext_ref[0:8, :]

    @pl.when(step == steps - 1)
    def _():
        skips = head_sum(jnp.broadcast_to(gskip_ref[...], (8, INNER)), et_ref)
        small_ref[6:7, D : D + 128] = gsmall_ref[0:1, :]
        small_ref[6:7, D + 128 : D + 256] = gsmall_ref[1:2, :]
        small_ref[6:7, D + 256 : D + 384] = skips[0:1, :]


def run_backward(proj, dy, through, states, bound, e2, et, params):
    n = proj.shape[0]
    steps = n // Q

    def rev(i):
        return (steps - 1 - i, 0)

    return pl.pallas_call(
        backward_kernel,
        grid=(steps,),
        in_specs=[
            pl.BlockSpec(memory_space=pltpu.SMEM),
            pl.BlockSpec((Q, LATE), rev),
            pl.BlockSpec((8, LATE), lambda i: (jnp.maximum((steps - 1 - i) * (Q // 8) - 1, 0), 0)),
            pl.BlockSpec((Q, INNER), rev),
            pl.BlockSpec((Q, 128), rev),
            pl.BlockSpec((1, STATE, INNER), lambda i: (steps - 1 - i, 0, 0)),
            const_spec((256, INNER)), const_spec((INNER, 128)),
            const_spec((8, XBC)), const_spec((1, XBC)), const_spec((1, 128)),
            const_spec((1, 128)), const_spec((1, INNER)),
        ],
        out_specs=[
            pl.BlockSpec((Q, LATE), rev),
            pl.BlockSpec((2, Q, WINDOW), lambda i: (0, steps - 1 - i, 0)),
            const_spec((8, XBC)),
        ],
        out_shape=[
            jax.ShapeDtypeStruct((n, LATE), BF16),
            jax.ShapeDtypeStruct((2, n, WINDOW), BF16),
            jax.ShapeDtypeStruct((8, XBC), F32),
        ],
        scratch_shapes=[
            pltpu.VMEM((1, INNER), F32),
            pltpu.VMEM((8, 128), F32),
            pltpu.VMEM((Q + 8, XBC), F32),
            pltpu.VMEM((Q, 128), F32),
            pltpu.VMEM((STATE, INNER), F32),
            pltpu.VMEM((8, 128), F32),
            pltpu.VMEM((Q, INNER), F32),
            pltpu.VMEM((Q, INNER), F32),
            pltpu.VMEM((Q + 8, XBC), F32),
            pltpu.VMEM((128, Q), F32),
        ],
        compiler_params=pltpu.CompilerParams(
            dimension_semantics=("arbitrary",), vmem_limit_bytes=48 * 2**20),
        cost_estimate=pl.CostEstimate(
            flops=50 * 10**9, bytes_accessed=50 * 2**20, transcendentals=2 * 10**7),
    )(bound, proj, proj, dy, through, states, e2, et, *params[:5])


BETA_ONE = 0.9
BETA_TWO = 0.95
EPS_ADAM = 1e-08
LANES = 128
NORM_ROWS = D // LANES
IN_ROWS = PROJ * D // LANES
CONVW_ROWS = CONV * XBC // LANES
CONVB_ROWS = XBC // LANES
GAIN_ROWS = INNER // LANES
OUT_ROWS = INNER * D // LANES
DT_ROWS = HEADS * D // LANES
SMALL_ROWS = DT_ROWS + CONVW_ROWS + CONVB_ROWS + 3 + GAIN_ROWS
OUT_START = NORM_ROWS + IN_ROWS + SMALL_ROWS - DT_ROWS
LATE_START = NORM_ROWS + INNER * NORM_ROWS
LEAD = 896
STAGE_ROWS = 16264
ADAM_BLOCKS = 10
F16_TOP = 30000.0
MARK = 16


PREP_STEPS = 7
IN_BLOCK = 512
OUT_BLOCK = 256
SMALL_START = NORM_ROWS + IN_ROWS


def prepare_kernel(
    flat_ref,
    in_ref, out_ref, norm_ref, convw_ref, convb_ref, dtb_ref, alog_ref, skip_ref, gain_ref,
    e_ref, et_ref,
    stage_ref,
):
    step = pl.program_id(0)

    @pl.when(step == 0)
    def _():
        rows = flat_ref[0:16, :].astype(F32)
        for lane in range(NORM_ROWS):
            norm_ref[:, lane * LANES : lane * LANES + LANES] = rows[lane : lane + 1, :]
        low = SMALL_START // 16 * 16
        stage_ref[0:112, :] = flat_ref[low : low + 112, :].astype(F32)
        at = SMALL_START - low
        convw_ref[...] = jnp.zeros_like(convw_ref)
        for tap in range(CONV):
            for lane in range(CONVB_ROWS):
                convw_ref[tap : tap + 1, lane * LANES : lane * LANES + LANES] = stage_ref[
                    at : at + 1, :]
                at += 1
        for lane in range(CONVB_ROWS):
            convb_ref[:, lane * LANES : lane * LANES + LANES] = stage_ref[at : at + 1, :]
            at += 1
        heads = iota((1, LANES), 1) < HEADS
        dtb_ref[...] = jnp.where(heads, stage_ref[at : at + 1, :], 0.0)
        alog_ref[...] = jnp.where(heads, stage_ref[at + 1 : at + 2, :], 0.0)
        skips = jnp.where(heads, stage_ref[at + 2 : at + 3, :], 0.0)
        at += 3
        for lane in range(GAIN_ROWS):
            gain_ref[:, lane * LANES : lane * LANES + LANES] = stage_ref[at : at + 1, :]
            at += 1
        one = (iota((128, INNER), 1) // HEADDIM == iota((128, INNER), 0)).astype(F32).astype(BF16)
        e_ref[0:128, :] = one
        e_ref[128:256, :] = one
        et_ref[...] = (
            iota((INNER, 128), 0) // HEADDIM == iota((INNER, 128), 1)).astype(F32).astype(BF16)
        skip_ref[...] = dot(jnp.broadcast_to(skips, (16, LANES)).astype(BF16), one)[0:1, :]

    def block(start, offset, rows, dest_ref):
        size = rows * NORM_ROWS + 16
        at = pl.multiple_of(start + step * (rows * NORM_ROWS), 16)
        stage_ref[0:size, :] = flat_ref[pl.ds(at, size), :].astype(F32)
        for lane in range(NORM_ROWS):
            dest_ref[:, lane * LANES : lane * LANES + LANES] = stage_ref[
                pl.ds(offset + lane, rows, stride=NORM_ROWS), :].astype(BF16)

    block(0, NORM_ROWS, IN_BLOCK, in_ref)

    @pl.when(step < INNER // OUT_BLOCK)
    def _():
        low = OUT_START // 16 * 16
        block(low, OUT_START - low, OUT_BLOCK, out_ref)


def run_prepare(flat):
    vector = lambda n: jax.ShapeDtypeStruct((1, n), F32)
    return pl.pallas_call(
        prepare_kernel,
        grid=(PREP_STEPS,),
        in_specs=[const_spec(flat.shape)],
        out_specs=[
            pl.BlockSpec((IN_BLOCK, D), lambda i: (i, 0)),
            pl.BlockSpec((OUT_BLOCK, D), lambda i: (jnp.minimum(i, INNER // OUT_BLOCK - 1), 0)),
            const_spec((1, D)), const_spec((8, XBC)), const_spec((1, XBC)), const_spec((1, 128)),
            const_spec((1, 128)), const_spec((1, INNER)), const_spec((1, INNER)),
            const_spec((256, INNER)), const_spec((INNER, 128)),
        ],
        out_shape=[
            jax.ShapeDtypeStruct((PROJ, D), BF16), jax.ShapeDtypeStruct((INNER, D), BF16),
            vector(D), jax.ShapeDtypeStruct((8, XBC), F32), vector(XBC), vector(128), vector(128),
            vector(INNER), vector(INNER),
            jax.ShapeDtypeStruct((256, INNER), BF16), jax.ShapeDtypeStruct((INNER, 128), BF16),
        ],
        scratch_shapes=[pltpu.VMEM((IN_BLOCK * NORM_ROWS + 16, LANES), F32)],
        compiler_params=pltpu.CompilerParams(
            dimension_semantics=("arbitrary",), vmem_limit_bytes=40 * 2**20),
        cost_estimate=pl.CostEstimate(
            flops=10**9, bytes_accessed=16 * 2**20, transcendentals=0),
    )(flat)


def adam_kernel(
    who_ref, rate_ref, early_ref, early_other_ref, late_ref, late_other_ref, small_ref,
    first_ref, second_ref,
    grad_ref, ratio_ref,
    stage_ref,
):
    step = pl.program_id(0)
    upper = who_ref[0]
    mine = who_ref[1]
    block = first_ref.shape[0]
    half = 2 * block * ADAM_BLOCKS

    @pl.when(step == 0)
    def _():
        early_at = LEAD + jnp.where(upper == 1, OUT_START - half, NORM_ROWS)
        window = LATE_START + (XBC - WINDOW) * NORM_ROWS
        late_at = LEAD + jnp.where(upper == 1, window - half, LATE_START)
        for source_ref, at, which in (
            (late_ref, late_at, mine), (late_other_ref, late_at, 1 - mine),
            (early_ref, early_at, mine), (early_other_ref, early_at, 1 - mine),
        ):
            size = source_ref.shape[0]
            start = at + which * (size * NORM_ROWS)
            for lane in range(NORM_ROWS):
                stage_ref[pl.ds(start + lane, size, stride=NORM_ROWS), :] = source_ref[
                    :, lane * LANES : lane * LANES + LANES]

        @pl.when(upper == 0)
        def _():
            for lane in range(NORM_ROWS):
                stage_ref[LEAD + lane : LEAD + lane + 1, :] = small_ref[
                    6:7, lane * LANES : lane * LANES + LANES]

        @pl.when(upper == 1)
        def _():
            at = LEAD + OUT_START - half - SMALL_ROWS
            for lane in range(NORM_ROWS):
                stage_ref[pl.ds(at + lane, HEADS, stride=NORM_ROWS), :] = small_ref[
                    8 : 8 + HEADS, lane * LANES : lane * LANES + LANES]
            at += DT_ROWS
            places = [(k, j) for k in range(CONV + 1) for j in range(CONVB_ROWS)]
            places += [(6, NORM_ROWS + j) for j in range(3)]
            places += [(5, j) for j in range(GAIN_ROWS)]
            for number, (line, lane) in enumerate(places):
                stage_ref[at + number : at + number + 1, :] = small_ref[
                    line : line + 1, lane * LANES : lane * LANES + LANES]
            at = LEAD + OUT_START + OUT_ROWS - half
            stage_ref[at : LEAD + half, :] = jnp.zeros((LEAD + half - at, LANES), F32)

    @pl.when(step > 0)
    def _():
        at = LEAD + mine * (half // 2) + (step - 1) * block
        grad = stage_ref[pl.ds(pl.multiple_of(at, 8), block), :]
        grad_ref[...] = grad
        first = BETA_ONE * first_ref[...] + (1.0 - BETA_ONE) * grad
        second = BETA_TWO * second_ref[...] + (1.0 - BETA_TWO) * grad * grad
        ratio_ref[...] = (first * rate_ref[0]) / (jnp.sqrt(second * rate_ref[1]) + EPS_ADAM)


def run_adam(who, rates, early, early_other, late, late_other, small, first, second):
    rows = first.shape[0]
    block = rows // ADAM_BLOCKS

    def at(i):
        return (jnp.maximum(i - 1, 0), 0)

    spec = pl.BlockSpec((block, LANES), at)
    out = jax.ShapeDtypeStruct((rows, LANES), F32)
    return pl.pallas_call(
        adam_kernel,
        grid=(ADAM_BLOCKS + 1,),
        in_specs=[
            pl.BlockSpec(memory_space=pltpu.SMEM), pl.BlockSpec(memory_space=pltpu.SMEM),
            const_spec(early.shape), const_spec(early.shape),
            const_spec(late.shape), const_spec(late.shape), const_spec(small.shape),
            spec, spec,
        ],
        out_specs=[spec, spec],
        out_shape=[out, out],
        scratch_shapes=[pltpu.VMEM((STAGE_ROWS, LANES), F32)],
        compiler_params=pltpu.CompilerParams(
            dimension_semantics=("arbitrary",), vmem_limit_bytes=48 * 2**20),
        cost_estimate=pl.CostEstimate(
            flops=10**8, bytes_accessed=24 * 2**20, transcendentals=10**6),
    )(who, rates, early, early_other, late, late_other, small, first, second)


def swap(values, axis, bit):
    size = lax.axis_size(axis)
    return lax.ppermute(values, axis, [(i, i ^ bit) for i in range(size)])


def power_for(bound):
    bound = jnp.maximum(bound, 1e-30).reshape(1, 1)
    return jnp.clip(jnp.floor(jnp.log2(F16_TOP / bound)), -126.0, 120.0)


def values_scaled(values, power):
    return values * jnp.exp2(power)


def to_wire(values, power):
    return values_scaled(values, power).astype(jnp.float16)


def from_wire(values, power):
    return values.astype(F32) * jnp.exp2(-power)


def halve(values, power, axis, bit):
    side = (lax.axis_index(axis) // bit) % 2
    rows = values.shape[-2] // 2
    mark = min(MARK, rows)
    dim = values.ndim - 2
    keep = lax.dynamic_slice_in_dim(values, side * rows, rows, dim)
    send = lax.dynamic_slice_in_dim(values, (1 - side) * (rows - mark), rows + mark, dim)
    line = lax.broadcasted_iota(jnp.int32, send.shape, dim)
    marked = jnp.where(side == 1, line >= rows, line < mark)
    wire = jnp.where(marked, power, values_scaled(send, power)).astype(jnp.float16)
    got = swap(wire, axis, bit)
    got_power = lax.dynamic_slice_in_dim(got, (1 - side) * rows, 1, dim)
    got_power = got_power.reshape(-1, D)[0:1, 0:1].astype(F32)
    body = lax.dynamic_slice_in_dim(got, side * mark, rows, dim)
    sum_bound = F16_TOP * (jnp.exp2(-power) + jnp.exp2(-got_power))
    return keep + from_wire(body, got_power), power_for(sum_bound)


def halve_data(values, power, bit):
    return halve(values, power, "dp", bit)


def data_bits():
    return [1 << k for k in range(lax.axis_size("dp").bit_length() - 1)]


def double_data(wire, bit):
    side = (lax.axis_index("dp") // bit) % 2
    got = swap(wire, "dp", bit)
    return jnp.where(side == 0, jnp.concatenate([wire, got]), jnp.concatenate([got, wire]))


def dot_tn(a, b):
    return lax.dot_general(a, b, (((0,), (0,)), ((), ())), preferred_element_type=F32)


def pick_rows(index, rows):
    chosen = index[:, None] == jnp.arange(rows.shape[0], dtype=jnp.int32)[None, :]
    return dot(chosen.astype(BF16), rows).astype(BF16)


def on_device(
    tokens, loss_sensitivity, lengths, holder_sequence_list, master, moment_one, moment_two,
    adam_rates, iteration_tally,
):
    group_devices = lax.axis_size("zero")
    data_devices = lax.axis_size("dp")
    zero_index = lax.axis_index("zero")
    dp_index = lax.axis_index("dp")
    seq_len = loss_sensitivity.shape[1]
    group_seqs = tokens.shape[0]
    span = tokens.shape[1]
    slots = group_seqs // data_devices
    shard_rows = master.shape[0] // LANES
    tie = lax.optimization_barrier

    own = master.reshape(shard_rows, LANES)
    flat = lax.all_gather(own.astype(BF16), "zero", axis=0, tiled=True)

    arranged = holder_sequence_list.reshape(data_devices, group_devices, slots)
    group_order = lax.dynamic_index_in_dim(arranged, zero_index, 1, keepdims=False).reshape(-1)
    local_ids = group_order - zero_index * group_seqs
    dealt = tokens.at[local_ids].get(mode="promise_in_bounds")
    local_tok = lax.all_to_all(dealt, "dp", split_axis=0, concat_axis=0, tiled=True)
    my_seqs = lax.dynamic_slice_in_dim(group_order, dp_index * slots, slots)
    bound = lengths[my_seqs[0]]
    positions = jnp.arange(seq_len, dtype=jnp.int32)

    in_w, out_w, norm_gain, *params, e2, et = run_prepare(flat)
    cot = loss_sensitivity[0]
    gm = dot_nt(cot, out_w)
    cot_top = jnp.max(jnp.abs(cot)).astype(F32)
    local_tok, in_w, gm, cot_top = tie((local_tok, in_w, gm, cot_top))
    own_late, _ = tie((own, flat[:8]))
    whole_master = lax.all_gather(own_late, "zero", axis=0, tiled=True)

    def place(slot, at):
        return (at // span) * (slots * span) + slot * span + at % span

    source = jnp.where(positions < bound, place(0, positions), place(1, positions - bound))
    packed = pick_rows(source, local_tok.reshape(slots * seq_len, D))
    blocks = jnp.arange(data_devices, dtype=jnp.int32)[:, None, None] * span
    within = blocks + jnp.arange(span, dtype=jnp.int32)[None, None, :]
    within = within + jnp.arange(slots, dtype=jnp.int32)[None, :, None] * bound
    unpack_rows = jnp.minimum(within, seq_len - 1).reshape(-1)

    def spread(rows):
        return pick_rows(unpack_rows, rows).reshape(data_devices * slots, span, D)

    def send_back(picked):
        return lax.all_to_all(picked, "dp", split_axis=0, concat_axis=0, tiled=True)

    restore = jnp.zeros_like(local_ids).at[local_ids].set(
        jnp.arange(group_seqs, dtype=jnp.int32))
    mine = lax.dynamic_slice_in_dim(lengths, zero_index * group_seqs, group_seqs)
    at = dp_index * span + jnp.arange(span, dtype=jnp.int32)
    live = (at[None, :] < mine[:, None])[:, :, None]

    bound_arr = bound.reshape(1)
    tok = packed.astype(F32)
    rinv = lax.rsqrt(jnp.mean(tok * tok, axis=1, keepdims=True) + EPS_NORM)
    nhat = tok * rinv
    normed = (nhat * norm_gain).astype(BF16)
    proj_z = dot_nt(normed, in_w[:INNER])
    proj = dot_nt(normed, in_w[INNER:])
    pair, dy, through, states, ggain, zmax = run_forward(
        proj_z, proj, gm, bound_arr, e2, et, params)
    result = (tok + dot(pair[1], out_w)).astype(BF16)
    picked = spread(result)
    picked, pair = tie((picked, pair))
    back_out = send_back(picked)
    root = float(seq_len) ** 0.5
    normed_norm = root * float(D) ** 0.5 * 1.02 * jnp.max(jnp.abs(norm_gain))
    mixed_norm = root * float(INNER) ** 0.5 * 1.02 * jnp.max(jnp.abs(params[5]))
    early_power = power_for(jnp.maximum(
        1.02 * root * jnp.max(zmax) * normed_norm, root * cot_top * mixed_norm))
    early = lax.dot_general(
        pair, jnp.stack([normed, cot]), (((1,), (1,)), ((0,), (0,))), preferred_element_type=F32)
    early, early_power = halve(early, early_power, "zero", 1)
    early = early.reshape(INNER, D)
    part_normed = dot(pair[0], in_w[:INNER])
    early, early_power, part_normed, dy = tie((early, early_power, part_normed, dy))
    early, early_power = halve(early, early_power, "zero", 2)
    gp, window, small8 = run_backward(proj, dy, through, states, bound_arr, e2, et, params)
    gp, window, back_out, early, early_power, whole_master = tie(
        (gp, window, back_out, early, early_power, whole_master))

    bits = data_bits()
    late = lax.dot_general(
        window, jnp.stack([normed, normed]), (((1,), (1,)), ((0,), (0,))),
        preferred_element_type=F32)
    late, gp = tie((late, gp))
    late_power = power_for(1.02 * root * jnp.max(small8[7:8]) * normed_norm)
    late, late_power = halve(late, late_power, "zero", 1)
    late = late.reshape(WINDOW, D)
    early, early_power = halve_data(early, early_power, bits[0])
    grad_normed = part_normed + dot(gp, in_w[INNER:])
    late, late_power, early, early_power, grad_normed = tie(
        (late, late_power, early, early_power, grad_normed))
    late, late_power = halve(late, late_power, "zero", 2)
    for bit in bits[1:-1]:
        early, early_power = halve_data(early, early_power, bit)
    gng = grad_normed * norm_gain
    grad_norm_gain = jnp.sum(nhat * grad_normed, axis=0, keepdims=True)
    grad_tok = cot.astype(F32) + rinv * (gng - nhat * jnp.mean(nhat * gng, axis=1, keepdims=True))
    grad_tok = grad_tok.astype(BF16)
    line = iota((8, 1), 0)
    small8 = jnp.where(line == 5, jnp.pad(ggain, ((0, 0), (0, XBC - INNER))), small8)
    small8 = small8 + jnp.where(line == 6, jnp.pad(grad_norm_gain, ((0, 0), (0, XBC - D))), 0.0)
    small = jnp.concatenate([
        small8, jnp.pad(dot_tn(gp[:, XBC:], normed), ((0, 0), (0, XBC - D)))])
    late, late_power, early, early_power, small, grad_tok = tie(
        (late, late_power, early, early_power, small, grad_tok))
    small = small + swap(small, "dp", bits[0])
    late, late_power = halve_data(late, late_power, bits[0])
    early, early_power = halve_data(early, early_power, bits[-1])
    early = to_wire(early, early_power)
    picked_grad = spread(grad_tok)
    late, late_power, early, picked_grad, small = tie(
        (late, late_power, early, picked_grad, small))
    for bit in bits[1:-1]:
        late, late_power = halve_data(late, late_power, bit)
        small = small + swap(small, "dp", bit)
        early = double_data(early, bits[-1]) if bit == bits[1] else early
    late, late_power, early, small = tie((late, late_power, early, small))
    late, late_power = halve_data(late, late_power, bits[-1])
    small = small + swap(small, "dp", bits[-1])
    late = to_wire(late, late_power)
    for bit in reversed(bits[1:-1]):
        early = double_data(early, bit)
    late, early, small = tie((late, early, small))
    late = double_data(late, bits[-1])
    small = small + swap(small, "zero", 1)
    early = from_wire(double_data(early, bits[0]), early_power)
    late, early, small = tie((late, early, small))
    for bit in reversed(bits[1:-1]):
        late = double_data(late, bit)
    small = small + swap(small, "zero", 2)
    early_other = swap(early, "zero", 1)
    late, early_other, picked_grad, small = tie((late, early_other, picked_grad, small))
    back_grad = send_back(picked_grad)
    late = from_wire(double_data(late, bits[0]), late_power)
    late_other = swap(late, "zero", 1)

    steps_f = iteration_tally[0].astype(F32)
    rates = jnp.stack([
        1.0 / (1.0 - jnp.power(BETA_ONE, steps_f)), 1.0 / (1.0 - jnp.power(BETA_TWO, steps_f))])
    who = jnp.stack([zero_index // 2, zero_index % 2]).astype(jnp.int32)
    first = moment_one.reshape(shard_rows, LANES)
    second = moment_two.reshape(shard_rows, LANES)
    grad_shard, ratio = run_adam(
        who, rates, early, early_other, late, late_other, small, first, second)
    mine = ratio.astype(jnp.float16)
    mine, grad_shard, back_out = tie((mine, grad_shard, back_out))
    core = swap(mine, "zero", 1)
    across = swap(mine, "zero", 2)
    first_next = BETA_ONE * first + (1.0 - BETA_ONE) * grad_shard
    second_next = BETA_TWO * second + (1.0 - BETA_TWO) * grad_shard * grad_shard
    back_rows = back_out.at[restore].get(mode="promise_in_bounds")
    tokens_out = jnp.where(live, back_rows, tokens)
    new_master = jnp.zeros((group_devices, shard_rows, LANES), F32)
    whole_master = whole_master.reshape(group_devices, shard_rows, LANES)

    def put(new_master, piece, offset):
        shard = zero_index ^ offset
        old = lax.dynamic_index_in_dim(whole_master, shard, 0, keepdims=False)
        new = old - adam_rates[0] * (piece.astype(F32) + adam_rates[1] * old)
        return lax.dynamic_update_index_in_dim(new_master, new, shard, 0)

    new_master = put(put(new_master, mine, 0), core, 1)
    across, new_master, tokens_out, first_next, second_next = tie(
        (across, new_master, tokens_out, first_next, second_next))
    across_core = swap(across, "zero", 1)
    new_master = put(new_master, across, 2)
    across_core, new_master = tie((across_core, new_master))
    new_master = put(new_master, across_core, 3)
    back_grad, new_master = tie((back_grad, new_master))
    grad_tokens = jnp.where(
        live, back_grad.at[restore].get(mode="promise_in_bounds"), jnp.zeros((), BF16))
    return (
        tokens_out, grad_tokens, new_master.reshape(-1), grad_shard.reshape(-1),
        first_next.reshape(-1), second_next.reshape(-1))


def solution(mesh):
    return jax.shard_map(
        on_device,
        mesh=mesh,
        in_specs=(
            P("zero", "dp", None), P(("dp", "zero"), None, None), P(), P(),
            P("zero"), P("zero"), P("zero"), P(), P(),
        ),
        out_specs=(
            P("zero", "dp", None), P("zero", "dp", None), P(), P("zero"), P("zero"), P("zero"),
        ),
        check_vma=False,
    )
```

```python
import jax
import jax.numpy as jnp
from jax import lax
from jax.experimental import pallas as pl
from jax.experimental.pallas import tpu as pltpu
from jax.sharding import PartitionSpec as P

D = 768
HEADS = 24
HEADDIM = 64
STATE = 128
CONV = 4
INNER = 1536
XBC = 1792
PROJ = 3352
Q = 128
LATE = PROJ - INNER
WINDOW = 1024
PAIRS = HEADS // 2
EPS_NORM = 1e-05
NEG = -1e30
F32 = jnp.float32
BF16 = jnp.bfloat16


def dot(a, b):
    return lax.dot_general(a, b, (((1,), (0,)), ((), ())), preferred_element_type=F32)


def dot_nt(a, b):
    return lax.dot_general(a, b, (((1,), (1,)), ((), ())), preferred_element_type=F32)


def split2(v):
    hi = v.astype(BF16)
    return hi, (v - hi.astype(F32)).astype(BF16)


def split3(v):
    hi = v.astype(BF16)
    rest = v - hi.astype(F32)
    mid = rest.astype(BF16)
    return hi, mid, (rest - mid.astype(F32)).astype(BF16)


def wide_left(v):
    hi, lo = split2(v)
    return jnp.concatenate([hi, lo, hi], axis=1)


def tall_right(v):
    hi, lo = split2(v)
    return jnp.concatenate([hi, hi, lo], axis=0)


def exact_left(v):
    return jnp.concatenate(split3(v), axis=1)


def sigmoid(v):
    return 1.0 / (1.0 + jnp.exp(-v))


def softplus(v):
    return jnp.maximum(v, 0.0) + jnp.log1p(jnp.exp(-jnp.abs(v)))


def iota(shape, dim):
    return lax.broadcasted_iota(jnp.int32, shape, dim)


def expand(v, e_ref):
    hi, lo = split2(v)
    return dot(jnp.concatenate([hi, lo], axis=1), e_ref[...])


def head_sum(v, et_ref):
    hi, lo = split2(v)
    return dot(hi, et_ref[...]) + dot(lo, et_ref[...])


def chunk_masks(t0, bound):
    rows = t0 + iota((Q, 1), 0)
    rr = t0 + iota((Q, Q), 0)
    cc = t0 + iota((Q, Q), 1)
    return rows, rr, cc


def conv_rows(ext_ref, w_ref, b_ref, rows, bound):
    total = b_ref[...] + w_ref[3:4, :] * ext_ref[8 : 8 + Q, :]
    for back in (1, 2, 3):
        ok = jnp.logical_or(rows - back >= bound, rows < bound).astype(F32)
        total = total + w_ref[3 - back : 4 - back, :] * (ext_ref[8 - back : 8 - back + Q, :] * ok)
    return total


def decay_parts(dt_raw, dtb_ref, alog_ref, rr, cc):
    dt_in = dt_raw + dtb_ref[...]
    dt_pos = softplus(dt_in)
    rate = -jnp.exp(alog_ref[...])
    step = dt_pos * rate
    tri = (cc <= rr).astype(F32).astype(BF16)
    s_hi, s_mid, s_lo = split3(step)
    cum = dot(tri, s_hi) + dot(tri, s_mid) + dot(tri, s_lo)
    return dt_in, dt_pos, rate, cum


def forward_kernel(
    bound_ref, z_ref, proj_ref, gm_ref, e_ref, et_ref, convw_ref, convb_ref, dtb_ref, alog_ref,
    skip_ref, gain_ref,
    pair_ref, dy_ref, through_ref, state_ref, ggain_ref, zmax_ref,
    ext_ref, dt_ref, carry_ref, xd_ref, acc_ref, cumt_ref,
):
    step = pl.program_id(0)
    bound = bound_ref[0]
    t0 = step * Q

    @pl.when(step == 0)
    def _():
        ext_ref[0:8, :] = jnp.zeros((8, XBC), F32)
        carry_ref[...] = jnp.zeros_like(carry_ref)
        dt_ref[...] = jnp.zeros_like(dt_ref)
        ggain_ref[...] = jnp.zeros_like(ggain_ref)
        zmax_ref[...] = jnp.zeros_like(zmax_ref)

    rows, rr, cc = chunk_masks(t0, bound)
    ext_ref[8 : 8 + Q, :] = proj_ref[:, :XBC]
    pre = conv_rows(ext_ref, convw_ref, convb_ref, rows, bound)
    ext_ref[0:8, :] = ext_ref[Q : Q + 8, :]
    conv_out = pre * sigmoid(pre)
    x = conv_out[:, :INNER]
    b_rows = conv_out[:, INNER : INNER + STATE]
    c_rows = conv_out[:, INNER + STATE :]
    dt_ref[:, 0:HEADS] = proj_ref[:, XBC:LATE]
    _, dt_pos, _, cum = decay_parts(dt_ref[...], dtb_ref, alog_ref, rr, cc)
    cum_end = cum[Q - 1 : Q, :]
    keep = jnp.logical_or(rows < bound, bound < t0).astype(F32)
    in_last = jnp.logical_or(rows >= bound, bound > t0 + Q - 1).astype(F32)
    whole = jnp.logical_or(bound < t0, bound > t0 + Q - 1).astype(F32)
    from_start = jnp.exp(cum) * keep
    to_end = jnp.exp(cum_end - cum) * in_last
    carry_scale = jnp.exp(cum_end) * whole
    allowed = jnp.logical_and(cc <= rr, (cc >= bound) == (rr >= bound))
    cumt_ref[...] = cum.T

    state = carry_ref[...]
    state_ref[0] = state
    xd = x * expand(dt_pos, e_ref)
    xd_ref[...] = xd
    acc = dot(wide_left(c_rows), tall_right(state)) * expand(from_start, e_ref)
    acc_ref[...] = acc + skip_ref[...] * x
    b_t = b_rows.T
    scale_all = expand(jnp.broadcast_to(carry_scale, (Q, Q)), e_ref)
    carry_ref[...] = state * scale_all + dot(
        wide_left(b_t), tall_right(xd * expand(to_end, e_ref))
    )
    gram = dot(wide_left(c_rows), tall_right(b_t))
    first = iota((Q, Q), 1) < HEADDIM
    for pair in range(PAIRS):
        parts = []
        for head in (2 * pair, 2 * pair + 1):
            differ = cum[:, head : head + 1] - cumt_ref[head : head + 1, :]
            parts.append(gram * jnp.exp(jnp.where(allowed, differ, NEG)))
        left = jnp.concatenate(split2(jnp.concatenate(parts, axis=1)), axis=0)
        lanes = slice(pair * 128, pair * 128 + 128)
        xp = xd_ref[:, lanes]
        diag = jnp.concatenate([jnp.where(first, xp, 0.0), jnp.where(first, 0.0, xp)], axis=0)
        out = dot(left, jnp.concatenate(split2(diag), axis=1))
        acc_ref[:, lanes] += out[:Q, :128] + (out[:Q, 128:] + out[Q:, :128])
    scanned = acc_ref[...]
    z = z_ref[...]
    sig_z = sigmoid(z)
    silu_z = z * sig_z
    gated = scanned * silu_z
    ginv = lax.rsqrt(jnp.mean(gated * gated, axis=1, keepdims=True) + EPS_NORM)
    mhat = gated * ginv
    pair_ref[1] = (mhat * gain_ref[...]).astype(BF16)
    gm = gm_ref[...]
    ggain_ref[...] += jnp.sum(mhat * gm, axis=0, keepdims=True)
    gmg = gm * gain_ref[...]
    ggated = ginv * (gmg - mhat * jnp.mean(mhat * gmg, axis=1, keepdims=True))
    dy = ggated * silu_z
    dy_ref[...] = dy
    grad_z = ggated * scanned * (sig_z * (1.0 + z * (1.0 - sig_z)))
    zmax_ref[...] = jnp.maximum(zmax_ref[...], jnp.max(jnp.abs(grad_z), axis=0, keepdims=True))
    pair_ref[0] = grad_z.astype(BF16)
    through_ref[...] = head_sum(dy * (scanned - skip_ref[...] * x), et_ref)


def const_spec(shape):
    return pl.BlockSpec(shape, lambda *_: (0,) * len(shape))


def run_forward(z, proj, gm, bound, e2, et, params):
    n = proj.shape[0]
    steps = n // Q
    return pl.pallas_call(
        forward_kernel,
        grid=(steps,),
        in_specs=[
            pl.BlockSpec(memory_space=pltpu.SMEM),
            pl.BlockSpec((Q, INNER), lambda i: (i, 0)),
            pl.BlockSpec((Q, LATE), lambda i: (i, 0)),
            pl.BlockSpec((Q, INNER), lambda i: (i, 0)),
            const_spec((256, INNER)), const_spec((INNER, 128)),
            const_spec((8, XBC)), const_spec((1, XBC)), const_spec((1, 128)),
            const_spec((1, 128)), const_spec((1, INNER)), const_spec((1, INNER)),
        ],
        out_specs=[
            pl.BlockSpec((2, Q, INNER), lambda i: (0, i, 0)),
            pl.BlockSpec((Q, INNER), lambda i: (i, 0)),
            pl.BlockSpec((Q, 128), lambda i: (i, 0)),
            pl.BlockSpec((1, STATE, INNER), lambda i: (i, 0, 0)),
            const_spec((1, INNER)), const_spec((1, INNER)),
        ],
        out_shape=[
            jax.ShapeDtypeStruct((2, n, INNER), BF16),
            jax.ShapeDtypeStruct((n, INNER), F32),
            jax.ShapeDtypeStruct((n, 128), F32),
            jax.ShapeDtypeStruct((steps, STATE, INNER), F32),
            jax.ShapeDtypeStruct((1, INNER), F32),
            jax.ShapeDtypeStruct((1, INNER), F32),
        ],
        scratch_shapes=[
            pltpu.VMEM((Q + 8, XBC), F32),
            pltpu.VMEM((Q, 128), F32),
            pltpu.VMEM((STATE, INNER), F32),
            pltpu.VMEM((Q, INNER), F32),
            pltpu.VMEM((Q, INNER), F32),
            pltpu.VMEM((128, Q), F32),
        ],
        compiler_params=pltpu.CompilerParams(
            dimension_semantics=("arbitrary",), vmem_limit_bytes=48 * 2**20),
        cost_estimate=pl.CostEstimate(
            flops=30 * 10**9, bytes_accessed=40 * 2**20, transcendentals=10**7),
    )(bound, z, proj, gm, e2, et, *params)


def backward_kernel(
    bound_ref, proj_ref, before_ref, dy_ref, through_ref, state_ref, gz_ref, tok_ref, cot_ref,
    in_ref, norm_ref, ggain_ref,
    e_ref, et_ref, convw_ref, convb_ref, dtb_ref, alog_ref, skip_ref,
    window_ref, gtok_ref, small_ref,
    gskip_ref, gsmall_ref, dtw_ref, ext_ref, dt_ref, lam_ref, dsum_ref, xd_ref, g_ref, gnext_ref, cumt_ref,
):
    step = pl.program_id(0)
    steps = pl.num_programs(0)
    bound = bound_ref[0]
    t0 = (steps - 1 - step) * Q

    @pl.when(step == 0)
    def _():
        lam_ref[...] = jnp.zeros_like(lam_ref)
        dsum_ref[...] = jnp.zeros_like(dsum_ref)
        dt_ref[...] = jnp.zeros_like(dt_ref)
        gnext_ref[Q : Q + 8, :] = jnp.zeros((8, XBC), F32)
        gskip_ref[...] = jnp.zeros_like(gskip_ref)
        small_ref[...] = jnp.zeros_like(small_ref)
        dtw_ref[...] = jnp.zeros_like(dtw_ref)
        gsmall_ref[...] = jnp.zeros_like(gsmall_ref)

    rows, rr, cc = chunk_masks(t0, bound)
    dy = dy_ref[...]
    first_chunk = (t0 > 0).astype(F32)
    ext_ref[0:8, :] = before_ref[:, :XBC] * first_chunk
    ext_ref[8 : 8 + Q, :] = proj_ref[:, :XBC]
    pre = conv_rows(ext_ref, convw_ref, convb_ref, rows, bound)
    sig_pre = sigmoid(pre)
    conv_out = pre * sig_pre
    x = conv_out[:, :INNER]
    b_rows = conv_out[:, INNER : INNER + STATE]
    c_rows = conv_out[:, INNER + STATE :]
    dt_ref[:, 0:HEADS] = proj_ref[:, XBC:LATE]
    dt_in, dt_pos, rate, cum = decay_parts(dt_ref[...], dtb_ref, alog_ref, rr, cc)
    cum_end = cum[Q - 1 : Q, :]
    keep = jnp.logical_or(rows < bound, bound < t0).astype(F32)
    in_last = jnp.logical_or(rows >= bound, bound > t0 + Q - 1).astype(F32)
    whole = jnp.logical_or(bound < t0, bound > t0 + Q - 1).astype(F32)
    from_start = jnp.exp(cum) * keep
    to_end = jnp.exp(cum_end - cum) * in_last
    carry_scale = jnp.exp(cum_end) * whole
    allowed_t = jnp.logical_and(rr <= cc, (cc >= bound) == (rr >= bound))
    cumt_ref[...] = cum.T
    c_t = c_rows.T
    gram_t = dot(wide_left(b_rows), tall_right(c_t))
    dt_all = expand(dt_pos, e_ref)
    end_all = expand(to_end, e_ref)
    xd = x * dt_all
    xd_ref[...] = xd
    skip = skip_ref[...]
    gskip_ref[...] += jnp.sum(dy * x, axis=0, keepdims=True)
    lam = lam_ref[...]
    lam_hi, lam_lo = split2(lam)
    g_ref[...] = (
        dot(wide_left(b_rows), jnp.concatenate([lam_hi, lam_hi, lam_lo], axis=0)) * end_all
    )
    xw_hi, xw_lo = split2(xd * end_all)
    grad_b = dot_nt(xw_hi, lam_hi) + (dot_nt(xw_hi, lam_lo) + dot_nt(xw_lo, lam_hi))
    state = state_ref[0]
    st_hi, st_lo = split2(state)
    dye = dy * expand(from_start, e_ref)
    dye_hi, dye_lo = split2(dye)
    grad_c = dot_nt(dye_hi, st_hi) + (dot_nt(dye_hi, st_lo) + dot_nt(dye_lo, st_hi))
    scale_all = expand(jnp.broadcast_to(carry_scale, (Q, Q)), e_ref)
    lam_new = lam * scale_all + dot(
        wide_left(c_t), jnp.concatenate([dye_hi, dye_hi, dye_lo], axis=0)
    )
    lam_ref[...] = lam_new
    ended = dsum_ref[0:1, :]
    first = iota((Q, Q), 1) < HEADDIM
    first_row = iota((Q, Q), 0) < HEADDIM
    gram_grad = jnp.zeros((Q, Q), F32)
    for pair in range(PAIRS):
        lanes = slice(pair * 128, pair * 128 + 128)
        weights = []
        for head in (2 * pair, 2 * pair + 1):
            differ = cumt_ref[head : head + 1, :] - cum[:, head : head + 1]
            weights.append(jnp.exp(jnp.where(allowed_t, differ, NEG)))
        left = jnp.concatenate([gram_t * weights[0], gram_t * weights[1]], axis=1)
        left = jnp.concatenate(split2(left), axis=0)
        dyp = dy_ref[:, lanes]
        diag = jnp.concatenate([jnp.where(first, dyp, 0.0), jnp.where(first, 0.0, dyp)], axis=0)
        out = dot(left, jnp.concatenate(split2(diag), axis=1))
        g_ref[:, lanes] += out[:Q, :128] + (out[:Q, 128:] + out[Q:, :128])
        dyt = dyp.T
        right = jnp.concatenate(
            [jnp.where(first_row, dyt, 0.0), jnp.where(first_row, 0.0, dyt)], axis=1)
        outer = dot(wide_left(xd_ref[:, lanes]), tall_right(right))
        gram_grad = gram_grad + (outer[:, :128] * weights[0] + outer[:, 128:] * weights[1])
    g = g_ref[...]
    grad_x = dt_all * g + skip * dy
    direct = head_sum(x * g, et_ref)
    balance = through_ref[...] - dt_pos * direct
    keep_t = allowed_t.astype(F32).astype(BF16)
    b_hi, b_mid, b_lo = split3(balance)
    grad_step = dot(keep_t, b_hi) + dot(keep_t, b_mid) + dot(keep_t, b_lo) + in_last * ended
    dsum_ref[...] = head_sum(
        jnp.broadcast_to(jnp.sum(lam_new * state, axis=0, keepdims=True), (8, INNER)), et_ref)
    grad_dt = (direct + rate * grad_step) * sigmoid(dt_in)
    gsmall_ref[0:1, :] += jnp.sum(grad_dt, axis=0, keepdims=True)
    gsmall_ref[1:2, :] += rate * jnp.sum(dt_pos * grad_step, axis=0, keepdims=True)
    grad_c = grad_c + dot(wide_left(gram_grad.T), tall_right(b_rows))
    grad_b = grad_b + dot(wide_left(gram_grad), tall_right(c_rows))
    slope = sig_pre * (1.0 + pre * (1.0 - sig_pre))
    gnext_ref[0:Q, :INNER] = grad_x * slope[:, :INNER]
    gnext_ref[0:Q, INNER : INNER + STATE] = grad_b * slope[:, INNER : INNER + STATE]
    gnext_ref[0:Q, INNER + STATE :] = grad_c * slope[:, INNER + STATE :]
    gcp = gnext_ref[0:Q, :]
    small_ref[4:5, :] += jnp.sum(gcp, axis=0, keepdims=True)
    small_ref[3:4, :] += jnp.sum(gcp * ext_ref[8 : 8 + Q, :], axis=0, keepdims=True)
    total = convw_ref[3:4, :] * gcp
    for back in (1, 2, 3):
        ok = jnp.logical_or(rows - back >= bound, rows < bound).astype(F32)
        small_ref[3 - back : 4 - back, :] += jnp.sum(
            gcp * (ext_ref[8 - back : 8 - back + Q, :] * ok), axis=0, keepdims=True)
        okn = jnp.logical_or(rows >= bound, rows + back < bound).astype(F32)
        total = total + convw_ref[3 - back : 4 - back, :] * (gnext_ref[back : back + Q, :] * okn)
    small_ref[7:8, :] = jnp.maximum(
        small_ref[7:8, :], jnp.max(jnp.abs(total), axis=0, keepdims=True))
    total = total.astype(BF16)
    window_ref[0] = total[:, :WINDOW]
    window_ref[1] = total[:, XBC - WINDOW :]
    gnext_ref[Q : Q + 8, :] = gnext_ref[0:8, :]
    grad_dt = grad_dt.astype(BF16)
    grad_normed = (
        dot(gz_ref[0], in_ref[:INNER, :]) + dot(total, in_ref[INNER : INNER + XBC, :])
        + dot(grad_dt, in_ref[INNER + XBC : INNER + XBC + 128, :]))
    tok = tok_ref[...].astype(F32)
    rinv = lax.rsqrt(jnp.mean(tok * tok, axis=1, keepdims=True) + EPS_NORM)
    nhat = tok * rinv
    gain = norm_ref[...]
    gng = grad_normed * gain
    gtok_ref[...] = (cot_ref[...].astype(F32) + rinv * (
        gng - nhat * jnp.mean(nhat * gng, axis=1, keepdims=True))).astype(BF16)
    small_ref[6:7, :D] += jnp.sum(nhat * grad_normed, axis=0, keepdims=True)
    dtw_ref[...] += dot(grad_dt.astype(F32).T.astype(BF16), (nhat * gain).astype(BF16))

    @pl.when(step == steps - 1)
    def _():
        skips = head_sum(jnp.broadcast_to(gskip_ref[...], (8, INNER)), et_ref)
        small_ref[5:6, :INNER] = ggain_ref[...]
        small_ref[6:7, D : D + 128] = gsmall_ref[0:1, :]
        small_ref[6:7, D + 128 : D + 256] = gsmall_ref[1:2, :]
        small_ref[6:7, D + 256 : D + 384] = skips[0:1, :]
        small_ref[8 : 8 + HEADS, :D] = dtw_ref[0:HEADS, :]


def run_backward(
    proj, dy, through, states, pair, tok, cot, in_w, norm_gain, ggain, bound, e2, et, params
):
    n = proj.shape[0]
    steps = n // Q

    def rev(i):
        return (steps - 1 - i, 0)

    return pl.pallas_call(
        backward_kernel,
        grid=(steps,),
        in_specs=[
            pl.BlockSpec(memory_space=pltpu.SMEM),
            pl.BlockSpec((Q, LATE), rev),
            pl.BlockSpec((8, LATE), lambda i: (jnp.maximum((steps - 1 - i) * (Q // 8) - 1, 0), 0)),
            pl.BlockSpec((Q, INNER), rev),
            pl.BlockSpec((Q, 128), rev),
            pl.BlockSpec((1, STATE, INNER), lambda i: (steps - 1 - i, 0, 0)),
            pl.BlockSpec((1, Q, INNER), lambda i: (0, steps - 1 - i, 0)),
            pl.BlockSpec((Q, D), rev), pl.BlockSpec((Q, D), rev),
            const_spec(in_w.shape), const_spec((1, D)), const_spec((1, INNER)),
            const_spec((256, INNER)), const_spec((INNER, 128)),
            const_spec((8, XBC)), const_spec((1, XBC)), const_spec((1, 128)),
            const_spec((1, 128)), const_spec((1, INNER)),
        ],
        out_specs=[
            pl.BlockSpec((2, Q, WINDOW), lambda i: (0, steps - 1 - i, 0)),
            pl.BlockSpec((Q, D), rev),
            const_spec((32, XBC)),
        ],
        out_shape=[
            jax.ShapeDtypeStruct((2, n, WINDOW), BF16),
            jax.ShapeDtypeStruct((n, D), BF16),
            jax.ShapeDtypeStruct((32, XBC), F32),
        ],
        scratch_shapes=[
            pltpu.VMEM((1, INNER), F32),
            pltpu.VMEM((8, 128), F32),
            pltpu.VMEM((128, D), F32),
            pltpu.VMEM((Q + 8, XBC), F32),
            pltpu.VMEM((Q, 128), F32),
            pltpu.VMEM((STATE, INNER), F32),
            pltpu.VMEM((8, 128), F32),
            pltpu.VMEM((Q, INNER), F32),
            pltpu.VMEM((Q, INNER), F32),
            pltpu.VMEM((Q + 8, XBC), F32),
            pltpu.VMEM((128, Q), F32),
        ],
        compiler_params=pltpu.CompilerParams(
            dimension_semantics=("arbitrary",), vmem_limit_bytes=48 * 2**20),
        cost_estimate=pl.CostEstimate(
            flops=50 * 10**9, bytes_accessed=50 * 2**20, transcendentals=2 * 10**7),
    )(bound, proj, proj, dy, through, states, pair, tok, cot, in_w, norm_gain, ggain,
      e2, et, *params[:5])


BETA_ONE = 0.9
BETA_TWO = 0.95
EPS_ADAM = 1e-08
LANES = 128
NORM_ROWS = D // LANES
IN_ROWS = PROJ * D // LANES
CONVW_ROWS = CONV * XBC // LANES
CONVB_ROWS = XBC // LANES
GAIN_ROWS = INNER // LANES
OUT_ROWS = INNER * D // LANES
DT_ROWS = HEADS * D // LANES
SMALL_ROWS = DT_ROWS + CONVW_ROWS + CONVB_ROWS + 3 + GAIN_ROWS
OUT_START = NORM_ROWS + IN_ROWS + SMALL_ROWS - DT_ROWS
LATE_START = NORM_ROWS + INNER * NORM_ROWS
LEAD = 896
STAGE_ROWS = 16264
ADAM_BLOCKS = 10
F16_TOP = 30000.0
MARK = 16


PREP_STEPS = 7
IN_BLOCK = 512
OUT_BLOCK = 256
SMALL_START = NORM_ROWS + IN_ROWS


def prepare_kernel(
    flat_ref,
    in_ref, out_ref, norm_ref, convw_ref, convb_ref, dtb_ref, alog_ref, skip_ref, gain_ref,
    e_ref, et_ref,
    stage_ref,
):
    step = pl.program_id(0)

    @pl.when(step == 0)
    def _():
        rows = flat_ref[0:16, :].astype(F32)
        for lane in range(NORM_ROWS):
            norm_ref[:, lane * LANES : lane * LANES + LANES] = rows[lane : lane + 1, :]
        low = SMALL_START // 16 * 16
        stage_ref[0:112, :] = flat_ref[low : low + 112, :].astype(F32)
        at = SMALL_START - low
        convw_ref[...] = jnp.zeros_like(convw_ref)
        for tap in range(CONV):
            for lane in range(CONVB_ROWS):
                convw_ref[tap : tap + 1, lane * LANES : lane * LANES + LANES] = stage_ref[
                    at : at + 1, :]
                at += 1
        for lane in range(CONVB_ROWS):
            convb_ref[:, lane * LANES : lane * LANES + LANES] = stage_ref[at : at + 1, :]
            at += 1
        heads = iota((1, LANES), 1) < HEADS
        dtb_ref[...] = jnp.where(heads, stage_ref[at : at + 1, :], 0.0)
        alog_ref[...] = jnp.where(heads, stage_ref[at + 1 : at + 2, :], 0.0)
        skips = jnp.where(heads, stage_ref[at + 2 : at + 3, :], 0.0)
        at += 3
        for lane in range(GAIN_ROWS):
            gain_ref[:, lane * LANES : lane * LANES + LANES] = stage_ref[at : at + 1, :]
            at += 1
        one = (iota((128, INNER), 1) // HEADDIM == iota((128, INNER), 0)).astype(F32).astype(BF16)
        e_ref[0:128, :] = one
        e_ref[128:256, :] = one
        et_ref[...] = (
            iota((INNER, 128), 0) // HEADDIM == iota((INNER, 128), 1)).astype(F32).astype(BF16)
        skip_ref[...] = dot(jnp.broadcast_to(skips, (16, LANES)).astype(BF16), one)[0:1, :]

    def block(start, offset, rows, dest_ref):
        size = rows * NORM_ROWS + 16
        at = pl.multiple_of(start + step * (rows * NORM_ROWS), 16)
        stage_ref[0:size, :] = flat_ref[pl.ds(at, size), :].astype(F32)
        for lane in range(NORM_ROWS):
            dest_ref[:, lane * LANES : lane * LANES + LANES] = stage_ref[
                pl.ds(offset + lane, rows, stride=NORM_ROWS), :].astype(BF16)

    block(0, NORM_ROWS, IN_BLOCK, in_ref)

    @pl.when(step == PREP_STEPS - 1)
    def _():
        used = PROJ - (PREP_STEPS - 1) * IN_BLOCK
        in_ref[used:, :] = jnp.zeros((IN_BLOCK - used, D), BF16)

    @pl.when(step < INNER // OUT_BLOCK)
    def _():
        low = OUT_START // 16 * 16
        block(low, OUT_START - low, OUT_BLOCK, out_ref)


def run_prepare(flat):
    vector = lambda n: jax.ShapeDtypeStruct((1, n), F32)
    return pl.pallas_call(
        prepare_kernel,
        grid=(PREP_STEPS,),
        in_specs=[const_spec(flat.shape)],
        out_specs=[
            pl.BlockSpec((IN_BLOCK, D), lambda i: (i, 0)),
            pl.BlockSpec((OUT_BLOCK, D), lambda i: (jnp.minimum(i, INNER // OUT_BLOCK - 1), 0)),
            const_spec((1, D)), const_spec((8, XBC)), const_spec((1, XBC)), const_spec((1, 128)),
            const_spec((1, 128)), const_spec((1, INNER)), const_spec((1, INNER)),
            const_spec((256, INNER)), const_spec((INNER, 128)),
        ],
        out_shape=[
            jax.ShapeDtypeStruct((PREP_STEPS * IN_BLOCK, D), BF16),
            jax.ShapeDtypeStruct((INNER, D), BF16),
            vector(D), jax.ShapeDtypeStruct((8, XBC), F32), vector(XBC), vector(128), vector(128),
            vector(INNER), vector(INNER),
            jax.ShapeDtypeStruct((256, INNER), BF16), jax.ShapeDtypeStruct((INNER, 128), BF16),
        ],
        scratch_shapes=[pltpu.VMEM((IN_BLOCK * NORM_ROWS + 16, LANES), F32)],
        compiler_params=pltpu.CompilerParams(
            dimension_semantics=("arbitrary",), vmem_limit_bytes=40 * 2**20),
        cost_estimate=pl.CostEstimate(
            flops=10**9, bytes_accessed=16 * 2**20, transcendentals=0),
    )(flat)


def adam_kernel(
    who_ref, rate_ref, early_ref, early_other_ref, late_ref, late_other_ref, small_ref,
    first_ref, second_ref,
    grad_ref, ratio_ref,
    stage_ref,
):
    step = pl.program_id(0)
    upper = who_ref[0]
    mine = who_ref[1]
    block = first_ref.shape[0]
    half = 2 * block * ADAM_BLOCKS

    @pl.when(step == 0)
    def _():
        early_at = LEAD + jnp.where(upper == 1, OUT_START - half, NORM_ROWS)
        window = LATE_START + (XBC - WINDOW) * NORM_ROWS
        late_at = LEAD + jnp.where(upper == 1, window - half, LATE_START)
        for source_ref, at, which in (
            (late_ref, late_at, mine), (late_other_ref, late_at, 1 - mine),
            (early_ref, early_at, mine), (early_other_ref, early_at, 1 - mine),
        ):
            size = source_ref.shape[0]
            start = at + which * (size * NORM_ROWS)
            for lane in range(NORM_ROWS):
                stage_ref[pl.ds(start + lane, size, stride=NORM_ROWS), :] = source_ref[
                    :, lane * LANES : lane * LANES + LANES]

        @pl.when(upper == 0)
        def _():
            for lane in range(NORM_ROWS):
                stage_ref[LEAD + lane : LEAD + lane + 1, :] = small_ref[
                    6:7, lane * LANES : lane * LANES + LANES]

        @pl.when(upper == 1)
        def _():
            at = LEAD + OUT_START - half - SMALL_ROWS
            for lane in range(NORM_ROWS):
                stage_ref[pl.ds(at + lane, HEADS, stride=NORM_ROWS), :] = small_ref[
                    8 : 8 + HEADS, lane * LANES : lane * LANES + LANES]
            at += DT_ROWS
            places = [(k, j) for k in range(CONV + 1) for j in range(CONVB_ROWS)]
            places += [(6, NORM_ROWS + j) for j in range(3)]
            places += [(5, j) for j in range(GAIN_ROWS)]
            for number, (line, lane) in enumerate(places):
                stage_ref[at + number : at + number + 1, :] = small_ref[
                    line : line + 1, lane * LANES : lane * LANES + LANES]
            at = LEAD + OUT_START + OUT_ROWS - half
            stage_ref[at : LEAD + half, :] = jnp.zeros((LEAD + half - at, LANES), F32)

    @pl.when(step > 0)
    def _():
        at = LEAD + mine * (half // 2) + (step - 1) * block
        grad = stage_ref[pl.ds(pl.multiple_of(at, 8), block), :]
        grad_ref[...] = grad
        first = BETA_ONE * first_ref[...] + (1.0 - BETA_ONE) * grad
        second = BETA_TWO * second_ref[...] + (1.0 - BETA_TWO) * grad * grad
        ratio_ref[...] = (first * rate_ref[0]) / (jnp.sqrt(second * rate_ref[1]) + EPS_ADAM)


def run_adam(who, rates, early, early_other, late, late_other, small, first, second):
    rows = first.shape[0]
    block = rows // ADAM_BLOCKS

    def at(i):
        return (jnp.maximum(i - 1, 0), 0)

    spec = pl.BlockSpec((block, LANES), at)
    out = jax.ShapeDtypeStruct((rows, LANES), F32)
    return pl.pallas_call(
        adam_kernel,
        grid=(ADAM_BLOCKS + 1,),
        in_specs=[
            pl.BlockSpec(memory_space=pltpu.SMEM), pl.BlockSpec(memory_space=pltpu.SMEM),
            const_spec(early.shape), const_spec(early.shape),
            const_spec(late.shape), const_spec(late.shape), const_spec(small.shape),
            spec, spec,
        ],
        out_specs=[spec, spec],
        out_shape=[out, out],
        scratch_shapes=[pltpu.VMEM((STAGE_ROWS, LANES), F32)],
        compiler_params=pltpu.CompilerParams(
            dimension_semantics=("arbitrary",), vmem_limit_bytes=48 * 2**20),
        cost_estimate=pl.CostEstimate(
            flops=10**8, bytes_accessed=24 * 2**20, transcendentals=10**6),
    )(who, rates, early, early_other, late, late_other, small, first, second)


def swap(values, axis, bit):
    size = lax.axis_size(axis)
    return lax.ppermute(values, axis, [(i, i ^ bit) for i in range(size)])


def power_for(bound):
    bound = jnp.maximum(bound, 1e-30).reshape(1, 1)
    return jnp.clip(jnp.floor(jnp.log2(F16_TOP / bound)), -126.0, 120.0)


def to_wire(values, power):
    return (values * jnp.exp2(power)).astype(jnp.float16)


def from_wire(values, power):
    return values.astype(F32) * jnp.exp2(-power)


def scatter(values, power, axis, bit=1, count=2):
    place = (lax.axis_index(axis) // bit) % count
    rows = values.shape[-2] // count
    mark = min(MARK, rows)
    dim = values.ndim - 2
    total = lax.dynamic_slice_in_dim(values, place * rows, rows, dim)
    least = power
    for offset in range(1, count):
        to = place ^ offset
        last = to == count - 1
        start = to * rows - jnp.where(last, mark, 0)
        send = lax.dynamic_slice_in_dim(values, start, rows + mark, dim)
        line = lax.broadcasted_iota(jnp.int32, send.shape, dim)
        marked = jnp.where(last, line < mark, line >= rows)
        wire = jnp.where(marked, power, send * jnp.exp2(power)).astype(jnp.float16)
        got = swap(wire, axis, bit * offset)
        last = place == count - 1
        got_power = lax.dynamic_slice_in_dim(got, jnp.where(last, 0, rows), 1, dim)
        got_power = got_power.reshape(-1, D)[0:1, 0:1].astype(F32)
        body = lax.dynamic_slice_in_dim(got, jnp.where(last, mark, 0), rows, dim)
        total = total + from_wire(body, got_power)
        least = jnp.minimum(least, got_power)
    return total, least - float(count.bit_length() - 1)


def everyones(values, axis, bit=1, count=2):
    place = (lax.axis_index(axis) // bit) % count
    pieces = [values] + [swap(values, axis, bit * offset) for offset in range(1, count)]
    step = 1
    while step < count:
        flip = (place // step) % 2 == 1
        pieces = [
            jnp.where(flip, pieces[i ^ step], pieces[i]) for i in range(count)]
        step *= 2
    return pieces


def gather(values, axis, bit=1, count=2):
    return jnp.concatenate(everyones(values, axis, bit, count))


def add_all(values, axis, bit=1, count=2):
    pieces = everyones(values, axis, bit, count) if count > 2 else [
        values, swap(values, axis, bit)]
    total = pieces[0]
    for piece in pieces[1:]:
        total = total + piece
    return total


def data_groups():
    size = lax.axis_size("dp")
    groups = [(1, 2)]
    bit = 2
    while bit < size:
        count = 4 if bit * 4 <= size else 2
        groups.append((bit, count))
        bit *= count
    return groups


def dot_tn(a, b):
    return lax.dot_general(a, b, (((0,), (0,)), ((), ())), preferred_element_type=F32)


def pick_rows(index, rows):
    chosen = index[:, None] == jnp.arange(rows.shape[0], dtype=jnp.int32)[None, :]
    return dot(chosen.astype(BF16), rows).astype(BF16)


def on_device(
    tokens, loss_sensitivity, lengths, holder_sequence_list, master, moment_one, moment_two,
    adam_rates, iteration_tally,
):
    group_devices = lax.axis_size("zero")
    data_devices = lax.axis_size("dp")
    zero_index = lax.axis_index("zero")
    dp_index = lax.axis_index("dp")
    seq_len = loss_sensitivity.shape[1]
    group_seqs = tokens.shape[0]
    span = tokens.shape[1]
    slots = group_seqs // data_devices
    shard_rows = master.shape[0] // LANES
    tie = lax.optimization_barrier

    own = master.reshape(shard_rows, LANES)
    flat = lax.all_gather(own.astype(BF16), "zero", axis=0, tiled=True)

    arranged = holder_sequence_list.reshape(data_devices, group_devices, slots)
    group_order = lax.dynamic_index_in_dim(arranged, zero_index, 1, keepdims=False).reshape(-1)
    local_ids = group_order - zero_index * group_seqs
    dealt = tokens.at[local_ids].get(mode="promise_in_bounds")
    local_tok = lax.all_to_all(dealt, "dp", split_axis=0, concat_axis=0, tiled=True)
    my_seqs = lax.dynamic_slice_in_dim(group_order, dp_index * slots, slots)
    bound = lengths[my_seqs[0]]
    positions = jnp.arange(seq_len, dtype=jnp.int32)

    in_w, out_w, norm_gain, *params, e2, et = run_prepare(flat)
    cot = loss_sensitivity[0]
    gm = dot_nt(cot, out_w)
    cot_top = jnp.max(jnp.abs(cot)).astype(F32)
    local_tok, in_w, gm, cot_top = tie((local_tok, in_w, gm, cot_top))
    own_late, _ = tie((own, flat[:8]))
    whole_master = lax.all_gather(own_late, "zero", axis=0, tiled=True)

    def place(slot, at):
        return (at // span) * (slots * span) + slot * span + at % span

    source = jnp.where(positions < bound, place(0, positions), place(1, positions - bound))
    packed = pick_rows(source, local_tok.reshape(slots * seq_len, D))
    blocks = jnp.arange(data_devices, dtype=jnp.int32)[:, None, None] * span
    within = blocks + jnp.arange(span, dtype=jnp.int32)[None, None, :]
    within = within + jnp.arange(slots, dtype=jnp.int32)[None, :, None] * bound
    unpack_rows = jnp.minimum(within, seq_len - 1).reshape(-1)

    def spread(rows):
        return pick_rows(unpack_rows, rows).reshape(data_devices * slots, span, D)

    def send_back(picked):
        return lax.all_to_all(picked, "dp", split_axis=0, concat_axis=0, tiled=True)

    restore = jnp.zeros_like(local_ids).at[local_ids].set(
        jnp.arange(group_seqs, dtype=jnp.int32))
    mine = lax.dynamic_slice_in_dim(lengths, zero_index * group_seqs, group_seqs)
    at = dp_index * span + jnp.arange(span, dtype=jnp.int32)
    live = (at[None, :] < mine[:, None])[:, :, None]

    bound_arr = bound.reshape(1)
    tok = packed.astype(F32)
    nhat = tok * lax.rsqrt(jnp.mean(tok * tok, axis=1, keepdims=True) + EPS_NORM)
    normed = (nhat * norm_gain).astype(BF16)
    proj_z = dot_nt(normed, in_w[:INNER])
    proj = dot_nt(normed, in_w[INNER:PROJ])
    pair, dy, through, states, ggain, zmax = run_forward(
        proj_z, proj, gm, bound_arr, e2, et, params)
    result = (tok + dot(pair[1], out_w)).astype(BF16)
    picked = spread(result)
    picked, pair = tie((picked, pair))
    back_out = send_back(picked)
    root = float(seq_len) ** 0.5
    normed_norm = root * float(D) ** 0.5 * 1.02 * jnp.max(jnp.abs(norm_gain))
    mixed_norm = root * float(INNER) ** 0.5 * 1.02 * jnp.max(jnp.abs(params[5]))
    early_power = power_for(jnp.maximum(
        1.02 * root * jnp.max(zmax) * normed_norm, root * cot_top * mixed_norm))
    early = lax.dot_general(
        pair, jnp.stack([normed, cot]), (((1,), (1,)), ((0,), (0,))), preferred_element_type=F32)
    early, early_power = scatter(early, early_power, "zero", 1)
    early, early_power, dy = tie((early.reshape(INNER, D), early_power, dy))
    early, early_power = scatter(early, early_power, "zero", 2)
    window, grad_tok, small = run_backward(
        proj, dy, through, states, pair, packed, cot, in_w, norm_gain, ggain,
        bound_arr, e2, et, params)
    window, small, back_out, early, early_power, whole_master = tie(
        (window, small, back_out, early, early_power, whole_master))

    groups = data_groups()
    late = lax.dot_general(
        window, jnp.stack([normed, normed]), (((1,), (1,)), ((0,), (0,))),
        preferred_element_type=F32)
    late_power = power_for(1.02 * root * jnp.max(small[7:8]) * normed_norm)
    late, late_power = scatter(late, late_power, "zero", 1)
    early, early_power = scatter(early, early_power, "dp", *groups[0])
    small = add_all(small, "zero", 1)
    late, late_power, early, early_power, small = tie(
        (late.reshape(WINDOW, D), late_power, early, early_power, small))
    late, late_power = scatter(late, late_power, "zero", 2)
    for group in groups[1:]:
        early, early_power = scatter(early, early_power, "dp", *group)
    early = to_wire(early, early_power)
    small = add_all(small, "zero", 2)
    picked_grad = spread(grad_tok)
    late, late_power, early, small, picked_grad = tie(
        (late, late_power, early, small, picked_grad))
    late, late_power = scatter(late, late_power, "dp", *groups[0])
    for group in reversed(groups[1:]):
        early = gather(early, "dp", *group)
    small = add_all(small, "dp", *groups[0])
    late, late_power, early, small = tie((late, late_power, early, small))
    for group in groups[1:]:
        late, late_power = scatter(late, late_power, "dp", *group)
        small = add_all(small, "dp", *group)
    late = to_wire(late, late_power)
    early = from_wire(gather(early, "dp", *groups[0]), early_power)
    late, early, small = tie((late, early, small))
    for group in reversed(groups[1:]):
        late = gather(late, "dp", *group)
    early_other = swap(early, "zero", 1)
    late, early_other, picked_grad = tie((late, early_other, picked_grad))
    back_grad = send_back(picked_grad)
    late = from_wire(gather(late, "dp", *groups[0]), late_power)
    late_other = swap(late, "zero", 1)

    steps_f = iteration_tally[0].astype(F32)
    rates = jnp.stack([
        1.0 / (1.0 - jnp.power(BETA_ONE, steps_f)), 1.0 / (1.0 - jnp.power(BETA_TWO, steps_f))])
    who = jnp.stack([zero_index // 2, zero_index % 2]).astype(jnp.int32)
    first = moment_one.reshape(shard_rows, LANES)
    second = moment_two.reshape(shard_rows, LANES)
    grad_shard, ratio = run_adam(
        who, rates, early, early_other, late, late_other, small, first, second)
    mine = ratio.astype(jnp.float16)
    mine, grad_shard, back_out = tie((mine, grad_shard, back_out))
    core = swap(mine, "zero", 1)
    across = swap(mine, "zero", 2)
    first_next = BETA_ONE * first + (1.0 - BETA_ONE) * grad_shard
    second_next = BETA_TWO * second + (1.0 - BETA_TWO) * grad_shard * grad_shard
    back_rows = back_out.at[restore].get(mode="promise_in_bounds")
    tokens_out = jnp.where(live, back_rows, tokens)
    new_master = jnp.zeros((group_devices, shard_rows, LANES), F32)
    whole_master = whole_master.reshape(group_devices, shard_rows, LANES)

    def put(new_master, piece, offset):
        shard = zero_index ^ offset
        old = lax.dynamic_index_in_dim(whole_master, shard, 0, keepdims=False)
        new = old - adam_rates[0] * (piece.astype(F32) + adam_rates[1] * old)
        return lax.dynamic_update_index_in_dim(new_master, new, shard, 0)

    new_master = put(put(new_master, mine, 0), core, 1)
    across, new_master, tokens_out, first_next, second_next = tie(
        (across, new_master, tokens_out, first_next, second_next))
    across_core = swap(across, "zero", 1)
    new_master = put(new_master, across, 2)
    across_core, new_master = tie((across_core, new_master))
    new_master = put(new_master, across_core, 3)
    back_grad, new_master = tie((back_grad, new_master))
    grad_tokens = jnp.where(
        live, back_grad.at[restore].get(mode="promise_in_bounds"), jnp.zeros((), BF16))
    return (
        tokens_out, grad_tokens, new_master.reshape(-1), grad_shard.reshape(-1),
        first_next.reshape(-1), second_next.reshape(-1))


def solution(mesh):
    return jax.shard_map(
        on_device,
        mesh=mesh,
        in_specs=(
            P("zero", "dp", None), P(("dp", "zero"), None, None), P(), P(),
            P("zero"), P("zero"), P("zero"), P(), P(),
        ),
        out_specs=(
            P("zero", "dp", None), P("zero", "dp", None), P(), P("zero"), P("zero"), P("zero"),
        ),
        check_vma=False,
    )
```

```python
import jax
import jax.numpy as jnp
from jax import lax
from jax.experimental import pallas as pl
from jax.experimental.pallas import tpu as pltpu
from jax.sharding import PartitionSpec as P

D = 768
HEADS = 24
HEADDIM = 64
STATE = 128
CONV = 4
INNER = 1536
XBC = 1792
PROJ = 3352
Q = 128
LATE = PROJ - INNER
WINDOW = 1024
PAIRS = HEADS // 2
EPS_NORM = 1e-05
NEG = -1e30
LOG2E = 1.4426950408889634
F32 = jnp.float32
BF16 = jnp.bfloat16


def dot(a, b):
    return lax.dot_general(a, b, (((1,), (0,)), ((), ())), preferred_element_type=F32)


def dot_nt(a, b):
    return lax.dot_general(a, b, (((1,), (1,)), ((), ())), preferred_element_type=F32)


def split2(v):
    hi = v.astype(BF16)
    return hi, (v - hi.astype(F32)).astype(BF16)


def split3(v):
    hi = v.astype(BF16)
    rest = v - hi.astype(F32)
    mid = rest.astype(BF16)
    return hi, mid, (rest - mid.astype(F32)).astype(BF16)


def wide_left(v):
    hi, lo = split2(v)
    return jnp.concatenate([hi, lo, hi], axis=1)


def tall_right(v):
    hi, lo = split2(v)
    return jnp.concatenate([hi, hi, lo], axis=0)


def split_pair(v, masks):
    hi, lo = split2(v)
    return jnp.concatenate([
        jnp.concatenate([hi * masks[0], lo * masks[0]], axis=1),
        jnp.concatenate([hi * masks[1], lo * masks[1]], axis=1)], axis=0)


def sigmoid(v):
    return lax.logistic(v)


def softplus(v):
    return jnp.maximum(v, 0.0) + jnp.log1p(jnp.exp(-jnp.abs(v)))


def iota(shape, dim):
    return lax.broadcasted_iota(jnp.int32, shape, dim)


def expand(v, e_ref):
    hi, lo = split2(v)
    return dot(jnp.concatenate([hi, lo], axis=1), e_ref[...])


def head_sum(v, et_ref):
    hi, lo = split2(v)
    return dot(hi, et_ref[...]) + dot(lo, et_ref[...])


def quarters(out):
    return out[:Q, :Q] + (out[:Q, Q:] + out[Q:, :Q])


def chunk_masks(t0, bound):
    rows = t0 + iota((Q, 1), 0)
    rr = t0 + iota((Q, Q), 0)
    cc = t0 + iota((Q, Q), 1)
    return rows, rr, cc


def conv_rows(ext_ref, w_ref, b_ref, rows, bound):
    total = b_ref[...] + w_ref[3:4, :] * ext_ref[8 : 8 + Q, :]
    for back in (1, 2, 3):
        ok = jnp.logical_or(rows - back >= bound, rows < bound).astype(F32)
        total = total + w_ref[3 - back : 4 - back, :] * (ext_ref[8 - back : 8 - back + Q, :] * ok)
    return total


def decay_parts(dt_raw, dtb_ref, alog_ref, rr, cc):
    dt_in = dt_raw + dtb_ref[...]
    dt_pos = softplus(dt_in)
    rate = -jnp.exp(alog_ref[...])
    step = dt_pos * rate
    tri = (cc <= rr).astype(F32).astype(BF16)
    s_hi, s_mid, s_lo = split3(step)
    cum = dot(tri, s_hi) + dot(tri, s_mid) + dot(tri, s_lo)
    return dt_in, dt_pos, rate, cum


def forward_kernel(
    bound_ref, z_ref, proj_ref, gm_ref, e_ref, et_ref, convw_ref, convb_ref, dtb_ref, alog_ref,
    skip_ref, gain_ref,
    pair_ref, dy_ref, through_ref, state_ref, ggain_ref, zmax_ref,
    ext_ref, dt_ref, carry_ref, xd_ref, acc_ref, cumt_ref,
):
    step = pl.program_id(0)
    bound = bound_ref[0]
    t0 = step * Q

    @pl.when(step == 0)
    def _():
        ext_ref[0:8, :] = jnp.zeros((8, XBC), F32)
        carry_ref[...] = jnp.zeros_like(carry_ref)
        dt_ref[...] = jnp.zeros_like(dt_ref)
        ggain_ref[...] = jnp.zeros_like(ggain_ref)
        zmax_ref[...] = jnp.zeros_like(zmax_ref)

    rows, rr, cc = chunk_masks(t0, bound)
    ext_ref[8 : 8 + Q, :] = proj_ref[:, :XBC]
    pre = conv_rows(ext_ref, convw_ref, convb_ref, rows, bound)
    ext_ref[0:8, :] = ext_ref[Q : Q + 8, :]
    conv_out = pre * sigmoid(pre)
    x = conv_out[:, :INNER]
    b_rows = conv_out[:, INNER : INNER + STATE]
    c_rows = conv_out[:, INNER + STATE :]
    dt_ref[:, 0:HEADS] = proj_ref[:, XBC:LATE]
    _, dt_pos, _, cum = decay_parts(dt_ref[...], dtb_ref, alog_ref, rr, cc)
    cum_end = cum[Q - 1 : Q, :]
    keep = jnp.logical_or(rows < bound, bound < t0).astype(F32)
    in_last = jnp.logical_or(rows >= bound, bound > t0 + Q - 1).astype(F32)
    whole = jnp.logical_or(bound < t0, bound > t0 + Q - 1).astype(F32)
    from_start = jnp.exp(cum) * keep
    to_end = jnp.exp(cum_end - cum) * in_last
    carry_scale = jnp.exp(cum_end) * whole
    allowed = jnp.logical_and(cc <= rr, (cc >= bound) == (rr >= bound))
    cum2 = cum * LOG2E
    cumt_ref[...] = cum2.T

    state = carry_ref[...]
    state_ref[0] = state
    spread = expand(jnp.concatenate(
        [dt_pos, to_end, from_start, jnp.broadcast_to(carry_scale, (16, 128))], axis=0), e_ref)
    xd = x * spread[:Q]
    xd_ref[...] = xd
    acc = dot(wide_left(c_rows), tall_right(state)) * spread[2 * Q : 3 * Q]
    acc_ref[...] = acc + skip_ref[...] * x
    b_t = b_rows.T
    carry_ref[...] = state * spread[3 * Q : 3 * Q + 1] + dot(
        wide_left(b_t), tall_right(xd * spread[Q : 2 * Q]))
    gram = dot(wide_left(c_rows), tall_right(b_t))
    first = iota((Q, Q), 1) < HEADDIM
    first_b = (first.astype(F32).astype(BF16), 1.0 - first.astype(F32).astype(BF16))
    for pair in range(PAIRS):
        parts = []
        for head in (2 * pair, 2 * pair + 1):
            differ = cum2[:, head : head + 1] - cumt_ref[head : head + 1, :]
            parts.append(gram * jnp.exp2(jnp.where(allowed, differ, NEG)))
        left = jnp.concatenate(split2(jnp.concatenate(parts, axis=1)), axis=0)
        lanes = slice(pair * 128, pair * 128 + 128)
        xp = xd_ref[:, lanes]
        out = dot(left, split_pair(xp, first_b))
        acc_ref[:, lanes] += out[:Q, :128] + (out[:Q, 128:] + out[Q:, :128])
    scanned = acc_ref[...]
    z = z_ref[...]
    sig_z = sigmoid(z)
    silu_z = z * sig_z
    gated = scanned * silu_z
    ginv = lax.rsqrt(jnp.mean(gated * gated, axis=1, keepdims=True) + EPS_NORM)
    mhat = gated * ginv
    pair_ref[1] = (mhat * gain_ref[...]).astype(BF16)
    gm = gm_ref[...]
    ggain_ref[...] += jnp.sum(mhat * gm, axis=0, keepdims=True)
    gmg = gm * gain_ref[...]
    ggated = ginv * (gmg - mhat * jnp.mean(mhat * gmg, axis=1, keepdims=True))
    dy = ggated * silu_z
    dy_ref[...] = dy
    grad_z = ggated * scanned * (sig_z * (1.0 + z * (1.0 - sig_z)))
    zmax_ref[...] = jnp.maximum(zmax_ref[...], jnp.max(jnp.abs(grad_z), axis=0, keepdims=True))
    pair_ref[0] = grad_z.astype(BF16)
    through_ref[...] = head_sum(dy * (scanned - skip_ref[...] * x), et_ref)


def const_spec(shape):
    return pl.BlockSpec(shape, lambda *_: (0,) * len(shape))


def run_forward(z, proj, gm, bound, e2, et, params):
    n = proj.shape[0]
    steps = n // Q
    return pl.pallas_call(
        forward_kernel,
        grid=(steps,),
        in_specs=[
            pl.BlockSpec(memory_space=pltpu.SMEM),
            pl.BlockSpec((Q, INNER), lambda i: (i, 0)),
            pl.BlockSpec((Q, LATE), lambda i: (i, 0)),
            pl.BlockSpec((Q, INNER), lambda i: (i, 0)),
            const_spec((256, INNER)), const_spec((INNER, 128)),
            const_spec((8, XBC)), const_spec((1, XBC)), const_spec((1, 128)),
            const_spec((1, 128)), const_spec((1, INNER)), const_spec((1, INNER)),
        ],
        out_specs=[
            pl.BlockSpec((2, Q, INNER), lambda i: (0, i, 0)),
            pl.BlockSpec((Q, INNER), lambda i: (i, 0)),
            pl.BlockSpec((Q, 128), lambda i: (i, 0)),
            pl.BlockSpec((1, STATE, INNER), lambda i: (i, 0, 0)),
            const_spec((1, INNER)), const_spec((1, INNER)),
        ],
        out_shape=[
            jax.ShapeDtypeStruct((2, n, INNER), BF16),
            jax.ShapeDtypeStruct((n, INNER), F32),
            jax.ShapeDtypeStruct((n, 128), F32),
            jax.ShapeDtypeStruct((steps, STATE, INNER), F32),
            jax.ShapeDtypeStruct((1, INNER), F32),
            jax.ShapeDtypeStruct((1, INNER), F32),
        ],
        scratch_shapes=[
            pltpu.VMEM((Q + 8, XBC), F32),
            pltpu.VMEM((Q, 128), F32),
            pltpu.VMEM((STATE, INNER), F32),
            pltpu.VMEM((Q, INNER), F32),
            pltpu.VMEM((Q, INNER), F32),
            pltpu.VMEM((128, Q), F32),
        ],
        compiler_params=pltpu.CompilerParams(
            dimension_semantics=("arbitrary",), vmem_limit_bytes=48 * 2**20),
        cost_estimate=pl.CostEstimate(
            flops=30 * 10**9, bytes_accessed=40 * 2**20, transcendentals=10**7),
    )(bound, z, proj, gm, e2, et, *params)


def backward_kernel(last, final, *refs):
    (bound_ref, proj_ref, before_ref, dy_ref, through_ref, state_ref, gz_ref, tok_ref, cot_ref,
     in_ref, norm_ref, ggain_ref,
     e_ref, et_ref, convw_ref, convb_ref, dtb_ref, alog_ref, skip_ref) = refs[:19]
    refs = refs[19:]
    if final:
        lam_in_ref, sum_in_ref, dtw_in_ref = refs[:3]
        window_ref, gtok_ref, small_ref = refs[5:8]
        refs = refs[8:]
    else:
        window_ref, gtok_ref, lamc_ref, sumc_ref, dtwc_ref = refs[:5]
        refs = refs[5:]
    (total_ref, gsmall_ref, dtw_ref, gp_ref, ext_ref, dt_ref, lam_ref, dsum_ref, xd_ref, g_ref,
     gnext_ref, cumt_ref) = refs
    gskip_ref = total_ref.at[32:33, 0:INNER]
    step = pl.program_id(0)
    steps = pl.num_programs(0)
    bound = bound_ref[0]
    chunk = last - step
    t0 = chunk * Q

    @pl.when(step == 0)
    def _():
        dt_ref[...] = jnp.zeros_like(dt_ref)
        if final:
            lam_ref[...] = lam_in_ref[...]
            total_ref[...] = sum_in_ref[0:40, :]
            gnext_ref[Q : Q + 8, :] = sum_in_ref[40:48, :]
            dsum_ref[...] = sum_in_ref[48:56, 0:128]
            gsmall_ref[...] = sum_in_ref[48:56, 128:256]
            dtw_ref[...] = dtw_in_ref[...]
        else:
            lam_ref[...] = jnp.zeros_like(lam_ref)
            total_ref[...] = jnp.zeros_like(total_ref)
            gnext_ref[Q : Q + 8, :] = jnp.zeros((8, XBC), F32)
            dsum_ref[...] = jnp.zeros_like(dsum_ref)
            gsmall_ref[...] = jnp.zeros_like(gsmall_ref)
            dtw_ref[...] = jnp.zeros_like(dtw_ref)

    rows, rr, cc = chunk_masks(t0, bound)
    dy = dy_ref[...]
    first_chunk = (t0 > 0).astype(F32)
    ext_ref[0:8, :] = before_ref[:, :XBC] * first_chunk
    ext_ref[8 : 8 + Q, :] = proj_ref[:, :XBC]
    pre = conv_rows(ext_ref, convw_ref, convb_ref, rows, bound)
    sig_pre = sigmoid(pre)
    conv_out = pre * sig_pre
    x = conv_out[:, :INNER]
    b_rows = conv_out[:, INNER : INNER + STATE]
    c_rows = conv_out[:, INNER + STATE :]
    dt_ref[:, 0:HEADS] = proj_ref[:, XBC:LATE]
    dt_in, dt_pos, rate, cum = decay_parts(dt_ref[...], dtb_ref, alog_ref, rr, cc)
    cum_end = cum[Q - 1 : Q, :]
    keep = jnp.logical_or(rows < bound, bound < t0).astype(F32)
    in_last = jnp.logical_or(rows >= bound, bound > t0 + Q - 1).astype(F32)
    whole = jnp.logical_or(bound < t0, bound > t0 + Q - 1).astype(F32)
    from_start = jnp.exp(cum) * keep
    to_end = jnp.exp(cum_end - cum) * in_last
    carry_scale = jnp.exp(cum_end) * whole
    allowed_t = jnp.logical_and(rr <= cc, (cc >= bound) == (rr >= bound))
    cum2 = cum * LOG2E
    cumt_ref[...] = cum2.T
    c_t = c_rows.T
    gram_t = dot(wide_left(b_rows), tall_right(c_t))
    spread = expand(jnp.concatenate(
        [dt_pos, to_end, from_start, jnp.broadcast_to(carry_scale, (16, 128))], axis=0), e_ref)
    dt_all = spread[:Q]
    end_all = spread[Q : 2 * Q]
    xd = x * dt_all
    xd_ref[...] = xd
    skip = skip_ref[...]
    gskip_ref[...] += jnp.sum(dy * x, axis=0, keepdims=True)
    lam = lam_ref[...]
    lam_hi, lam_lo = split2(lam)
    g_ref[...] = (
        dot(wide_left(b_rows), jnp.concatenate([lam_hi, lam_hi, lam_lo], axis=0)) * end_all
    )
    grad_b = quarters(dot_nt(
        jnp.concatenate(split2(xd * end_all), axis=0), jnp.concatenate([lam_hi, lam_lo], axis=0)))
    state = state_ref[0]
    dye_hi, dye_lo = split2(dy * spread[2 * Q : 3 * Q])
    grad_c = quarters(dot_nt(
        jnp.concatenate([dye_hi, dye_lo], axis=0), jnp.concatenate(split2(state), axis=0)))
    lam_new = lam * spread[3 * Q : 3 * Q + 1] + dot(
        wide_left(c_t), jnp.concatenate([dye_hi, dye_hi, dye_lo], axis=0)
    )
    lam_ref[...] = lam_new
    ended = dsum_ref[0:1, :]
    first = iota((Q, Q), 1) < HEADDIM
    first_b = (first.astype(F32).astype(BF16), 1.0 - first.astype(F32).astype(BF16))
    first_row = (iota((Q, Q), 0) < HEADDIM).astype(F32).astype(BF16)
    first_row = (first_row, 1.0 - first_row)
    gram_grad = jnp.zeros((Q, Q), F32)
    for pair in range(PAIRS):
        lanes = slice(pair * 128, pair * 128 + 128)
        weights = []
        for head in (2 * pair, 2 * pair + 1):
            differ = cumt_ref[head : head + 1, :] - cum2[:, head : head + 1]
            weights.append(jnp.exp2(jnp.where(allowed_t, differ, NEG)))
        left = jnp.concatenate([gram_t * weights[0], gram_t * weights[1]], axis=1)
        left = jnp.concatenate(split2(left), axis=0)
        dyp = dy_ref[:, lanes]
        out = dot(left, split_pair(dyp, first_b))
        g_ref[:, lanes] += out[:Q, :128] + (out[:Q, 128:] + out[Q:, :128])
        dyt_hi, dyt_lo = split2(dyp.T)
        right_hi = jnp.concatenate([dyt_hi * first_row[0], dyt_hi * first_row[1]], axis=1)
        right_lo = jnp.concatenate([dyt_lo * first_row[0], dyt_lo * first_row[1]], axis=1)
        outer = dot(
            wide_left(xd_ref[:, lanes]), jnp.concatenate([right_hi, right_hi, right_lo], axis=0))
        gram_grad = gram_grad + (outer[:, :128] * weights[0] + outer[:, 128:] * weights[1])
    g = g_ref[...]
    grad_x = dt_all * g + skip * dy
    sums = dot(jnp.concatenate(
        split2(x * g) + split2(jnp.broadcast_to(
            jnp.sum(lam_new * state, axis=0, keepdims=True), (16, INNER))), axis=0), et_ref[...])
    direct = sums[:Q] + sums[Q : 2 * Q]
    balance = through_ref[...] - dt_pos * direct
    keep_t = allowed_t.astype(F32).astype(BF16)
    b_hi, b_mid, b_lo = split3(balance)
    grad_step = dot(keep_t, b_hi) + dot(keep_t, b_mid) + dot(keep_t, b_lo) + in_last * ended
    dsum_ref[...] = sums[2 * Q : 2 * Q + 8] + sums[2 * Q + 16 : 2 * Q + 24]
    grad_dt = (direct + rate * grad_step) * sigmoid(dt_in)
    gsmall_ref[0:1, :] += jnp.sum(grad_dt, axis=0, keepdims=True)
    gsmall_ref[1:2, :] += rate * jnp.sum(dt_pos * grad_step, axis=0, keepdims=True)
    grad_c = grad_c + dot(wide_left(gram_grad.T), tall_right(b_rows))
    grad_b = grad_b + dot(wide_left(gram_grad), tall_right(c_rows))
    slope = sig_pre * (1.0 + pre * (1.0 - sig_pre))
    gnext_ref[0:Q, :INNER] = grad_x * slope[:, :INNER]
    gnext_ref[0:Q, INNER : INNER + STATE] = grad_b * slope[:, INNER : INNER + STATE]
    gnext_ref[0:Q, INNER + STATE :] = grad_c * slope[:, INNER + STATE :]
    gcp = gnext_ref[0:Q, :]
    total_ref[4:5, :] += jnp.sum(gcp, axis=0, keepdims=True)
    total_ref[3:4, :] += jnp.sum(gcp * ext_ref[8 : 8 + Q, :], axis=0, keepdims=True)
    total = convw_ref[3:4, :] * gcp
    for back in (1, 2, 3):
        ok = jnp.logical_or(rows - back >= bound, rows < bound).astype(F32)
        total_ref[3 - back : 4 - back, :] += jnp.sum(
            gcp * (ext_ref[8 - back : 8 - back + Q, :] * ok), axis=0, keepdims=True)
        okn = jnp.logical_or(rows >= bound, rows + back < bound).astype(F32)
        total = total + convw_ref[3 - back : 4 - back, :] * (gnext_ref[back : back + Q, :] * okn)
    total_ref[7:8, :] = jnp.maximum(
        total_ref[7:8, :], jnp.max(jnp.abs(total), axis=0, keepdims=True))
    total = total.astype(BF16)
    window_ref[0] = total[:, :WINDOW]
    window_ref[1] = total[:, XBC - WINDOW :]
    gnext_ref[Q : Q + 8, :] = gnext_ref[0:8, :]
    half = chunk % 2
    at = pl.multiple_of(half * Q, Q)
    gp_ref[pl.ds(at, Q), :INNER] = gz_ref[0]
    gp_ref[pl.ds(at, Q), INNER : INNER + XBC] = total
    gp_ref[pl.ds(at, Q), INNER + XBC :] = grad_dt.astype(BF16)

    @pl.when(half == 0)
    def _():
        grad_normed = dot(gp_ref[...], in_ref[: INNER + XBC + 128, :])
        tok = tok_ref[...].astype(F32)
        rinv = lax.rsqrt(jnp.mean(tok * tok, axis=1, keepdims=True) + EPS_NORM)
        nhat = tok * rinv
        gain = norm_ref[...]
        gng = grad_normed * gain
        gtok_ref[...] = (cot_ref[...].astype(F32) + rinv * (
            gng - nhat * jnp.mean(nhat * gng, axis=1, keepdims=True))).astype(BF16)
        total_ref[6:7, :D] += jnp.sum(nhat * grad_normed, axis=0, keepdims=True)
        normed = (nhat * gain).astype(BF16)
        gdt = gp_ref[:, INNER + XBC :].astype(F32)
        dtw_ref[...] += dot(jnp.concatenate(
            [gdt[:Q].T, gdt[Q:].T], axis=1).astype(BF16), normed)

    @pl.when(step == steps - 1)
    def _():
        if final:
            skips = head_sum(jnp.broadcast_to(gskip_ref[...], (8, INNER)), et_ref)
            small_ref[...] = total_ref[0:32, :]
            small_ref[5:6, :INNER] = ggain_ref[...]
            small_ref[6:7, D : D + 128] = gsmall_ref[0:1, :]
            small_ref[6:7, D + 128 : D + 256] = gsmall_ref[1:2, :]
            small_ref[6:7, D + 256 : D + 384] = skips[0:1, :]
            small_ref[8 : 8 + HEADS, :D] = dtw_ref[0:HEADS, :]
        else:
            lamc_ref[...] = lam_ref[...]
            sumc_ref[0:40, :] = total_ref[...]
            sumc_ref[40:48, :] = gnext_ref[Q : Q + 8, :]
            sumc_ref[48:56, 0:128] = dsum_ref[...]
            sumc_ref[48:56, 128:256] = gsmall_ref[...]
            sumc_ref[48:56, 256:] = jnp.zeros((8, XBC - 256), F32)
            dtwc_ref[...] = dtw_ref[...]


def run_backward(
    half, carried, proj, dy, through, states, pair, tok, cot, in_w, norm_gain, ggain, bound, e2, et,
    params
):
    n = proj.shape[0]
    chunks = n // Q
    steps = chunks // 2
    last = chunks - 1 - half * steps
    final = half == 1

    def rev(i):
        return (last - i, 0)

    def rev_two(i):
        return ((last - i) // 2, 0)

    arrays = [bound, proj, proj, dy, through, states, pair, tok, cot, in_w, norm_gain, ggain,
              e2, et, *params[:5]]
    in_specs = [
        pl.BlockSpec(memory_space=pltpu.SMEM),
        pl.BlockSpec((Q, LATE), rev),
        pl.BlockSpec((8, LATE), lambda i: (jnp.maximum((last - i) * (Q // 8) - 1, 0), 0)),
        pl.BlockSpec((Q, INNER), rev),
        pl.BlockSpec((Q, 128), rev),
        pl.BlockSpec((1, STATE, INNER), lambda i: (last - i, 0, 0)),
        pl.BlockSpec((1, Q, INNER), lambda i: (0, last - i, 0)),
        pl.BlockSpec((2 * Q, D), rev_two), pl.BlockSpec((2 * Q, D), rev_two),
        const_spec(in_w.shape), const_spec((1, D)), const_spec((1, INNER)),
        const_spec((256, INNER)), const_spec((INNER, 128)),
        const_spec((8, XBC)), const_spec((1, XBC)), const_spec((1, 128)),
        const_spec((1, 128)), const_spec((1, INNER)),
    ]
    out_specs = [
        pl.BlockSpec((2, Q, WINDOW), lambda i: (0, last - i, 0)),
        pl.BlockSpec((2 * Q, D), rev_two),
    ]
    out_shape = [
        jax.ShapeDtypeStruct((2, n, WINDOW), BF16), jax.ShapeDtypeStruct((n, D), BF16)]
    carry_shapes = [(STATE, INNER), (56, XBC), (128, D)]
    aliases = {}
    if final:
        window, gtok, *carry = carried
        arrays += carry + [window, gtok]
        in_specs += [const_spec(shape) for shape in carry_shapes]
        in_specs += [pl.BlockSpec(memory_space=pl.ANY), pl.BlockSpec(memory_space=pl.ANY)]
        aliases = {len(arrays) - 2: 0, len(arrays) - 1: 1}
        out_specs.append(const_spec((32, XBC)))
        out_shape.append(jax.ShapeDtypeStruct((32, XBC), F32))
    else:
        out_specs += [const_spec(shape) for shape in carry_shapes]
        out_shape += [jax.ShapeDtypeStruct(shape, F32) for shape in carry_shapes]

    def kernel(*refs):
        backward_kernel(last, final, *refs)

    return pl.pallas_call(
        kernel,
        grid=(steps,),
        in_specs=in_specs,
        out_specs=out_specs,
        out_shape=out_shape,
        scratch_shapes=[
            pltpu.VMEM((40, XBC), F32),
            pltpu.VMEM((8, 128), F32),
            pltpu.VMEM((128, D), F32),
            pltpu.VMEM((2 * Q, INNER + XBC + 128), BF16),
            pltpu.VMEM((Q + 8, XBC), F32),
            pltpu.VMEM((Q, 128), F32),
            pltpu.VMEM((STATE, INNER), F32),
            pltpu.VMEM((8, 128), F32),
            pltpu.VMEM((Q, INNER), F32),
            pltpu.VMEM((Q, INNER), F32),
            pltpu.VMEM((Q + 8, XBC), F32),
            pltpu.VMEM((128, Q), F32),
        ],
        input_output_aliases=aliases,
        compiler_params=pltpu.CompilerParams(
            dimension_semantics=("arbitrary",), vmem_limit_bytes=48 * 2**20),
        cost_estimate=pl.CostEstimate(
            flops=28 * 10**9, bytes_accessed=26 * 2**20, transcendentals=10**7),
    )(*arrays)


BETA_ONE = 0.9
BETA_TWO = 0.95
EPS_ADAM = 1e-08
LANES = 128
NORM_ROWS = D // LANES
IN_ROWS = PROJ * D // LANES
CONVW_ROWS = CONV * XBC // LANES
CONVB_ROWS = XBC // LANES
GAIN_ROWS = INNER // LANES
OUT_ROWS = INNER * D // LANES
DT_ROWS = HEADS * D // LANES
SMALL_ROWS = DT_ROWS + CONVW_ROWS + CONVB_ROWS + 3 + GAIN_ROWS
OUT_START = NORM_ROWS + IN_ROWS + SMALL_ROWS - DT_ROWS
LATE_START = NORM_ROWS + INNER * NORM_ROWS
LEAD = 896
STAGE_ROWS = 16264
ADAM_BLOCKS = 10
F16_TOP = 30000.0
MARK = 16


PREP_STEPS = 7
IN_BLOCK = 512
OUT_BLOCK = 256
SMALL_START = NORM_ROWS + IN_ROWS


def prepare_kernel(
    flat_ref,
    in_ref, out_ref, norm_ref, convw_ref, convb_ref, dtb_ref, alog_ref, skip_ref, gain_ref,
    e_ref, et_ref,
    stage_ref,
):
    step = pl.program_id(0)

    @pl.when(step == 0)
    def _():
        rows = flat_ref[0:16, :].astype(F32)
        for lane in range(NORM_ROWS):
            norm_ref[:, lane * LANES : lane * LANES + LANES] = rows[lane : lane + 1, :]
        low = SMALL_START // 16 * 16
        stage_ref[0:112, :] = flat_ref[low : low + 112, :].astype(F32)
        at = SMALL_START - low
        convw_ref[...] = jnp.zeros_like(convw_ref)
        for tap in range(CONV):
            for lane in range(CONVB_ROWS):
                convw_ref[tap : tap + 1, lane * LANES : lane * LANES + LANES] = stage_ref[
                    at : at + 1, :]
                at += 1
        for lane in range(CONVB_ROWS):
            convb_ref[:, lane * LANES : lane * LANES + LANES] = stage_ref[at : at + 1, :]
            at += 1
        heads = iota((1, LANES), 1) < HEADS
        dtb_ref[...] = jnp.where(heads, stage_ref[at : at + 1, :], 0.0)
        alog_ref[...] = jnp.where(heads, stage_ref[at + 1 : at + 2, :], 0.0)
        skips = jnp.where(heads, stage_ref[at + 2 : at + 3, :], 0.0)
        at += 3
        for lane in range(GAIN_ROWS):
            gain_ref[:, lane * LANES : lane * LANES + LANES] = stage_ref[at : at + 1, :]
            at += 1
        one = (iota((128, INNER), 1) // HEADDIM == iota((128, INNER), 0)).astype(F32).astype(BF16)
        e_ref[0:128, :] = one
        e_ref[128:256, :] = one
        et_ref[...] = (
            iota((INNER, 128), 0) // HEADDIM == iota((INNER, 128), 1)).astype(F32).astype(BF16)
        skip_ref[...] = dot(jnp.broadcast_to(skips, (16, LANES)).astype(BF16), one)[0:1, :]

    def block(start, offset, rows, dest_ref):
        size = rows * NORM_ROWS + 16
        at = pl.multiple_of(start + step * (rows * NORM_ROWS), 16)
        stage_ref[0:size, :] = flat_ref[pl.ds(at, size), :].astype(F32)
        for lane in range(NORM_ROWS):
            dest_ref[:, lane * LANES : lane * LANES + LANES] = stage_ref[
                pl.ds(offset + lane, rows, stride=NORM_ROWS), :].astype(BF16)

    block(0, NORM_ROWS, IN_BLOCK, in_ref)

    @pl.when(step == PREP_STEPS - 1)
    def _():
        used = PROJ - (PREP_STEPS - 1) * IN_BLOCK
        in_ref[used:, :] = jnp.zeros((IN_BLOCK - used, D), BF16)

    @pl.when(step < INNER // OUT_BLOCK)
    def _():
        low = OUT_START // 16 * 16
        block(low, OUT_START - low, OUT_BLOCK, out_ref)


def run_prepare(flat):
    vector = lambda n: jax.ShapeDtypeStruct((1, n), F32)
    return pl.pallas_call(
        prepare_kernel,
        grid=(PREP_STEPS,),
        in_specs=[const_spec(flat.shape)],
        out_specs=[
            pl.BlockSpec((IN_BLOCK, D), lambda i: (i, 0)),
            pl.BlockSpec((OUT_BLOCK, D), lambda i: (jnp.minimum(i, INNER // OUT_BLOCK - 1), 0)),
            const_spec((1, D)), const_spec((8, XBC)), const_spec((1, XBC)), const_spec((1, 128)),
            const_spec((1, 128)), const_spec((1, INNER)), const_spec((1, INNER)),
            const_spec((256, INNER)), const_spec((INNER, 128)),
        ],
        out_shape=[
            jax.ShapeDtypeStruct((PREP_STEPS * IN_BLOCK, D), BF16),
            jax.ShapeDtypeStruct((INNER, D), BF16),
            vector(D), jax.ShapeDtypeStruct((8, XBC), F32), vector(XBC), vector(128), vector(128),
            vector(INNER), vector(INNER),
            jax.ShapeDtypeStruct((256, INNER), BF16), jax.ShapeDtypeStruct((INNER, 128), BF16),
        ],
        scratch_shapes=[pltpu.VMEM((IN_BLOCK * NORM_ROWS + 16, LANES), F32)],
        compiler_params=pltpu.CompilerParams(
            dimension_semantics=("arbitrary",), vmem_limit_bytes=40 * 2**20),
        cost_estimate=pl.CostEstimate(
            flops=10**9, bytes_accessed=16 * 2**20, transcendentals=0),
    )(flat)


def adam_kernel(
    who_ref, rate_ref, early_ref, early_other_ref, late_ref, late_other_ref, small_ref,
    first_ref, second_ref,
    grad_ref, ratio_ref,
    stage_ref,
):
    step = pl.program_id(0)
    upper = who_ref[0]
    mine = who_ref[1]
    block = first_ref.shape[0]
    half = 2 * block * ADAM_BLOCKS

    @pl.when(step == 0)
    def _():
        early_at = LEAD + jnp.where(upper == 1, OUT_START - half, NORM_ROWS)
        window = LATE_START + (XBC - WINDOW) * NORM_ROWS
        late_at = LEAD + jnp.where(upper == 1, window - half, LATE_START)
        for source_ref, at, which in (
            (late_ref, late_at, mine), (late_other_ref, late_at, 1 - mine),
            (early_ref, early_at, mine), (early_other_ref, early_at, 1 - mine),
        ):
            size = source_ref.shape[0]
            start = at + which * (size * NORM_ROWS)
            for lane in range(NORM_ROWS):
                stage_ref[pl.ds(start + lane, size, stride=NORM_ROWS), :] = source_ref[
                    :, lane * LANES : lane * LANES + LANES]

        @pl.when(upper == 0)
        def _():
            for lane in range(NORM_ROWS):
                stage_ref[LEAD + lane : LEAD + lane + 1, :] = small_ref[
                    6:7, lane * LANES : lane * LANES + LANES]

        @pl.when(upper == 1)
        def _():
            at = LEAD + OUT_START - half - SMALL_ROWS
            for lane in range(NORM_ROWS):
                stage_ref[pl.ds(at + lane, HEADS, stride=NORM_ROWS), :] = small_ref[
                    8 : 8 + HEADS, lane * LANES : lane * LANES + LANES]
            at += DT_ROWS
            places = [(k, j) for k in range(CONV + 1) for j in range(CONVB_ROWS)]
            places += [(6, NORM_ROWS + j) for j in range(3)]
            places += [(5, j) for j in range(GAIN_ROWS)]
            for number, (line, lane) in enumerate(places):
                stage_ref[at + number : at + number + 1, :] = small_ref[
                    line : line + 1, lane * LANES : lane * LANES + LANES]
            at = LEAD + OUT_START + OUT_ROWS - half
            stage_ref[at : LEAD + half, :] = jnp.zeros((LEAD + half - at, LANES), F32)

    @pl.when(step > 0)
    def _():
        at = LEAD + mine * (half // 2) + (step - 1) * block
        grad = stage_ref[pl.ds(pl.multiple_of(at, 8), block), :]
        grad_ref[...] = grad
        first = BETA_ONE * first_ref[...] + (1.0 - BETA_ONE) * grad
        second = BETA_TWO * second_ref[...] + (1.0 - BETA_TWO) * grad * grad
        ratio_ref[...] = (first * rate_ref[0]) / (jnp.sqrt(second * rate_ref[1]) + EPS_ADAM)


def run_adam(who, rates, early, early_other, late, late_other, small, first, second):
    rows = first.shape[0]
    block = rows // ADAM_BLOCKS

    def at(i):
        return (jnp.maximum(i - 1, 0), 0)

    spec = pl.BlockSpec((block, LANES), at)
    out = jax.ShapeDtypeStruct((rows, LANES), F32)
    return pl.pallas_call(
        adam_kernel,
        grid=(ADAM_BLOCKS + 1,),
        in_specs=[
            pl.BlockSpec(memory_space=pltpu.SMEM), pl.BlockSpec(memory_space=pltpu.SMEM),
            const_spec(early.shape), const_spec(early.shape),
            const_spec(late.shape), const_spec(late.shape), const_spec(small.shape),
            spec, spec,
        ],
        out_specs=[spec, spec],
        out_shape=[out, out],
        scratch_shapes=[pltpu.VMEM((STAGE_ROWS, LANES), F32)],
        compiler_params=pltpu.CompilerParams(
            dimension_semantics=("arbitrary",), vmem_limit_bytes=48 * 2**20),
        cost_estimate=pl.CostEstimate(
            flops=10**8, bytes_accessed=24 * 2**20, transcendentals=10**6),
    )(who, rates, early, early_other, late, late_other, small, first, second)


def swap(values, axis, bit):
    size = lax.axis_size(axis)
    return lax.ppermute(values, axis, [(i, i ^ bit) for i in range(size)])


def power_for(bound):
    bound = jnp.maximum(bound, 1e-30).reshape(1, 1)
    return jnp.clip(jnp.floor(jnp.log2(F16_TOP / bound)), -126.0, 120.0)


def to_wire(values, power):
    return (values * jnp.exp2(power)).astype(jnp.float16)


def from_wire(values, power):
    return values.astype(F32) * jnp.exp2(-power)


def scatter(values, power, axis, bit=1, count=2):
    place = (lax.axis_index(axis) // bit) % count
    rows = values.shape[-2] // count
    mark = min(MARK, rows)
    dim = values.ndim - 2
    total = lax.dynamic_slice_in_dim(values, place * rows, rows, dim)
    least = power
    for offset in range(1, count):
        to = place ^ offset
        last = to == count - 1
        start = to * rows - jnp.where(last, mark, 0)
        send = lax.dynamic_slice_in_dim(values, start, rows + mark, dim)
        line = lax.broadcasted_iota(jnp.int32, send.shape, dim)
        marked = jnp.where(last, line < mark, line >= rows)
        wire = jnp.where(marked, power, send * jnp.exp2(power)).astype(jnp.float16)
        got = swap(wire, axis, bit * offset)
        last = place == count - 1
        got_power = lax.dynamic_slice_in_dim(got, jnp.where(last, 0, rows), 1, dim)
        got_power = got_power.reshape(-1, D)[0:1, 0:1].astype(F32)
        body = lax.dynamic_slice_in_dim(got, jnp.where(last, mark, 0), rows, dim)
        total = total + from_wire(body, got_power)
        least = jnp.minimum(least, got_power)
    return total, least - float(count.bit_length() - 1)


def everyones(values, axis, bit=1, count=2):
    place = (lax.axis_index(axis) // bit) % count
    pieces = [values] + [swap(values, axis, bit * offset) for offset in range(1, count)]
    step = 1
    while step < count:
        flip = (place // step) % 2 == 1
        pieces = [
            jnp.where(flip, pieces[i ^ step], pieces[i]) for i in range(count)]
        step *= 2
    return pieces


def gather(values, axis, bit=1, count=2):
    return jnp.concatenate(everyones(values, axis, bit, count))


def add_all(values, axis, bit=1, count=2):
    pieces = everyones(values, axis, bit, count) if count > 2 else [
        values, swap(values, axis, bit)]
    total = pieces[0]
    for piece in pieces[1:]:
        total = total + piece
    return total


def data_groups():
    size = lax.axis_size("dp")
    groups = [(1, 2)]
    bit = 2
    while bit < size:
        count = 4 if bit * 4 <= size else 2
        groups.append((bit, count))
        bit *= count
    return groups


def dot_tn(a, b):
    return lax.dot_general(a, b, (((0,), (0,)), ((), ())), preferred_element_type=F32)


def pick_rows(index, rows):
    chosen = index[:, None] == jnp.arange(rows.shape[0], dtype=jnp.int32)[None, :]
    return dot(chosen.astype(BF16), rows).astype(BF16)


def on_device(
    tokens, loss_sensitivity, lengths, holder_sequence_list, master, moment_one, moment_two,
    adam_rates, iteration_tally,
):
    group_devices = lax.axis_size("zero")
    data_devices = lax.axis_size("dp")
    zero_index = lax.axis_index("zero")
    dp_index = lax.axis_index("dp")
    seq_len = loss_sensitivity.shape[1]
    group_seqs = tokens.shape[0]
    span = tokens.shape[1]
    slots = group_seqs // data_devices
    shard_rows = master.shape[0] // LANES
    tie = lax.optimization_barrier

    own = master.reshape(shard_rows, LANES)
    flat = lax.all_gather(own.astype(BF16), "zero", axis=0, tiled=True)

    arranged = holder_sequence_list.reshape(data_devices, group_devices, slots)
    group_order = lax.dynamic_index_in_dim(arranged, zero_index, 1, keepdims=False).reshape(-1)
    local_ids = group_order - zero_index * group_seqs
    dealt = tokens.at[local_ids].get(mode="promise_in_bounds")
    local_tok = lax.all_to_all(dealt, "dp", split_axis=0, concat_axis=0, tiled=True)
    my_seqs = lax.dynamic_slice_in_dim(group_order, dp_index * slots, slots)
    bound = lengths[my_seqs[0]]
    positions = jnp.arange(seq_len, dtype=jnp.int32)

    in_w, out_w, norm_gain, *params, e2, et = run_prepare(flat)
    cot = loss_sensitivity[0]
    gm = dot_nt(cot, out_w)
    cot_top = jnp.max(jnp.abs(cot)).astype(F32)
    local_tok, in_w, gm, cot_top = tie((local_tok, in_w, gm, cot_top))
    own_late, _ = tie((own, flat[:8]))
    whole_master = lax.all_gather(own_late, "zero", axis=0, tiled=True)

    def place(slot, at):
        return (at // span) * (slots * span) + slot * span + at % span

    source = jnp.where(positions < bound, place(0, positions), place(1, positions - bound))
    packed = pick_rows(source, local_tok.reshape(slots * seq_len, D))
    blocks = jnp.arange(data_devices, dtype=jnp.int32)[:, None, None] * span
    within = blocks + jnp.arange(span, dtype=jnp.int32)[None, None, :]
    within = within + jnp.arange(slots, dtype=jnp.int32)[None, :, None] * bound
    unpack_rows = jnp.minimum(within, seq_len - 1).reshape(-1)

    def spread(rows):
        return pick_rows(unpack_rows, rows).reshape(data_devices * slots, span, D)

    def send_back(picked):
        return lax.all_to_all(picked, "dp", split_axis=0, concat_axis=0, tiled=True)

    restore = jnp.zeros_like(local_ids).at[local_ids].set(
        jnp.arange(group_seqs, dtype=jnp.int32))
    mine = lax.dynamic_slice_in_dim(lengths, zero_index * group_seqs, group_seqs)
    at = dp_index * span + jnp.arange(span, dtype=jnp.int32)
    live = (at[None, :] < mine[:, None])[:, :, None]

    bound_arr = bound.reshape(1)
    tok = packed.astype(F32)
    nhat = tok * lax.rsqrt(jnp.mean(tok * tok, axis=1, keepdims=True) + EPS_NORM)
    normed = (nhat * norm_gain).astype(BF16)
    proj_z = dot_nt(normed, in_w[:INNER])
    proj = dot_nt(normed, in_w[INNER:PROJ])
    pair, dy, through, states, ggain, zmax = run_forward(
        proj_z, proj, gm, bound_arr, e2, et, params)
    result = (tok + dot(pair[1], out_w)).astype(BF16)
    picked = spread(result)
    picked, pair = tie((picked, pair))
    back_out = send_back(picked)
    root = float(seq_len) ** 0.5
    normed_norm = root * float(D) ** 0.5 * 1.02 * jnp.max(jnp.abs(norm_gain))
    mixed_norm = root * float(INNER) ** 0.5 * 1.02 * jnp.max(jnp.abs(params[5]))
    early_power = power_for(jnp.maximum(
        1.02 * root * jnp.max(zmax) * normed_norm, root * cot_top * mixed_norm))
    early = lax.dot_general(
        pair, jnp.stack([normed, cot]), (((1,), (1,)), ((0,), (0,))), preferred_element_type=F32)
    early, early_power = scatter(early, early_power, "zero", 1)
    early, early_power, dy = tie((early.reshape(INNER, D), early_power, dy))
    early, early_power = scatter(early, early_power, "zero", 2)
    groups = data_groups()
    back_args = (
        proj, dy, through, states, pair, packed, cot, in_w, norm_gain, ggain,
        bound_arr, e2, et, params)
    carried = run_backward(0, None, *back_args)
    carried, early, early_power = tie((carried, early, early_power))
    early, early_power = scatter(early, early_power, "dp", *groups[0])
    window, grad_tok, small = run_backward(1, carried, *back_args)
    window, small, back_out, early, early_power, whole_master = tie(
        (window, small, back_out, early, early_power, whole_master))

    late = lax.dot_general(
        window, jnp.stack([normed, normed]), (((1,), (1,)), ((0,), (0,))),
        preferred_element_type=F32)
    late_power = power_for(1.02 * root * jnp.max(small[7:8]) * normed_norm)
    late, late_power = scatter(late, late_power, "zero", 1)
    for group in groups[1:]:
        early, early_power = scatter(early, early_power, "dp", *group)
    early = to_wire(early, early_power)
    small = add_all(small, "zero", 1)
    late, late_power, early, small = tie((late.reshape(WINDOW, D), late_power, early, small))
    late, late_power = scatter(late, late_power, "zero", 2)
    for group in reversed(groups[1:]):
        early = gather(early, "dp", *group)
    small = add_all(small, "zero", 2)
    picked_grad = spread(grad_tok)
    late, late_power, early, small, picked_grad = tie(
        (late, late_power, early, small, picked_grad))
    late, late_power = scatter(late, late_power, "dp", *groups[0])
    early = from_wire(gather(early, "dp", *groups[0]), early_power)
    small = add_all(small, "dp", *groups[0])
    late, late_power, early, small = tie((late, late_power, early, small))
    for group in groups[1:]:
        late, late_power = scatter(late, late_power, "dp", *group)
        small = add_all(small, "dp", *group)
    late = to_wire(late, late_power)
    early_other = swap(early, "zero", 1)
    late, early, early_other, small = tie((late, early, early_other, small))
    for group in reversed(groups[1:]):
        late = gather(late, "dp", *group)
    late, picked_grad = tie((late, picked_grad))
    back_grad = send_back(picked_grad)
    late = from_wire(gather(late, "dp", *groups[0]), late_power)
    late_other = swap(late, "zero", 1)

    steps_f = iteration_tally[0].astype(F32)
    rates = jnp.stack([
        1.0 / (1.0 - jnp.power(BETA_ONE, steps_f)), 1.0 / (1.0 - jnp.power(BETA_TWO, steps_f))])
    who = jnp.stack([zero_index // 2, zero_index % 2]).astype(jnp.int32)
    first = moment_one.reshape(shard_rows, LANES)
    second = moment_two.reshape(shard_rows, LANES)
    grad_shard, ratio = run_adam(
        who, rates, early, early_other, late, late_other, small, first, second)
    mine = ratio.astype(jnp.float16)
    mine, grad_shard, back_out = tie((mine, grad_shard, back_out))
    core = swap(mine, "zero", 1)
    across = swap(mine, "zero", 2)
    first_next = BETA_ONE * first + (1.0 - BETA_ONE) * grad_shard
    second_next = BETA_TWO * second + (1.0 - BETA_TWO) * grad_shard * grad_shard
    back_rows = back_out.at[restore].get(mode="promise_in_bounds")
    tokens_out = jnp.where(live, back_rows, tokens)
    new_master = jnp.zeros((group_devices, shard_rows, LANES), F32)
    whole_master = whole_master.reshape(group_devices, shard_rows, LANES)

    def put(new_master, piece, offset):
        shard = zero_index ^ offset
        old = lax.dynamic_index_in_dim(whole_master, shard, 0, keepdims=False)
        new = old - adam_rates[0] * (piece.astype(F32) + adam_rates[1] * old)
        return lax.dynamic_update_index_in_dim(new_master, new, shard, 0)

    new_master = put(put(new_master, mine, 0), core, 1)
    across, new_master, tokens_out, first_next, second_next, back_grad = tie(
        (across, new_master, tokens_out, first_next, second_next, back_grad))
    across_core = swap(across, "zero", 1)
    new_master = put(new_master, across, 2)
    across_core, new_master = tie((across_core, new_master))
    new_master = put(new_master, across_core, 3)
    grad_tokens = jnp.where(
        live, back_grad.at[restore].get(mode="promise_in_bounds"), jnp.zeros((), BF16))
    return (
        tokens_out, grad_tokens, new_master.reshape(-1), grad_shard.reshape(-1),
        first_next.reshape(-1), second_next.reshape(-1))


def solution(mesh):
    return jax.shard_map(
        on_device,
        mesh=mesh,
        in_specs=(
            P("zero", "dp", None), P(("dp", "zero"), None, None), P(), P(),
            P("zero"), P("zero"), P("zero"), P(), P(),
        ),
        out_specs=(
            P("zero", "dp", None), P("zero", "dp", None), P(), P("zero"), P("zero"), P("zero"),
        ),
        check_vma=False,
    )
```

```python
import jax
import jax.numpy as jnp
from jax import lax
from jax.experimental import pallas as pl
from jax.experimental.pallas import tpu as pltpu
from jax.sharding import PartitionSpec as P

D = 768
HEADS = 24
HEADDIM = 64
STATE = 128
CONV = 4
INNER = 1536
XBC = 1792
PROJ = 3352
Q = 128
LATE = PROJ - INNER
WINDOW = 1024
PAIRS = HEADS // 2
EPS_NORM = 1e-05
NEG = -1e30
F16_TOP = 30000.0
LOG2E = 1.4426950408889634
F32 = jnp.float32
BF16 = jnp.bfloat16


def dot(a, b):
    return lax.dot_general(a, b, (((1,), (0,)), ((), ())), preferred_element_type=F32)


def dot_nt(a, b):
    return lax.dot_general(a, b, (((1,), (1,)), ((), ())), preferred_element_type=F32)


def split2(v):
    hi = v.astype(BF16)
    return hi, (v - hi.astype(F32)).astype(BF16)


def split3(v):
    hi = v.astype(BF16)
    rest = v - hi.astype(F32)
    mid = rest.astype(BF16)
    return hi, mid, (rest - mid.astype(F32)).astype(BF16)


def wide_left(v):
    hi, lo = split2(v)
    return jnp.concatenate([hi, lo, hi], axis=1)


def tall_right(v):
    hi, lo = split2(v)
    return jnp.concatenate([hi, hi, lo], axis=0)


def split_pair(v, masks):
    hi, lo = split2(v)
    return jnp.concatenate([
        jnp.concatenate([hi * masks[0], lo * masks[0]], axis=1),
        jnp.concatenate([hi * masks[1], lo * masks[1]], axis=1)], axis=0)


def sigmoid(v):
    return lax.logistic(v)


def softplus(v):
    return jnp.maximum(v, 0.0) + jnp.log1p(jnp.exp(-jnp.abs(v)))


def iota(shape, dim):
    return lax.broadcasted_iota(jnp.int32, shape, dim)


def expand(v, e_ref):
    hi, lo = split2(v)
    return dot(jnp.concatenate([hi, lo], axis=1), e_ref[...])


def head_sum(v, et_ref):
    hi, lo = split2(v)
    return dot(hi, et_ref[...]) + dot(lo, et_ref[...])


def quarters(out):
    return out[:Q, :Q] + (out[:Q, Q:] + out[Q:, :Q])


def power_for(bound):
    scale = jnp.log(0.9 * F16_TOP / jnp.maximum(bound, 1e-30)) * LOG2E
    return jnp.clip(jnp.floor(scale), -126.0, 120.0)


def chunk_masks(t0, bound):
    rows = t0 + iota((Q, 1), 0)
    rr = t0 + iota((Q, Q), 0)
    cc = t0 + iota((Q, Q), 1)
    return rows, rr, cc


def conv_rows(ext_ref, w_ref, b_ref, rows, bound):
    total = b_ref[...] + w_ref[3:4, :] * ext_ref[8 : 8 + Q, :]
    for back in (1, 2, 3):
        ok = jnp.logical_or(rows - back >= bound, rows < bound).astype(F32)
        total = total + w_ref[3 - back : 4 - back, :] * (ext_ref[8 - back : 8 - back + Q, :] * ok)
    return total


def decay_parts(dt_raw, dtb_ref, alog_ref, rr, cc):
    dt_in = dt_raw + dtb_ref[...]
    dt_pos = softplus(dt_in)
    rate = -jnp.exp(alog_ref[...])
    step = dt_pos * rate
    tri = (cc <= rr).astype(F32).astype(BF16)
    s_hi, s_mid, s_lo = split3(step)
    cum = dot(tri, s_hi) + dot(tri, s_mid) + dot(tri, s_lo)
    return dt_in, dt_pos, rate, cum


def forward_kernel(
    bound_ref, cot_ref, z_ref, proj_ref, gm_ref, norm_ref, e_ref, et_ref, convw_ref, convb_ref, dtb_ref, alog_ref,
    skip_ref, gain_ref,
    pair_ref, dy_ref, through_ref, state_ref, ggain_ref, power_ref,
    zmax_ref, ext_ref, dt_ref, carry_ref, xd_ref, acc_ref, cumt_ref,
):
    step = pl.program_id(0)
    bound = bound_ref[0]
    t0 = step * Q

    @pl.when(step == 0)
    def _():
        ext_ref[0:8, :] = jnp.zeros((8, XBC), F32)
        carry_ref[...] = jnp.zeros_like(carry_ref)
        dt_ref[...] = jnp.zeros_like(dt_ref)
        ggain_ref[...] = jnp.zeros_like(ggain_ref)
        zmax_ref[...] = jnp.zeros_like(zmax_ref)

    rows, rr, cc = chunk_masks(t0, bound)
    ext_ref[8 : 8 + Q, :] = proj_ref[:, :XBC]
    pre = conv_rows(ext_ref, convw_ref, convb_ref, rows, bound)
    ext_ref[0:8, :] = ext_ref[Q : Q + 8, :]
    conv_out = pre * sigmoid(pre)
    x = conv_out[:, :INNER]
    b_rows = conv_out[:, INNER : INNER + STATE]
    c_rows = conv_out[:, INNER + STATE :]
    dt_ref[:, 0:HEADS] = proj_ref[:, XBC:LATE]
    _, dt_pos, _, cum = decay_parts(dt_ref[...], dtb_ref, alog_ref, rr, cc)
    cum_end = cum[Q - 1 : Q, :]
    keep = jnp.logical_or(rows < bound, bound < t0).astype(F32)
    in_last = jnp.logical_or(rows >= bound, bound > t0 + Q - 1).astype(F32)
    whole = jnp.logical_or(bound < t0, bound > t0 + Q - 1).astype(F32)
    from_start = jnp.exp(cum) * keep
    to_end = jnp.exp(cum_end - cum) * in_last
    carry_scale = jnp.exp(cum_end) * whole
    allowed = jnp.logical_and(cc <= rr, (cc >= bound) == (rr >= bound))
    cum2 = cum * LOG2E
    cumt_ref[...] = cum2.T

    state = carry_ref[...]
    state_ref[0] = state
    spread = expand(jnp.concatenate(
        [dt_pos, to_end, from_start, jnp.broadcast_to(carry_scale, (16, 128))], axis=0), e_ref)
    xd = x * spread[:Q]
    xd_ref[...] = xd
    acc = dot(wide_left(c_rows), tall_right(state)) * spread[2 * Q : 3 * Q]
    acc_ref[...] = acc + skip_ref[...] * x
    b_t = b_rows.T
    carry_ref[...] = state * spread[3 * Q : 3 * Q + 1] + dot(
        wide_left(b_t), tall_right(xd * spread[Q : 2 * Q]))
    gram = dot(wide_left(c_rows), tall_right(b_t))
    first = iota((Q, Q), 1) < HEADDIM
    first_b = (first.astype(F32).astype(BF16), 1.0 - first.astype(F32).astype(BF16))
    for pair in range(PAIRS):
        parts = []
        for head in (2 * pair, 2 * pair + 1):
            differ = cum2[:, head : head + 1] - cumt_ref[head : head + 1, :]
            parts.append(gram * jnp.exp2(jnp.where(allowed, differ, NEG)))
        left = jnp.concatenate(split2(jnp.concatenate(parts, axis=1)), axis=0)
        lanes = slice(pair * 128, pair * 128 + 128)
        xp = xd_ref[:, lanes]
        out = dot(left, split_pair(xp, first_b))
        acc_ref[:, lanes] += out[:Q, :128] + (out[:Q, 128:] + out[Q:, :128])
    scanned = acc_ref[...]
    z = z_ref[...]
    sig_z = sigmoid(z)
    silu_z = z * sig_z
    gated = scanned * silu_z
    ginv = lax.rsqrt(jnp.mean(gated * gated, axis=1, keepdims=True) + EPS_NORM)
    mhat = gated * ginv
    pair_ref[1] = (mhat * gain_ref[...]).astype(BF16)
    gm = gm_ref[...]
    ggain_ref[...] += jnp.sum(mhat * gm, axis=0, keepdims=True)
    gmg = gm * gain_ref[...]
    ggated = ginv * (gmg - mhat * jnp.mean(mhat * gmg, axis=1, keepdims=True))
    dy = ggated * silu_z
    dy_ref[...] = dy
    grad_z = ggated * scanned * (sig_z * (1.0 + z * (1.0 - sig_z)))
    zmax_ref[...] = jnp.maximum(zmax_ref[...], jnp.max(jnp.abs(grad_z), axis=0, keepdims=True))
    pair_ref[0] = grad_z.astype(BF16)
    through_ref[...] = head_sum(dy * (scanned - skip_ref[...] * x), et_ref)

    @pl.when(step == pl.num_programs(0) - 1)
    def _():
        count = float(Q * pl.num_programs(0))
        largest = jnp.max(zmax_ref[...], axis=1, keepdims=True)
        normed = jnp.max(jnp.abs(norm_ref[...]), axis=1, keepdims=True) * (D ** 0.5)
        mixed = jnp.max(jnp.abs(gain_ref[...]), axis=1, keepdims=True) * (INNER ** 0.5)
        power_ref[...] = jnp.broadcast_to(power_for(
            1.05 * count * jnp.maximum(largest * normed, cot_ref[0] * mixed)), (8, 128))


def const_spec(shape):
    return pl.BlockSpec(shape, lambda *_: (0,) * len(shape))


def run_forward(z, proj, gm, bound, cot_top, norm_gain, e2, et, params):
    n = proj.shape[0]
    steps = n // Q
    return pl.pallas_call(
        forward_kernel,
        grid=(steps,),
        in_specs=[
            pl.BlockSpec(memory_space=pltpu.SMEM), pl.BlockSpec(memory_space=pltpu.SMEM),
            pl.BlockSpec((Q, INNER), lambda i: (i, 0)),
            pl.BlockSpec((Q, LATE), lambda i: (i, 0)),
            pl.BlockSpec((Q, INNER), lambda i: (i, 0)),
            const_spec((1, D)),
            const_spec((256, INNER)), const_spec((INNER, 128)),
            const_spec((8, XBC)), const_spec((1, XBC)), const_spec((1, 128)),
            const_spec((1, 128)), const_spec((1, INNER)), const_spec((1, INNER)),
        ],
        out_specs=[
            pl.BlockSpec((2, Q, INNER), lambda i: (0, i, 0)),
            pl.BlockSpec((Q, INNER), lambda i: (i, 0)),
            pl.BlockSpec((Q, 128), lambda i: (i, 0)),
            pl.BlockSpec((1, STATE, INNER), lambda i: (i, 0, 0)),
            const_spec((1, INNER)), const_spec((8, 128)),
        ],
        out_shape=[
            jax.ShapeDtypeStruct((2, n, INNER), BF16),
            jax.ShapeDtypeStruct((n, INNER), F32),
            jax.ShapeDtypeStruct((n, 128), F32),
            jax.ShapeDtypeStruct((steps, STATE, INNER), F32),
            jax.ShapeDtypeStruct((1, INNER), F32),
            jax.ShapeDtypeStruct((8, 128), F32),
        ],
        scratch_shapes=[
            pltpu.VMEM((1, INNER), F32),
            pltpu.VMEM((Q + 8, XBC), F32),
            pltpu.VMEM((Q, 128), F32),
            pltpu.VMEM((STATE, INNER), F32),
            pltpu.VMEM((Q, INNER), F32),
            pltpu.VMEM((Q, INNER), F32),
            pltpu.VMEM((128, Q), F32),
        ],
        compiler_params=pltpu.CompilerParams(
            dimension_semantics=("arbitrary",), vmem_limit_bytes=48 * 2**20),
        cost_estimate=pl.CostEstimate(
            flops=30 * 10**9, bytes_accessed=40 * 2**20, transcendentals=10**7),
    )(bound, cot_top, z, proj, gm, norm_gain, e2, et, *params)


def backward_kernel(
    bound_ref, proj_ref, before_ref, dy_ref, through_ref, state_ref, gz_ref, tok_ref, cot_ref,
    in_ref, norm_ref, ggain_ref,
    e_ref, et_ref, convw_ref, convb_ref, dtb_ref, alog_ref, skip_ref,
    window_ref, gtok_ref, small_ref, power_ref,
    total_ref, gskip_ref, gsmall_ref, dtw_ref, gp_ref, ext_ref, dt_ref, lam_ref, dsum_ref, xd_ref, g_ref, gnext_ref, cumt_ref,
):
    step = pl.program_id(0)
    steps = pl.num_programs(0)
    bound = bound_ref[0]
    t0 = (steps - 1 - step) * Q

    @pl.when(step == 0)
    def _():
        lam_ref[...] = jnp.zeros_like(lam_ref)
        dsum_ref[...] = jnp.zeros_like(dsum_ref)
        dt_ref[...] = jnp.zeros_like(dt_ref)
        gnext_ref[Q : Q + 8, :] = jnp.zeros((8, XBC), F32)
        gskip_ref[...] = jnp.zeros_like(gskip_ref)
        total_ref[...] = jnp.zeros_like(total_ref)
        dtw_ref[...] = jnp.zeros_like(dtw_ref)
        gsmall_ref[...] = jnp.zeros_like(gsmall_ref)

    rows, rr, cc = chunk_masks(t0, bound)
    dy = dy_ref[...]
    first_chunk = (t0 > 0).astype(F32)
    ext_ref[0:8, :] = before_ref[:, :XBC] * first_chunk
    ext_ref[8 : 8 + Q, :] = proj_ref[:, :XBC]
    pre = conv_rows(ext_ref, convw_ref, convb_ref, rows, bound)
    sig_pre = sigmoid(pre)
    conv_out = pre * sig_pre
    x = conv_out[:, :INNER]
    b_rows = conv_out[:, INNER : INNER + STATE]
    c_rows = conv_out[:, INNER + STATE :]
    dt_ref[:, 0:HEADS] = proj_ref[:, XBC:LATE]
    dt_in, dt_pos, rate, cum = decay_parts(dt_ref[...], dtb_ref, alog_ref, rr, cc)
    cum_end = cum[Q - 1 : Q, :]
    keep = jnp.logical_or(rows < bound, bound < t0).astype(F32)
    in_last = jnp.logical_or(rows >= bound, bound > t0 + Q - 1).astype(F32)
    whole = jnp.logical_or(bound < t0, bound > t0 + Q - 1).astype(F32)
    from_start = jnp.exp(cum) * keep
    to_end = jnp.exp(cum_end - cum) * in_last
    carry_scale = jnp.exp(cum_end) * whole
    allowed_t = jnp.logical_and(rr <= cc, (cc >= bound) == (rr >= bound))
    cum2 = cum * LOG2E
    cumt_ref[...] = cum2.T
    c_t = c_rows.T
    gram_t = dot(wide_left(b_rows), tall_right(c_t))
    spread = expand(jnp.concatenate(
        [dt_pos, to_end, from_start, jnp.broadcast_to(carry_scale, (16, 128))], axis=0), e_ref)
    dt_all = spread[:Q]
    end_all = spread[Q : 2 * Q]
    xd = x * dt_all
    xd_ref[...] = xd
    skip = skip_ref[...]
    gskip_ref[...] += jnp.sum(dy * x, axis=0, keepdims=True)
    lam = lam_ref[...]
    lam_hi, lam_lo = split2(lam)
    g_ref[...] = (
        dot(wide_left(b_rows), jnp.concatenate([lam_hi, lam_hi, lam_lo], axis=0)) * end_all
    )
    grad_b = quarters(dot_nt(
        jnp.concatenate(split2(xd * end_all), axis=0), jnp.concatenate([lam_hi, lam_lo], axis=0)))
    state = state_ref[0]
    dye_hi, dye_lo = split2(dy * spread[2 * Q : 3 * Q])
    grad_c = quarters(dot_nt(
        jnp.concatenate([dye_hi, dye_lo], axis=0), jnp.concatenate(split2(state), axis=0)))
    lam_new = lam * spread[3 * Q : 3 * Q + 1] + dot(
        wide_left(c_t), jnp.concatenate([dye_hi, dye_hi, dye_lo], axis=0)
    )
    lam_ref[...] = lam_new
    ended = dsum_ref[0:1, :]
    first = iota((Q, Q), 1) < HEADDIM
    first_b = (first.astype(F32).astype(BF16), 1.0 - first.astype(F32).astype(BF16))
    first_row = (iota((Q, Q), 0) < HEADDIM).astype(F32).astype(BF16)
    first_row = (first_row, 1.0 - first_row)
    gram_grad = jnp.zeros((Q, Q), F32)
    for pair in range(PAIRS):
        lanes = slice(pair * 128, pair * 128 + 128)
        weights = []
        for head in (2 * pair, 2 * pair + 1):
            differ = cumt_ref[head : head + 1, :] - cum2[:, head : head + 1]
            weights.append(jnp.exp2(jnp.where(allowed_t, differ, NEG)))
        left = jnp.concatenate([gram_t * weights[0], gram_t * weights[1]], axis=1)
        left = jnp.concatenate(split2(left), axis=0)
        dyp = dy_ref[:, lanes]
        out = dot(left, split_pair(dyp, first_b))
        g_ref[:, lanes] += out[:Q, :128] + (out[:Q, 128:] + out[Q:, :128])
        dyt_hi, dyt_lo = split2(dyp.T)
        right_hi = jnp.concatenate([dyt_hi * first_row[0], dyt_hi * first_row[1]], axis=1)
        right_lo = jnp.concatenate([dyt_lo * first_row[0], dyt_lo * first_row[1]], axis=1)
        outer = dot(
            wide_left(xd_ref[:, lanes]), jnp.concatenate([right_hi, right_hi, right_lo], axis=0))
        gram_grad = gram_grad + (outer[:, :128] * weights[0] + outer[:, 128:] * weights[1])
    g = g_ref[...]
    grad_x = dt_all * g + skip * dy
    sums = dot(jnp.concatenate(
        split2(x * g) + split2(jnp.broadcast_to(
            jnp.sum(lam_new * state, axis=0, keepdims=True), (16, INNER))), axis=0), et_ref[...])
    direct = sums[:Q] + sums[Q : 2 * Q]
    balance = through_ref[...] - dt_pos * direct
    keep_t = allowed_t.astype(F32).astype(BF16)
    b_hi, b_mid, b_lo = split3(balance)
    grad_step = dot(keep_t, b_hi) + dot(keep_t, b_mid) + dot(keep_t, b_lo) + in_last * ended
    dsum_ref[...] = sums[2 * Q : 2 * Q + 8] + sums[2 * Q + 16 : 2 * Q + 24]
    grad_dt = (direct + rate * grad_step) * sigmoid(dt_in)
    gsmall_ref[0:1, :] += jnp.sum(grad_dt, axis=0, keepdims=True)
    gsmall_ref[1:2, :] += rate * jnp.sum(dt_pos * grad_step, axis=0, keepdims=True)
    grad_c = grad_c + dot(wide_left(gram_grad.T), tall_right(b_rows))
    grad_b = grad_b + dot(wide_left(gram_grad), tall_right(c_rows))
    slope = sig_pre * (1.0 + pre * (1.0 - sig_pre))
    gnext_ref[0:Q, :INNER] = grad_x * slope[:, :INNER]
    gnext_ref[0:Q, INNER : INNER + STATE] = grad_b * slope[:, INNER : INNER + STATE]
    gnext_ref[0:Q, INNER + STATE :] = grad_c * slope[:, INNER + STATE :]
    gcp = gnext_ref[0:Q, :]
    total_ref[4:5, :] += jnp.sum(gcp, axis=0, keepdims=True)
    total_ref[3:4, :] += jnp.sum(gcp * ext_ref[8 : 8 + Q, :], axis=0, keepdims=True)
    total = convw_ref[3:4, :] * gcp
    for back in (1, 2, 3):
        ok = jnp.logical_or(rows - back >= bound, rows < bound).astype(F32)
        total_ref[3 - back : 4 - back, :] += jnp.sum(
            gcp * (ext_ref[8 - back : 8 - back + Q, :] * ok), axis=0, keepdims=True)
        okn = jnp.logical_or(rows >= bound, rows + back < bound).astype(F32)
        total = total + convw_ref[3 - back : 4 - back, :] * (gnext_ref[back : back + Q, :] * okn)
    total_ref[7:8, :] = jnp.maximum(
        total_ref[7:8, :], jnp.max(jnp.abs(total), axis=0, keepdims=True))
    total = total.astype(BF16)
    window_ref[0] = total[:, :WINDOW]
    window_ref[1] = total[:, XBC - WINDOW :]
    gnext_ref[Q : Q + 8, :] = gnext_ref[0:8, :]
    half = (steps - 1 - step) % 2
    at = pl.multiple_of(half * Q, Q)
    gp_ref[pl.ds(at, Q), :INNER] = gz_ref[0]
    gp_ref[pl.ds(at, Q), INNER : INNER + XBC] = total
    gp_ref[pl.ds(at, Q), INNER + XBC :] = grad_dt.astype(BF16)

    @pl.when(half == 0)
    def _():
        grad_normed = dot(gp_ref[...], in_ref[: INNER + XBC + 128, :])
        tok = tok_ref[...].astype(F32)
        rinv = lax.rsqrt(jnp.mean(tok * tok, axis=1, keepdims=True) + EPS_NORM)
        nhat = tok * rinv
        gain = norm_ref[...]
        gng = grad_normed * gain
        gtok_ref[...] = (cot_ref[...].astype(F32) + rinv * (
            gng - nhat * jnp.mean(nhat * gng, axis=1, keepdims=True))).astype(BF16)
        total_ref[6:7, :D] += jnp.sum(nhat * grad_normed, axis=0, keepdims=True)
        normed = (nhat * gain).astype(BF16)
        gdt = gp_ref[:, INNER + XBC :].astype(F32)
        dtw_ref[...] += dot(jnp.concatenate(
            [gdt[:Q].T, gdt[Q:].T], axis=1).astype(BF16), normed)

    @pl.when(step == steps - 1)
    def _():
        skips = head_sum(jnp.broadcast_to(gskip_ref[...], (8, INNER)), et_ref)
        small_ref[...] = jnp.zeros_like(small_ref)
        small_ref[0:HEADS, :] = dtw_ref[0:HEADS, :]
        pieces = [
            total_ref[k : k + 1, j * 128 : j * 128 + 128]
            for k in range(CONV + 1) for j in range(XBC // 128)]
        pieces += [gsmall_ref[0:1, :], gsmall_ref[1:2, :], skips[0:1, :]]
        pieces += [ggain_ref[:, j * 128 : j * 128 + 128] for j in range(INNER // 128)]
        lines = D // 128
        for number, piece in enumerate(pieces):
            line = HEADS + number // lines
            at = number % lines * 128
            small_ref[line : line + 1, at : at + 128] = piece
        small_ref[40:41, :] = total_ref[6:7, :D]
        count = float(Q * steps)
        largest = jnp.max(total_ref[7:8, :], axis=1, keepdims=True)
        normed = jnp.max(jnp.abs(norm_ref[...]), axis=1, keepdims=True) * (D ** 0.5)
        others = jnp.max(jnp.max(jnp.abs(small_ref[...]), axis=1, keepdims=True), axis=0, keepdims=True)
        power_ref[...] = jnp.broadcast_to(power_for(
            jnp.maximum(1.05 * count * largest * normed, others)), (8, 128))


def run_backward(
    proj, dy, through, states, pair, tok, cot, in_w, norm_gain, ggain, bound, e2, et, params
):
    n = proj.shape[0]
    steps = n // Q

    def rev(i):
        return (steps - 1 - i, 0)

    def rev_two(i):
        return ((steps - 1 - i) // 2, 0)

    return pl.pallas_call(
        backward_kernel,
        grid=(steps,),
        in_specs=[
            pl.BlockSpec(memory_space=pltpu.SMEM),
            pl.BlockSpec((Q, LATE), rev),
            pl.BlockSpec((8, LATE), lambda i: (jnp.maximum((steps - 1 - i) * (Q // 8) - 1, 0), 0)),
            pl.BlockSpec((Q, INNER), rev),
            pl.BlockSpec((Q, 128), rev),
            pl.BlockSpec((1, STATE, INNER), lambda i: (steps - 1 - i, 0, 0)),
            pl.BlockSpec((1, Q, INNER), lambda i: (0, steps - 1 - i, 0)),
            pl.BlockSpec((2 * Q, D), rev_two), pl.BlockSpec((2 * Q, D), rev_two),
            const_spec(in_w.shape), const_spec((1, D)), const_spec((1, INNER)),
            const_spec((256, INNER)), const_spec((INNER, 128)),
            const_spec((8, XBC)), const_spec((1, XBC)), const_spec((1, 128)),
            const_spec((1, 128)), const_spec((1, INNER)),
        ],
        out_specs=[
            pl.BlockSpec((2, Q, WINDOW), lambda i: (0, steps - 1 - i, 0)),
            pl.BlockSpec((2 * Q, D), rev_two),
            const_spec((48, D)), const_spec((8, 128)),
        ],
        out_shape=[
            jax.ShapeDtypeStruct((2, n, WINDOW), BF16),
            jax.ShapeDtypeStruct((n, D), BF16),
            jax.ShapeDtypeStruct((48, D), F32),
            jax.ShapeDtypeStruct((8, 128), F32),
        ],
        scratch_shapes=[
            pltpu.VMEM((8, XBC), F32),
            pltpu.VMEM((1, INNER), F32),
            pltpu.VMEM((8, 128), F32),
            pltpu.VMEM((128, D), F32),
            pltpu.VMEM((2 * Q, INNER + XBC + 128), BF16),
            pltpu.VMEM((Q + 8, XBC), F32),
            pltpu.VMEM((Q, 128), F32),
            pltpu.VMEM((STATE, INNER), F32),
            pltpu.VMEM((8, 128), F32),
            pltpu.VMEM((Q, INNER), F32),
            pltpu.VMEM((Q, INNER), F32),
            pltpu.VMEM((Q + 8, XBC), F32),
            pltpu.VMEM((128, Q), F32),
        ],
        compiler_params=pltpu.CompilerParams(
            dimension_semantics=("arbitrary",), vmem_limit_bytes=48 * 2**20),
        cost_estimate=pl.CostEstimate(
            flops=50 * 10**9, bytes_accessed=50 * 2**20, transcendentals=2 * 10**7),
    )(bound, proj, proj, dy, through, states, pair, tok, cot, in_w, norm_gain, ggain,
      e2, et, *params[:5])


BETA_ONE = 0.9
BETA_TWO = 0.95
EPS_ADAM = 1e-08
LANES = 128
NORM_ROWS = D // LANES
IN_ROWS = PROJ * D // LANES
CONVW_ROWS = CONV * XBC // LANES
CONVB_ROWS = XBC // LANES
GAIN_ROWS = INNER // LANES
OUT_ROWS = INNER * D // LANES
DT_ROWS = HEADS * D // LANES
SMALL_ROWS = DT_ROWS + CONVW_ROWS + CONVB_ROWS + 3 + GAIN_ROWS
OUT_START = NORM_ROWS + IN_ROWS + SMALL_ROWS - DT_ROWS
LATE_START = NORM_ROWS + INNER * NORM_ROWS
LEAD = 896
STAGE_ROWS = 16264
ADAM_BLOCKS = 10
MARK = 16


PREP_STEPS = 7
IN_BLOCK = 512
OUT_BLOCK = 256
SMALL_START = NORM_ROWS + IN_ROWS


def prepare_kernel(
    flat_ref,
    in_ref, out_ref, norm_ref, convw_ref, convb_ref, dtb_ref, alog_ref, skip_ref, gain_ref,
    e_ref, et_ref,
    stage_ref,
):
    step = pl.program_id(0)

    @pl.when(step == 0)
    def _():
        rows = flat_ref[0:16, :].astype(F32)
        for lane in range(NORM_ROWS):
            norm_ref[:, lane * LANES : lane * LANES + LANES] = rows[lane : lane + 1, :]
        low = SMALL_START // 16 * 16
        stage_ref[0:112, :] = flat_ref[low : low + 112, :].astype(F32)
        at = SMALL_START - low
        convw_ref[...] = jnp.zeros_like(convw_ref)
        for tap in range(CONV):
            for lane in range(CONVB_ROWS):
                convw_ref[tap : tap + 1, lane * LANES : lane * LANES + LANES] = stage_ref[
                    at : at + 1, :]
                at += 1
        for lane in range(CONVB_ROWS):
            convb_ref[:, lane * LANES : lane * LANES + LANES] = stage_ref[at : at + 1, :]
            at += 1
        heads = iota((1, LANES), 1) < HEADS
        dtb_ref[...] = jnp.where(heads, stage_ref[at : at + 1, :], 0.0)
        alog_ref[...] = jnp.where(heads, stage_ref[at + 1 : at + 2, :], 0.0)
        skips = jnp.where(heads, stage_ref[at + 2 : at + 3, :], 0.0)
        at += 3
        for lane in range(GAIN_ROWS):
            gain_ref[:, lane * LANES : lane * LANES + LANES] = stage_ref[at : at + 1, :]
            at += 1
        one = (iota((128, INNER), 1) // HEADDIM == iota((128, INNER), 0)).astype(F32).astype(BF16)
        e_ref[0:128, :] = one
        e_ref[128:256, :] = one
        et_ref[...] = (
            iota((INNER, 128), 0) // HEADDIM == iota((INNER, 128), 1)).astype(F32).astype(BF16)
        skip_ref[...] = dot(jnp.broadcast_to(skips, (16, LANES)).astype(BF16), one)[0:1, :]

    def block(start, offset, rows, dest_ref):
        size = rows * NORM_ROWS + 16
        at = pl.multiple_of(start + step * (rows * NORM_ROWS), 16)
        stage_ref[0:size, :] = flat_ref[pl.ds(at, size), :].astype(F32)
        for lane in range(NORM_ROWS):
            dest_ref[:, lane * LANES : lane * LANES + LANES] = stage_ref[
                pl.ds(offset + lane, rows, stride=NORM_ROWS), :].astype(BF16)

    block(0, NORM_ROWS, IN_BLOCK, in_ref)

    @pl.when(step == PREP_STEPS - 1)
    def _():
        used = PROJ - (PREP_STEPS - 1) * IN_BLOCK
        in_ref[used:, :] = jnp.zeros((IN_BLOCK - used, D), BF16)

    @pl.when(step < INNER // OUT_BLOCK)
    def _():
        low = OUT_START // 16 * 16
        block(low, OUT_START - low, OUT_BLOCK, out_ref)


def run_prepare(flat):
    vector = lambda n: jax.ShapeDtypeStruct((1, n), F32)
    return pl.pallas_call(
        prepare_kernel,
        grid=(PREP_STEPS,),
        in_specs=[const_spec(flat.shape)],
        out_specs=[
            pl.BlockSpec((IN_BLOCK, D), lambda i: (i, 0)),
            pl.BlockSpec((OUT_BLOCK, D), lambda i: (jnp.minimum(i, INNER // OUT_BLOCK - 1), 0)),
            const_spec((1, D)), const_spec((8, XBC)), const_spec((1, XBC)), const_spec((1, 128)),
            const_spec((1, 128)), const_spec((1, INNER)), const_spec((1, INNER)),
            const_spec((256, INNER)), const_spec((INNER, 128)),
        ],
        out_shape=[
            jax.ShapeDtypeStruct((PREP_STEPS * IN_BLOCK, D), BF16),
            jax.ShapeDtypeStruct((INNER, D), BF16),
            vector(D), jax.ShapeDtypeStruct((8, XBC), F32), vector(XBC), vector(128), vector(128),
            vector(INNER), vector(INNER),
            jax.ShapeDtypeStruct((256, INNER), BF16), jax.ShapeDtypeStruct((INNER, 128), BF16),
        ],
        scratch_shapes=[pltpu.VMEM((IN_BLOCK * NORM_ROWS + 16, LANES), F32)],
        compiler_params=pltpu.CompilerParams(
            dimension_semantics=("arbitrary",), vmem_limit_bytes=40 * 2**20),
        cost_estimate=pl.CostEstimate(
            flops=10**9, bytes_accessed=16 * 2**20, transcendentals=0),
    )(flat)


def adam_kernel(
    who_ref, rate_ref, early_ref, early_other_ref, late_ref, late_other_ref, small_ref,
    first_ref, second_ref,
    grad_ref, ratio_ref,
    stage_ref,
):
    step = pl.program_id(0)
    upper = who_ref[0]
    mine = who_ref[1]
    block = first_ref.shape[0]
    half = 2 * block * ADAM_BLOCKS

    @pl.when(step == 0)
    def _():
        early_at = LEAD + jnp.where(upper == 1, OUT_START - half, NORM_ROWS)
        window = LATE_START + (XBC - WINDOW) * NORM_ROWS
        late_at = LEAD + jnp.where(upper == 1, window - half, LATE_START)
        def lay(source_ref, start, size):
            for lane in range(NORM_ROWS):
                stage_ref[pl.ds(start + lane, size, stride=NORM_ROWS), :] = source_ref[
                    0:size, lane * LANES : lane * LANES + LANES]

        lines = late_ref.shape[0]
        lay(late_ref, late_at + mine * (lines * NORM_ROWS), lines)
        lay(late_other_ref, late_at + (1 - mine) * (lines * NORM_ROWS), lines)

        @pl.when(upper == 1)
        def _():
            lay(small_ref, LEAD + OUT_START - half - SMALL_ROWS, -(-SMALL_ROWS // NORM_ROWS))

        lines = early_ref.shape[0]
        lay(early_ref, early_at + mine * (lines * NORM_ROWS), lines)
        lay(early_other_ref, early_at + (1 - mine) * (lines * NORM_ROWS), lines)

        @pl.when(upper == 0)
        def _():
            for lane in range(NORM_ROWS):
                stage_ref[LEAD + lane : LEAD + lane + 1, :] = small_ref[
                    40:41, lane * LANES : lane * LANES + LANES]

        @pl.when(upper == 1)
        def _():
            at = LEAD + OUT_START + OUT_ROWS - half
            stage_ref[at : LEAD + half, :] = jnp.zeros((LEAD + half - at, LANES), F32)

    @pl.when(step > 0)
    def _():
        at = LEAD + mine * (half // 2) + (step - 1) * block
        grad = stage_ref[pl.ds(pl.multiple_of(at, 8), block), :]
        grad_ref[...] = grad
        first = BETA_ONE * first_ref[...] + (1.0 - BETA_ONE) * grad
        second = BETA_TWO * second_ref[...] + (1.0 - BETA_TWO) * grad * grad
        ratio_ref[...] = (first * rate_ref[0]) / (jnp.sqrt(second * rate_ref[1]) + EPS_ADAM)


def run_adam(who, rates, early, early_other, late, late_other, small, first, second):
    rows = first.shape[0]
    block = rows // ADAM_BLOCKS

    def at(i):
        return (jnp.maximum(i - 1, 0), 0)

    spec = pl.BlockSpec((block, LANES), at)
    out = jax.ShapeDtypeStruct((rows, LANES), F32)
    return pl.pallas_call(
        adam_kernel,
        grid=(ADAM_BLOCKS + 1,),
        in_specs=[
            pl.BlockSpec(memory_space=pltpu.SMEM), pl.BlockSpec(memory_space=pltpu.SMEM),
            const_spec(early.shape), const_spec(early.shape),
            const_spec(late.shape), const_spec(late.shape), const_spec(small.shape),
            spec, spec,
        ],
        out_specs=[spec, spec],
        out_shape=[out, out],
        scratch_shapes=[pltpu.VMEM((STAGE_ROWS, LANES), F32)],
        compiler_params=pltpu.CompilerParams(
            dimension_semantics=("arbitrary",), vmem_limit_bytes=48 * 2**20),
        cost_estimate=pl.CostEstimate(
            flops=10**8, bytes_accessed=24 * 2**20, transcendentals=10**6),
    )(who, rates, early, early_other, late, late_other, small, first, second)


def swap(values, axis, bit):
    size = lax.axis_size(axis)
    return lax.ppermute(values, axis, [(i, i ^ bit) for i in range(size)])


def to_wire(values, power):
    return (values * jnp.exp2(power)).astype(jnp.float16)


def from_wire(values, power):
    return values.astype(F32) * jnp.exp2(-power)


def scatter(values, power, axis, bit=1, count=2):
    place = (lax.axis_index(axis) // bit) % count
    rows = values.shape[-2] // count
    mark = min(MARK, rows)
    dim = values.ndim - 2
    total = lax.dynamic_slice_in_dim(values, place * rows, rows, dim)
    least = power
    for offset in range(1, count):
        to = place ^ offset
        last = to == count - 1
        start = to * rows - jnp.where(last, mark, 0)
        send = lax.dynamic_slice_in_dim(values, start, rows + mark, dim)
        line = lax.broadcasted_iota(jnp.int32, send.shape, dim)
        marked = jnp.where(last, line < mark, line >= rows)
        wire = jnp.where(marked, power, send * jnp.exp2(power)).astype(jnp.float16)
        got = swap(wire, axis, bit * offset)
        last = place == count - 1
        got_power = lax.dynamic_slice_in_dim(got, jnp.where(last, 0, rows), 1, dim)
        got_power = got_power.reshape(-1, D)[0:1, 0:1].astype(F32)
        body = lax.dynamic_slice_in_dim(got, jnp.where(last, mark, 0), rows, dim)
        total = total + from_wire(body, got_power)
        least = jnp.minimum(least, got_power)
    return total, least - float(count.bit_length() - 1)


def everyones(values, axis, bit=1, count=2):
    place = (lax.axis_index(axis) // bit) % count
    pieces = [values] + [swap(values, axis, bit * offset) for offset in range(1, count)]
    step = 1
    while step < count:
        flip = (place // step) % 2 == 1
        pieces = [
            jnp.where(flip, pieces[i ^ step], pieces[i]) for i in range(count)]
        step *= 2
    return pieces


def gather(values, axis, bit=1, count=2):
    return jnp.concatenate(everyones(values, axis, bit, count))


def add_pair(values, axis, bit):
    return values + swap(values, axis, bit)


def data_groups():
    size = lax.axis_size("dp")
    groups = [(1, 2)]
    bit = 2
    while bit < size:
        count = 4 if bit * 4 <= size else 2
        groups.append((bit, count))
        bit *= count
    return groups


def dot_tn(a, b):
    return lax.dot_general(a, b, (((0,), (0,)), ((), ())), preferred_element_type=F32)


def pick_rows(index, rows):
    chosen = index[:, None] == jnp.arange(rows.shape[0], dtype=jnp.int32)[None, :]
    return dot(chosen.astype(BF16), rows).astype(BF16)


def on_device(
    tokens, loss_sensitivity, lengths, holder_sequence_list, master, moment_one, moment_two,
    adam_rates, iteration_tally,
):
    group_devices = lax.axis_size("zero")
    data_devices = lax.axis_size("dp")
    zero_index = lax.axis_index("zero")
    dp_index = lax.axis_index("dp")
    seq_len = loss_sensitivity.shape[1]
    group_seqs = tokens.shape[0]
    span = tokens.shape[1]
    slots = group_seqs // data_devices
    shard_rows = master.shape[0] // LANES
    tie = lax.optimization_barrier

    own = master.reshape(shard_rows, LANES)
    arranged = holder_sequence_list.reshape(data_devices, group_devices, slots)
    group_order = lax.dynamic_index_in_dim(arranged, zero_index, 1, keepdims=False).reshape(-1)
    local_ids = group_order - zero_index * group_seqs
    dealt = tokens.at[local_ids].get(mode="promise_in_bounds")
    own, dealt = tie((own, dealt))
    flat = lax.all_gather(own.astype(BF16), "zero", axis=0, tiled=True)

    local_tok = lax.all_to_all(dealt, "dp", split_axis=0, concat_axis=0, tiled=True)
    my_seqs = lax.dynamic_slice_in_dim(group_order, dp_index * slots, slots)
    bound = lengths[my_seqs[0]]
    positions = jnp.arange(seq_len, dtype=jnp.int32)

    in_w, out_w, norm_gain, *params, e2, et = run_prepare(flat)
    cot = loss_sensitivity[0]
    gm = dot_nt(cot, out_w)
    cot_top = jnp.max(jnp.abs(cot)).astype(F32).reshape(1)
    local_tok, in_w, gm, cot_top = tie((local_tok, in_w, gm, cot_top))
    own_late, _ = tie((own, flat[:8]))
    whole_master = lax.all_gather(own_late, "zero", axis=0, tiled=True)

    def place(slot, at):
        return (at // span) * (slots * span) + slot * span + at % span

    source = jnp.where(positions < bound, place(0, positions), place(1, positions - bound))
    packed = pick_rows(source, local_tok.reshape(slots * seq_len, D))
    blocks = jnp.arange(data_devices, dtype=jnp.int32)[:, None, None] * span
    within = blocks + jnp.arange(span, dtype=jnp.int32)[None, None, :]
    within = within + jnp.arange(slots, dtype=jnp.int32)[None, :, None] * bound
    unpack_rows = jnp.minimum(within, seq_len - 1).reshape(-1)

    def spread(rows):
        return pick_rows(unpack_rows, rows).reshape(data_devices * slots, span, D)

    def send_back(picked):
        return lax.all_to_all(picked, "dp", split_axis=0, concat_axis=0, tiled=True)

    restore = jnp.zeros_like(local_ids).at[local_ids].set(
        jnp.arange(group_seqs, dtype=jnp.int32))
    mine = lax.dynamic_slice_in_dim(lengths, zero_index * group_seqs, group_seqs)
    at = dp_index * span + jnp.arange(span, dtype=jnp.int32)
    live = (at[None, :] < mine[:, None])[:, :, None]

    bound_arr = bound.reshape(1)
    tok = packed.astype(F32)
    nhat = tok * lax.rsqrt(jnp.mean(tok * tok, axis=1, keepdims=True) + EPS_NORM)
    normed = (nhat * norm_gain).astype(BF16)
    proj_z = dot_nt(normed, in_w[:INNER])
    proj = dot_nt(normed, in_w[INNER:PROJ])
    pair, dy, through, states, ggain, early_power = run_forward(
        proj_z, proj, gm, bound_arr, cot_top, norm_gain, e2, et, params)
    result = (tok + dot(pair[1], out_w)).astype(BF16)
    picked = spread(result)
    picked, pair = tie((picked, pair))
    back_out = send_back(picked)
    early_power = early_power[0:1, 0:1]
    early = lax.dot_general(
        pair, jnp.stack([normed, cot]), (((1,), (1,)), ((0,), (0,))), preferred_element_type=F32)
    early, early_power = scatter(early, early_power, "zero", 1)
    early, early_power, dy = tie((early.reshape(INNER, D), early_power, dy))
    early, early_power = scatter(early, early_power, "zero", 2)
    window, grad_tok, small, late_power = run_backward(
        proj, dy, through, states, pair, packed, cot, in_w, norm_gain, ggain,
        bound_arr, e2, et, params)
    window, small, late_power, back_out, early, early_power, whole_master = tie(
        (window, small, late_power, back_out, early, early_power, whole_master))

    groups = data_groups()
    late = lax.dot_general(
        window, jnp.stack([normed, normed]), (((1,), (1,)), ((0,), (0,))),
        preferred_element_type=F32)
    late_power = late_power[0:1, 0:1]
    late, late_power = scatter(late, late_power, "zero", 1)
    early, early_power = scatter(early, early_power, "dp", *groups[0])
    small = add_pair(small, "zero", 1)
    late, late_power, early, early_power, small = tie(
        (late.reshape(WINDOW, D), late_power, early, early_power, small))
    late, late_power = scatter(late, late_power, "zero", 2)
    for group in groups[1:]:
        early, early_power = scatter(early, early_power, "dp", *group)
    early = to_wire(early, early_power)
    small = add_pair(small, "zero", 2)
    picked_grad = spread(grad_tok)
    lines = small.shape[0]
    late = jnp.concatenate([late, small, jnp.zeros((WINDOW // 8 - lines, D), F32)])
    late, late_power, early, picked_grad = tie((late, late_power, early, picked_grad))
    late, late_power = scatter(late, late_power, "dp", *groups[0])
    for group in reversed(groups[1:]):
        early = gather(early, "dp", *group)
    late, late_power, early = tie((late, late_power, early))
    for group in groups[1:]:
        late, late_power = scatter(late, late_power, "dp", *group)
    late = to_wire(late, late_power)
    early = from_wire(gather(early, "dp", *groups[0]), early_power)
    late, early = tie((late, early))
    for group in reversed(groups[1:]):
        late = gather(late, "dp", *group)
    early_other = swap(early, "zero", 1)
    late, early_other, picked_grad = tie((late, early_other, picked_grad))
    back_grad = send_back(picked_grad)
    wire = gather(late, "dp", *groups[0])
    late = from_wire(wire[: WINDOW // 2], late_power)
    small = from_wire(wire[WINDOW // 2 : WINDOW // 2 + lines], late_power)
    late_other = swap(late, "zero", 1)

    steps_f = iteration_tally[0].astype(F32)
    rates = jnp.stack([
        1.0 / (1.0 - jnp.power(BETA_ONE, steps_f)), 1.0 / (1.0 - jnp.power(BETA_TWO, steps_f))])
    who = jnp.stack([zero_index // 2, zero_index % 2]).astype(jnp.int32)
    first = moment_one.reshape(shard_rows, LANES)
    second = moment_two.reshape(shard_rows, LANES)
    grad_shard, ratio = run_adam(
        who, rates, early, early_other, late, late_other, small, first, second)
    mine = ratio.astype(jnp.float16)
    mine, grad_shard, back_out = tie((mine, grad_shard, back_out))
    core = swap(mine, "zero", 1)
    across = swap(mine, "zero", 2)
    first_next = BETA_ONE * first + (1.0 - BETA_ONE) * grad_shard
    second_next = BETA_TWO * second + (1.0 - BETA_TWO) * grad_shard * grad_shard
    back_rows = back_out.at[restore].get(mode="promise_in_bounds")
    tokens_out = jnp.where(live, back_rows, tokens)
    new_master = jnp.zeros((group_devices, shard_rows, LANES), F32)
    whole_master = whole_master.reshape(group_devices, shard_rows, LANES)

    def put(new_master, piece, offset):
        shard = zero_index ^ offset
        old = lax.dynamic_index_in_dim(whole_master, shard, 0, keepdims=False)
        new = old - adam_rates[0] * (piece.astype(F32) + adam_rates[1] * old)
        return lax.dynamic_update_index_in_dim(new_master, new, shard, 0)

    new_master = put(put(new_master, mine, 0), core, 1)
    across, new_master, tokens_out, first_next, second_next = tie(
        (across, new_master, tokens_out, first_next, second_next))
    across_core = swap(across, "zero", 1)
    new_master = put(new_master, across, 2)
    across_core, new_master = tie((across_core, new_master))
    new_master = put(new_master, across_core, 3)
    back_grad, new_master = tie((back_grad, new_master))
    grad_tokens = jnp.where(
        live, back_grad.at[restore].get(mode="promise_in_bounds"), jnp.zeros((), BF16))
    return (
        tokens_out, grad_tokens, new_master.reshape(-1), grad_shard.reshape(-1),
        first_next.reshape(-1), second_next.reshape(-1))


def solution(mesh):
    return jax.shard_map(
        on_device,
        mesh=mesh,
        in_specs=(
            P("zero", "dp", None), P(("dp", "zero"), None, None), P(), P(),
            P("zero"), P("zero"), P("zero"), P(), P(),
        ),
        out_specs=(
            P("zero", "dp", None), P("zero", "dp", None), P(), P("zero"), P("zero"), P("zero"),
        ),
        check_vma=False,
    )
```

```python
import jax
import jax.numpy as jnp
from jax import lax
from jax.experimental import pallas as pl
from jax.experimental.pallas import tpu as pltpu
from jax.sharding import PartitionSpec as P

D = 768
HEADS = 24
HEADDIM = 64
STATE = 128
CONV = 4
INNER = 1536
XBC = 1792
PROJ = 3352
Q = 128
LATE = PROJ - INNER
WINDOW = 1024
PAIRS = HEADS // 2
EPS_NORM = 1e-05
NEG = -1e30
F16_TOP = 30000.0
LOG2E = 1.4426950408889634
F32 = jnp.float32
BF16 = jnp.bfloat16


def dot(a, b):
    return lax.dot_general(a, b, (((1,), (0,)), ((), ())), preferred_element_type=F32)


def dot_nt(a, b):
    return lax.dot_general(a, b, (((1,), (1,)), ((), ())), preferred_element_type=F32)


def split2(v):
    hi = v.astype(BF16)
    return hi, (v - hi.astype(F32)).astype(BF16)


def split3(v):
    hi = v.astype(BF16)
    rest = v - hi.astype(F32)
    mid = rest.astype(BF16)
    return hi, mid, (rest - mid.astype(F32)).astype(BF16)


def wide_left(v):
    hi, lo = split2(v)
    return jnp.concatenate([hi, lo, hi], axis=1)


def tall_right(v):
    hi, lo = split2(v)
    return jnp.concatenate([hi, hi, lo], axis=0)


def split_pair(v, masks):
    hi, lo = split2(v)
    return jnp.concatenate([
        jnp.concatenate([hi * masks[0], lo * masks[0]], axis=1),
        jnp.concatenate([hi * masks[1], lo * masks[1]], axis=1)], axis=0)


def sigmoid(v):
    return lax.logistic(v)


def softplus(v):
    return jnp.maximum(v, 0.0) + jnp.log1p(jnp.exp(-jnp.abs(v)))


def iota(shape, dim):
    return lax.broadcasted_iota(jnp.int32, shape, dim)


def expand(v, e_ref):
    hi, lo = split2(v)
    return dot(jnp.concatenate([hi, lo], axis=1), e_ref[...])


def head_sum(v, et_ref):
    hi, lo = split2(v)
    return dot(hi, et_ref[...]) + dot(lo, et_ref[...])


def quarters(out):
    return out[:Q, :Q] + (out[:Q, Q:] + out[Q:, :Q])


def power_for(bound):
    scale = jnp.log(0.9 * F16_TOP / jnp.maximum(bound, 1e-30)) * LOG2E
    return jnp.clip(jnp.floor(scale), -126.0, 120.0)


def chunk_masks(t0, bound):
    rows = t0 + iota((Q, 1), 0)
    rr = t0 + iota((Q, Q), 0)
    cc = t0 + iota((Q, Q), 1)
    return rows, rr, cc


def conv_rows(ext_ref, w_ref, b_ref, rows, bound):
    total = b_ref[...] + w_ref[3:4, :] * ext_ref[8 : 8 + Q, :]
    for back in (1, 2, 3):
        ok = jnp.logical_or(rows - back >= bound, rows < bound).astype(F32)
        total = total + w_ref[3 - back : 4 - back, :] * (ext_ref[8 - back : 8 - back + Q, :] * ok)
    return total


def decay_parts(dt_raw, dtb_ref, alog_ref, rr, cc):
    dt_in = dt_raw + dtb_ref[...]
    dt_pos = softplus(dt_in)
    rate = -jnp.exp(alog_ref[...])
    step = dt_pos * rate
    tri = (cc <= rr).astype(F32).astype(BF16)
    s_hi, s_mid, s_lo = split3(step)
    cum = dot(tri, s_hi) + dot(tri, s_mid) + dot(tri, s_lo)
    return dt_in, dt_pos, rate, cum


def forward_kernel(
    bound_ref, cot_ref, z_ref, proj_ref, gm_ref, norm_ref, e_ref, et_ref, convw_ref, convb_ref, dtb_ref, alog_ref,
    skip_ref, gain_ref,
    pair_ref, dy_ref, through_ref, state_ref, ggain_ref, power_ref,
    zmax_ref, ext_ref, dt_ref, carry_ref, xd_ref, acc_ref, cumt_ref,
):
    step = pl.program_id(0)
    bound = bound_ref[0]
    t0 = step * Q

    @pl.when(step == 0)
    def _():
        ext_ref[0:8, :] = jnp.zeros((8, XBC), F32)
        carry_ref[...] = jnp.zeros_like(carry_ref)
        dt_ref[...] = jnp.zeros_like(dt_ref)
        ggain_ref[...] = jnp.zeros_like(ggain_ref)
        zmax_ref[...] = jnp.zeros_like(zmax_ref)

    rows, rr, cc = chunk_masks(t0, bound)
    ext_ref[8 : 8 + Q, :] = proj_ref[:, :XBC]
    pre = conv_rows(ext_ref, convw_ref, convb_ref, rows, bound)
    ext_ref[0:8, :] = ext_ref[Q : Q + 8, :]
    conv_out = pre * sigmoid(pre)
    x = conv_out[:, :INNER]
    b_rows = conv_out[:, INNER : INNER + STATE]
    c_rows = conv_out[:, INNER + STATE :]
    dt_ref[:, 0:HEADS] = proj_ref[:, XBC:LATE]
    _, dt_pos, _, cum = decay_parts(dt_ref[...], dtb_ref, alog_ref, rr, cc)
    cum_end = cum[Q - 1 : Q, :]
    keep = jnp.logical_or(rows < bound, bound < t0).astype(F32)
    in_last = jnp.logical_or(rows >= bound, bound > t0 + Q - 1).astype(F32)
    whole = jnp.logical_or(bound < t0, bound > t0 + Q - 1).astype(F32)
    from_start = jnp.exp(cum) * keep
    to_end = jnp.exp(cum_end - cum) * in_last
    carry_scale = jnp.exp(cum_end) * whole
    allowed = jnp.logical_and(cc <= rr, (cc >= bound) == (rr >= bound))
    cum2 = cum * LOG2E
    cumt_ref[...] = cum2.T

    state = carry_ref[...]
    state_ref[0] = state
    spread = expand(jnp.concatenate(
        [dt_pos, to_end, from_start, jnp.broadcast_to(carry_scale, (16, 128))], axis=0), e_ref)
    xd = x * spread[:Q]
    xd_ref[...] = xd
    acc = dot(wide_left(c_rows), tall_right(state)) * spread[2 * Q : 3 * Q]
    acc_ref[...] = acc + skip_ref[...] * x
    b_t = b_rows.T
    carry_ref[...] = state * spread[3 * Q : 3 * Q + 1] + dot(
        wide_left(b_t), tall_right(xd * spread[Q : 2 * Q]))
    gram = dot(wide_left(c_rows), tall_right(b_t))
    first = iota((Q, Q), 1) < HEADDIM
    first_b = (first.astype(F32).astype(BF16), 1.0 - first.astype(F32).astype(BF16))
    for pair in range(PAIRS):
        parts = []
        for head in (2 * pair, 2 * pair + 1):
            differ = cum2[:, head : head + 1] - cumt_ref[head : head + 1, :]
            parts.append(gram * jnp.exp2(jnp.where(allowed, differ, NEG)))
        left = jnp.concatenate(split2(jnp.concatenate(parts, axis=1)), axis=0)
        lanes = slice(pair * 128, pair * 128 + 128)
        xp = xd_ref[:, lanes]
        out = dot(left, split_pair(xp, first_b))
        acc_ref[:, lanes] += out[:Q, :128] + (out[:Q, 128:] + out[Q:, :128])
    scanned = acc_ref[...]
    z = z_ref[...]
    sig_z = sigmoid(z)
    silu_z = z * sig_z
    gated = scanned * silu_z
    ginv = lax.rsqrt(jnp.mean(gated * gated, axis=1, keepdims=True) + EPS_NORM)
    mhat = gated * ginv
    pair_ref[1] = (mhat * gain_ref[...]).astype(BF16)
    gm = gm_ref[...]
    ggain_ref[...] += jnp.sum(mhat * gm, axis=0, keepdims=True)
    gmg = gm * gain_ref[...]
    ggated = ginv * (gmg - mhat * jnp.mean(mhat * gmg, axis=1, keepdims=True))
    dy = ggated * silu_z
    dy_ref[...] = dy
    grad_z = ggated * scanned * (sig_z * (1.0 + z * (1.0 - sig_z)))
    zmax_ref[...] = jnp.maximum(zmax_ref[...], jnp.max(jnp.abs(grad_z), axis=0, keepdims=True))
    pair_ref[0] = grad_z.astype(BF16)
    through_ref[...] = head_sum(dy * (scanned - skip_ref[...] * x), et_ref)

    @pl.when(step == pl.num_programs(0) - 1)
    def _():
        count = float(Q * pl.num_programs(0))
        largest = jnp.max(zmax_ref[...], axis=1, keepdims=True)
        normed = jnp.max(jnp.abs(norm_ref[...]), axis=1, keepdims=True) * (D ** 0.5)
        mixed = jnp.max(jnp.abs(gain_ref[...]), axis=1, keepdims=True) * (INNER ** 0.5)
        power_ref[...] = jnp.broadcast_to(power_for(
            1.05 * count * jnp.maximum(largest * normed, cot_ref[0] * mixed)), (8, 128))


def const_spec(shape):
    return pl.BlockSpec(shape, lambda *_: (0,) * len(shape))


def run_forward(z, proj, gm, bound, cot_top, norm_gain, e2, et, params):
    n = proj.shape[0]
    steps = n // Q
    return pl.pallas_call(
        forward_kernel,
        grid=(steps,),
        in_specs=[
            pl.BlockSpec(memory_space=pltpu.SMEM), pl.BlockSpec(memory_space=pltpu.SMEM),
            pl.BlockSpec((Q, INNER), lambda i: (i, 0)),
            pl.BlockSpec((Q, LATE), lambda i: (i, 0)),
            pl.BlockSpec((Q, INNER), lambda i: (i, 0)),
            const_spec((1, D)),
            const_spec((256, INNER)), const_spec((INNER, 128)),
            const_spec((8, XBC)), const_spec((1, XBC)), const_spec((1, 128)),
            const_spec((1, 128)), const_spec((1, INNER)), const_spec((1, INNER)),
        ],
        out_specs=[
            pl.BlockSpec((2, Q, INNER), lambda i: (0, i, 0)),
            pl.BlockSpec((Q, INNER), lambda i: (i, 0)),
            pl.BlockSpec((Q, 128), lambda i: (i, 0)),
            pl.BlockSpec((1, STATE, INNER), lambda i: (i, 0, 0)),
            const_spec((1, INNER)), const_spec((8, 128)),
        ],
        out_shape=[
            jax.ShapeDtypeStruct((2, n, INNER), BF16),
            jax.ShapeDtypeStruct((n, INNER), F32),
            jax.ShapeDtypeStruct((n, 128), F32),
            jax.ShapeDtypeStruct((steps, STATE, INNER), F32),
            jax.ShapeDtypeStruct((1, INNER), F32),
            jax.ShapeDtypeStruct((8, 128), F32),
        ],
        scratch_shapes=[
            pltpu.VMEM((1, INNER), F32),
            pltpu.VMEM((Q + 8, XBC), F32),
            pltpu.VMEM((Q, 128), F32),
            pltpu.VMEM((STATE, INNER), F32),
            pltpu.VMEM((Q, INNER), F32),
            pltpu.VMEM((Q, INNER), F32),
            pltpu.VMEM((128, Q), F32),
        ],
        compiler_params=pltpu.CompilerParams(
            dimension_semantics=("arbitrary",), vmem_limit_bytes=48 * 2**20),
        cost_estimate=pl.CostEstimate(
            flops=30 * 10**9, bytes_accessed=40 * 2**20, transcendentals=10**7),
    )(bound, cot_top, z, proj, gm, norm_gain, e2, et, *params)


def backward_kernel(
    bound_ref, proj_ref, before_ref, dy_ref, through_ref, state_ref, gz_ref, tok_ref, cot_ref,
    in_ref, norm_ref, ggain_ref,
    e_ref, et_ref, convw_ref, convb_ref, dtb_ref, alog_ref, skip_ref,
    window_ref, gtok_ref, small_ref, power_ref,
    total_ref, gskip_ref, gsmall_ref, dtw_ref, gp_ref, ext_ref, dt_ref, lam_ref, dsum_ref, xd_ref, g_ref, gnext_ref, cumt_ref,
):
    step = pl.program_id(0)
    steps = pl.num_programs(0)
    bound = bound_ref[0]
    t0 = (steps - 1 - step) * Q

    @pl.when(step == 0)
    def _():
        lam_ref[...] = jnp.zeros_like(lam_ref)
        dsum_ref[...] = jnp.zeros_like(dsum_ref)
        dt_ref[...] = jnp.zeros_like(dt_ref)
        gnext_ref[Q : Q + 8, :] = jnp.zeros((8, XBC), F32)
        gskip_ref[...] = jnp.zeros_like(gskip_ref)
        total_ref[...] = jnp.zeros_like(total_ref)
        dtw_ref[...] = jnp.zeros_like(dtw_ref)
        gsmall_ref[...] = jnp.zeros_like(gsmall_ref)

    rows, rr, cc = chunk_masks(t0, bound)
    dy = dy_ref[...]
    first_chunk = (t0 > 0).astype(F32)
    ext_ref[0:8, :] = before_ref[:, :XBC] * first_chunk
    ext_ref[8 : 8 + Q, :] = proj_ref[:, :XBC]
    pre = conv_rows(ext_ref, convw_ref, convb_ref, rows, bound)
    sig_pre = sigmoid(pre)
    conv_out = pre * sig_pre
    x = conv_out[:, :INNER]
    b_rows = conv_out[:, INNER : INNER + STATE]
    c_rows = conv_out[:, INNER + STATE :]
    dt_ref[:, 0:HEADS] = proj_ref[:, XBC:LATE]
    dt_in, dt_pos, rate, cum = decay_parts(dt_ref[...], dtb_ref, alog_ref, rr, cc)
    cum_end = cum[Q - 1 : Q, :]
    keep = jnp.logical_or(rows < bound, bound < t0).astype(F32)
    in_last = jnp.logical_or(rows >= bound, bound > t0 + Q - 1).astype(F32)
    whole = jnp.logical_or(bound < t0, bound > t0 + Q - 1).astype(F32)
    from_start = jnp.exp(cum) * keep
    to_end = jnp.exp(cum_end - cum) * in_last
    carry_scale = jnp.exp(cum_end) * whole
    allowed_t = jnp.logical_and(rr <= cc, (cc >= bound) == (rr >= bound))
    cum2 = cum * LOG2E
    cumt_ref[...] = cum2.T
    c_t = c_rows.T
    gram_t = dot(wide_left(b_rows), tall_right(c_t))
    spread = expand(jnp.concatenate(
        [dt_pos, to_end, from_start, jnp.broadcast_to(carry_scale, (16, 128))], axis=0), e_ref)
    dt_all = spread[:Q]
    end_all = spread[Q : 2 * Q]
    xd = x * dt_all
    xd_ref[...] = xd
    skip = skip_ref[...]
    gskip_ref[...] += jnp.sum(dy * x, axis=0, keepdims=True)
    lam = lam_ref[...]
    lam_hi, lam_lo = split2(lam)
    g_ref[...] = (
        dot(wide_left(b_rows), jnp.concatenate([lam_hi, lam_hi, lam_lo], axis=0)) * end_all
    )
    grad_b = quarters(dot_nt(
        jnp.concatenate(split2(xd * end_all), axis=0), jnp.concatenate([lam_hi, lam_lo], axis=0)))
    state = state_ref[0]
    dye_hi, dye_lo = split2(dy * spread[2 * Q : 3 * Q])
    grad_c = quarters(dot_nt(
        jnp.concatenate([dye_hi, dye_lo], axis=0), jnp.concatenate(split2(state), axis=0)))
    lam_new = lam * spread[3 * Q : 3 * Q + 1] + dot(
        wide_left(c_t), jnp.concatenate([dye_hi, dye_hi, dye_lo], axis=0)
    )
    lam_ref[...] = lam_new
    ended = dsum_ref[0:1, :]
    first = iota((Q, Q), 1) < HEADDIM
    first_b = (first.astype(F32).astype(BF16), 1.0 - first.astype(F32).astype(BF16))
    first_row = (iota((Q, Q), 0) < HEADDIM).astype(F32).astype(BF16)
    first_row = (first_row, 1.0 - first_row)
    gram_grad = jnp.zeros((Q, Q), F32)
    for pair in range(PAIRS):
        lanes = slice(pair * 128, pair * 128 + 128)
        weights = []
        for head in (2 * pair, 2 * pair + 1):
            differ = cumt_ref[head : head + 1, :] - cum2[:, head : head + 1]
            weights.append(jnp.exp2(jnp.where(allowed_t, differ, NEG)))
        left = jnp.concatenate([gram_t * weights[0], gram_t * weights[1]], axis=1)
        left = jnp.concatenate(split2(left), axis=0)
        dyp = dy_ref[:, lanes]
        out = dot(left, split_pair(dyp, first_b))
        g_ref[:, lanes] += out[:Q, :128] + (out[:Q, 128:] + out[Q:, :128])
        dyt_hi, dyt_lo = split2(dyp.T)
        right_hi = jnp.concatenate([dyt_hi * first_row[0], dyt_hi * first_row[1]], axis=1)
        right_lo = jnp.concatenate([dyt_lo * first_row[0], dyt_lo * first_row[1]], axis=1)
        outer = dot(
            wide_left(xd_ref[:, lanes]), jnp.concatenate([right_hi, right_hi, right_lo], axis=0))
        gram_grad = gram_grad + (outer[:, :128] * weights[0] + outer[:, 128:] * weights[1])
    g = g_ref[...]
    grad_x = dt_all * g + skip * dy
    sums = dot(jnp.concatenate(
        split2(x * g) + split2(jnp.broadcast_to(
            jnp.sum(lam_new * state, axis=0, keepdims=True), (16, INNER))), axis=0), et_ref[...])
    direct = sums[:Q] + sums[Q : 2 * Q]
    balance = through_ref[...] - dt_pos * direct
    keep_t = allowed_t.astype(F32).astype(BF16)
    b_hi, b_mid, b_lo = split3(balance)
    grad_step = dot(keep_t, b_hi) + dot(keep_t, b_mid) + dot(keep_t, b_lo) + in_last * ended
    dsum_ref[...] = sums[2 * Q : 2 * Q + 8] + sums[2 * Q + 16 : 2 * Q + 24]
    grad_dt = (direct + rate * grad_step) * sigmoid(dt_in)
    gsmall_ref[0:1, :] += jnp.sum(grad_dt, axis=0, keepdims=True)
    gsmall_ref[1:2, :] += rate * jnp.sum(dt_pos * grad_step, axis=0, keepdims=True)
    grad_c = grad_c + dot(wide_left(gram_grad.T), tall_right(b_rows))
    grad_b = grad_b + dot(wide_left(gram_grad), tall_right(c_rows))
    slope = sig_pre * (1.0 + pre * (1.0 - sig_pre))
    gnext_ref[0:Q, :INNER] = grad_x * slope[:, :INNER]
    gnext_ref[0:Q, INNER : INNER + STATE] = grad_b * slope[:, INNER : INNER + STATE]
    gnext_ref[0:Q, INNER + STATE :] = grad_c * slope[:, INNER + STATE :]
    gcp = gnext_ref[0:Q, :]
    total_ref[4:5, :] += jnp.sum(gcp, axis=0, keepdims=True)
    total_ref[3:4, :] += jnp.sum(gcp * ext_ref[8 : 8 + Q, :], axis=0, keepdims=True)
    total = convw_ref[3:4, :] * gcp
    for back in (1, 2, 3):
        ok = jnp.logical_or(rows - back >= bound, rows < bound).astype(F32)
        total_ref[3 - back : 4 - back, :] += jnp.sum(
            gcp * (ext_ref[8 - back : 8 - back + Q, :] * ok), axis=0, keepdims=True)
        okn = jnp.logical_or(rows >= bound, rows + back < bound).astype(F32)
        total = total + convw_ref[3 - back : 4 - back, :] * (gnext_ref[back : back + Q, :] * okn)
    total_ref[7:8, :] = jnp.maximum(
        total_ref[7:8, :], jnp.max(jnp.abs(total), axis=0, keepdims=True))
    total = total.astype(BF16)
    window_ref[0] = total[:, :WINDOW]
    window_ref[1] = total[:, XBC - WINDOW :]
    gnext_ref[Q : Q + 8, :] = gnext_ref[0:8, :]
    half = (steps - 1 - step) % 2
    at = pl.multiple_of(half * Q, Q)
    gp_ref[pl.ds(at, Q), :INNER] = gz_ref[0]
    gp_ref[pl.ds(at, Q), INNER : INNER + XBC] = total
    gp_ref[pl.ds(at, Q), INNER + XBC :] = grad_dt.astype(BF16)

    @pl.when(half == 0)
    def _():
        grad_normed = dot(gp_ref[...], in_ref[: INNER + XBC + 128, :])
        tok = tok_ref[...].astype(F32)
        rinv = lax.rsqrt(jnp.mean(tok * tok, axis=1, keepdims=True) + EPS_NORM)
        nhat = tok * rinv
        gain = norm_ref[...]
        gng = grad_normed * gain
        gtok_ref[...] = (cot_ref[...].astype(F32) + rinv * (
            gng - nhat * jnp.mean(nhat * gng, axis=1, keepdims=True))).astype(BF16)
        total_ref[6:7, :D] += jnp.sum(nhat * grad_normed, axis=0, keepdims=True)
        normed = (nhat * gain).astype(BF16)
        gdt = gp_ref[:, INNER + XBC :].astype(F32)
        dtw_ref[...] += dot(jnp.concatenate(
            [gdt[:Q].T, gdt[Q:].T], axis=1).astype(BF16), normed)

    @pl.when(step == steps - 1)
    def _():
        skips = head_sum(jnp.broadcast_to(gskip_ref[...], (8, INNER)), et_ref)
        small_ref[...] = jnp.zeros_like(small_ref)
        small_ref[0:HEADS, :] = dtw_ref[0:HEADS, :]
        pieces = [
            total_ref[k : k + 1, j * 128 : j * 128 + 128]
            for k in range(CONV + 1) for j in range(XBC // 128)]
        pieces += [gsmall_ref[0:1, :], gsmall_ref[1:2, :], skips[0:1, :]]
        pieces += [ggain_ref[:, j * 128 : j * 128 + 128] for j in range(INNER // 128)]
        lines = D // 128
        for number, piece in enumerate(pieces):
            line = HEADS + number // lines
            at = number % lines * 128
            small_ref[line : line + 1, at : at + 128] = piece
        small_ref[40:41, :] = total_ref[6:7, :D]
        count = float(Q * steps)
        largest = jnp.max(total_ref[7:8, :], axis=1, keepdims=True)
        normed = jnp.max(jnp.abs(norm_ref[...]), axis=1, keepdims=True) * (D ** 0.5)
        others = jnp.max(jnp.max(jnp.abs(small_ref[...]), axis=1, keepdims=True), axis=0, keepdims=True)
        power_ref[...] = jnp.broadcast_to(power_for(
            jnp.maximum(1.05 * count * largest * normed, others)), (8, 128))


def run_backward(
    proj, dy, through, states, pair, tok, cot, in_w, norm_gain, ggain, bound, e2, et, params
):
    n = proj.shape[0]
    steps = n // Q

    def rev(i):
        return (steps - 1 - i, 0)

    def rev_two(i):
        return ((steps - 1 - i) // 2, 0)

    return pl.pallas_call(
        backward_kernel,
        grid=(steps,),
        in_specs=[
            pl.BlockSpec(memory_space=pltpu.SMEM),
            pl.BlockSpec((Q, LATE), rev),
            pl.BlockSpec((8, LATE), lambda i: (jnp.maximum((steps - 1 - i) * (Q // 8) - 1, 0), 0)),
            pl.BlockSpec((Q, INNER), rev),
            pl.BlockSpec((Q, 128), rev),
            pl.BlockSpec((1, STATE, INNER), lambda i: (steps - 1 - i, 0, 0)),
            pl.BlockSpec((1, Q, INNER), lambda i: (0, steps - 1 - i, 0)),
            pl.BlockSpec((2 * Q, D), rev_two), pl.BlockSpec((2 * Q, D), rev_two),
            const_spec(in_w.shape), const_spec((1, D)), const_spec((1, INNER)),
            const_spec((256, INNER)), const_spec((INNER, 128)),
            const_spec((8, XBC)), const_spec((1, XBC)), const_spec((1, 128)),
            const_spec((1, 128)), const_spec((1, INNER)),
        ],
        out_specs=[
            pl.BlockSpec((2, Q, WINDOW), lambda i: (0, steps - 1 - i, 0)),
            pl.BlockSpec((2 * Q, D), rev_two),
            const_spec((48, D)), const_spec((8, 128)),
        ],
        out_shape=[
            jax.ShapeDtypeStruct((2, n, WINDOW), BF16),
            jax.ShapeDtypeStruct((n, D), BF16),
            jax.ShapeDtypeStruct((48, D), F32),
            jax.ShapeDtypeStruct((8, 128), F32),
        ],
        scratch_shapes=[
            pltpu.VMEM((8, XBC), F32),
            pltpu.VMEM((1, INNER), F32),
            pltpu.VMEM((8, 128), F32),
            pltpu.VMEM((128, D), F32),
            pltpu.VMEM((2 * Q, INNER + XBC + 128), BF16),
            pltpu.VMEM((Q + 8, XBC), F32),
            pltpu.VMEM((Q, 128), F32),
            pltpu.VMEM((STATE, INNER), F32),
            pltpu.VMEM((8, 128), F32),
            pltpu.VMEM((Q, INNER), F32),
            pltpu.VMEM((Q, INNER), F32),
            pltpu.VMEM((Q + 8, XBC), F32),
            pltpu.VMEM((128, Q), F32),
        ],
        compiler_params=pltpu.CompilerParams(
            dimension_semantics=("arbitrary",), vmem_limit_bytes=48 * 2**20),
        cost_estimate=pl.CostEstimate(
            flops=50 * 10**9, bytes_accessed=50 * 2**20, transcendentals=2 * 10**7),
    )(bound, proj, proj, dy, through, states, pair, tok, cot, in_w, norm_gain, ggain,
      e2, et, *params[:5])


BETA_ONE = 0.9
BETA_TWO = 0.95
EPS_ADAM = 1e-08
LANES = 128
NORM_ROWS = D // LANES
IN_ROWS = PROJ * D // LANES
CONVW_ROWS = CONV * XBC // LANES
CONVB_ROWS = XBC // LANES
GAIN_ROWS = INNER // LANES
OUT_ROWS = INNER * D // LANES
DT_ROWS = HEADS * D // LANES
SMALL_ROWS = DT_ROWS + CONVW_ROWS + CONVB_ROWS + 3 + GAIN_ROWS
OUT_START = NORM_ROWS + IN_ROWS + SMALL_ROWS - DT_ROWS
LATE_START = NORM_ROWS + INNER * NORM_ROWS
LEAD = 896
STAGE_ROWS = 16264
ADAM_BLOCKS = 10
MARK = 16


PREP_STEPS = 7
IN_BLOCK = 512
OUT_BLOCK = 256
SMALL_START = NORM_ROWS + IN_ROWS


def prepare_kernel(
    flat_ref,
    in_ref, out_ref, norm_ref, convw_ref, convb_ref, dtb_ref, alog_ref, skip_ref, gain_ref,
    e_ref, et_ref,
    stage_ref,
):
    step = pl.program_id(0)

    @pl.when(step == 0)
    def _():
        rows = flat_ref[0:16, :].astype(F32)
        for lane in range(NORM_ROWS):
            norm_ref[:, lane * LANES : lane * LANES + LANES] = rows[lane : lane + 1, :]
        low = SMALL_START // 16 * 16
        stage_ref[0:112, :] = flat_ref[low : low + 112, :].astype(F32)
        at = SMALL_START - low
        convw_ref[...] = jnp.zeros_like(convw_ref)
        for tap in range(CONV):
            for lane in range(CONVB_ROWS):
                convw_ref[tap : tap + 1, lane * LANES : lane * LANES + LANES] = stage_ref[
                    at : at + 1, :]
                at += 1
        for lane in range(CONVB_ROWS):
            convb_ref[:, lane * LANES : lane * LANES + LANES] = stage_ref[at : at + 1, :]
            at += 1
        heads = iota((1, LANES), 1) < HEADS
        dtb_ref[...] = jnp.where(heads, stage_ref[at : at + 1, :], 0.0)
        alog_ref[...] = jnp.where(heads, stage_ref[at + 1 : at + 2, :], 0.0)
        skips = jnp.where(heads, stage_ref[at + 2 : at + 3, :], 0.0)
        at += 3
        for lane in range(GAIN_ROWS):
            gain_ref[:, lane * LANES : lane * LANES + LANES] = stage_ref[at : at + 1, :]
            at += 1
        one = (iota((128, INNER), 1) // HEADDIM == iota((128, INNER), 0)).astype(F32).astype(BF16)
        e_ref[0:128, :] = one
        e_ref[128:256, :] = one
        et_ref[...] = (
            iota((INNER, 128), 0) // HEADDIM == iota((INNER, 128), 1)).astype(F32).astype(BF16)
        skip_ref[...] = dot(jnp.broadcast_to(skips, (16, LANES)).astype(BF16), one)[0:1, :]

    def block(start, offset, rows, dest_ref):
        size = rows * NORM_ROWS + 16
        at = pl.multiple_of(start + step * (rows * NORM_ROWS), 16)
        stage_ref[0:size, :] = flat_ref[pl.ds(at, size), :].astype(F32)
        for lane in range(NORM_ROWS):
            dest_ref[:, lane * LANES : lane * LANES + LANES] = stage_ref[
                pl.ds(offset + lane, rows, stride=NORM_ROWS), :].astype(BF16)

    block(0, NORM_ROWS, IN_BLOCK, in_ref)

    @pl.when(step == PREP_STEPS - 1)
    def _():
        used = PROJ - (PREP_STEPS - 1) * IN_BLOCK
        in_ref[used:, :] = jnp.zeros((IN_BLOCK - used, D), BF16)

    @pl.when(step < INNER // OUT_BLOCK)
    def _():
        low = OUT_START // 16 * 16
        block(low, OUT_START - low, OUT_BLOCK, out_ref)


def run_prepare(flat):
    vector = lambda n: jax.ShapeDtypeStruct((1, n), F32)
    return pl.pallas_call(
        prepare_kernel,
        grid=(PREP_STEPS,),
        in_specs=[const_spec(flat.shape)],
        out_specs=[
            pl.BlockSpec((IN_BLOCK, D), lambda i: (i, 0)),
            pl.BlockSpec((OUT_BLOCK, D), lambda i: (jnp.minimum(i, INNER // OUT_BLOCK - 1), 0)),
            const_spec((1, D)), const_spec((8, XBC)), const_spec((1, XBC)), const_spec((1, 128)),
            const_spec((1, 128)), const_spec((1, INNER)), const_spec((1, INNER)),
            const_spec((256, INNER)), const_spec((INNER, 128)),
        ],
        out_shape=[
            jax.ShapeDtypeStruct((PREP_STEPS * IN_BLOCK, D), BF16),
            jax.ShapeDtypeStruct((INNER, D), BF16),
            vector(D), jax.ShapeDtypeStruct((8, XBC), F32), vector(XBC), vector(128), vector(128),
            vector(INNER), vector(INNER),
            jax.ShapeDtypeStruct((256, INNER), BF16), jax.ShapeDtypeStruct((INNER, 128), BF16),
        ],
        scratch_shapes=[pltpu.VMEM((IN_BLOCK * NORM_ROWS + 16, LANES), F32)],
        compiler_params=pltpu.CompilerParams(
            dimension_semantics=("arbitrary",), vmem_limit_bytes=40 * 2**20),
        cost_estimate=pl.CostEstimate(
            flops=10**9, bytes_accessed=16 * 2**20, transcendentals=0),
    )(flat)


def adam_kernel(
    who_ref, rate_ref, early_ref, early_other_ref, late_ref, late_other_ref, small_ref,
    first_ref, second_ref,
    grad_ref, ratio_ref,
    stage_ref,
):
    step = pl.program_id(0)
    upper = who_ref[0]
    mine = who_ref[1]
    block = first_ref.shape[0]
    half = 2 * block * ADAM_BLOCKS

    @pl.when(step == 0)
    def _():
        early_at = LEAD + jnp.where(upper == 1, OUT_START - half, NORM_ROWS)
        window = LATE_START + (XBC - WINDOW) * NORM_ROWS
        late_at = LEAD + jnp.where(upper == 1, window - half, LATE_START)
        def lay(source_ref, start, size):
            for lane in range(NORM_ROWS):
                stage_ref[pl.ds(start + lane, size, stride=NORM_ROWS), :] = source_ref[
                    0:size, lane * LANES : lane * LANES + LANES]

        lines = late_ref.shape[0]
        lay(late_ref, late_at + mine * (lines * NORM_ROWS), lines)
        lay(late_other_ref, late_at + (1 - mine) * (lines * NORM_ROWS), lines)

        @pl.when(upper == 1)
        def _():
            lay(small_ref, LEAD + OUT_START - half - SMALL_ROWS, -(-SMALL_ROWS // NORM_ROWS))

        lines = early_ref.shape[0]
        lay(early_ref, early_at + mine * (lines * NORM_ROWS), lines)
        lay(early_other_ref, early_at + (1 - mine) * (lines * NORM_ROWS), lines)

        @pl.when(upper == 0)
        def _():
            for lane in range(NORM_ROWS):
                stage_ref[LEAD + lane : LEAD + lane + 1, :] = small_ref[
                    40:41, lane * LANES : lane * LANES + LANES]

        @pl.when(upper == 1)
        def _():
            at = LEAD + OUT_START + OUT_ROWS - half
            stage_ref[at : LEAD + half, :] = jnp.zeros((LEAD + half - at, LANES), F32)

    @pl.when(step > 0)
    def _():
        at = LEAD + mine * (half // 2) + (step - 1) * block
        grad = stage_ref[pl.ds(pl.multiple_of(at, 8), block), :]
        grad_ref[...] = grad
        first = BETA_ONE * first_ref[...] + (1.0 - BETA_ONE) * grad
        second = BETA_TWO * second_ref[...] + (1.0 - BETA_TWO) * grad * grad
        ratio_ref[...] = (first * rate_ref[0]) / (jnp.sqrt(second * rate_ref[1]) + EPS_ADAM)


def run_adam(who, rates, early, early_other, late, late_other, small, first, second):
    rows = first.shape[0]
    block = rows // ADAM_BLOCKS

    def at(i):
        return (jnp.maximum(i - 1, 0), 0)

    spec = pl.BlockSpec((block, LANES), at)
    out = jax.ShapeDtypeStruct((rows, LANES), F32)
    return pl.pallas_call(
        adam_kernel,
        grid=(ADAM_BLOCKS + 1,),
        in_specs=[
            pl.BlockSpec(memory_space=pltpu.SMEM), pl.BlockSpec(memory_space=pltpu.SMEM),
            const_spec(early.shape), const_spec(early.shape),
            const_spec(late.shape), const_spec(late.shape), const_spec(small.shape),
            spec, spec,
        ],
        out_specs=[spec, spec],
        out_shape=[out, out],
        scratch_shapes=[pltpu.VMEM((STAGE_ROWS, LANES), F32)],
        compiler_params=pltpu.CompilerParams(
            dimension_semantics=("arbitrary",), vmem_limit_bytes=48 * 2**20),
        cost_estimate=pl.CostEstimate(
            flops=10**8, bytes_accessed=24 * 2**20, transcendentals=10**6),
    )(who, rates, early, early_other, late, late_other, small, first, second)


def swap(values, axis, bit):
    size = lax.axis_size(axis)
    return lax.ppermute(values, axis, [(i, i ^ bit) for i in range(size)])


def to_wire(values, power):
    return (values * jnp.exp2(power)).astype(jnp.float16)


def from_wire(values, power):
    return values.astype(F32) * jnp.exp2(-power)


def scatter(values, power, axis, bit=1, count=2):
    place = (lax.axis_index(axis) // bit) % count
    rows = values.shape[-2] // count
    mark = min(MARK, rows)
    dim = values.ndim - 2
    total = lax.dynamic_slice_in_dim(values, place * rows, rows, dim)
    least = power
    for offset in range(1, count):
        to = place ^ offset
        last = to == count - 1
        start = to * rows - jnp.where(last, mark, 0)
        send = lax.dynamic_slice_in_dim(values, start, rows + mark, dim)
        line = lax.broadcasted_iota(jnp.int32, send.shape, dim)
        marked = jnp.where(last, line < mark, line >= rows)
        wire = jnp.where(marked, power, send * jnp.exp2(power)).astype(jnp.float16)
        got = swap(wire, axis, bit * offset)
        last = place == count - 1
        got_power = lax.dynamic_slice_in_dim(got, jnp.where(last, 0, rows), 1, dim)
        got_power = got_power.reshape(-1, D)[0:1, 0:1].astype(F32)
        body = lax.dynamic_slice_in_dim(got, jnp.where(last, mark, 0), rows, dim)
        total = total + from_wire(body, got_power)
        least = jnp.minimum(least, got_power)
    return total, least - float(count.bit_length() - 1)


def everyones(values, axis, bit=1, count=2):
    place = (lax.axis_index(axis) // bit) % count
    pieces = [values] + [swap(values, axis, bit * offset) for offset in range(1, count)]
    step = 1
    while step < count:
        flip = (place // step) % 2 == 1
        pieces = [
            jnp.where(flip, pieces[i ^ step], pieces[i]) for i in range(count)]
        step *= 2
    return pieces


def gather(values, axis, bit=1, count=2):
    return jnp.concatenate(everyones(values, axis, bit, count))


def add_pair(values, axis, bit):
    return values + swap(values, axis, bit)


def data_groups():
    size = lax.axis_size("dp")
    groups = [(1, 2)]
    bit = 2
    while bit < size:
        count = 4 if bit * 4 <= size else 2
        groups.append((bit, count))
        bit *= count
    return groups


def dot_tn(a, b):
    return lax.dot_general(a, b, (((0,), (0,)), ((), ())), preferred_element_type=F32)


def rows_from(ref, start):
    low = pl.multiple_of(start // 8 * 8, 8)
    window = ref[pl.ds(low, Q + 8), :]
    return pltpu.roll(window, (Q + 8 - start % 8) % (Q + 8), 0)[:Q]


def pack_kernel(
    bound_ref, slots_ref, cot_ref, gain_ref, packed_ref, both_ref, later_ref,
):
    step = pl.program_id(0)
    bound = bound_ref[0]
    senders, _, span, _ = slots_ref.shape

    @pl.when(step == 0)
    def _():
        later_ref[0:Q, :] = jnp.zeros((Q, D), F32)

        def lay(sender, carry):
            at = pl.multiple_of(Q + sender * span, 8)
            later_ref[pl.ds(at, span), :] = slots_ref[sender, 1].astype(F32)
            return carry

        lax.fori_loop(0, senders, lay, 0)

    count = Q // span
    rows = slots_ref[pl.ds(step * count, count), 0].reshape(Q, D).astype(F32)
    start = jnp.maximum(Q + step * Q - bound, 0)
    tok = jnp.where(
        step * Q + iota((Q, 1), 0) < bound, rows, rows_from(later_ref, start))
    packed_ref[...] = tok.astype(BF16)
    nhat = tok * lax.rsqrt(jnp.mean(tok * tok, axis=1, keepdims=True) + EPS_NORM)
    both_ref[0] = (nhat * gain_ref[...]).astype(BF16)
    both_ref[1] = cot_ref[...]


def run_pack(bound, slots, cot, gain):
    n = cot.shape[0]
    return pl.pallas_call(
        pack_kernel,
        grid=(n // Q,),
        in_specs=[
            pl.BlockSpec(memory_space=pltpu.SMEM), const_spec(slots.shape),
            pl.BlockSpec((Q, D), lambda i: (i, 0)), const_spec((1, D)),
        ],
        out_specs=[
            pl.BlockSpec((Q, D), lambda i: (i, 0)), pl.BlockSpec((2, Q, D), lambda i: (0, i, 0))],
        out_shape=[
            jax.ShapeDtypeStruct((n, D), BF16), jax.ShapeDtypeStruct((2, n, D), BF16)],
        scratch_shapes=[pltpu.VMEM((n + Q + 8, D), F32)],
        compiler_params=pltpu.CompilerParams(
            dimension_semantics=("arbitrary",), vmem_limit_bytes=24 * 2**20),
        cost_estimate=pl.CostEstimate(
            flops=10**7, bytes_accessed=10 * 2**20, transcendentals=1024),
    )(bound, slots, cot, gain)


def spread_kernel(bound_ref, rows_ref, out_ref, wide_ref):
    step = pl.program_id(0)
    n = rows_ref.shape[0]
    count, _, span, _ = out_ref.shape

    @pl.when(step == 0)
    def _():
        wide_ref[0:n, :] = rows_ref[...].astype(F32)
        wide_ref[n : n + Q, :] = jnp.zeros((Q, D), F32)

    at = pl.multiple_of(step * Q, Q)
    out_ref[:, 0] = rows_ref[pl.ds(at, Q), :].reshape(count, span, D)
    start = jnp.minimum(bound_ref[0] + step * Q, n)
    out_ref[:, 1] = rows_from(wide_ref, start).astype(BF16).reshape(count, span, D)


def run_spread(bound, rows, receivers):
    n = rows.shape[0]
    span = n // receivers
    return pl.pallas_call(
        spread_kernel,
        grid=(n // Q,),
        in_specs=[pl.BlockSpec(memory_space=pltpu.SMEM), const_spec((n, D))],
        out_specs=pl.BlockSpec((Q // span, 2, span, D), lambda i: (i, 0, 0, 0)),
        out_shape=jax.ShapeDtypeStruct((receivers, 2, span, D), BF16),
        scratch_shapes=[pltpu.VMEM((n + Q + 8, D), F32)],
        compiler_params=pltpu.CompilerParams(
            dimension_semantics=("arbitrary",), vmem_limit_bytes=24 * 2**20),
        cost_estimate=pl.CostEstimate(
            flops=10**7, bytes_accessed=5 * 2**20, transcendentals=0),
    )(bound, rows)


def on_device(
    tokens, loss_sensitivity, lengths, holder_sequence_list, master, moment_one, moment_two,
    adam_rates, iteration_tally,
):
    group_devices = lax.axis_size("zero")
    data_devices = lax.axis_size("dp")
    zero_index = lax.axis_index("zero")
    dp_index = lax.axis_index("dp")
    seq_len = loss_sensitivity.shape[1]
    group_seqs = tokens.shape[0]
    span = tokens.shape[1]
    slots = group_seqs // data_devices
    shard_rows = master.shape[0] // LANES
    tie = lax.optimization_barrier

    own = master.reshape(shard_rows, LANES)
    arranged = holder_sequence_list.reshape(data_devices, group_devices, slots)
    group_order = lax.dynamic_index_in_dim(arranged, zero_index, 1, keepdims=False).reshape(-1)
    local_ids = group_order - zero_index * group_seqs
    dealt = tokens.at[local_ids].get(mode="promise_in_bounds")
    flat = lax.all_gather(own.astype(BF16), "zero", axis=0, tiled=True)

    local_tok = lax.all_to_all(dealt, "dp", split_axis=0, concat_axis=0, tiled=True)
    my_seqs = lax.dynamic_slice_in_dim(group_order, dp_index * slots, slots)
    bound = lengths[my_seqs[0]]
    in_w, out_w, norm_gain, *params, e2, et = run_prepare(flat)
    cot = loss_sensitivity[0]
    gm = dot_nt(cot, out_w)
    cot_top = jnp.max(jnp.abs(cot)).astype(F32).reshape(1)
    local_tok, in_w, gm, cot_top = tie((local_tok, in_w, gm, cot_top))
    own_late, _ = tie((own, flat[:8]))
    whole_master = lax.all_gather(own_late, "zero", axis=0, tiled=True)

    def spread(rows):
        return run_spread(bound_arr, rows, data_devices).reshape(data_devices * slots, span, D)

    def send_back(picked):
        return lax.all_to_all(picked, "dp", split_axis=0, concat_axis=0, tiled=True)

    restore = jnp.zeros_like(local_ids).at[local_ids].set(
        jnp.arange(group_seqs, dtype=jnp.int32))
    mine = lax.dynamic_slice_in_dim(lengths, zero_index * group_seqs, group_seqs)
    at = dp_index * span + jnp.arange(span, dtype=jnp.int32)
    live = (at[None, :] < mine[:, None])[:, :, None]

    bound_arr = bound.reshape(1)
    packed, both = run_pack(
        bound_arr, local_tok.reshape(data_devices, slots, span, D), cot, norm_gain)
    normed = both[0]
    proj_z = dot_nt(normed, in_w[:INNER])
    proj = dot_nt(normed, in_w[INNER:PROJ])
    pair, dy, through, states, ggain, early_power = run_forward(
        proj_z, proj, gm, bound_arr, cot_top, norm_gain, e2, et, params)
    result = (packed.astype(F32) + dot(pair[1], out_w)).astype(BF16)
    picked = spread(result)
    picked, pair = tie((picked, pair))
    back_out = send_back(picked)
    early_power = early_power[0:1, 0:1]
    early = lax.dot_general(
        pair, both, (((1,), (1,)), ((0,), (0,))), preferred_element_type=F32)
    early, early_power = scatter(early, early_power, "zero", 1)
    early, early_power, dy = tie((early.reshape(INNER, D), early_power, dy))
    early, early_power = scatter(early, early_power, "zero", 2)
    window, grad_tok, small, late_power = run_backward(
        proj, dy, through, states, pair, packed, cot, in_w, norm_gain, ggain,
        bound_arr, e2, et, params)
    window, small, late_power, back_out, early, early_power, whole_master = tie(
        (window, small, late_power, back_out, early, early_power, whole_master))

    groups = data_groups()
    late = lax.dot_general(
        window, jnp.stack([normed, normed]), (((1,), (1,)), ((0,), (0,))),
        preferred_element_type=F32)
    late_power = late_power[0:1, 0:1]
    late, late_power = scatter(late, late_power, "zero", 1)
    early, early_power = scatter(early, early_power, "dp", *groups[0])
    small = add_pair(small, "zero", 1)
    late, late_power, early, early_power, small = tie(
        (late.reshape(WINDOW, D), late_power, early, early_power, small))
    late, late_power = scatter(late, late_power, "zero", 2)
    for group in groups[1:]:
        early, early_power = scatter(early, early_power, "dp", *group)
    early = to_wire(early, early_power)
    small = add_pair(small, "zero", 2)
    picked_grad = spread(grad_tok)
    lines = small.shape[0]
    late = jnp.concatenate([late, small, jnp.zeros((WINDOW // 8 - lines, D), F32)])
    late, late_power, early, picked_grad = tie((late, late_power, early, picked_grad))
    late, late_power = scatter(late, late_power, "dp", *groups[0])
    for group in reversed(groups[1:]):
        early = gather(early, "dp", *group)
    late, late_power, early = tie((late, late_power, early))
    for group in groups[1:]:
        late, late_power = scatter(late, late_power, "dp", *group)
    late = to_wire(late, late_power)
    early = from_wire(gather(early, "dp", *groups[0]), early_power)
    late, early = tie((late, early))
    for group in reversed(groups[1:]):
        late = gather(late, "dp", *group)
    early_other = swap(early, "zero", 1)
    late, early_other, picked_grad = tie((late, early_other, picked_grad))
    back_grad = send_back(picked_grad)
    wire = gather(late, "dp", *groups[0])
    late = from_wire(wire[: WINDOW // 2], late_power)
    small = from_wire(wire[WINDOW // 2 : WINDOW // 2 + lines], late_power)
    late_other = swap(late, "zero", 1)

    steps_f = iteration_tally[0].astype(F32)
    rates = jnp.stack([
        1.0 / (1.0 - jnp.power(BETA_ONE, steps_f)), 1.0 / (1.0 - jnp.power(BETA_TWO, steps_f))])
    who = jnp.stack([zero_index // 2, zero_index % 2]).astype(jnp.int32)
    first = moment_one.reshape(shard_rows, LANES)
    second = moment_two.reshape(shard_rows, LANES)
    grad_shard, ratio = run_adam(
        who, rates, early, early_other, late, late_other, small, first, second)
    mine = ratio.astype(jnp.float16)
    mine, grad_shard, back_out = tie((mine, grad_shard, back_out))
    core = swap(mine, "zero", 1)
    across = swap(mine, "zero", 2)
    first_next = BETA_ONE * first + (1.0 - BETA_ONE) * grad_shard
    second_next = BETA_TWO * second + (1.0 - BETA_TWO) * grad_shard * grad_shard
    back_rows = back_out.at[restore].get(mode="promise_in_bounds")
    tokens_out = jnp.where(live, back_rows, tokens)
    new_master = jnp.zeros((group_devices, shard_rows, LANES), F32)
    whole_master = whole_master.reshape(group_devices, shard_rows, LANES)

    def put(new_master, piece, offset):
        shard = zero_index ^ offset
        old = lax.dynamic_index_in_dim(whole_master, shard, 0, keepdims=False)
        new = old - adam_rates[0] * (piece.astype(F32) + adam_rates[1] * old)
        return lax.dynamic_update_index_in_dim(new_master, new, shard, 0)

    new_master = put(put(new_master, mine, 0), core, 1)
    across, new_master, tokens_out, first_next, second_next = tie(
        (across, new_master, tokens_out, first_next, second_next))
    across_core = swap(across, "zero", 1)
    new_master = put(new_master, across, 2)
    across_core, new_master = tie((across_core, new_master))
    new_master = put(new_master, across_core, 3)
    back_grad, new_master = tie((back_grad, new_master))
    grad_tokens = jnp.where(
        live, back_grad.at[restore].get(mode="promise_in_bounds"), jnp.zeros((), BF16))
    return (
        tokens_out, grad_tokens, new_master.reshape(-1), grad_shard.reshape(-1),
        first_next.reshape(-1), second_next.reshape(-1))


def solution(mesh):
    return jax.shard_map(
        on_device,
        mesh=mesh,
        in_specs=(
            P("zero", "dp", None), P(("dp", "zero"), None, None), P(), P(),
            P("zero"), P("zero"), P("zero"), P(), P(),
        ),
        out_specs=(
            P("zero", "dp", None), P("zero", "dp", None), P(), P("zero"), P("zero"), P("zero"),
        ),
        check_vma=False,
    )
```

```python
import jax
import jax.numpy as jnp
from jax import lax
from jax.experimental import pallas as pl
from jax.experimental.pallas import tpu as pltpu
from jax.sharding import PartitionSpec as P

D = 768
HEADS = 24
HEADDIM = 64
STATE = 128
CONV = 4
INNER = 1536
XBC = 1792
PROJ = 3352
Q = 128
LATE = PROJ - INNER
WINDOW = 1024
PAIRS = HEADS // 2
EPS_NORM = 1e-05
NEG = -1e30
F16_TOP = 30000.0
LOG2E = 1.4426950408889634
F32 = jnp.float32
BF16 = jnp.bfloat16


def dot(a, b):
    return lax.dot_general(a, b, (((1,), (0,)), ((), ())), preferred_element_type=F32)


def dot_nt(a, b):
    return lax.dot_general(a, b, (((1,), (1,)), ((), ())), preferred_element_type=F32)


def split2(v):
    hi = v.astype(BF16)
    return hi, (v - hi.astype(F32)).astype(BF16)


def split3(v):
    hi = v.astype(BF16)
    rest = v - hi.astype(F32)
    mid = rest.astype(BF16)
    return hi, mid, (rest - mid.astype(F32)).astype(BF16)


def wide_left(v):
    hi, lo = split2(v)
    return jnp.concatenate([hi, lo, hi], axis=1)


def tall_right(v):
    hi, lo = split2(v)
    return jnp.concatenate([hi, hi, lo], axis=0)


def split_pair(v, masks):
    hi, lo = split2(v)
    return jnp.concatenate([
        jnp.concatenate([hi * masks[0], lo * masks[0]], axis=1),
        jnp.concatenate([hi * masks[1], lo * masks[1]], axis=1)], axis=0)


def sigmoid(v):
    return lax.logistic(v)


def softplus(v):
    return jnp.maximum(v, 0.0) + jnp.log1p(jnp.exp(-jnp.abs(v)))


def iota(shape, dim):
    return lax.broadcasted_iota(jnp.int32, shape, dim)


def expand(v, e_ref):
    hi, lo = split2(v)
    return dot(jnp.concatenate([hi, lo], axis=1), e_ref[...])


def head_sum(v, et_ref):
    hi, lo = split2(v)
    return dot(hi, et_ref[...]) + dot(lo, et_ref[...])


def quarters(out):
    return out[:Q, :Q] + (out[:Q, Q:] + out[Q:, :Q])


def power_for(bound):
    scale = jnp.log(0.9 * F16_TOP / jnp.maximum(bound, 1e-30)) * LOG2E
    return jnp.clip(jnp.floor(scale), -126.0, 120.0)


def chunk_masks(t0, bound):
    rows = t0 + iota((Q, 1), 0)
    rr = t0 + iota((Q, Q), 0)
    cc = t0 + iota((Q, Q), 1)
    return rows, rr, cc


def conv_rows(ext_ref, w_ref, b_ref, rows, bound):
    total = b_ref[...] + w_ref[3:4, :] * ext_ref[8 : 8 + Q, :]
    for back in (1, 2, 3):
        ok = jnp.logical_or(rows - back >= bound, rows < bound).astype(F32)
        total = total + w_ref[3 - back : 4 - back, :] * (ext_ref[8 - back : 8 - back + Q, :] * ok)
    return total


def decay_parts(dt_raw, dtb_ref, alog_ref, rr, cc):
    dt_in = dt_raw + dtb_ref[...]
    dt_pos = softplus(dt_in)
    rate = -jnp.exp(alog_ref[...])
    step = dt_pos * rate
    tri = (cc <= rr).astype(F32).astype(BF16)
    s_hi, s_mid, s_lo = split3(step)
    cum = dot(tri, s_hi) + dot(tri, s_mid) + dot(tri, s_lo)
    return dt_in, dt_pos, rate, cum


def forward_kernel(
    bound_ref, cot_ref, z_ref, proj_ref, gm_ref, norm_ref, e_ref, et_ref, convw_ref, convb_ref, dtb_ref, alog_ref,
    skip_ref, gain_ref,
    pair_ref, dy_ref, through_ref, state_ref, ggain_ref, power_ref,
    zmax_ref, ext_ref, dt_ref, carry_ref, xd_ref, acc_ref, cumt_ref,
):
    step = pl.program_id(0)
    bound = bound_ref[0]
    t0 = step * Q

    @pl.when(step == 0)
    def _():
        ext_ref[0:8, :] = jnp.zeros((8, XBC), F32)
        carry_ref[...] = jnp.zeros_like(carry_ref)
        dt_ref[...] = jnp.zeros_like(dt_ref)
        ggain_ref[...] = jnp.zeros_like(ggain_ref)
        zmax_ref[...] = jnp.zeros_like(zmax_ref)

    rows, rr, cc = chunk_masks(t0, bound)
    ext_ref[8 : 8 + Q, :] = proj_ref[:, :XBC]
    pre = conv_rows(ext_ref, convw_ref, convb_ref, rows, bound)
    ext_ref[0:8, :] = ext_ref[Q : Q + 8, :]
    conv_out = pre * sigmoid(pre)
    x = conv_out[:, :INNER]
    b_rows = conv_out[:, INNER : INNER + STATE]
    c_rows = conv_out[:, INNER + STATE :]
    dt_ref[:, 0:HEADS] = proj_ref[:, XBC:LATE]
    _, dt_pos, _, cum = decay_parts(dt_ref[...], dtb_ref, alog_ref, rr, cc)
    cum_end = cum[Q - 1 : Q, :]
    keep = jnp.logical_or(rows < bound, bound < t0).astype(F32)
    in_last = jnp.logical_or(rows >= bound, bound > t0 + Q - 1).astype(F32)
    whole = jnp.logical_or(bound < t0, bound > t0 + Q - 1).astype(F32)
    from_start = jnp.exp(cum) * keep
    to_end = jnp.exp(cum_end - cum) * in_last
    carry_scale = jnp.exp(cum_end) * whole
    allowed = jnp.logical_and(cc <= rr, (cc >= bound) == (rr >= bound))
    cum2 = cum * LOG2E
    cumt_ref[...] = cum2.T

    state = carry_ref[...]
    state_ref[0] = state
    spread = expand(jnp.concatenate(
        [dt_pos, to_end, from_start, jnp.broadcast_to(carry_scale, (16, 128))], axis=0), e_ref)
    xd = x * spread[:Q]
    xd_ref[...] = xd
    acc = dot(wide_left(c_rows), tall_right(state)) * spread[2 * Q : 3 * Q]
    acc_ref[...] = acc + skip_ref[...] * x
    b_t = b_rows.T
    carry_ref[...] = state * spread[3 * Q : 3 * Q + 1] + dot(
        wide_left(b_t), tall_right(xd * spread[Q : 2 * Q]))
    gram = dot(wide_left(c_rows), tall_right(b_t))
    first = iota((Q, Q), 1) < HEADDIM
    first_b = (first.astype(F32).astype(BF16), 1.0 - first.astype(F32).astype(BF16))
    for pair in range(PAIRS):
        parts = []
        for head in (2 * pair, 2 * pair + 1):
            differ = cum2[:, head : head + 1] - cumt_ref[head : head + 1, :]
            parts.append(gram * jnp.exp2(jnp.where(allowed, differ, NEG)))
        left = jnp.concatenate(split2(jnp.concatenate(parts, axis=1)), axis=0)
        lanes = slice(pair * 128, pair * 128 + 128)
        xp = xd_ref[:, lanes]
        out = dot(left, split_pair(xp, first_b))
        acc_ref[:, lanes] += out[:Q, :128] + (out[:Q, 128:] + out[Q:, :128])
    scanned = acc_ref[...]
    z = z_ref[...]
    sig_z = sigmoid(z)
    silu_z = z * sig_z
    gated = scanned * silu_z
    ginv = lax.rsqrt(jnp.mean(gated * gated, axis=1, keepdims=True) + EPS_NORM)
    mhat = gated * ginv
    pair_ref[1] = (mhat * gain_ref[...]).astype(BF16)
    gm = gm_ref[...]
    ggain_ref[...] += jnp.sum(mhat * gm, axis=0, keepdims=True)
    gmg = gm * gain_ref[...]
    ggated = ginv * (gmg - mhat * jnp.mean(mhat * gmg, axis=1, keepdims=True))
    dy = ggated * silu_z
    dy_ref[...] = dy
    grad_z = ggated * scanned * (sig_z * (1.0 + z * (1.0 - sig_z)))
    zmax_ref[...] = jnp.maximum(zmax_ref[...], jnp.max(jnp.abs(grad_z), axis=0, keepdims=True))
    pair_ref[0] = grad_z.astype(BF16)
    through_ref[...] = head_sum(dy * (scanned - skip_ref[...] * x), et_ref)

    @pl.when(step == pl.num_programs(0) - 1)
    def _():
        count = float(Q * pl.num_programs(0))
        largest = jnp.max(zmax_ref[...], axis=1, keepdims=True)
        normed = jnp.max(jnp.abs(norm_ref[...]), axis=1, keepdims=True) * (D ** 0.5)
        mixed = jnp.max(jnp.abs(gain_ref[...]), axis=1, keepdims=True) * (INNER ** 0.5)
        power_ref[...] = jnp.broadcast_to(power_for(
            1.05 * count * jnp.maximum(largest * normed, cot_ref[0] * mixed)), (8, 128))


def const_spec(shape):
    return pl.BlockSpec(shape, lambda *_: (0,) * len(shape))


def run_forward(z, proj, gm, bound, cot_top, norm_gain, e2, et, params):
    n = proj.shape[0]
    steps = n // Q
    return pl.pallas_call(
        forward_kernel,
        grid=(steps,),
        in_specs=[
            pl.BlockSpec(memory_space=pltpu.SMEM), pl.BlockSpec(memory_space=pltpu.SMEM),
            pl.BlockSpec((Q, INNER), lambda i: (i, 0)),
            pl.BlockSpec((Q, LATE), lambda i: (i, 0)),
            pl.BlockSpec((Q, INNER), lambda i: (i, 0)),
            const_spec((1, D)),
            const_spec((256, INNER)), const_spec((INNER, 128)),
            const_spec((8, XBC)), const_spec((1, XBC)), const_spec((1, 128)),
            const_spec((1, 128)), const_spec((1, INNER)), const_spec((1, INNER)),
        ],
        out_specs=[
            pl.BlockSpec((2, Q, INNER), lambda i: (0, i, 0)),
            pl.BlockSpec((Q, INNER), lambda i: (i, 0)),
            pl.BlockSpec((Q, 128), lambda i: (i, 0)),
            pl.BlockSpec((1, STATE, INNER), lambda i: (i, 0, 0)),
            const_spec((1, INNER)), const_spec((8, 128)),
        ],
        out_shape=[
            jax.ShapeDtypeStruct((2, n, INNER), BF16),
            jax.ShapeDtypeStruct((n, INNER), F32),
            jax.ShapeDtypeStruct((n, 128), F32),
            jax.ShapeDtypeStruct((steps, STATE, INNER), F32),
            jax.ShapeDtypeStruct((1, INNER), F32),
            jax.ShapeDtypeStruct((8, 128), F32),
        ],
        scratch_shapes=[
            pltpu.VMEM((1, INNER), F32),
            pltpu.VMEM((Q + 8, XBC), F32),
            pltpu.VMEM((Q, 128), F32),
            pltpu.VMEM((STATE, INNER), F32),
            pltpu.VMEM((Q, INNER), F32),
            pltpu.VMEM((Q, INNER), F32),
            pltpu.VMEM((128, Q), F32),
        ],
        compiler_params=pltpu.CompilerParams(
            dimension_semantics=("arbitrary",), vmem_limit_bytes=48 * 2**20),
        cost_estimate=pl.CostEstimate(
            flops=30 * 10**9, bytes_accessed=40 * 2**20, transcendentals=10**7),
    )(bound, cot_top, z, proj, gm, norm_gain, e2, et, *params)


def backward_kernel(
    bound_ref, proj_ref, before_ref, dy_ref, through_ref, state_ref, gz_ref, tok_ref, cot_ref,
    in_ref, norm_ref, ggain_ref,
    e_ref, et_ref, convw_ref, convb_ref, dtb_ref, alog_ref, skip_ref,
    window_ref, gtok_ref, small_ref, power_ref,
    total_ref, gskip_ref, gsmall_ref, dtw_ref, gp_ref, ext_ref, dt_ref, lam_ref, dsum_ref, xd_ref, g_ref, gnext_ref, cumt_ref,
):
    step = pl.program_id(0)
    steps = pl.num_programs(0)
    bound = bound_ref[0]
    t0 = (steps - 1 - step) * Q

    @pl.when(step == 0)
    def _():
        lam_ref[...] = jnp.zeros_like(lam_ref)
        dsum_ref[...] = jnp.zeros_like(dsum_ref)
        dt_ref[...] = jnp.zeros_like(dt_ref)
        gnext_ref[Q : Q + 8, :] = jnp.zeros((8, XBC), F32)
        gskip_ref[...] = jnp.zeros_like(gskip_ref)
        total_ref[...] = jnp.zeros_like(total_ref)
        dtw_ref[...] = jnp.zeros_like(dtw_ref)
        gsmall_ref[...] = jnp.zeros_like(gsmall_ref)

    rows, rr, cc = chunk_masks(t0, bound)
    dy = dy_ref[...]
    first_chunk = (t0 > 0).astype(F32)
    ext_ref[0:8, :] = before_ref[:, :XBC] * first_chunk
    ext_ref[8 : 8 + Q, :] = proj_ref[:, :XBC]
    pre = conv_rows(ext_ref, convw_ref, convb_ref, rows, bound)
    sig_pre = sigmoid(pre)
    conv_out = pre * sig_pre
    x = conv_out[:, :INNER]
    b_rows = conv_out[:, INNER : INNER + STATE]
    c_rows = conv_out[:, INNER + STATE :]
    dt_ref[:, 0:HEADS] = proj_ref[:, XBC:LATE]
    dt_in, dt_pos, rate, cum = decay_parts(dt_ref[...], dtb_ref, alog_ref, rr, cc)
    cum_end = cum[Q - 1 : Q, :]
    keep = jnp.logical_or(rows < bound, bound < t0).astype(F32)
    in_last = jnp.logical_or(rows >= bound, bound > t0 + Q - 1).astype(F32)
    whole = jnp.logical_or(bound < t0, bound > t0 + Q - 1).astype(F32)
    from_start = jnp.exp(cum) * keep
    to_end = jnp.exp(cum_end - cum) * in_last
    carry_scale = jnp.exp(cum_end) * whole
    allowed_t = jnp.logical_and(rr <= cc, (cc >= bound) == (rr >= bound))
    cum2 = cum * LOG2E
    cumt_ref[...] = cum2.T
    c_t = c_rows.T
    gram_t = dot(wide_left(b_rows), tall_right(c_t))
    spread = expand(jnp.concatenate(
        [dt_pos, to_end, from_start, jnp.broadcast_to(carry_scale, (16, 128))], axis=0), e_ref)
    dt_all = spread[:Q]
    end_all = spread[Q : 2 * Q]
    xd = x * dt_all
    xd_ref[...] = xd
    skip = skip_ref[...]
    gskip_ref[...] += jnp.sum(dy * x, axis=0, keepdims=True)
    lam = lam_ref[...]
    lam_hi, lam_lo = split2(lam)
    g_ref[...] = (
        dot(wide_left(b_rows), jnp.concatenate([lam_hi, lam_hi, lam_lo], axis=0)) * end_all
    )
    grad_b = quarters(dot_nt(
        jnp.concatenate(split2(xd * end_all), axis=0), jnp.concatenate([lam_hi, lam_lo], axis=0)))
    state = state_ref[0]
    dye_hi, dye_lo = split2(dy * spread[2 * Q : 3 * Q])
    grad_c = quarters(dot_nt(
        jnp.concatenate([dye_hi, dye_lo], axis=0), jnp.concatenate(split2(state), axis=0)))
    lam_new = lam * spread[3 * Q : 3 * Q + 1] + dot(
        wide_left(c_t), jnp.concatenate([dye_hi, dye_hi, dye_lo], axis=0)
    )
    lam_ref[...] = lam_new
    ended = dsum_ref[0:1, :]
    first = iota((Q, Q), 1) < HEADDIM
    first_b = (first.astype(F32).astype(BF16), 1.0 - first.astype(F32).astype(BF16))
    first_row = (iota((Q, Q), 0) < HEADDIM).astype(F32).astype(BF16)
    first_row = (first_row, 1.0 - first_row)
    gram_grad = jnp.zeros((Q, Q), F32)
    for pair in range(PAIRS):
        lanes = slice(pair * 128, pair * 128 + 128)
        weights = []
        for head in (2 * pair, 2 * pair + 1):
            differ = cumt_ref[head : head + 1, :] - cum2[:, head : head + 1]
            weights.append(jnp.exp2(jnp.where(allowed_t, differ, NEG)))
        left = jnp.concatenate([gram_t * weights[0], gram_t * weights[1]], axis=1)
        left = jnp.concatenate(split2(left), axis=0)
        dyp = dy_ref[:, lanes]
        out = dot(left, split_pair(dyp, first_b))
        g_ref[:, lanes] += out[:Q, :128] + (out[:Q, 128:] + out[Q:, :128])
        dyt_hi, dyt_lo = split2(dyp.T)
        right_hi = jnp.concatenate([dyt_hi * first_row[0], dyt_hi * first_row[1]], axis=1)
        right_lo = jnp.concatenate([dyt_lo * first_row[0], dyt_lo * first_row[1]], axis=1)
        outer = dot(
            wide_left(xd_ref[:, lanes]), jnp.concatenate([right_hi, right_hi, right_lo], axis=0))
        gram_grad = gram_grad + (outer[:, :128] * weights[0] + outer[:, 128:] * weights[1])
    g = g_ref[...]
    grad_x = dt_all * g + skip * dy
    sums = dot(jnp.concatenate(
        split2(x * g) + split2(jnp.broadcast_to(
            jnp.sum(lam_new * state, axis=0, keepdims=True), (16, INNER))), axis=0), et_ref[...])
    direct = sums[:Q] + sums[Q : 2 * Q]
    balance = through_ref[...] - dt_pos * direct
    keep_t = allowed_t.astype(F32).astype(BF16)
    b_hi, b_mid, b_lo = split3(balance)
    grad_step = dot(keep_t, b_hi) + dot(keep_t, b_mid) + dot(keep_t, b_lo) + in_last * ended
    dsum_ref[...] = sums[2 * Q : 2 * Q + 8] + sums[2 * Q + 16 : 2 * Q + 24]
    grad_dt = (direct + rate * grad_step) * sigmoid(dt_in)
    gsmall_ref[0:1, :] += jnp.sum(grad_dt, axis=0, keepdims=True)
    gsmall_ref[1:2, :] += rate * jnp.sum(dt_pos * grad_step, axis=0, keepdims=True)
    grad_c = grad_c + dot(wide_left(gram_grad.T), tall_right(b_rows))
    grad_b = grad_b + dot(wide_left(gram_grad), tall_right(c_rows))
    slope = sig_pre * (1.0 + pre * (1.0 - sig_pre))
    gnext_ref[0:Q, :INNER] = grad_x * slope[:, :INNER]
    gnext_ref[0:Q, INNER : INNER + STATE] = grad_b * slope[:, INNER : INNER + STATE]
    gnext_ref[0:Q, INNER + STATE :] = grad_c * slope[:, INNER + STATE :]
    gcp = gnext_ref[0:Q, :]
    total_ref[4:5, :] += jnp.sum(gcp, axis=0, keepdims=True)
    total_ref[3:4, :] += jnp.sum(gcp * ext_ref[8 : 8 + Q, :], axis=0, keepdims=True)
    total = convw_ref[3:4, :] * gcp
    for back in (1, 2, 3):
        ok = jnp.logical_or(rows - back >= bound, rows < bound).astype(F32)
        total_ref[3 - back : 4 - back, :] += jnp.sum(
            gcp * (ext_ref[8 - back : 8 - back + Q, :] * ok), axis=0, keepdims=True)
        okn = jnp.logical_or(rows >= bound, rows + back < bound).astype(F32)
        total = total + convw_ref[3 - back : 4 - back, :] * (gnext_ref[back : back + Q, :] * okn)
    total_ref[7:8, :] = jnp.maximum(
        total_ref[7:8, :], jnp.max(jnp.abs(total), axis=0, keepdims=True))
    total = total.astype(BF16)
    window_ref[0] = total[:, :WINDOW]
    window_ref[1] = total[:, XBC - WINDOW :]
    gnext_ref[Q : Q + 8, :] = gnext_ref[0:8, :]
    half = (steps - 1 - step) % 2
    at = pl.multiple_of(half * Q, Q)
    gp_ref[pl.ds(at, Q), :INNER] = gz_ref[0]
    gp_ref[pl.ds(at, Q), INNER : INNER + XBC] = total
    gp_ref[pl.ds(at, Q), INNER + XBC :] = grad_dt.astype(BF16)

    @pl.when(half == 0)
    def _():
        grad_normed = dot(gp_ref[...], in_ref[: INNER + XBC + 128, :])
        tok = tok_ref[...].astype(F32)
        rinv = lax.rsqrt(jnp.mean(tok * tok, axis=1, keepdims=True) + EPS_NORM)
        nhat = tok * rinv
        gain = norm_ref[...]
        gng = grad_normed * gain
        gtok_ref[...] = (cot_ref[...].astype(F32) + rinv * (
            gng - nhat * jnp.mean(nhat * gng, axis=1, keepdims=True))).astype(BF16)
        total_ref[6:7, :D] += jnp.sum(nhat * grad_normed, axis=0, keepdims=True)
        normed = (nhat * gain).astype(BF16)
        gdt = gp_ref[:, INNER + XBC :].astype(F32)
        dtw_ref[...] += dot(jnp.concatenate(
            [gdt[:Q].T, gdt[Q:].T], axis=1).astype(BF16), normed)

    @pl.when(step == steps - 1)
    def _():
        skips = head_sum(jnp.broadcast_to(gskip_ref[...], (8, INNER)), et_ref)
        small_ref[...] = jnp.zeros_like(small_ref)
        small_ref[0:HEADS, :] = dtw_ref[0:HEADS, :]
        pieces = [
            total_ref[k : k + 1, j * 128 : j * 128 + 128]
            for k in range(CONV + 1) for j in range(XBC // 128)]
        pieces += [gsmall_ref[0:1, :], gsmall_ref[1:2, :], skips[0:1, :]]
        pieces += [ggain_ref[:, j * 128 : j * 128 + 128] for j in range(INNER // 128)]
        lines = D // 128
        for number, piece in enumerate(pieces):
            line = HEADS + number // lines
            at = number % lines * 128
            small_ref[line : line + 1, at : at + 128] = piece
        small_ref[40:41, :] = total_ref[6:7, :D]
        count = float(Q * steps)
        largest = jnp.max(total_ref[7:8, :], axis=1, keepdims=True)
        normed = jnp.max(jnp.abs(norm_ref[...]), axis=1, keepdims=True) * (D ** 0.5)
        others = jnp.max(jnp.max(jnp.abs(small_ref[...]), axis=1, keepdims=True), axis=0, keepdims=True)
        power_ref[...] = jnp.broadcast_to(power_for(
            jnp.maximum(1.05 * count * largest * normed, others)), (8, 128))


def run_backward(
    proj, dy, through, states, pair, tok, cot, in_w, norm_gain, ggain, bound, e2, et, params
):
    n = proj.shape[0]
    steps = n // Q

    def rev(i):
        return (steps - 1 - i, 0)

    def rev_two(i):
        return ((steps - 1 - i) // 2, 0)

    return pl.pallas_call(
        backward_kernel,
        grid=(steps,),
        in_specs=[
            pl.BlockSpec(memory_space=pltpu.SMEM),
            pl.BlockSpec((Q, LATE), rev),
            pl.BlockSpec((8, LATE), lambda i: (jnp.maximum((steps - 1 - i) * (Q // 8) - 1, 0), 0)),
            pl.BlockSpec((Q, INNER), rev),
            pl.BlockSpec((Q, 128), rev),
            pl.BlockSpec((1, STATE, INNER), lambda i: (steps - 1 - i, 0, 0)),
            pl.BlockSpec((1, Q, INNER), lambda i: (0, steps - 1 - i, 0)),
            pl.BlockSpec((2 * Q, D), rev_two), pl.BlockSpec((2 * Q, D), rev_two),
            const_spec(in_w.shape), const_spec((1, D)), const_spec((1, INNER)),
            const_spec((256, INNER)), const_spec((INNER, 128)),
            const_spec((8, XBC)), const_spec((1, XBC)), const_spec((1, 128)),
            const_spec((1, 128)), const_spec((1, INNER)),
        ],
        out_specs=[
            pl.BlockSpec((2, Q, WINDOW), lambda i: (0, steps - 1 - i, 0)),
            pl.BlockSpec((2 * Q, D), rev_two),
            const_spec((48, D)), const_spec((8, 128)),
        ],
        out_shape=[
            jax.ShapeDtypeStruct((2, n, WINDOW), BF16),
            jax.ShapeDtypeStruct((n, D), BF16),
            jax.ShapeDtypeStruct((48, D), F32),
            jax.ShapeDtypeStruct((8, 128), F32),
        ],
        scratch_shapes=[
            pltpu.VMEM((8, XBC), F32),
            pltpu.VMEM((1, INNER), F32),
            pltpu.VMEM((8, 128), F32),
            pltpu.VMEM((128, D), F32),
            pltpu.VMEM((2 * Q, INNER + XBC + 128), BF16),
            pltpu.VMEM((Q + 8, XBC), F32),
            pltpu.VMEM((Q, 128), F32),
            pltpu.VMEM((STATE, INNER), F32),
            pltpu.VMEM((8, 128), F32),
            pltpu.VMEM((Q, INNER), F32),
            pltpu.VMEM((Q, INNER), F32),
            pltpu.VMEM((Q + 8, XBC), F32),
            pltpu.VMEM((128, Q), F32),
        ],
        compiler_params=pltpu.CompilerParams(
            dimension_semantics=("arbitrary",), vmem_limit_bytes=48 * 2**20),
        cost_estimate=pl.CostEstimate(
            flops=50 * 10**9, bytes_accessed=50 * 2**20, transcendentals=2 * 10**7),
    )(bound, proj, proj, dy, through, states, pair, tok, cot, in_w, norm_gain, ggain,
      e2, et, *params[:5])


BETA_ONE = 0.9
BETA_TWO = 0.95
EPS_ADAM = 1e-08
LANES = 128
NORM_ROWS = D // LANES
IN_ROWS = PROJ * D // LANES
CONVW_ROWS = CONV * XBC // LANES
CONVB_ROWS = XBC // LANES
GAIN_ROWS = INNER // LANES
OUT_ROWS = INNER * D // LANES
DT_ROWS = HEADS * D // LANES
SMALL_ROWS = DT_ROWS + CONVW_ROWS + CONVB_ROWS + 3 + GAIN_ROWS
OUT_START = NORM_ROWS + IN_ROWS + SMALL_ROWS - DT_ROWS
LATE_START = NORM_ROWS + INNER * NORM_ROWS
LEAD = 896
STAGE_ROWS = 16264
STAGE_BLOCKS = 5
MARK = 16


PREP_STEPS = 7
IN_BLOCK = 512
OUT_BLOCK = 256
SMALL_START = NORM_ROWS + IN_ROWS


def prepare_kernel(
    flat_ref,
    in_ref, out_ref, norm_ref, convw_ref, convb_ref, dtb_ref, alog_ref, skip_ref, gain_ref,
    e_ref, et_ref,
    stage_ref,
):
    step = pl.program_id(0)

    @pl.when(step == 0)
    def _():
        rows = flat_ref[0:16, :].astype(F32)
        for lane in range(NORM_ROWS):
            norm_ref[:, lane * LANES : lane * LANES + LANES] = rows[lane : lane + 1, :]
        low = SMALL_START // 16 * 16
        stage_ref[0:112, :] = flat_ref[low : low + 112, :].astype(F32)
        at = SMALL_START - low
        convw_ref[...] = jnp.zeros_like(convw_ref)
        for tap in range(CONV):
            for lane in range(CONVB_ROWS):
                convw_ref[tap : tap + 1, lane * LANES : lane * LANES + LANES] = stage_ref[
                    at : at + 1, :]
                at += 1
        for lane in range(CONVB_ROWS):
            convb_ref[:, lane * LANES : lane * LANES + LANES] = stage_ref[at : at + 1, :]
            at += 1
        heads = iota((1, LANES), 1) < HEADS
        dtb_ref[...] = jnp.where(heads, stage_ref[at : at + 1, :], 0.0)
        alog_ref[...] = jnp.where(heads, stage_ref[at + 1 : at + 2, :], 0.0)
        skips = jnp.where(heads, stage_ref[at + 2 : at + 3, :], 0.0)
        at += 3
        for lane in range(GAIN_ROWS):
            gain_ref[:, lane * LANES : lane * LANES + LANES] = stage_ref[at : at + 1, :]
            at += 1
        one = (iota((128, INNER), 1) // HEADDIM == iota((128, INNER), 0)).astype(F32).astype(BF16)
        e_ref[0:128, :] = one
        e_ref[128:256, :] = one
        et_ref[...] = (
            iota((INNER, 128), 0) // HEADDIM == iota((INNER, 128), 1)).astype(F32).astype(BF16)
        skip_ref[...] = dot(jnp.broadcast_to(skips, (16, LANES)).astype(BF16), one)[0:1, :]

    def block(start, offset, rows, dest_ref):
        size = rows * NORM_ROWS + 16
        at = pl.multiple_of(start + step * (rows * NORM_ROWS), 16)
        stage_ref[0:size, :] = flat_ref[pl.ds(at, size), :].astype(F32)
        for lane in range(NORM_ROWS):
            dest_ref[:, lane * LANES : lane * LANES + LANES] = stage_ref[
                pl.ds(offset + lane, rows, stride=NORM_ROWS), :].astype(BF16)

    block(0, NORM_ROWS, IN_BLOCK, in_ref)

    @pl.when(step == PREP_STEPS - 1)
    def _():
        used = PROJ - (PREP_STEPS - 1) * IN_BLOCK
        in_ref[used:, :] = jnp.zeros((IN_BLOCK - used, D), BF16)

    @pl.when(step < INNER // OUT_BLOCK)
    def _():
        low = OUT_START // 16 * 16
        block(low, OUT_START - low, OUT_BLOCK, out_ref)


def run_prepare(flat):
    vector = lambda n: jax.ShapeDtypeStruct((1, n), F32)
    return pl.pallas_call(
        prepare_kernel,
        grid=(PREP_STEPS,),
        in_specs=[const_spec(flat.shape)],
        out_specs=[
            pl.BlockSpec((IN_BLOCK, D), lambda i: (i, 0)),
            pl.BlockSpec((OUT_BLOCK, D), lambda i: (jnp.minimum(i, INNER // OUT_BLOCK - 1), 0)),
            const_spec((1, D)), const_spec((8, XBC)), const_spec((1, XBC)), const_spec((1, 128)),
            const_spec((1, 128)), const_spec((1, INNER)), const_spec((1, INNER)),
            const_spec((256, INNER)), const_spec((INNER, 128)),
        ],
        out_shape=[
            jax.ShapeDtypeStruct((PREP_STEPS * IN_BLOCK, D), BF16),
            jax.ShapeDtypeStruct((INNER, D), BF16),
            vector(D), jax.ShapeDtypeStruct((8, XBC), F32), vector(XBC), vector(128), vector(128),
            vector(INNER), vector(INNER),
            jax.ShapeDtypeStruct((256, INNER), BF16), jax.ShapeDtypeStruct((INNER, 128), BF16),
        ],
        scratch_shapes=[pltpu.VMEM((IN_BLOCK * NORM_ROWS + 16, LANES), F32)],
        compiler_params=pltpu.CompilerParams(
            dimension_semantics=("arbitrary",), vmem_limit_bytes=40 * 2**20),
        cost_estimate=pl.CostEstimate(
            flops=10**9, bytes_accessed=16 * 2**20, transcendentals=0),
    )(flat)


def stage_kernel(
    who_ref, early_ref, early_other_ref, late_ref, late_other_ref, small_ref,
    grad_ref,
    stage_ref,
):
    step = pl.program_id(0)
    upper = who_ref[0]
    mine = who_ref[1]
    block = grad_ref.shape[0]
    half = 2 * block * STAGE_BLOCKS

    @pl.when(step == 0)
    def _():
        early_at = LEAD + jnp.where(upper == 1, OUT_START - half, NORM_ROWS)
        window = LATE_START + (XBC - WINDOW) * NORM_ROWS
        late_at = LEAD + jnp.where(upper == 1, window - half, LATE_START)
        def lay(source_ref, start, size):
            for lane in range(NORM_ROWS):
                stage_ref[pl.ds(start + lane, size, stride=NORM_ROWS), :] = source_ref[
                    0:size, lane * LANES : lane * LANES + LANES]

        lines = late_ref.shape[0]
        lay(late_ref, late_at + mine * (lines * NORM_ROWS), lines)
        lay(late_other_ref, late_at + (1 - mine) * (lines * NORM_ROWS), lines)

        @pl.when(upper == 1)
        def _():
            lay(small_ref, LEAD + OUT_START - half - SMALL_ROWS, -(-SMALL_ROWS // NORM_ROWS))

        lines = early_ref.shape[0]
        lay(early_ref, early_at + mine * (lines * NORM_ROWS), lines)
        lay(early_other_ref, early_at + (1 - mine) * (lines * NORM_ROWS), lines)

        @pl.when(upper == 0)
        def _():
            for lane in range(NORM_ROWS):
                stage_ref[LEAD + lane : LEAD + lane + 1, :] = small_ref[
                    40:41, lane * LANES : lane * LANES + LANES]

        @pl.when(upper == 1)
        def _():
            at = LEAD + OUT_START + OUT_ROWS - half
            stage_ref[at : LEAD + half, :] = jnp.zeros((LEAD + half - at, LANES), F32)

    @pl.when(step > 0)
    def _():
        at = LEAD + mine * (half // 2) + (step - 1) * block
        grad_ref[...] = stage_ref[pl.ds(pl.multiple_of(at, 8), block), :]


def run_stage(who, rows, early, early_other, late, late_other, small):
    block = rows // STAGE_BLOCKS
    return pl.pallas_call(
        stage_kernel,
        grid=(STAGE_BLOCKS + 1,),
        in_specs=[
            pl.BlockSpec(memory_space=pltpu.SMEM),
            const_spec(early.shape), const_spec(early.shape),
            const_spec(late.shape), const_spec(late.shape), const_spec(small.shape),
        ],
        out_specs=pl.BlockSpec((block, LANES), lambda i: (jnp.maximum(i - 1, 0), 0)),
        out_shape=jax.ShapeDtypeStruct((rows, LANES), F32),
        scratch_shapes=[pltpu.VMEM((STAGE_ROWS, LANES), F32)],
        compiler_params=pltpu.CompilerParams(
            dimension_semantics=("arbitrary",), vmem_limit_bytes=48 * 2**20),
        cost_estimate=pl.CostEstimate(
            flops=10**6, bytes_accessed=12 * 2**20, transcendentals=0),
    )(who, early, early_other, late, late_other, small)


def swap(values, axis, bit):
    size = lax.axis_size(axis)
    return lax.ppermute(values, axis, [(i, i ^ bit) for i in range(size)])


def to_wire(values, power):
    return (values * jnp.exp2(power)).astype(jnp.float16)


def from_wire(values, power):
    return values.astype(F32) * jnp.exp2(-power)


def scatter(values, power, axis, bit=1, count=2):
    place = (lax.axis_index(axis) // bit) % count
    rows = values.shape[-2] // count
    mark = min(MARK, rows)
    dim = values.ndim - 2
    total = lax.dynamic_slice_in_dim(values, place * rows, rows, dim)
    least = power
    for offset in range(1, count):
        to = place ^ offset
        last = to == count - 1
        start = to * rows - jnp.where(last, mark, 0)
        send = lax.dynamic_slice_in_dim(values, start, rows + mark, dim)
        line = lax.broadcasted_iota(jnp.int32, send.shape, dim)
        marked = jnp.where(last, line < mark, line >= rows)
        wire = jnp.where(marked, power, send * jnp.exp2(power)).astype(jnp.float16)
        got = swap(wire, axis, bit * offset)
        last = place == count - 1
        got_power = lax.dynamic_slice_in_dim(got, jnp.where(last, 0, rows), 1, dim)
        got_power = got_power.reshape(-1, D)[0:1, 0:1].astype(F32)
        body = lax.dynamic_slice_in_dim(got, jnp.where(last, mark, 0), rows, dim)
        total = total + from_wire(body, got_power)
        least = jnp.minimum(least, got_power)
    return total, least - float(count.bit_length() - 1)


def everyones(values, axis, bit=1, count=2):
    place = (lax.axis_index(axis) // bit) % count
    pieces = [values] + [swap(values, axis, bit * offset) for offset in range(1, count)]
    step = 1
    while step < count:
        flip = (place // step) % 2 == 1
        pieces = [
            jnp.where(flip, pieces[i ^ step], pieces[i]) for i in range(count)]
        step *= 2
    return pieces


def gather(values, axis, bit=1, count=2):
    return jnp.concatenate(everyones(values, axis, bit, count))


def add_pair(values, axis, bit):
    return values + swap(values, axis, bit)


def data_groups():
    size = lax.axis_size("dp")
    groups = [(1, 2)]
    bit = 2
    while bit < size:
        count = 4 if bit * 4 <= size else 2
        groups.append((bit, count))
        bit *= count
    return groups


def dot_tn(a, b):
    return lax.dot_general(a, b, (((0,), (0,)), ((), ())), preferred_element_type=F32)


def pick_rows(index, rows):
    chosen = index[:, None] == jnp.arange(rows.shape[0], dtype=jnp.int32)[None, :]
    return dot(chosen.astype(BF16), rows).astype(BF16)


def on_device(
    tokens, loss_sensitivity, lengths, holder_sequence_list, master, moment_one, moment_two,
    adam_rates, iteration_tally,
):
    group_devices = lax.axis_size("zero")
    data_devices = lax.axis_size("dp")
    zero_index = lax.axis_index("zero")
    dp_index = lax.axis_index("dp")
    seq_len = loss_sensitivity.shape[1]
    group_seqs = tokens.shape[0]
    span = tokens.shape[1]
    slots = group_seqs // data_devices
    shard_rows = master.shape[0] // LANES
    tie = lax.optimization_barrier

    own = master.reshape(shard_rows, LANES)
    arranged = holder_sequence_list.reshape(data_devices, group_devices, slots)
    group_order = lax.dynamic_index_in_dim(arranged, zero_index, 1, keepdims=False).reshape(-1)
    local_ids = group_order - zero_index * group_seqs
    dealt = tokens.at[local_ids].get(mode="promise_in_bounds")
    flat = lax.all_gather(own.astype(BF16), "zero", axis=0, tiled=True)

    local_tok = lax.all_to_all(dealt, "dp", split_axis=0, concat_axis=0, tiled=True)
    my_seqs = lax.dynamic_slice_in_dim(group_order, dp_index * slots, slots)
    bound = lengths[my_seqs[0]]
    positions = jnp.arange(seq_len, dtype=jnp.int32)

    in_w, out_w, norm_gain, *params, e2, et = run_prepare(flat)
    cot = loss_sensitivity[0]
    gm = dot_nt(cot, out_w)
    cot_top = jnp.max(jnp.abs(cot)).astype(F32).reshape(1)
    local_tok, in_w, gm, cot_top = tie((local_tok, in_w, gm, cot_top))
    own_late, _ = tie((own, flat[:8]))
    whole_master = lax.all_gather(own_late, "zero", axis=0, tiled=True)

    def place(slot, at):
        return (at // span) * (slots * span) + slot * span + at % span

    source = jnp.where(positions < bound, place(0, positions), place(1, positions - bound))
    packed = pick_rows(source, local_tok.reshape(slots * seq_len, D))
    blocks = jnp.arange(data_devices, dtype=jnp.int32)[:, None, None] * span
    within = blocks + jnp.arange(span, dtype=jnp.int32)[None, None, :]
    within = within + jnp.arange(slots, dtype=jnp.int32)[None, :, None] * bound
    unpack_rows = jnp.minimum(within, seq_len - 1).reshape(-1)

    def spread(rows):
        return pick_rows(unpack_rows, rows).reshape(data_devices * slots, span, D)

    def send_back(picked):
        return lax.all_to_all(picked, "dp", split_axis=0, concat_axis=0, tiled=True)

    restore = jnp.zeros_like(local_ids).at[local_ids].set(
        jnp.arange(group_seqs, dtype=jnp.int32))
    mine = lax.dynamic_slice_in_dim(lengths, zero_index * group_seqs, group_seqs)
    at = dp_index * span + jnp.arange(span, dtype=jnp.int32)
    live = (at[None, :] < mine[:, None])[:, :, None]

    bound_arr = bound.reshape(1)
    tok = packed.astype(F32)
    nhat = tok * lax.rsqrt(jnp.mean(tok * tok, axis=1, keepdims=True) + EPS_NORM)
    normed = (nhat * norm_gain).astype(BF16)
    proj_z = dot_nt(normed, in_w[:INNER])
    proj = dot_nt(normed, in_w[INNER:PROJ])
    pair, dy, through, states, ggain, early_power = run_forward(
        proj_z, proj, gm, bound_arr, cot_top, norm_gain, e2, et, params)
    result = (tok + dot(pair[1], out_w)).astype(BF16)
    picked = spread(result)
    picked, pair = tie((picked, pair))
    back_out = send_back(picked)
    early_power = early_power[0:1, 0:1]
    early = lax.dot_general(
        pair, jnp.stack([normed, cot]), (((1,), (1,)), ((0,), (0,))), preferred_element_type=F32)
    early, early_power = scatter(early, early_power, "zero", 1)
    early, early_power, dy = tie((early.reshape(INNER, D), early_power, dy))
    early, early_power = scatter(early, early_power, "zero", 2)
    window, grad_tok, small, late_power = run_backward(
        proj, dy, through, states, pair, packed, cot, in_w, norm_gain, ggain,
        bound_arr, e2, et, params)
    window, small, late_power, back_out, early, early_power, whole_master = tie(
        (window, small, late_power, back_out, early, early_power, whole_master))

    groups = data_groups()
    late = lax.dot_general(
        window, jnp.stack([normed, normed]), (((1,), (1,)), ((0,), (0,))),
        preferred_element_type=F32)
    late_power = late_power[0:1, 0:1]
    late, late_power = scatter(late, late_power, "zero", 1)
    late = late.reshape(WINDOW, D)
    early, early_power = scatter(early, early_power, "dp", *groups[0])
    small = add_pair(small, "zero", 1)
    early, early_power, grad_tok, _ = tie((early, early_power, grad_tok, late))
    late, late_power = scatter(late, late_power, "zero", 2)
    small = add_pair(small, "zero", 2)
    for group in groups[1:]:
        early, early_power = scatter(early, early_power, "dp", *group)
    early = to_wire(early, early_power)
    picked_grad = spread(grad_tok)
    lines = small.shape[0]
    late = jnp.concatenate([late, small, jnp.zeros((WINDOW // 8 - lines, D), F32)])
    early, _ = tie((early, late))
    late, late_power = scatter(late, late_power, "dp", *groups[0])
    for group in reversed(groups[1:]):
        early = gather(early, "dp", *group)
    early, _ = tie((early, late))
    for group in groups[1:]:
        late, late_power = scatter(late, late_power, "dp", *group)
    late = to_wire(late, late_power)
    early = from_wire(gather(early, "dp", *groups[0]), early_power)
    early, picked_grad, _ = tie((early, picked_grad, late))
    for group in reversed(groups[1:]):
        late = gather(late, "dp", *group)
    early_other = swap(early, "zero", 1)
    back_grad = send_back(picked_grad)
    wire = gather(late, "dp", *groups[0])
    late = from_wire(wire[: WINDOW // 2], late_power)
    small = from_wire(wire[WINDOW // 2 : WINDOW // 2 + lines], late_power)
    late_other = swap(late, "zero", 1)

    steps_f = iteration_tally[0].astype(F32)
    who = jnp.stack([zero_index // 2, zero_index % 2]).astype(jnp.int32)
    first = moment_one.reshape(shard_rows, LANES)
    second = moment_two.reshape(shard_rows, LANES)
    grad_shard = run_stage(who, shard_rows, early, early_other, late, late_other, small)
    first_scale = 1.0 / (1.0 - jnp.power(BETA_ONE, steps_f))
    second_scale = 1.0 / (1.0 - jnp.power(BETA_TWO, steps_f))

    def moments(grad, first, second):
        return (
            BETA_ONE * first + (1.0 - BETA_ONE) * grad,
            BETA_TWO * second + (1.0 - BETA_TWO) * grad * grad)

    def quotient(rows):
        first_next, second_next = moments(grad_shard[rows], first[rows], second[rows])
        return ((first_next * first_scale) / (
            jnp.sqrt(second_next * second_scale) + EPS_ADAM)).astype(jnp.float16)

    part = shard_rows // 2
    whole_master = whole_master.reshape(2 * group_devices, part, LANES)
    new_master = jnp.zeros((2 * group_devices, part, LANES), F32)

    def put(new_master, piece, offset, half):
        place = 2 * (zero_index ^ offset) + half
        old = lax.dynamic_index_in_dim(whole_master, place, 0, keepdims=False)
        new = old - adam_rates[0] * (piece.astype(F32) + adam_rates[1] * old)
        return lax.dynamic_update_index_in_dim(new_master, new, place, 0)

    front = quotient(slice(0, part))
    front, grad_late, back_out = tie((front, grad_shard, back_out))
    front_across = swap(front, "zero", 2)
    grad_shard = grad_late
    back = quotient(slice(part, shard_rows))
    back, grad_shard, new_master = tie((back, grad_shard, new_master))
    back_across = swap(back, "zero", 2)
    front_core = swap(front, "zero", 1)
    back_core = swap(back, "zero", 1)
    first_next, second_next = moments(grad_shard, first, second)
    back_rows = back_out.at[restore].get(mode="promise_in_bounds")
    tokens_out = jnp.where(live, back_rows, tokens)
    new_master = put(put(new_master, front, 0, 0), front_core, 1, 0)
    front_across, new_master, tokens_out, first_next, second_next = tie(
        (front_across, new_master, tokens_out, first_next, second_next))
    front_last = swap(front_across, "zero", 1)
    new_master = put(put(new_master, back, 0, 1), back_core, 1, 1)
    new_master = put(put(new_master, front_across, 2, 0), front_last, 3, 0)
    back_across, new_master = tie((back_across, new_master))
    back_last = swap(back_across, "zero", 1)
    new_master = put(new_master, back_across, 2, 1)
    back_last, new_master = tie((back_last, new_master))
    new_master = put(new_master, back_last, 3, 1)
    back_grad, new_master = tie((back_grad, new_master))
    grad_tokens = jnp.where(
        live, back_grad.at[restore].get(mode="promise_in_bounds"), jnp.zeros((), BF16))
    return (
        tokens_out, grad_tokens, new_master.reshape(-1), grad_shard.reshape(-1),
        first_next.reshape(-1), second_next.reshape(-1))


def solution(mesh):
    return jax.shard_map(
        on_device,
        mesh=mesh,
        in_specs=(
            P("zero", "dp", None), P(("dp", "zero"), None, None), P(), P(),
            P("zero"), P("zero"), P("zero"), P(), P(),
        ),
        out_specs=(
            P("zero", "dp", None), P("zero", "dp", None), P(), P("zero"), P("zero"), P("zero"),
        ),
        check_vma=False,
    )
```

```python
import jax
import jax.numpy as jnp
from jax import lax
from jax.experimental import pallas as pl
from jax.experimental.pallas import tpu as pltpu
from jax.sharding import PartitionSpec as P

D = 768
HEADS = 24
HEADDIM = 64
STATE = 128
CONV = 4
INNER = 1536
XBC = 1792
PROJ = 3352
Q = 128
LATE = PROJ - INNER
WINDOW = 1024
PAIRS = HEADS // 2
EPS_NORM = 1e-05
NEG = -1e30
F16_TOP = 30000.0
LOG2E = 1.4426950408889634
F32 = jnp.float32
BF16 = jnp.bfloat16


def dot(a, b):
    return lax.dot_general(a, b, (((1,), (0,)), ((), ())), preferred_element_type=F32)


def dot_nt(a, b):
    return lax.dot_general(a, b, (((1,), (1,)), ((), ())), preferred_element_type=F32)


def split2(v):
    hi = v.astype(BF16)
    return hi, (v - hi.astype(F32)).astype(BF16)


def split3(v):
    hi = v.astype(BF16)
    rest = v - hi.astype(F32)
    mid = rest.astype(BF16)
    return hi, mid, (rest - mid.astype(F32)).astype(BF16)


def wide_left(v):
    hi, lo = split2(v)
    return jnp.concatenate([hi, lo, hi], axis=1)


def tall_right(v):
    hi, lo = split2(v)
    return jnp.concatenate([hi, hi, lo], axis=0)


def split_pair(v, masks):
    hi, lo = split2(v)
    return jnp.concatenate([
        jnp.concatenate([hi * masks[0], lo * masks[0]], axis=1),
        jnp.concatenate([hi * masks[1], lo * masks[1]], axis=1)], axis=0)


def sigmoid(v):
    return lax.logistic(v)


def softplus(v):
    return jnp.maximum(v, 0.0) + jnp.log1p(jnp.exp(-jnp.abs(v)))


def iota(shape, dim):
    return lax.broadcasted_iota(jnp.int32, shape, dim)


def expand(v, e_ref):
    hi, lo = split2(v)
    return dot(jnp.concatenate([hi, lo], axis=1), e_ref[...])


def head_sum(v, et_ref):
    hi, lo = split2(v)
    return dot(hi, et_ref[...]) + dot(lo, et_ref[...])


def quarters(out):
    return out[:Q, :Q] + (out[:Q, Q:] + out[Q:, :Q])


def power_for(bound):
    scale = jnp.log(0.9 * F16_TOP / jnp.maximum(bound, 1e-30)) * LOG2E
    return jnp.clip(jnp.floor(scale), -126.0, 120.0)


def chunk_masks(t0, bound):
    rows = t0 + iota((Q, 1), 0)
    rr = t0 + iota((Q, Q), 0)
    cc = t0 + iota((Q, Q), 1)
    return rows, rr, cc


def conv_rows(ext_ref, w_ref, b_ref, rows, bound):
    total = b_ref[...] + w_ref[3:4, :] * ext_ref[8 : 8 + Q, :]
    for back in (1, 2, 3):
        ok = jnp.logical_or(rows - back >= bound, rows < bound).astype(F32)
        total = total + w_ref[3 - back : 4 - back, :] * (ext_ref[8 - back : 8 - back + Q, :] * ok)
    return total


def decay_parts(dt_raw, dtb_ref, alog_ref, rr, cc):
    dt_in = dt_raw + dtb_ref[...]
    dt_pos = softplus(dt_in)
    rate = -jnp.exp(alog_ref[...])
    step = dt_pos * rate
    tri = (cc <= rr).astype(F32).astype(BF16)
    s_hi, s_mid, s_lo = split3(step)
    cum = dot(tri, s_hi) + dot(tri, s_mid) + dot(tri, s_lo)
    return dt_in, dt_pos, rate, cum


def forward_kernel(
    bound_ref, cot_ref, z_ref, proj_ref, gm_ref, norm_ref, e_ref, et_ref, convw_ref, convb_ref, dtb_ref, alog_ref,
    skip_ref, gain_ref,
    pair_ref, dy_ref, through_ref, state_ref, ggain_ref, power_ref,
    zmax_ref, ext_ref, dt_ref, carry_ref, xd_ref, acc_ref, cumt_ref,
):
    step = pl.program_id(0)
    bound = bound_ref[0]
    t0 = step * Q

    @pl.when(step == 0)
    def _():
        ext_ref[0:8, :] = jnp.zeros((8, XBC), F32)
        carry_ref[...] = jnp.zeros_like(carry_ref)
        dt_ref[...] = jnp.zeros_like(dt_ref)
        ggain_ref[...] = jnp.zeros_like(ggain_ref)
        zmax_ref[...] = jnp.zeros_like(zmax_ref)

    rows, rr, cc = chunk_masks(t0, bound)
    ext_ref[8 : 8 + Q, :] = proj_ref[:, :XBC]
    pre = conv_rows(ext_ref, convw_ref, convb_ref, rows, bound)
    ext_ref[0:8, :] = ext_ref[Q : Q + 8, :]
    conv_out = pre * sigmoid(pre)
    x = conv_out[:, :INNER]
    b_rows = conv_out[:, INNER : INNER + STATE]
    c_rows = conv_out[:, INNER + STATE :]
    dt_ref[:, 0:HEADS] = proj_ref[:, XBC:LATE]
    _, dt_pos, _, cum = decay_parts(dt_ref[...], dtb_ref, alog_ref, rr, cc)
    cum_end = cum[Q - 1 : Q, :]
    keep = jnp.logical_or(rows < bound, bound < t0).astype(F32)
    in_last = jnp.logical_or(rows >= bound, bound > t0 + Q - 1).astype(F32)
    whole = jnp.logical_or(bound < t0, bound > t0 + Q - 1).astype(F32)
    from_start = jnp.exp(cum) * keep
    to_end = jnp.exp(cum_end - cum) * in_last
    carry_scale = jnp.exp(cum_end) * whole
    allowed = jnp.logical_and(cc <= rr, (cc >= bound) == (rr >= bound))
    cum2 = cum * LOG2E
    cumt_ref[...] = cum2.T

    state = carry_ref[...]
    state_ref[0] = state
    spread = expand(jnp.concatenate(
        [dt_pos, to_end, from_start, jnp.broadcast_to(carry_scale, (16, 128))], axis=0), e_ref)
    xd = x * spread[:Q]
    xd_ref[...] = xd
    acc = dot(wide_left(c_rows), tall_right(state)) * spread[2 * Q : 3 * Q]
    acc_ref[...] = acc + skip_ref[...] * x
    b_t = b_rows.T
    carry_ref[...] = state * spread[3 * Q : 3 * Q + 1] + dot(
        wide_left(b_t), tall_right(xd * spread[Q : 2 * Q]))
    gram = dot(wide_left(c_rows), tall_right(b_t))
    first = iota((Q, Q), 1) < HEADDIM
    first_b = (first.astype(F32).astype(BF16), 1.0 - first.astype(F32).astype(BF16))
    for pair in range(PAIRS):
        parts = []
        for head in (2 * pair, 2 * pair + 1):
            differ = cum2[:, head : head + 1] - cumt_ref[head : head + 1, :]
            parts.append(gram * jnp.exp2(jnp.where(allowed, differ, NEG)))
        left = jnp.concatenate(split2(jnp.concatenate(parts, axis=1)), axis=0)
        lanes = slice(pair * 128, pair * 128 + 128)
        xp = xd_ref[:, lanes]
        out = dot(left, split_pair(xp, first_b))
        acc_ref[:, lanes] += out[:Q, :128] + (out[:Q, 128:] + out[Q:, :128])
    scanned = acc_ref[...]
    z = z_ref[...]
    sig_z = sigmoid(z)
    silu_z = z * sig_z
    gated = scanned * silu_z
    ginv = lax.rsqrt(jnp.mean(gated * gated, axis=1, keepdims=True) + EPS_NORM)
    mhat = gated * ginv
    pair_ref[1] = (mhat * gain_ref[...]).astype(BF16)
    gm = gm_ref[...]
    ggain_ref[...] += jnp.sum(mhat * gm, axis=0, keepdims=True)
    gmg = gm * gain_ref[...]
    ggated = ginv * (gmg - mhat * jnp.mean(mhat * gmg, axis=1, keepdims=True))
    dy = ggated * silu_z
    dy_ref[...] = dy
    grad_z = ggated * scanned * (sig_z * (1.0 + z * (1.0 - sig_z)))
    zmax_ref[...] = jnp.maximum(zmax_ref[...], jnp.max(jnp.abs(grad_z), axis=0, keepdims=True))
    pair_ref[0] = grad_z.astype(BF16)
    through_ref[...] = head_sum(dy * (scanned - skip_ref[...] * x), et_ref)

    @pl.when(step == pl.num_programs(0) - 1)
    def _():
        count = float(Q * pl.num_programs(0))
        largest = jnp.max(zmax_ref[...], axis=1, keepdims=True)
        normed = jnp.max(jnp.abs(norm_ref[...]), axis=1, keepdims=True) * (D ** 0.5)
        mixed = jnp.max(jnp.abs(gain_ref[...]), axis=1, keepdims=True) * (INNER ** 0.5)
        power_ref[...] = jnp.broadcast_to(power_for(
            1.05 * count * jnp.maximum(largest * normed, cot_ref[0] * mixed)), (8, 128))


def const_spec(shape):
    return pl.BlockSpec(shape, lambda *_: (0,) * len(shape))


def run_forward(z, proj, gm, bound, cot_top, norm_gain, e2, et, params):
    n = proj.shape[0]
    steps = n // Q
    return pl.pallas_call(
        forward_kernel,
        grid=(steps,),
        in_specs=[
            pl.BlockSpec(memory_space=pltpu.SMEM), pl.BlockSpec(memory_space=pltpu.SMEM),
            pl.BlockSpec((Q, INNER), lambda i: (i, 0)),
            pl.BlockSpec((Q, LATE), lambda i: (i, 0)),
            pl.BlockSpec((Q, INNER), lambda i: (i, 0)),
            const_spec((1, D)),
            const_spec((256, INNER)), const_spec((INNER, 128)),
            const_spec((8, XBC)), const_spec((1, XBC)), const_spec((1, 128)),
            const_spec((1, 128)), const_spec((1, INNER)), const_spec((1, INNER)),
        ],
        out_specs=[
            pl.BlockSpec((2, Q, INNER), lambda i: (0, i, 0)),
            pl.BlockSpec((Q, INNER), lambda i: (i, 0)),
            pl.BlockSpec((Q, 128), lambda i: (i, 0)),
            pl.BlockSpec((1, STATE, INNER), lambda i: (i, 0, 0)),
            const_spec((1, INNER)), const_spec((8, 128)),
        ],
        out_shape=[
            jax.ShapeDtypeStruct((2, n, INNER), BF16),
            jax.ShapeDtypeStruct((n, INNER), F32),
            jax.ShapeDtypeStruct((n, 128), F32),
            jax.ShapeDtypeStruct((steps, STATE, INNER), F32),
            jax.ShapeDtypeStruct((1, INNER), F32),
            jax.ShapeDtypeStruct((8, 128), F32),
        ],
        scratch_shapes=[
            pltpu.VMEM((1, INNER), F32),
            pltpu.VMEM((Q + 8, XBC), F32),
            pltpu.VMEM((Q, 128), F32),
            pltpu.VMEM((STATE, INNER), F32),
            pltpu.VMEM((Q, INNER), F32),
            pltpu.VMEM((Q, INNER), F32),
            pltpu.VMEM((128, Q), F32),
        ],
        compiler_params=pltpu.CompilerParams(
            dimension_semantics=("arbitrary",), vmem_limit_bytes=48 * 2**20),
        cost_estimate=pl.CostEstimate(
            flops=30 * 10**9, bytes_accessed=40 * 2**20, transcendentals=10**7),
    )(bound, cot_top, z, proj, gm, norm_gain, e2, et, *params)


def backward_kernel(
    bound_ref, proj_ref, before_ref, dy_ref, through_ref, state_ref, gz_ref, tok_ref, cot_ref,
    in_ref, norm_ref, ggain_ref,
    e_ref, et_ref, convw_ref, convb_ref, dtb_ref, alog_ref, skip_ref,
    window_ref, gtok_ref, small_ref, power_ref,
    total_ref, gskip_ref, gsmall_ref, dtw_ref, gp_ref, ext_ref, dt_ref, lam_ref, dsum_ref, xd_ref, g_ref, gnext_ref, cumt_ref,
):
    step = pl.program_id(0)
    steps = pl.num_programs(0)
    bound = bound_ref[0]
    t0 = (steps - 1 - step) * Q

    @pl.when(step == 0)
    def _():
        lam_ref[...] = jnp.zeros_like(lam_ref)
        dsum_ref[...] = jnp.zeros_like(dsum_ref)
        dt_ref[...] = jnp.zeros_like(dt_ref)
        gnext_ref[Q : Q + 8, :] = jnp.zeros((8, XBC), F32)
        gskip_ref[...] = jnp.zeros_like(gskip_ref)
        total_ref[...] = jnp.zeros_like(total_ref)
        dtw_ref[...] = jnp.zeros_like(dtw_ref)
        gsmall_ref[...] = jnp.zeros_like(gsmall_ref)

    rows, rr, cc = chunk_masks(t0, bound)
    dy = dy_ref[...]
    first_chunk = (t0 > 0).astype(F32)
    ext_ref[0:8, :] = before_ref[:, :XBC] * first_chunk
    ext_ref[8 : 8 + Q, :] = proj_ref[:, :XBC]
    pre = conv_rows(ext_ref, convw_ref, convb_ref, rows, bound)
    sig_pre = sigmoid(pre)
    conv_out = pre * sig_pre
    x = conv_out[:, :INNER]
    b_rows = conv_out[:, INNER : INNER + STATE]
    c_rows = conv_out[:, INNER + STATE :]
    dt_ref[:, 0:HEADS] = proj_ref[:, XBC:LATE]
    dt_in, dt_pos, rate, cum = decay_parts(dt_ref[...], dtb_ref, alog_ref, rr, cc)
    cum_end = cum[Q - 1 : Q, :]
    keep = jnp.logical_or(rows < bound, bound < t0).astype(F32)
    in_last = jnp.logical_or(rows >= bound, bound > t0 + Q - 1).astype(F32)
    whole = jnp.logical_or(bound < t0, bound > t0 + Q - 1).astype(F32)
    from_start = jnp.exp(cum) * keep
    to_end = jnp.exp(cum_end - cum) * in_last
    carry_scale = jnp.exp(cum_end) * whole
    allowed_t = jnp.logical_and(rr <= cc, (cc >= bound) == (rr >= bound))
    cum2 = cum * LOG2E
    cumt_ref[...] = cum2.T
    c_t = c_rows.T
    gram_t = dot(wide_left(b_rows), tall_right(c_t))
    spread = expand(jnp.concatenate(
        [dt_pos, to_end, from_start, jnp.broadcast_to(carry_scale, (16, 128))], axis=0), e_ref)
    dt_all = spread[:Q]
    end_all = spread[Q : 2 * Q]
    xd = x * dt_all
    xd_ref[...] = xd
    skip = skip_ref[...]
    gskip_ref[...] += jnp.sum(dy * x, axis=0, keepdims=True)
    lam = lam_ref[...]
    lam_hi, lam_lo = split2(lam)
    g_ref[...] = (
        dot(wide_left(b_rows), jnp.concatenate([lam_hi, lam_hi, lam_lo], axis=0)) * end_all
    )
    grad_b = quarters(dot_nt(
        jnp.concatenate(split2(xd * end_all), axis=0), jnp.concatenate([lam_hi, lam_lo], axis=0)))
    state = state_ref[0]
    dye_hi, dye_lo = split2(dy * spread[2 * Q : 3 * Q])
    grad_c = quarters(dot_nt(
        jnp.concatenate([dye_hi, dye_lo], axis=0), jnp.concatenate(split2(state), axis=0)))
    lam_new = lam * spread[3 * Q : 3 * Q + 1] + dot(
        wide_left(c_t), jnp.concatenate([dye_hi, dye_hi, dye_lo], axis=0)
    )
    lam_ref[...] = lam_new
    ended = dsum_ref[0:1, :]
    first = iota((Q, Q), 1) < HEADDIM
    first_b = (first.astype(F32).astype(BF16), 1.0 - first.astype(F32).astype(BF16))
    first_row = (iota((Q, Q), 0) < HEADDIM).astype(F32).astype(BF16)
    first_row = (first_row, 1.0 - first_row)
    gram_grad = jnp.zeros((Q, Q), F32)
    for pair in range(PAIRS):
        lanes = slice(pair * 128, pair * 128 + 128)
        weights = []
        for head in (2 * pair, 2 * pair + 1):
            differ = cumt_ref[head : head + 1, :] - cum2[:, head : head + 1]
            weights.append(jnp.exp2(jnp.where(allowed_t, differ, NEG)))
        left = jnp.concatenate([gram_t * weights[0], gram_t * weights[1]], axis=1)
        left = jnp.concatenate(split2(left), axis=0)
        dyp = dy_ref[:, lanes]
        out = dot(left, split_pair(dyp, first_b))
        g_ref[:, lanes] += out[:Q, :128] + (out[:Q, 128:] + out[Q:, :128])
        dyt_hi, dyt_lo = split2(dyp.T)
        right_hi = jnp.concatenate([dyt_hi * first_row[0], dyt_hi * first_row[1]], axis=1)
        right_lo = jnp.concatenate([dyt_lo * first_row[0], dyt_lo * first_row[1]], axis=1)
        outer = dot(
            wide_left(xd_ref[:, lanes]), jnp.concatenate([right_hi, right_hi, right_lo], axis=0))
        gram_grad = gram_grad + (outer[:, :128] * weights[0] + outer[:, 128:] * weights[1])
    g = g_ref[...]
    grad_x = dt_all * g + skip * dy
    sums = dot(jnp.concatenate(
        split2(x * g) + split2(jnp.broadcast_to(
            jnp.sum(lam_new * state, axis=0, keepdims=True), (16, INNER))), axis=0), et_ref[...])
    direct = sums[:Q] + sums[Q : 2 * Q]
    balance = through_ref[...] - dt_pos * direct
    keep_t = allowed_t.astype(F32).astype(BF16)
    b_hi, b_mid, b_lo = split3(balance)
    grad_step = dot(keep_t, b_hi) + dot(keep_t, b_mid) + dot(keep_t, b_lo) + in_last * ended
    dsum_ref[...] = sums[2 * Q : 2 * Q + 8] + sums[2 * Q + 16 : 2 * Q + 24]
    grad_dt = (direct + rate * grad_step) * sigmoid(dt_in)
    gsmall_ref[0:1, :] += jnp.sum(grad_dt, axis=0, keepdims=True)
    gsmall_ref[1:2, :] += rate * jnp.sum(dt_pos * grad_step, axis=0, keepdims=True)
    grad_c = grad_c + dot(wide_left(gram_grad.T), tall_right(b_rows))
    grad_b = grad_b + dot(wide_left(gram_grad), tall_right(c_rows))
    slope = sig_pre * (1.0 + pre * (1.0 - sig_pre))
    gnext_ref[0:Q, :INNER] = grad_x * slope[:, :INNER]
    gnext_ref[0:Q, INNER : INNER + STATE] = grad_b * slope[:, INNER : INNER + STATE]
    gnext_ref[0:Q, INNER + STATE :] = grad_c * slope[:, INNER + STATE :]
    gcp = gnext_ref[0:Q, :]
    total_ref[4:5, :] += jnp.sum(gcp, axis=0, keepdims=True)
    total_ref[3:4, :] += jnp.sum(gcp * ext_ref[8 : 8 + Q, :], axis=0, keepdims=True)
    total = convw_ref[3:4, :] * gcp
    for back in (1, 2, 3):
        ok = jnp.logical_or(rows - back >= bound, rows < bound).astype(F32)
        total_ref[3 - back : 4 - back, :] += jnp.sum(
            gcp * (ext_ref[8 - back : 8 - back + Q, :] * ok), axis=0, keepdims=True)
        okn = jnp.logical_or(rows >= bound, rows + back < bound).astype(F32)
        total = total + convw_ref[3 - back : 4 - back, :] * (gnext_ref[back : back + Q, :] * okn)
    total_ref[7:8, :] = jnp.maximum(
        total_ref[7:8, :], jnp.max(jnp.abs(total), axis=0, keepdims=True))
    total = total.astype(BF16)
    window_ref[0] = total[:, :WINDOW]
    window_ref[1] = total[:, XBC - WINDOW :]
    gnext_ref[Q : Q + 8, :] = gnext_ref[0:8, :]
    half = (steps - 1 - step) % 2
    at = pl.multiple_of(half * Q, Q)
    gp_ref[pl.ds(at, Q), :INNER] = gz_ref[0]
    gp_ref[pl.ds(at, Q), INNER : INNER + XBC] = total
    gp_ref[pl.ds(at, Q), INNER + XBC :] = grad_dt.astype(BF16)

    @pl.when(half == 0)
    def _():
        grad_normed = dot(gp_ref[...], in_ref[: INNER + XBC + 128, :])
        tok = tok_ref[...].astype(F32)
        rinv = lax.rsqrt(jnp.mean(tok * tok, axis=1, keepdims=True) + EPS_NORM)
        nhat = tok * rinv
        gain = norm_ref[...]
        gng = grad_normed * gain
        gtok_ref[...] = (cot_ref[...].astype(F32) + rinv * (
            gng - nhat * jnp.mean(nhat * gng, axis=1, keepdims=True))).astype(BF16)
        total_ref[6:7, :D] += jnp.sum(nhat * grad_normed, axis=0, keepdims=True)
        normed = (nhat * gain).astype(BF16)
        gdt = gp_ref[:, INNER + XBC :].astype(F32)
        dtw_ref[...] += dot(jnp.concatenate(
            [gdt[:Q].T, gdt[Q:].T], axis=1).astype(BF16), normed)

    @pl.when(step == steps - 1)
    def _():
        skips = head_sum(jnp.broadcast_to(gskip_ref[...], (8, INNER)), et_ref)
        small_ref[...] = jnp.zeros_like(small_ref)
        small_ref[0:HEADS, :] = dtw_ref[0:HEADS, :]
        pieces = [
            total_ref[k : k + 1, j * 128 : j * 128 + 128]
            for k in range(CONV + 1) for j in range(XBC // 128)]
        pieces += [gsmall_ref[0:1, :], gsmall_ref[1:2, :], skips[0:1, :]]
        pieces += [ggain_ref[:, j * 128 : j * 128 + 128] for j in range(INNER // 128)]
        lines = D // 128
        for number, piece in enumerate(pieces):
            line = HEADS + number // lines
            at = number % lines * 128
            small_ref[line : line + 1, at : at + 128] = piece
        small_ref[40:41, :] = total_ref[6:7, :D]
        count = float(Q * steps)
        largest = jnp.max(total_ref[7:8, :], axis=1, keepdims=True)
        normed = jnp.max(jnp.abs(norm_ref[...]), axis=1, keepdims=True) * (D ** 0.5)
        others = jnp.max(jnp.max(jnp.abs(small_ref[...]), axis=1, keepdims=True), axis=0, keepdims=True)
        power_ref[...] = jnp.broadcast_to(power_for(
            jnp.maximum(1.05 * count * largest * normed, others)), (8, 128))


def run_backward(
    proj, dy, through, states, pair, tok, cot, in_w, norm_gain, ggain, bound, e2, et, params
):
    n = proj.shape[0]
    steps = n // Q

    def rev(i):
        return (steps - 1 - i, 0)

    def rev_two(i):
        return ((steps - 1 - i) // 2, 0)

    return pl.pallas_call(
        backward_kernel,
        grid=(steps,),
        in_specs=[
            pl.BlockSpec(memory_space=pltpu.SMEM),
            pl.BlockSpec((Q, LATE), rev),
            pl.BlockSpec((8, LATE), lambda i: (jnp.maximum((steps - 1 - i) * (Q // 8) - 1, 0), 0)),
            pl.BlockSpec((Q, INNER), rev),
            pl.BlockSpec((Q, 128), rev),
            pl.BlockSpec((1, STATE, INNER), lambda i: (steps - 1 - i, 0, 0)),
            pl.BlockSpec((1, Q, INNER), lambda i: (0, steps - 1 - i, 0)),
            pl.BlockSpec((2 * Q, D), rev_two), pl.BlockSpec((2 * Q, D), rev_two),
            const_spec(in_w.shape), const_spec((1, D)), const_spec((1, INNER)),
            const_spec((256, INNER)), const_spec((INNER, 128)),
            const_spec((8, XBC)), const_spec((1, XBC)), const_spec((1, 128)),
            const_spec((1, 128)), const_spec((1, INNER)),
        ],
        out_specs=[
            pl.BlockSpec((2, Q, WINDOW), lambda i: (0, steps - 1 - i, 0)),
            pl.BlockSpec((2 * Q, D), rev_two),
            const_spec((48, D)), const_spec((8, 128)),
        ],
        out_shape=[
            jax.ShapeDtypeStruct((2, n, WINDOW), BF16),
            jax.ShapeDtypeStruct((n, D), BF16),
            jax.ShapeDtypeStruct((48, D), F32),
            jax.ShapeDtypeStruct((8, 128), F32),
        ],
        scratch_shapes=[
            pltpu.VMEM((8, XBC), F32),
            pltpu.VMEM((1, INNER), F32),
            pltpu.VMEM((8, 128), F32),
            pltpu.VMEM((128, D), F32),
            pltpu.VMEM((2 * Q, INNER + XBC + 128), BF16),
            pltpu.VMEM((Q + 8, XBC), F32),
            pltpu.VMEM((Q, 128), F32),
            pltpu.VMEM((STATE, INNER), F32),
            pltpu.VMEM((8, 128), F32),
            pltpu.VMEM((Q, INNER), F32),
            pltpu.VMEM((Q, INNER), F32),
            pltpu.VMEM((Q + 8, XBC), F32),
            pltpu.VMEM((128, Q), F32),
        ],
        compiler_params=pltpu.CompilerParams(
            dimension_semantics=("arbitrary",), vmem_limit_bytes=48 * 2**20),
        cost_estimate=pl.CostEstimate(
            flops=50 * 10**9, bytes_accessed=50 * 2**20, transcendentals=2 * 10**7),
    )(bound, proj, proj, dy, through, states, pair, tok, cot, in_w, norm_gain, ggain,
      e2, et, *params[:5])


BETA_ONE = 0.9
BETA_TWO = 0.95
EPS_ADAM = 1e-08
LANES = 128
NORM_ROWS = D // LANES
IN_ROWS = PROJ * D // LANES
CONVW_ROWS = CONV * XBC // LANES
CONVB_ROWS = XBC // LANES
GAIN_ROWS = INNER // LANES
OUT_ROWS = INNER * D // LANES
DT_ROWS = HEADS * D // LANES
SMALL_ROWS = DT_ROWS + CONVW_ROWS + CONVB_ROWS + 3 + GAIN_ROWS
OUT_START = NORM_ROWS + IN_ROWS + SMALL_ROWS - DT_ROWS
LATE_START = NORM_ROWS + INNER * NORM_ROWS
LEAD = 896
STAGE_ROWS = 16264
STAGE_BLOCKS = 5
MARK = 16


PREP_STEPS = 7
IN_BLOCK = 512
OUT_BLOCK = 256
SMALL_START = NORM_ROWS + IN_ROWS


def prepare_kernel(
    flat_ref,
    in_ref, out_ref, norm_ref, convw_ref, convb_ref, dtb_ref, alog_ref, skip_ref, gain_ref,
    e_ref, et_ref,
    stage_ref,
):
    step = pl.program_id(0)

    @pl.when(step == 0)
    def _():
        rows = flat_ref[0:16, :].astype(F32)
        for lane in range(NORM_ROWS):
            norm_ref[:, lane * LANES : lane * LANES + LANES] = rows[lane : lane + 1, :]
        low = SMALL_START // 16 * 16
        stage_ref[0:112, :] = flat_ref[low : low + 112, :].astype(F32)
        at = SMALL_START - low
        convw_ref[...] = jnp.zeros_like(convw_ref)
        for tap in range(CONV):
            for lane in range(CONVB_ROWS):
                convw_ref[tap : tap + 1, lane * LANES : lane * LANES + LANES] = stage_ref[
                    at : at + 1, :]
                at += 1
        for lane in range(CONVB_ROWS):
            convb_ref[:, lane * LANES : lane * LANES + LANES] = stage_ref[at : at + 1, :]
            at += 1
        heads = iota((1, LANES), 1) < HEADS
        dtb_ref[...] = jnp.where(heads, stage_ref[at : at + 1, :], 0.0)
        alog_ref[...] = jnp.where(heads, stage_ref[at + 1 : at + 2, :], 0.0)
        skips = jnp.where(heads, stage_ref[at + 2 : at + 3, :], 0.0)
        at += 3
        for lane in range(GAIN_ROWS):
            gain_ref[:, lane * LANES : lane * LANES + LANES] = stage_ref[at : at + 1, :]
            at += 1
        one = (iota((128, INNER), 1) // HEADDIM == iota((128, INNER), 0)).astype(F32).astype(BF16)
        e_ref[0:128, :] = one
        e_ref[128:256, :] = one
        et_ref[...] = (
            iota((INNER, 128), 0) // HEADDIM == iota((INNER, 128), 1)).astype(F32).astype(BF16)
        skip_ref[...] = dot(jnp.broadcast_to(skips, (16, LANES)).astype(BF16), one)[0:1, :]

    def block(start, offset, rows, dest_ref):
        size = rows * NORM_ROWS + 16
        at = pl.multiple_of(start + step * (rows * NORM_ROWS), 16)
        stage_ref[0:size, :] = flat_ref[pl.ds(at, size), :].astype(F32)
        for lane in range(NORM_ROWS):
            dest_ref[:, lane * LANES : lane * LANES + LANES] = stage_ref[
                pl.ds(offset + lane, rows, stride=NORM_ROWS), :].astype(BF16)

    block(0, NORM_ROWS, IN_BLOCK, in_ref)

    @pl.when(step == PREP_STEPS - 1)
    def _():
        used = PROJ - (PREP_STEPS - 1) * IN_BLOCK
        in_ref[used:, :] = jnp.zeros((IN_BLOCK - used, D), BF16)

    @pl.when(step < INNER // OUT_BLOCK)
    def _():
        low = OUT_START // 16 * 16
        block(low, OUT_START - low, OUT_BLOCK, out_ref)


def run_prepare(flat):
    vector = lambda n: jax.ShapeDtypeStruct((1, n), F32)
    return pl.pallas_call(
        prepare_kernel,
        grid=(PREP_STEPS,),
        in_specs=[const_spec(flat.shape)],
        out_specs=[
            pl.BlockSpec((IN_BLOCK, D), lambda i: (i, 0)),
            pl.BlockSpec((OUT_BLOCK, D), lambda i: (jnp.minimum(i, INNER // OUT_BLOCK - 1), 0)),
            const_spec((1, D)), const_spec((8, XBC)), const_spec((1, XBC)), const_spec((1, 128)),
            const_spec((1, 128)), const_spec((1, INNER)), const_spec((1, INNER)),
            const_spec((256, INNER)), const_spec((INNER, 128)),
        ],
        out_shape=[
            jax.ShapeDtypeStruct((PREP_STEPS * IN_BLOCK, D), BF16),
            jax.ShapeDtypeStruct((INNER, D), BF16),
            vector(D), jax.ShapeDtypeStruct((8, XBC), F32), vector(XBC), vector(128), vector(128),
            vector(INNER), vector(INNER),
            jax.ShapeDtypeStruct((256, INNER), BF16), jax.ShapeDtypeStruct((INNER, 128), BF16),
        ],
        scratch_shapes=[pltpu.VMEM((IN_BLOCK * NORM_ROWS + 16, LANES), F32)],
        compiler_params=pltpu.CompilerParams(
            dimension_semantics=("arbitrary",), vmem_limit_bytes=40 * 2**20),
        cost_estimate=pl.CostEstimate(
            flops=10**9, bytes_accessed=16 * 2**20, transcendentals=0),
    )(flat)


def stage_kernel(
    who_ref, early_ref, early_other_ref, late_ref, late_other_ref, small_ref,
    grad_ref,
    stage_ref,
):
    step = pl.program_id(0)
    upper = who_ref[0]
    mine = who_ref[1]
    block = grad_ref.shape[0]
    half = 2 * block * STAGE_BLOCKS

    @pl.when(step == 0)
    def _():
        early_at = LEAD + jnp.where(upper == 1, OUT_START - half, NORM_ROWS)
        window = LATE_START + (XBC - WINDOW) * NORM_ROWS
        late_at = LEAD + jnp.where(upper == 1, window - half, LATE_START)
        def lay(source_ref, start, size):
            for lane in range(NORM_ROWS):
                stage_ref[pl.ds(start + lane, size, stride=NORM_ROWS), :] = source_ref[
                    0:size, lane * LANES : lane * LANES + LANES]

        lines = late_ref.shape[0]
        lay(late_ref, late_at + mine * (lines * NORM_ROWS), lines)
        lay(late_other_ref, late_at + (1 - mine) * (lines * NORM_ROWS), lines)

        @pl.when(upper == 1)
        def _():
            lay(small_ref, LEAD + OUT_START - half - SMALL_ROWS, -(-SMALL_ROWS // NORM_ROWS))

        lines = early_ref.shape[0]
        lay(early_ref, early_at + mine * (lines * NORM_ROWS), lines)
        lay(early_other_ref, early_at + (1 - mine) * (lines * NORM_ROWS), lines)

        @pl.when(upper == 0)
        def _():
            for lane in range(NORM_ROWS):
                stage_ref[LEAD + lane : LEAD + lane + 1, :] = small_ref[
                    40:41, lane * LANES : lane * LANES + LANES]

        @pl.when(upper == 1)
        def _():
            at = LEAD + OUT_START + OUT_ROWS - half
            stage_ref[at : LEAD + half, :] = jnp.zeros((LEAD + half - at, LANES), F32)

    @pl.when(step > 0)
    def _():
        at = LEAD + mine * (half // 2) + (step - 1) * block
        grad_ref[...] = stage_ref[pl.ds(pl.multiple_of(at, 8), block), :]


def run_stage(who, rows, early, early_other, late, late_other, small):
    block = rows // STAGE_BLOCKS
    return pl.pallas_call(
        stage_kernel,
        grid=(STAGE_BLOCKS + 1,),
        in_specs=[
            pl.BlockSpec(memory_space=pltpu.SMEM),
            const_spec(early.shape), const_spec(early.shape),
            const_spec(late.shape), const_spec(late.shape), const_spec(small.shape),
        ],
        out_specs=pl.BlockSpec((block, LANES), lambda i: (jnp.maximum(i - 1, 0), 0)),
        out_shape=jax.ShapeDtypeStruct((rows, LANES), F32),
        scratch_shapes=[pltpu.VMEM((STAGE_ROWS, LANES), F32)],
        compiler_params=pltpu.CompilerParams(
            dimension_semantics=("arbitrary",), vmem_limit_bytes=48 * 2**20),
        cost_estimate=pl.CostEstimate(
            flops=10**6, bytes_accessed=12 * 2**20, transcendentals=0),
    )(who, early, early_other, late, late_other, small)


def swap(values, axis, bit):
    size = lax.axis_size(axis)
    return lax.ppermute(values, axis, [(i, i ^ bit) for i in range(size)])


def to_wire(values, power):
    return (values * jnp.exp2(power)).astype(jnp.float16)


def from_wire(values, power):
    return values.astype(F32) * jnp.exp2(-power)


def scatter(values, power, axis, bit=1, count=2, after=None):
    place = (lax.axis_index(axis) // bit) % count
    rows = values.shape[-2] // count
    mark = min(MARK, rows)
    dim = values.ndim - 2
    total = lax.dynamic_slice_in_dim(values, place * rows, rows, dim)
    least = power
    arrived = []
    for offset in range(1, count):
        to = place ^ offset
        last = to == count - 1
        start = to * rows - jnp.where(last, mark, 0)
        send = lax.dynamic_slice_in_dim(values, start, rows + mark, dim)
        line = lax.broadcasted_iota(jnp.int32, send.shape, dim)
        marked = jnp.where(last, line < mark, line >= rows)
        wire = jnp.where(marked, power, send * jnp.exp2(power)).astype(jnp.float16)
        arrived.append(swap(wire, axis, bit * offset))
    if after is not None:
        arrived, _ = lax.optimization_barrier((arrived, after))
    last = place == count - 1
    for got in arrived:
        got_power = lax.dynamic_slice_in_dim(got, jnp.where(last, 0, rows), 1, dim)
        got_power = got_power.reshape(-1, D)[0:1, 0:1].astype(F32)
        body = lax.dynamic_slice_in_dim(got, jnp.where(last, mark, 0), rows, dim)
        total = total + from_wire(body, got_power)
        least = jnp.minimum(least, got_power)
    return total, least - float(count.bit_length() - 1)


def everyones(values, axis, bit=1, count=2):
    place = (lax.axis_index(axis) // bit) % count
    pieces = [values] + [swap(values, axis, bit * offset) for offset in range(1, count)]
    step = 1
    while step < count:
        flip = (place // step) % 2 == 1
        pieces = [
            jnp.where(flip, pieces[i ^ step], pieces[i]) for i in range(count)]
        step *= 2
    return pieces


def gather(values, axis, bit=1, count=2):
    return jnp.concatenate(everyones(values, axis, bit, count))


def add_pair(values, axis, bit, after=None):
    got = swap(values, axis, bit)
    if after is not None:
        got, _ = lax.optimization_barrier((got, after))
    return values + got


def data_groups():
    size = lax.axis_size("dp")
    groups = [(1, 2)]
    bit = 2
    while bit < size:
        count = 4 if bit * 4 <= size else 2
        groups.append((bit, count))
        bit *= count
    return groups


def dot_tn(a, b):
    return lax.dot_general(a, b, (((0,), (0,)), ((), ())), preferred_element_type=F32)


def pick_rows(index, rows):
    chosen = index[:, None] == jnp.arange(rows.shape[0], dtype=jnp.int32)[None, :]
    return dot(chosen.astype(BF16), rows).astype(BF16)


def on_device(
    tokens, loss_sensitivity, lengths, holder_sequence_list, master, moment_one, moment_two,
    adam_rates, iteration_tally,
):
    group_devices = lax.axis_size("zero")
    data_devices = lax.axis_size("dp")
    zero_index = lax.axis_index("zero")
    dp_index = lax.axis_index("dp")
    seq_len = loss_sensitivity.shape[1]
    group_seqs = tokens.shape[0]
    span = tokens.shape[1]
    slots = group_seqs // data_devices
    shard_rows = master.shape[0] // LANES
    tie = lax.optimization_barrier

    own = master.reshape(shard_rows, LANES)
    arranged = holder_sequence_list.reshape(data_devices, group_devices, slots)
    group_order = lax.dynamic_index_in_dim(arranged, zero_index, 1, keepdims=False).reshape(-1)
    local_ids = group_order - zero_index * group_seqs
    dealt = tokens.at[local_ids].get(mode="promise_in_bounds")
    flat = lax.all_gather(own.astype(BF16), "zero", axis=0, tiled=True)

    local_tok = lax.all_to_all(dealt, "dp", split_axis=0, concat_axis=0, tiled=True)
    my_seqs = lax.dynamic_slice_in_dim(group_order, dp_index * slots, slots)
    bound = lengths[my_seqs[0]]
    positions = jnp.arange(seq_len, dtype=jnp.int32)

    in_w, out_w, norm_gain, *params, e2, et = run_prepare(flat)
    cot = loss_sensitivity[0]
    gm = dot_nt(cot, out_w)
    cot_top = jnp.max(jnp.abs(cot)).astype(F32).reshape(1)
    local_tok, in_w, gm, cot_top = tie((local_tok, in_w, gm, cot_top))
    own_late, _ = tie((own, flat[:8]))
    whole_master = lax.all_gather(own_late, "zero", axis=0, tiled=True)

    def place(slot, at):
        return (at // span) * (slots * span) + slot * span + at % span

    source = jnp.where(positions < bound, place(0, positions), place(1, positions - bound))
    packed = pick_rows(source, local_tok.reshape(slots * seq_len, D))
    blocks = jnp.arange(data_devices, dtype=jnp.int32)[:, None, None] * span
    within = blocks + jnp.arange(span, dtype=jnp.int32)[None, None, :]
    within = within + jnp.arange(slots, dtype=jnp.int32)[None, :, None] * bound
    unpack_rows = jnp.minimum(within, seq_len - 1).reshape(-1)

    def spread(rows):
        return pick_rows(unpack_rows, rows).reshape(data_devices * slots, span, D)

    def send_back(picked):
        return lax.all_to_all(picked, "dp", split_axis=0, concat_axis=0, tiled=True)

    restore = jnp.zeros_like(local_ids).at[local_ids].set(
        jnp.arange(group_seqs, dtype=jnp.int32))
    mine = lax.dynamic_slice_in_dim(lengths, zero_index * group_seqs, group_seqs)
    at = dp_index * span + jnp.arange(span, dtype=jnp.int32)
    live = (at[None, :] < mine[:, None])[:, :, None]

    bound_arr = bound.reshape(1)
    tok = packed.astype(F32)
    nhat = tok * lax.rsqrt(jnp.mean(tok * tok, axis=1, keepdims=True) + EPS_NORM)
    normed = (nhat * norm_gain).astype(BF16)
    proj_z = dot_nt(normed, in_w[:INNER])
    proj = dot_nt(normed, in_w[INNER:PROJ])
    pair, dy, through, states, ggain, early_power = run_forward(
        proj_z, proj, gm, bound_arr, cot_top, norm_gain, e2, et, params)
    result = (tok + dot(pair[1], out_w)).astype(BF16)
    picked = spread(result)
    picked, pair = tie((picked, pair))
    back_out = send_back(picked)
    early_power = early_power[0:1, 0:1]
    early = lax.dot_general(
        pair, jnp.stack([normed, cot]), (((1,), (1,)), ((0,), (0,))), preferred_element_type=F32)
    early, early_power = scatter(early, early_power, "zero", 1)
    early, early_power, dy = tie((early.reshape(INNER, D), early_power, dy))
    early, early_power = scatter(early, early_power, "zero", 2)
    window, grad_tok, small, late_power = run_backward(
        proj, dy, through, states, pair, packed, cot, in_w, norm_gain, ggain,
        bound_arr, e2, et, params)
    window, small, late_power, early, early_power, whole_master = tie(
        (window, small, late_power, early, early_power, whole_master))

    groups = data_groups()
    late = lax.dot_general(
        window, jnp.stack([normed, normed]), (((1,), (1,)), ((0,), (0,))),
        preferred_element_type=F32)
    late_power = late_power[0:1, 0:1]
    late, late_power = scatter(late, late_power, "zero", 1)
    late = late.reshape(WINDOW, D)
    small = add_pair(small, "zero", 1)
    early, early_power, grad_tok, _ = tie((early, early_power, grad_tok, late))
    late, late_power = scatter(late, late_power, "zero", 2)
    early, early_power = scatter(early, early_power, "dp", *groups[0])
    small = add_pair(small, "zero", 2, late)
    early_before, power_before = early, early_power
    picked_grad = spread(grad_tok)
    tokens, back_out, _ = tie((tokens, back_out, grad_tok))
    back_rows = back_out.at[restore].get(mode="promise_in_bounds")
    tokens_out = jnp.where(live, back_rows, tokens)
    new_master = jnp.zeros((group_devices, shard_rows, LANES), F32)
    late, tokens_out, new_master, picked_grad = tie((late, tokens_out, new_master, picked_grad))
    lines = small.shape[0]
    late = jnp.concatenate([late, small, jnp.zeros((WINDOW // 8 - lines, D), F32)])
    late, late_power = scatter(late, late_power, "dp", *groups[0])
    early, early_power = early_before, power_before
    for group in groups[1:]:
        early, early_power = scatter(early, early_power, "dp", *group, after=late)
    early = to_wire(early, early_power)
    for group in reversed(groups[1:]):
        early = gather(early, "dp", *group)
    early, _ = tie((early, late))
    for group in groups[1:]:
        late, late_power = scatter(late, late_power, "dp", *group)
    late = to_wire(late, late_power)
    early = from_wire(gather(early, "dp", *groups[0]), early_power)
    early, picked_grad, _ = tie((early, picked_grad, late))
    for group in reversed(groups[1:]):
        late = gather(late, "dp", *group)
    early_other = swap(early, "zero", 1)
    back_grad = send_back(picked_grad)
    wire = gather(late, "dp", *groups[0])
    late = from_wire(wire[: WINDOW // 2], late_power)
    small = from_wire(wire[WINDOW // 2 : WINDOW // 2 + lines], late_power)
    late_other = swap(late, "zero", 1)

    steps_f = iteration_tally[0].astype(F32)
    who = jnp.stack([zero_index // 2, zero_index % 2]).astype(jnp.int32)
    first = moment_one.reshape(shard_rows, LANES)
    second = moment_two.reshape(shard_rows, LANES)
    grad_shard = run_stage(who, shard_rows, early, early_other, late, late_other, small)
    first_scale = 1.0 / (1.0 - jnp.power(BETA_ONE, steps_f))
    second_scale = 1.0 / (1.0 - jnp.power(BETA_TWO, steps_f))

    def moments(grad, first, second):
        return (
            BETA_ONE * first + (1.0 - BETA_ONE) * grad,
            BETA_TWO * second + (1.0 - BETA_TWO) * grad * grad)

    def quotient(rows):
        first_next, second_next = moments(grad_shard[rows], first[rows], second[rows])
        return ((first_next * first_scale) / (
            jnp.sqrt(second_next * second_scale) + EPS_ADAM)).astype(jnp.float16)

    whole_master = whole_master.reshape(group_devices, shard_rows, LANES)

    def put(new_master, piece, offset):
        shard = zero_index ^ offset
        old = lax.dynamic_index_in_dim(whole_master, shard, 0, keepdims=False)
        new = old - adam_rates[0] * (piece.astype(F32) + adam_rates[1] * old)
        return lax.dynamic_update_index_in_dim(new_master, new, shard, 0)

    own_part, first, second = tie((quotient(slice(0, shard_rows)), first, second))
    across = swap(own_part, "zero", 2)
    core = swap(own_part, "zero", 1)
    first_next, second_next = moments(grad_shard, first, second)
    new_master = put(put(new_master, own_part, 0), core, 1)
    across, new_master, first_next, second_next = tie(
        (across, new_master, first_next, second_next))
    last = swap(across, "zero", 1)
    new_master = put(new_master, across, 2)
    last, new_master = tie((last, new_master))
    new_master = put(new_master, last, 3)
    back_grad, new_master = tie((back_grad, new_master))
    grad_tokens = jnp.where(
        live, back_grad.at[restore].get(mode="promise_in_bounds"), jnp.zeros((), BF16))
    return (
        tokens_out, grad_tokens, new_master.reshape(-1), grad_shard.reshape(-1),
        first_next.reshape(-1), second_next.reshape(-1))


def solution(mesh):
    return jax.shard_map(
        on_device,
        mesh=mesh,
        in_specs=(
            P("zero", "dp", None), P(("dp", "zero"), None, None), P(), P(),
            P("zero"), P("zero"), P("zero"), P(), P(),
        ),
        out_specs=(
            P("zero", "dp", None), P("zero", "dp", None), P(), P("zero"), P("zero"), P("zero"),
        ),
        check_vma=False,
    )
```

```python
import jax
import jax.numpy as jnp
from jax import lax
from jax.experimental import pallas as pl
from jax.experimental.pallas import tpu as pltpu
from jax.sharding import PartitionSpec as P

D = 768
HEADS = 24
HEADDIM = 64
STATE = 128
CONV = 4
INNER = 1536
XBC = 1792
PROJ = 3352
Q = 128
LATE = PROJ - INNER
WINDOW = 1024
PAIRS = HEADS // 2
EPS_NORM = 1e-05
NEG = -1e30
F16_TOP = 30000.0
LOG2E = 1.4426950408889634
F32 = jnp.float32
BF16 = jnp.bfloat16


def dot(a, b):
    return lax.dot_general(a, b, (((1,), (0,)), ((), ())), preferred_element_type=F32)


def dot_nt(a, b):
    return lax.dot_general(a, b, (((1,), (1,)), ((), ())), preferred_element_type=F32)


def split2(v):
    hi = v.astype(BF16)
    return hi, (v - hi.astype(F32)).astype(BF16)


def split3(v):
    hi = v.astype(BF16)
    rest = v - hi.astype(F32)
    mid = rest.astype(BF16)
    return hi, mid, (rest - mid.astype(F32)).astype(BF16)


def wide_left(v):
    hi, lo = split2(v)
    return jnp.concatenate([hi, lo, hi], axis=1)


def tall_right(v):
    hi, lo = split2(v)
    return jnp.concatenate([hi, hi, lo], axis=0)


def split_pair(v, masks):
    hi, lo = split2(v)
    return jnp.concatenate([
        jnp.concatenate([hi * masks[0], lo * masks[0]], axis=1),
        jnp.concatenate([hi * masks[1], lo * masks[1]], axis=1)], axis=0)


def sigmoid(v):
    return lax.logistic(v)


def softplus(v):
    return jnp.maximum(v, 0.0) + jnp.log1p(jnp.exp(-jnp.abs(v)))


def iota(shape, dim):
    return lax.broadcasted_iota(jnp.int32, shape, dim)


def expand(v, e_ref):
    hi, lo = split2(v)
    return dot(jnp.concatenate([hi, lo], axis=1), e_ref[...])


def head_sum(v, et_ref):
    hi, lo = split2(v)
    return dot(hi, et_ref[...]) + dot(lo, et_ref[...])


def quarters(out):
    return out[:Q, :Q] + (out[:Q, Q:] + out[Q:, :Q])


def power_for(bound):
    scale = jnp.log(0.9 * F16_TOP / jnp.maximum(bound, 1e-30)) * LOG2E
    return jnp.clip(jnp.floor(scale), -126.0, 120.0)


def chunk_masks(t0, bound):
    rows = t0 + iota((Q, 1), 0)
    rr = t0 + iota((Q, Q), 0)
    cc = t0 + iota((Q, Q), 1)
    return rows, rr, cc


def conv_rows(ext_ref, w_ref, b_ref, rows, bound):
    total = b_ref[...] + w_ref[3:4, :] * ext_ref[8 : 8 + Q, :]
    for back in (1, 2, 3):
        ok = jnp.logical_or(rows - back >= bound, rows < bound).astype(F32)
        total = total + w_ref[3 - back : 4 - back, :] * (ext_ref[8 - back : 8 - back + Q, :] * ok)
    return total


def decay_parts(dt_raw, dtb_ref, alog_ref, rr, cc):
    dt_in = dt_raw + dtb_ref[...]
    dt_pos = softplus(dt_in)
    rate = -jnp.exp(alog_ref[...])
    step = dt_pos * rate
    tri = (cc <= rr).astype(F32).astype(BF16)
    s_hi, s_mid, s_lo = split3(step)
    cum = dot(tri, s_hi) + dot(tri, s_mid) + dot(tri, s_lo)
    return dt_in, dt_pos, rate, cum


def forward_kernel(
    bound_ref, cot_ref, z_ref, proj_ref, gm_ref, norm_ref, e_ref, et_ref, convw_ref, convb_ref, dtb_ref, alog_ref,
    skip_ref, gain_ref,
    pair_ref, dy_ref, through_ref, state_ref, ggain_ref, power_ref,
    zmax_ref, ext_ref, dt_ref, carry_ref, xd_ref, acc_ref, cumt_ref,
):
    step = pl.program_id(0)
    bound = bound_ref[0]
    t0 = step * Q

    @pl.when(step == 0)
    def _():
        ext_ref[0:8, :] = jnp.zeros((8, XBC), F32)
        carry_ref[...] = jnp.zeros_like(carry_ref)
        dt_ref[...] = jnp.zeros_like(dt_ref)
        ggain_ref[...] = jnp.zeros_like(ggain_ref)
        zmax_ref[...] = jnp.zeros_like(zmax_ref)

    rows, rr, cc = chunk_masks(t0, bound)
    ext_ref[8 : 8 + Q, :] = proj_ref[:, :XBC]
    pre = conv_rows(ext_ref, convw_ref, convb_ref, rows, bound)
    ext_ref[0:8, :] = ext_ref[Q : Q + 8, :]
    conv_out = pre * sigmoid(pre)
    x = conv_out[:, :INNER]
    b_rows = conv_out[:, INNER : INNER + STATE]
    c_rows = conv_out[:, INNER + STATE :]
    dt_ref[:, 0:HEADS] = proj_ref[:, XBC:LATE]
    _, dt_pos, _, cum = decay_parts(dt_ref[...], dtb_ref, alog_ref, rr, cc)
    cum_end = cum[Q - 1 : Q, :]
    keep = jnp.logical_or(rows < bound, bound < t0).astype(F32)
    in_last = jnp.logical_or(rows >= bound, bound > t0 + Q - 1).astype(F32)
    whole = jnp.logical_or(bound < t0, bound > t0 + Q - 1).astype(F32)
    from_start = jnp.exp(cum) * keep
    to_end = jnp.exp(cum_end - cum) * in_last
    carry_scale = jnp.exp(cum_end) * whole
    allowed = jnp.logical_and(cc <= rr, (cc >= bound) == (rr >= bound))
    cum2 = cum * LOG2E
    cumt_ref[...] = cum2.T

    state = carry_ref[...]
    state_ref[0] = state
    spread = expand(jnp.concatenate(
        [dt_pos, to_end, from_start, jnp.broadcast_to(carry_scale, (16, 128))], axis=0), e_ref)
    xd = x * spread[:Q]
    xd_ref[...] = xd
    acc = dot(wide_left(c_rows), tall_right(state)) * spread[2 * Q : 3 * Q]
    acc_ref[...] = acc + skip_ref[...] * x
    b_t = b_rows.T
    carry_ref[...] = state * spread[3 * Q : 3 * Q + 1] + dot(
        wide_left(b_t), tall_right(xd * spread[Q : 2 * Q]))
    gram = dot(wide_left(c_rows), tall_right(b_t))
    first = iota((Q, Q), 1) < HEADDIM
    first_b = (first.astype(F32).astype(BF16), 1.0 - first.astype(F32).astype(BF16))
    for pair in range(PAIRS):
        parts = []
        for head in (2 * pair, 2 * pair + 1):
            differ = cum2[:, head : head + 1] - cumt_ref[head : head + 1, :]
            parts.append(gram * jnp.exp2(jnp.where(allowed, differ, NEG)))
        left = jnp.concatenate(split2(jnp.concatenate(parts, axis=1)), axis=0)
        lanes = slice(pair * 128, pair * 128 + 128)
        xp = xd_ref[:, lanes]
        out = dot(left, split_pair(xp, first_b))
        acc_ref[:, lanes] += out[:Q, :128] + (out[:Q, 128:] + out[Q:, :128])
    scanned = acc_ref[...]
    z = z_ref[...]
    sig_z = sigmoid(z)
    silu_z = z * sig_z
    gated = scanned * silu_z
    ginv = lax.rsqrt(jnp.mean(gated * gated, axis=1, keepdims=True) + EPS_NORM)
    mhat = gated * ginv
    pair_ref[1] = (mhat * gain_ref[...]).astype(BF16)
    gm = gm_ref[...]
    ggain_ref[...] += jnp.sum(mhat * gm, axis=0, keepdims=True)
    gmg = gm * gain_ref[...]
    ggated = ginv * (gmg - mhat * jnp.mean(mhat * gmg, axis=1, keepdims=True))
    dy = ggated * silu_z
    dy_ref[...] = dy
    grad_z = ggated * scanned * (sig_z * (1.0 + z * (1.0 - sig_z)))
    zmax_ref[...] = jnp.maximum(zmax_ref[...], jnp.max(jnp.abs(grad_z), axis=0, keepdims=True))
    pair_ref[0] = grad_z.astype(BF16)
    through_ref[...] = head_sum(dy * (scanned - skip_ref[...] * x), et_ref)

    @pl.when(step == pl.num_programs(0) - 1)
    def _():
        count = float(Q * pl.num_programs(0))
        largest = jnp.max(zmax_ref[...], axis=1, keepdims=True)
        normed = jnp.max(jnp.abs(norm_ref[...]), axis=1, keepdims=True) * (D ** 0.5)
        mixed = jnp.max(jnp.abs(gain_ref[...]), axis=1, keepdims=True) * (INNER ** 0.5)
        power_ref[...] = jnp.broadcast_to(power_for(
            1.05 * count * jnp.maximum(largest * normed, cot_ref[0] * mixed)), (8, 128))


def const_spec(shape):
    return pl.BlockSpec(shape, lambda *_: (0,) * len(shape))


def run_forward(z, proj, gm, bound, cot_top, norm_gain, e2, et, params):
    n = proj.shape[0]
    steps = n // Q
    return pl.pallas_call(
        forward_kernel,
        grid=(steps,),
        in_specs=[
            pl.BlockSpec(memory_space=pltpu.SMEM), pl.BlockSpec(memory_space=pltpu.SMEM),
            pl.BlockSpec((Q, INNER), lambda i: (i, 0)),
            pl.BlockSpec((Q, LATE), lambda i: (i, 0)),
            pl.BlockSpec((Q, INNER), lambda i: (i, 0)),
            const_spec((1, D)),
            const_spec((256, INNER)), const_spec((INNER, 128)),
            const_spec((8, XBC)), const_spec((1, XBC)), const_spec((1, 128)),
            const_spec((1, 128)), const_spec((1, INNER)), const_spec((1, INNER)),
        ],
        out_specs=[
            pl.BlockSpec((2, Q, INNER), lambda i: (0, i, 0)),
            pl.BlockSpec((Q, INNER), lambda i: (i, 0)),
            pl.BlockSpec((Q, 128), lambda i: (i, 0)),
            pl.BlockSpec((1, STATE, INNER), lambda i: (i, 0, 0)),
            const_spec((1, INNER)), const_spec((8, 128)),
        ],
        out_shape=[
            jax.ShapeDtypeStruct((2, n, INNER), BF16),
            jax.ShapeDtypeStruct((n, INNER), F32),
            jax.ShapeDtypeStruct((n, 128), F32),
            jax.ShapeDtypeStruct((steps, STATE, INNER), F32),
            jax.ShapeDtypeStruct((1, INNER), F32),
            jax.ShapeDtypeStruct((8, 128), F32),
        ],
        scratch_shapes=[
            pltpu.VMEM((1, INNER), F32),
            pltpu.VMEM((Q + 8, XBC), F32),
            pltpu.VMEM((Q, 128), F32),
            pltpu.VMEM((STATE, INNER), F32),
            pltpu.VMEM((Q, INNER), F32),
            pltpu.VMEM((Q, INNER), F32),
            pltpu.VMEM((128, Q), F32),
        ],
        compiler_params=pltpu.CompilerParams(
            dimension_semantics=("arbitrary",), vmem_limit_bytes=48 * 2**20),
        cost_estimate=pl.CostEstimate(
            flops=30 * 10**9, bytes_accessed=40 * 2**20, transcendentals=10**7),
    )(bound, cot_top, z, proj, gm, norm_gain, e2, et, *params)


def backward_kernel(
    bound_ref, proj_ref, before_ref, dy_ref, through_ref, state_ref, gz_ref, tok_ref, cot_ref,
    in_ref, norm_ref, ggain_ref,
    e_ref, et_ref, convw_ref, convb_ref, dtb_ref, alog_ref, skip_ref,
    window_ref, gtok_ref, small_ref, power_ref,
    total_ref, gskip_ref, gsmall_ref, dtw_ref, gp_ref, ext_ref, dt_ref, lam_ref, dsum_ref, xd_ref, g_ref, gnext_ref, cumt_ref,
):
    step = pl.program_id(0)
    steps = pl.num_programs(0)
    bound = bound_ref[0]
    t0 = (steps - 1 - step) * Q

    @pl.when(step == 0)
    def _():
        lam_ref[...] = jnp.zeros_like(lam_ref)
        dsum_ref[...] = jnp.zeros_like(dsum_ref)
        dt_ref[...] = jnp.zeros_like(dt_ref)
        gnext_ref[Q : Q + 8, :] = jnp.zeros((8, XBC), F32)
        gskip_ref[...] = jnp.zeros_like(gskip_ref)
        total_ref[...] = jnp.zeros_like(total_ref)
        dtw_ref[...] = jnp.zeros_like(dtw_ref)
        gsmall_ref[...] = jnp.zeros_like(gsmall_ref)

    rows, rr, cc = chunk_masks(t0, bound)
    dy = dy_ref[...]
    first_chunk = (t0 > 0).astype(F32)
    ext_ref[0:8, :] = before_ref[:, :XBC] * first_chunk
    ext_ref[8 : 8 + Q, :] = proj_ref[:, :XBC]
    pre = conv_rows(ext_ref, convw_ref, convb_ref, rows, bound)
    sig_pre = sigmoid(pre)
    conv_out = pre * sig_pre
    x = conv_out[:, :INNER]
    b_rows = conv_out[:, INNER : INNER + STATE]
    c_rows = conv_out[:, INNER + STATE :]
    dt_ref[:, 0:HEADS] = proj_ref[:, XBC:LATE]
    dt_in, dt_pos, rate, cum = decay_parts(dt_ref[...], dtb_ref, alog_ref, rr, cc)
    cum_end = cum[Q - 1 : Q, :]
    keep = jnp.logical_or(rows < bound, bound < t0).astype(F32)
    in_last = jnp.logical_or(rows >= bound, bound > t0 + Q - 1).astype(F32)
    whole = jnp.logical_or(bound < t0, bound > t0 + Q - 1).astype(F32)
    from_start = jnp.exp(cum) * keep
    to_end = jnp.exp(cum_end - cum) * in_last
    carry_scale = jnp.exp(cum_end) * whole
    allowed_t = jnp.logical_and(rr <= cc, (cc >= bound) == (rr >= bound))
    cum2 = cum * LOG2E
    cumt_ref[...] = cum2.T
    c_t = c_rows.T
    gram_t = dot(wide_left(b_rows), tall_right(c_t))
    spread = expand(jnp.concatenate(
        [dt_pos, to_end, from_start, jnp.broadcast_to(carry_scale, (16, 128))], axis=0), e_ref)
    dt_all = spread[:Q]
    end_all = spread[Q : 2 * Q]
    xd = x * dt_all
    xd_ref[...] = xd
    skip = skip_ref[...]
    gskip_ref[...] += jnp.sum(dy * x, axis=0, keepdims=True)
    lam = lam_ref[...]
    lam_hi, lam_lo = split2(lam)
    g_ref[...] = (
        dot(wide_left(b_rows), jnp.concatenate([lam_hi, lam_hi, lam_lo], axis=0)) * end_all
    )
    grad_b = quarters(dot_nt(
        jnp.concatenate(split2(xd * end_all), axis=0), jnp.concatenate([lam_hi, lam_lo], axis=0)))
    state = state_ref[0]
    dye_hi, dye_lo = split2(dy * spread[2 * Q : 3 * Q])
    grad_c = quarters(dot_nt(
        jnp.concatenate([dye_hi, dye_lo], axis=0), jnp.concatenate(split2(state), axis=0)))
    lam_new = lam * spread[3 * Q : 3 * Q + 1] + dot(
        wide_left(c_t), jnp.concatenate([dye_hi, dye_hi, dye_lo], axis=0)
    )
    lam_ref[...] = lam_new
    ended = dsum_ref[0:1, :]
    first = iota((Q, Q), 1) < HEADDIM
    first_b = (first.astype(F32).astype(BF16), 1.0 - first.astype(F32).astype(BF16))
    first_row = (iota((Q, Q), 0) < HEADDIM).astype(F32).astype(BF16)
    first_row = (first_row, 1.0 - first_row)
    gram_grad = jnp.zeros((Q, Q), F32)
    for pair in range(PAIRS):
        lanes = slice(pair * 128, pair * 128 + 128)
        weights = []
        for head in (2 * pair, 2 * pair + 1):
            differ = cumt_ref[head : head + 1, :] - cum2[:, head : head + 1]
            weights.append(jnp.exp2(jnp.where(allowed_t, differ, NEG)))
        left = jnp.concatenate([gram_t * weights[0], gram_t * weights[1]], axis=1)
        left = jnp.concatenate(split2(left), axis=0)
        dyp = dy_ref[:, lanes]
        out = dot(left, split_pair(dyp, first_b))
        g_ref[:, lanes] += out[:Q, :128] + (out[:Q, 128:] + out[Q:, :128])
        dyt_hi, dyt_lo = split2(dyp.T)
        right_hi = jnp.concatenate([dyt_hi * first_row[0], dyt_hi * first_row[1]], axis=1)
        right_lo = jnp.concatenate([dyt_lo * first_row[0], dyt_lo * first_row[1]], axis=1)
        outer = dot(
            wide_left(xd_ref[:, lanes]), jnp.concatenate([right_hi, right_hi, right_lo], axis=0))
        gram_grad = gram_grad + (outer[:, :128] * weights[0] + outer[:, 128:] * weights[1])
    g = g_ref[...]
    grad_x = dt_all * g + skip * dy
    sums = dot(jnp.concatenate(
        split2(x * g) + split2(jnp.broadcast_to(
            jnp.sum(lam_new * state, axis=0, keepdims=True), (16, INNER))), axis=0), et_ref[...])
    direct = sums[:Q] + sums[Q : 2 * Q]
    balance = through_ref[...] - dt_pos * direct
    keep_t = allowed_t.astype(F32).astype(BF16)
    b_hi, b_mid, b_lo = split3(balance)
    grad_step = dot(keep_t, b_hi) + dot(keep_t, b_mid) + dot(keep_t, b_lo) + in_last * ended
    dsum_ref[...] = sums[2 * Q : 2 * Q + 8] + sums[2 * Q + 16 : 2 * Q + 24]
    grad_dt = (direct + rate * grad_step) * sigmoid(dt_in)
    gsmall_ref[0:1, :] += jnp.sum(grad_dt, axis=0, keepdims=True)
    gsmall_ref[1:2, :] += rate * jnp.sum(dt_pos * grad_step, axis=0, keepdims=True)
    grad_c = grad_c + dot(wide_left(gram_grad.T), tall_right(b_rows))
    grad_b = grad_b + dot(wide_left(gram_grad), tall_right(c_rows))
    slope = sig_pre * (1.0 + pre * (1.0 - sig_pre))
    gnext_ref[0:Q, :INNER] = grad_x * slope[:, :INNER]
    gnext_ref[0:Q, INNER : INNER + STATE] = grad_b * slope[:, INNER : INNER + STATE]
    gnext_ref[0:Q, INNER + STATE :] = grad_c * slope[:, INNER + STATE :]
    gcp = gnext_ref[0:Q, :]
    total_ref[4:5, :] += jnp.sum(gcp, axis=0, keepdims=True)
    total_ref[3:4, :] += jnp.sum(gcp * ext_ref[8 : 8 + Q, :], axis=0, keepdims=True)
    total = convw_ref[3:4, :] * gcp
    for back in (1, 2, 3):
        ok = jnp.logical_or(rows - back >= bound, rows < bound).astype(F32)
        total_ref[3 - back : 4 - back, :] += jnp.sum(
            gcp * (ext_ref[8 - back : 8 - back + Q, :] * ok), axis=0, keepdims=True)
        okn = jnp.logical_or(rows >= bound, rows + back < bound).astype(F32)
        total = total + convw_ref[3 - back : 4 - back, :] * (gnext_ref[back : back + Q, :] * okn)
    total_ref[7:8, :] = jnp.maximum(
        total_ref[7:8, :], jnp.max(jnp.abs(total), axis=0, keepdims=True))
    total = total.astype(BF16)
    window_ref[0] = total[:, :WINDOW]
    window_ref[1] = total[:, XBC - WINDOW :]
    gnext_ref[Q : Q + 8, :] = gnext_ref[0:8, :]
    half = (steps - 1 - step) % 2
    at = pl.multiple_of(half * Q, Q)
    gp_ref[pl.ds(at, Q), :INNER] = gz_ref[0]
    gp_ref[pl.ds(at, Q), INNER : INNER + XBC] = total
    gp_ref[pl.ds(at, Q), INNER + XBC :] = grad_dt.astype(BF16)

    @pl.when(half == 0)
    def _():
        grad_normed = dot(gp_ref[...], in_ref[: INNER + XBC + 128, :])
        tok = tok_ref[...].astype(F32)
        rinv = lax.rsqrt(jnp.mean(tok * tok, axis=1, keepdims=True) + EPS_NORM)
        nhat = tok * rinv
        gain = norm_ref[...]
        gng = grad_normed * gain
        gtok_ref[...] = (cot_ref[...].astype(F32) + rinv * (
            gng - nhat * jnp.mean(nhat * gng, axis=1, keepdims=True))).astype(BF16)
        total_ref[6:7, :D] += jnp.sum(nhat * grad_normed, axis=0, keepdims=True)
        normed = (nhat * gain).astype(BF16)
        gdt = gp_ref[:, INNER + XBC :].astype(F32)
        dtw_ref[...] += dot(jnp.concatenate(
            [gdt[:Q].T, gdt[Q:].T], axis=1).astype(BF16), normed)

    @pl.when(step == steps - 1)
    def _():
        skips = head_sum(jnp.broadcast_to(gskip_ref[...], (8, INNER)), et_ref)
        small_ref[...] = jnp.zeros_like(small_ref)
        small_ref[0:HEADS, :] = dtw_ref[0:HEADS, :]
        pieces = [
            total_ref[k : k + 1, j * 128 : j * 128 + 128]
            for k in range(CONV + 1) for j in range(XBC // 128)]
        pieces += [gsmall_ref[0:1, :], gsmall_ref[1:2, :], skips[0:1, :]]
        pieces += [ggain_ref[:, j * 128 : j * 128 + 128] for j in range(INNER // 128)]
        lines = D // 128
        for number, piece in enumerate(pieces):
            line = HEADS + number // lines
            at = number % lines * 128
            small_ref[line : line + 1, at : at + 128] = piece
        small_ref[40:41, :] = total_ref[6:7, :D]
        count = float(Q * steps)
        largest = jnp.max(total_ref[7:8, :], axis=1, keepdims=True)
        normed = jnp.max(jnp.abs(norm_ref[...]), axis=1, keepdims=True) * (D ** 0.5)
        others = jnp.max(jnp.max(jnp.abs(small_ref[...]), axis=1, keepdims=True), axis=0, keepdims=True)
        power_ref[...] = jnp.broadcast_to(power_for(
            jnp.maximum(1.05 * count * largest * normed, others)), (8, 128))


def run_backward(
    proj, dy, through, states, pair, tok, cot, in_w, norm_gain, ggain, bound, e2, et, params
):
    n = proj.shape[0]
    steps = n // Q

    def rev(i):
        return (steps - 1 - i, 0)

    def rev_two(i):
        return ((steps - 1 - i) // 2, 0)

    return pl.pallas_call(
        backward_kernel,
        grid=(steps,),
        in_specs=[
            pl.BlockSpec(memory_space=pltpu.SMEM),
            pl.BlockSpec((Q, LATE), rev),
            pl.BlockSpec((8, LATE), lambda i: (jnp.maximum((steps - 1 - i) * (Q // 8) - 1, 0), 0)),
            pl.BlockSpec((Q, INNER), rev),
            pl.BlockSpec((Q, 128), rev),
            pl.BlockSpec((1, STATE, INNER), lambda i: (steps - 1 - i, 0, 0)),
            pl.BlockSpec((1, Q, INNER), lambda i: (0, steps - 1 - i, 0)),
            pl.BlockSpec((2 * Q, D), rev_two), pl.BlockSpec((2 * Q, D), rev_two),
            const_spec(in_w.shape), const_spec((1, D)), const_spec((1, INNER)),
            const_spec((256, INNER)), const_spec((INNER, 128)),
            const_spec((8, XBC)), const_spec((1, XBC)), const_spec((1, 128)),
            const_spec((1, 128)), const_spec((1, INNER)),
        ],
        out_specs=[
            pl.BlockSpec((2, Q, WINDOW), lambda i: (0, steps - 1 - i, 0)),
            pl.BlockSpec((2 * Q, D), rev_two),
            const_spec((48, D)), const_spec((8, 128)),
        ],
        out_shape=[
            jax.ShapeDtypeStruct((2, n, WINDOW), BF16),
            jax.ShapeDtypeStruct((n, D), BF16),
            jax.ShapeDtypeStruct((48, D), F32),
            jax.ShapeDtypeStruct((8, 128), F32),
        ],
        scratch_shapes=[
            pltpu.VMEM((8, XBC), F32),
            pltpu.VMEM((1, INNER), F32),
            pltpu.VMEM((8, 128), F32),
            pltpu.VMEM((128, D), F32),
            pltpu.VMEM((2 * Q, INNER + XBC + 128), BF16),
            pltpu.VMEM((Q + 8, XBC), F32),
            pltpu.VMEM((Q, 128), F32),
            pltpu.VMEM((STATE, INNER), F32),
            pltpu.VMEM((8, 128), F32),
            pltpu.VMEM((Q, INNER), F32),
            pltpu.VMEM((Q, INNER), F32),
            pltpu.VMEM((Q + 8, XBC), F32),
            pltpu.VMEM((128, Q), F32),
        ],
        compiler_params=pltpu.CompilerParams(
            dimension_semantics=("arbitrary",), vmem_limit_bytes=48 * 2**20),
        cost_estimate=pl.CostEstimate(
            flops=50 * 10**9, bytes_accessed=50 * 2**20, transcendentals=2 * 10**7),
    )(bound, proj, proj, dy, through, states, pair, tok, cot, in_w, norm_gain, ggain,
      e2, et, *params[:5])


BETA_ONE = 0.9
BETA_TWO = 0.95
EPS_ADAM = 1e-08
LANES = 128
NORM_ROWS = D // LANES
IN_ROWS = PROJ * D // LANES
CONVW_ROWS = CONV * XBC // LANES
CONVB_ROWS = XBC // LANES
GAIN_ROWS = INNER // LANES
OUT_ROWS = INNER * D // LANES
DT_ROWS = HEADS * D // LANES
SMALL_ROWS = DT_ROWS + CONVW_ROWS + CONVB_ROWS + 3 + GAIN_ROWS
OUT_START = NORM_ROWS + IN_ROWS + SMALL_ROWS - DT_ROWS
LATE_START = NORM_ROWS + INNER * NORM_ROWS
LEAD = 896
STAGE_ROWS = 16264
STAGE_BLOCKS = 5
MARK = 16


PREP_STEPS = 7
IN_BLOCK = 512
OUT_BLOCK = 256
SMALL_START = NORM_ROWS + IN_ROWS


def prepare_kernel(
    flat_ref,
    in_ref, out_ref, norm_ref, convw_ref, convb_ref, dtb_ref, alog_ref, skip_ref, gain_ref,
    e_ref, et_ref,
    stage_ref,
):
    step = pl.program_id(0)

    @pl.when(step == 0)
    def _():
        rows = flat_ref[0:16, :].astype(F32)
        for lane in range(NORM_ROWS):
            norm_ref[:, lane * LANES : lane * LANES + LANES] = rows[lane : lane + 1, :]
        low = SMALL_START // 16 * 16
        stage_ref[0:112, :] = flat_ref[low : low + 112, :].astype(F32)
        at = SMALL_START - low
        convw_ref[...] = jnp.zeros_like(convw_ref)
        for tap in range(CONV):
            for lane in range(CONVB_ROWS):
                convw_ref[tap : tap + 1, lane * LANES : lane * LANES + LANES] = stage_ref[
                    at : at + 1, :]
                at += 1
        for lane in range(CONVB_ROWS):
            convb_ref[:, lane * LANES : lane * LANES + LANES] = stage_ref[at : at + 1, :]
            at += 1
        heads = iota((1, LANES), 1) < HEADS
        dtb_ref[...] = jnp.where(heads, stage_ref[at : at + 1, :], 0.0)
        alog_ref[...] = jnp.where(heads, stage_ref[at + 1 : at + 2, :], 0.0)
        skips = jnp.where(heads, stage_ref[at + 2 : at + 3, :], 0.0)
        at += 3
        for lane in range(GAIN_ROWS):
            gain_ref[:, lane * LANES : lane * LANES + LANES] = stage_ref[at : at + 1, :]
            at += 1
        one = (iota((128, INNER), 1) // HEADDIM == iota((128, INNER), 0)).astype(F32).astype(BF16)
        e_ref[0:128, :] = one
        e_ref[128:256, :] = one
        et_ref[...] = (
            iota((INNER, 128), 0) // HEADDIM == iota((INNER, 128), 1)).astype(F32).astype(BF16)
        skip_ref[...] = dot(jnp.broadcast_to(skips, (16, LANES)).astype(BF16), one)[0:1, :]

    def block(start, offset, rows, dest_ref):
        size = rows * NORM_ROWS + 16
        at = pl.multiple_of(start + step * (rows * NORM_ROWS), 16)
        stage_ref[0:size, :] = flat_ref[pl.ds(at, size), :].astype(F32)
        for lane in range(NORM_ROWS):
            dest_ref[:, lane * LANES : lane * LANES + LANES] = stage_ref[
                pl.ds(offset + lane, rows, stride=NORM_ROWS), :].astype(BF16)

    block(0, NORM_ROWS, IN_BLOCK, in_ref)

    @pl.when(step == PREP_STEPS - 1)
    def _():
        used = PROJ - (PREP_STEPS - 1) * IN_BLOCK
        in_ref[used:, :] = jnp.zeros((IN_BLOCK - used, D), BF16)

    @pl.when(step < INNER // OUT_BLOCK)
    def _():
        low = OUT_START // 16 * 16
        block(low, OUT_START - low, OUT_BLOCK, out_ref)


def run_prepare(flat):
    vector = lambda n: jax.ShapeDtypeStruct((1, n), F32)
    return pl.pallas_call(
        prepare_kernel,
        grid=(PREP_STEPS,),
        in_specs=[const_spec(flat.shape)],
        out_specs=[
            pl.BlockSpec((IN_BLOCK, D), lambda i: (i, 0)),
            pl.BlockSpec((OUT_BLOCK, D), lambda i: (jnp.minimum(i, INNER // OUT_BLOCK - 1), 0)),
            const_spec((1, D)), const_spec((8, XBC)), const_spec((1, XBC)), const_spec((1, 128)),
            const_spec((1, 128)), const_spec((1, INNER)), const_spec((1, INNER)),
            const_spec((256, INNER)), const_spec((INNER, 128)),
        ],
        out_shape=[
            jax.ShapeDtypeStruct((PREP_STEPS * IN_BLOCK, D), BF16),
            jax.ShapeDtypeStruct((INNER, D), BF16),
            vector(D), jax.ShapeDtypeStruct((8, XBC), F32), vector(XBC), vector(128), vector(128),
            vector(INNER), vector(INNER),
            jax.ShapeDtypeStruct((256, INNER), BF16), jax.ShapeDtypeStruct((INNER, 128), BF16),
        ],
        scratch_shapes=[pltpu.VMEM((IN_BLOCK * NORM_ROWS + 16, LANES), F32)],
        compiler_params=pltpu.CompilerParams(
            dimension_semantics=("arbitrary",), vmem_limit_bytes=40 * 2**20),
        cost_estimate=pl.CostEstimate(
            flops=10**9, bytes_accessed=16 * 2**20, transcendentals=0),
    )(flat)


def stage_kernel(
    who_ref, early_ref, early_other_ref, late_ref, late_other_ref, small_ref,
    grad_ref,
    stage_ref,
):
    step = pl.program_id(0)
    upper = who_ref[0]
    mine = who_ref[1]
    block = grad_ref.shape[0]
    half = 2 * block * STAGE_BLOCKS

    @pl.when(step == 0)
    def _():
        early_at = LEAD + jnp.where(upper == 1, OUT_START - half, NORM_ROWS)
        window = LATE_START + (XBC - WINDOW) * NORM_ROWS
        late_at = LEAD + jnp.where(upper == 1, window - half, LATE_START)
        def lay(source_ref, start, size):
            for lane in range(NORM_ROWS):
                stage_ref[pl.ds(start + lane, size, stride=NORM_ROWS), :] = source_ref[
                    0:size, lane * LANES : lane * LANES + LANES]

        lines = late_ref.shape[0]
        lay(late_ref, late_at + mine * (lines * NORM_ROWS), lines)
        lay(late_other_ref, late_at + (1 - mine) * (lines * NORM_ROWS), lines)

        @pl.when(upper == 1)
        def _():
            lay(small_ref, LEAD + OUT_START - half - SMALL_ROWS, -(-SMALL_ROWS // NORM_ROWS))

        lines = early_ref.shape[0]
        lay(early_ref, early_at + mine * (lines * NORM_ROWS), lines)
        lay(early_other_ref, early_at + (1 - mine) * (lines * NORM_ROWS), lines)

        @pl.when(upper == 0)
        def _():
            for lane in range(NORM_ROWS):
                stage_ref[LEAD + lane : LEAD + lane + 1, :] = small_ref[
                    40:41, lane * LANES : lane * LANES + LANES]

        @pl.when(upper == 1)
        def _():
            at = LEAD + OUT_START + OUT_ROWS - half
            stage_ref[at : LEAD + half, :] = jnp.zeros((LEAD + half - at, LANES), F32)

    @pl.when(step > 0)
    def _():
        at = LEAD + mine * (half // 2) + (step - 1) * block
        grad_ref[...] = stage_ref[pl.ds(pl.multiple_of(at, 8), block), :]


def run_stage(who, rows, early, early_other, late, late_other, small):
    block = rows // STAGE_BLOCKS
    return pl.pallas_call(
        stage_kernel,
        grid=(STAGE_BLOCKS + 1,),
        in_specs=[
            pl.BlockSpec(memory_space=pltpu.SMEM),
            const_spec(early.shape), const_spec(early.shape),
            const_spec(late.shape), const_spec(late.shape), const_spec(small.shape),
        ],
        out_specs=pl.BlockSpec((block, LANES), lambda i: (jnp.maximum(i - 1, 0), 0)),
        out_shape=jax.ShapeDtypeStruct((rows, LANES), F32),
        scratch_shapes=[pltpu.VMEM((STAGE_ROWS, LANES), F32)],
        compiler_params=pltpu.CompilerParams(
            dimension_semantics=("arbitrary",), vmem_limit_bytes=48 * 2**20),
        cost_estimate=pl.CostEstimate(
            flops=10**6, bytes_accessed=12 * 2**20, transcendentals=0),
    )(who, early, early_other, late, late_other, small)


def swap(values, axis, bit):
    size = lax.axis_size(axis)
    return lax.ppermute(values, axis, [(i, i ^ bit) for i in range(size)])


def to_wire(values, power):
    return (values * jnp.exp2(power)).astype(jnp.float16)


def from_wire(values, power):
    return values.astype(F32) * jnp.exp2(-power)


def scatter(values, power, axis, bit=1, count=2, after=None, sent=None):
    place = (lax.axis_index(axis) // bit) % count
    rows = values.shape[-2] // count
    mark = min(MARK, rows)
    dim = values.ndim - 2
    total = lax.dynamic_slice_in_dim(values, place * rows, rows, dim)
    least = power
    arrived = []
    for offset in range(1, count):
        to = place ^ offset
        last = to == count - 1
        start = to * rows - jnp.where(last, mark, 0)
        send = lax.dynamic_slice_in_dim(values, start, rows + mark, dim)
        line = lax.broadcasted_iota(jnp.int32, send.shape, dim)
        marked = jnp.where(last, line < mark, line >= rows)
        wire = jnp.where(marked, power, send * jnp.exp2(power)).astype(jnp.float16)
        arrived.append(swap(wire, axis, bit * offset))
        if sent is not None:
            sent.append(wire)
    if after is not None:
        arrived, _ = lax.optimization_barrier((arrived, after))
    last = place == count - 1
    for got in arrived:
        got_power = lax.dynamic_slice_in_dim(got, jnp.where(last, 0, rows), 1, dim)
        got_power = got_power.reshape(-1, D)[0:1, 0:1].astype(F32)
        body = lax.dynamic_slice_in_dim(got, jnp.where(last, mark, 0), rows, dim)
        total = total + from_wire(body, got_power)
        least = jnp.minimum(least, got_power)
    return total, least - float(count.bit_length() - 1)


def scatter_product(left, right, power, axis, bit):
    def product(part):
        return lax.dot_general(
            part, right, (((1,), (1,)), ((0,), (0,))), preferred_element_type=F32)

    side = (lax.axis_index(axis) // bit) % 2
    rows = left.shape[2] // 2
    send = product(jnp.where(side == 1, left[:, :, : rows + LANES], left[:, :, rows - LANES :]))
    line = lax.broadcasted_iota(jnp.int32, send.shape, 1)
    marked = jnp.where(side == 1, line >= rows, line < LANES)
    wire = jnp.where(marked, power, send * jnp.exp2(power)).astype(jnp.float16)
    got = swap(wire, axis, bit)
    left, _ = lax.optimization_barrier((left, wire))
    keep = product(jnp.where(side == 0, left[:, :, :rows], left[:, :, rows:]))
    keep, got = lax.optimization_barrier((keep, got))
    got_power = lax.dynamic_slice(
        got, (0, (1 - side) * rows, 0), (1, 1, LANES))[0, :, 0:1].astype(F32)
    body = lax.dynamic_slice_in_dim(got, side * LANES, rows, 1)
    return keep + from_wire(body, got_power), jnp.minimum(power, got_power) - 1.0


def everyones(values, axis, bit=1, count=2):
    place = (lax.axis_index(axis) // bit) % count
    pieces = [values] + [swap(values, axis, bit * offset) for offset in range(1, count)]
    step = 1
    while step < count:
        flip = (place // step) % 2 == 1
        pieces = [
            jnp.where(flip, pieces[i ^ step], pieces[i]) for i in range(count)]
        step *= 2
    return pieces


def gather(values, axis, bit=1, count=2):
    return jnp.concatenate(everyones(values, axis, bit, count))


def add_pair(values, axis, bit, after=None):
    got = swap(values, axis, bit)
    if after is not None:
        got, _ = lax.optimization_barrier((got, after))
    return values + got


def data_groups():
    size = lax.axis_size("dp")
    groups = [(1, 2)]
    bit = 2
    while bit < size:
        count = 4 if bit * 4 <= size else 2
        groups.append((bit, count))
        bit *= count
    return groups


def dot_tn(a, b):
    return lax.dot_general(a, b, (((0,), (0,)), ((), ())), preferred_element_type=F32)


def pick_rows(index, rows):
    chosen = index[:, None] == jnp.arange(rows.shape[0], dtype=jnp.int32)[None, :]
    return dot(chosen.astype(BF16), rows).astype(BF16)


def on_device(
    tokens, loss_sensitivity, lengths, holder_sequence_list, master, moment_one, moment_two,
    adam_rates, iteration_tally,
):
    group_devices = lax.axis_size("zero")
    data_devices = lax.axis_size("dp")
    zero_index = lax.axis_index("zero")
    dp_index = lax.axis_index("dp")
    seq_len = loss_sensitivity.shape[1]
    group_seqs = tokens.shape[0]
    span = tokens.shape[1]
    slots = group_seqs // data_devices
    shard_rows = master.shape[0] // LANES
    tie = lax.optimization_barrier

    own = master.reshape(shard_rows, LANES)
    arranged = holder_sequence_list.reshape(data_devices, group_devices, slots)
    group_order = lax.dynamic_index_in_dim(arranged, zero_index, 1, keepdims=False).reshape(-1)
    local_ids = group_order - zero_index * group_seqs
    dealt = tokens.at[local_ids].get(mode="promise_in_bounds")
    flat = lax.all_gather(own.astype(BF16), "zero", axis=0, tiled=True)

    local_tok = lax.all_to_all(dealt, "dp", split_axis=0, concat_axis=0, tiled=True)
    my_seqs = lax.dynamic_slice_in_dim(group_order, dp_index * slots, slots)
    bound = lengths[my_seqs[0]]
    positions = jnp.arange(seq_len, dtype=jnp.int32)

    in_w, out_w, norm_gain, *params, e2, et = run_prepare(flat)
    cot = loss_sensitivity[0]
    gm = dot_nt(cot, out_w)
    cot_top = jnp.max(jnp.abs(cot)).astype(F32).reshape(1)
    local_tok, in_w, gm, cot_top = tie((local_tok, in_w, gm, cot_top))
    own_late, _ = tie((own, flat[:8]))
    whole_master = lax.all_gather(own_late, "zero", axis=0, tiled=True)

    def place(slot, at):
        return (at // span) * (slots * span) + slot * span + at % span

    source = jnp.where(positions < bound, place(0, positions), place(1, positions - bound))
    packed = pick_rows(source, local_tok.reshape(slots * seq_len, D))
    blocks = jnp.arange(data_devices, dtype=jnp.int32)[:, None, None] * span
    within = blocks + jnp.arange(span, dtype=jnp.int32)[None, None, :]
    within = within + jnp.arange(slots, dtype=jnp.int32)[None, :, None] * bound
    unpack_rows = jnp.minimum(within, seq_len - 1).reshape(-1)

    def spread(rows):
        return pick_rows(unpack_rows, rows).reshape(data_devices * slots, span, D)

    def send_back(picked):
        return lax.all_to_all(picked, "dp", split_axis=0, concat_axis=0, tiled=True)

    restore = jnp.zeros_like(local_ids).at[local_ids].set(
        jnp.arange(group_seqs, dtype=jnp.int32))
    mine = lax.dynamic_slice_in_dim(lengths, zero_index * group_seqs, group_seqs)
    at = dp_index * span + jnp.arange(span, dtype=jnp.int32)
    live = (at[None, :] < mine[:, None])[:, :, None]

    bound_arr = bound.reshape(1)
    tok = packed.astype(F32)
    nhat = tok * lax.rsqrt(jnp.mean(tok * tok, axis=1, keepdims=True) + EPS_NORM)
    normed = (nhat * norm_gain).astype(BF16)
    proj_z = dot_nt(normed, in_w[:INNER])
    proj = dot_nt(normed, in_w[INNER:PROJ])
    pair, dy, through, states, ggain, early_power = run_forward(
        proj_z, proj, gm, bound_arr, cot_top, norm_gain, e2, et, params)
    result = (tok + dot(pair[1], out_w)).astype(BF16)
    picked = spread(result)
    picked, pair = tie((picked, pair))
    back_out = send_back(picked)
    early_power = early_power[0:1, 0:1]
    early, early_power = scatter_product(
        pair, jnp.stack([normed, cot]), early_power, "zero", 1)
    early, early_power, dy = tie((early.reshape(INNER, D), early_power, dy))
    early, early_power = scatter(early, early_power, "zero", 2)
    window, grad_tok, small, late_power = run_backward(
        proj, dy, through, states, pair, packed, cot, in_w, norm_gain, ggain,
        bound_arr, e2, et, params)
    window, small, late_power, early, early_power, whole_master = tie(
        (window, small, late_power, early, early_power, whole_master))

    groups = data_groups()
    late_power = late_power[0:1, 0:1]
    late, late_power = scatter_product(
        window, jnp.stack([normed, normed]), late_power, "zero", 1)
    late = late.reshape(WINDOW, D)
    small = add_pair(small, "zero", 1)
    early, early_power, grad_tok, _ = tie((early, early_power, grad_tok, late))
    late, late_power = scatter(late, late_power, "zero", 2)
    early, early_power = scatter(early, early_power, "dp", *groups[0])
    small = add_pair(small, "zero", 2, late)
    early_before, power_before = early, early_power
    picked_grad = spread(grad_tok)
    tokens, back_out, _ = tie((tokens, back_out, grad_tok))
    back_rows = back_out.at[restore].get(mode="promise_in_bounds")
    tokens_out = jnp.where(live, back_rows, tokens)
    new_master = jnp.zeros((group_devices, shard_rows, LANES), F32)
    late, tokens_out, new_master, picked_grad = tie((late, tokens_out, new_master, picked_grad))
    lines = small.shape[0]
    late = jnp.concatenate([late, small, jnp.zeros((WINDOW // 8 - lines, D), F32)])
    late, late_power = scatter(late, late_power, "dp", *groups[0])
    sent = []
    for group in groups[1:]:
        late, late_power = scatter(late, late_power, "dp", *group, sent=sent)
    early, early_power = early_before, power_before
    for group in groups[1:]:
        early, early_power = scatter(early, early_power, "dp", *group, after=sent)
    early = to_wire(early, early_power)
    for group in reversed(groups[1:]):
        early = gather(early, "dp", *group)
    early, _ = tie((early, late))
    late = to_wire(late, late_power)
    early = from_wire(gather(early, "dp", *groups[0]), early_power)
    early, picked_grad, _ = tie((early, picked_grad, late))
    for group in reversed(groups[1:]):
        late = gather(late, "dp", *group)
    early_other = swap(early, "zero", 1)
    back_grad = send_back(picked_grad)
    wire = gather(late, "dp", *groups[0])
    late = from_wire(wire[: WINDOW // 2], late_power)
    small = from_wire(wire[WINDOW // 2 : WINDOW // 2 + lines], late_power)
    late_other = swap(late, "zero", 1)

    steps_f = iteration_tally[0].astype(F32)
    who = jnp.stack([zero_index // 2, zero_index % 2]).astype(jnp.int32)
    first = moment_one.reshape(shard_rows, LANES)
    second = moment_two.reshape(shard_rows, LANES)
    grad_shard = run_stage(who, shard_rows, early, early_other, late, late_other, small)
    first_scale = 1.0 / (1.0 - jnp.power(BETA_ONE, steps_f))
    second_scale = 1.0 / (1.0 - jnp.power(BETA_TWO, steps_f))

    def moments(grad, first, second):
        return (
            BETA_ONE * first + (1.0 - BETA_ONE) * grad,
            BETA_TWO * second + (1.0 - BETA_TWO) * grad * grad)

    def quotient(rows):
        first_next, second_next = moments(grad_shard[rows], first[rows], second[rows])
        return ((first_next * first_scale) / (
            jnp.sqrt(second_next * second_scale) + EPS_ADAM)).astype(jnp.float16)

    whole_master = whole_master.reshape(group_devices, shard_rows, LANES)

    def put(new_master, piece, offset):
        shard = zero_index ^ offset
        old = lax.dynamic_index_in_dim(whole_master, shard, 0, keepdims=False)
        new = old - adam_rates[0] * (piece.astype(F32) + adam_rates[1] * old)
        return lax.dynamic_update_index_in_dim(new_master, new, shard, 0)

    own_part, first, second = tie((quotient(slice(0, shard_rows)), first, second))
    across = swap(own_part, "zero", 2)
    core = swap(own_part, "zero", 1)
    first_next, second_next = moments(grad_shard, first, second)
    new_master = put(put(new_master, own_part, 0), core, 1)
    across, new_master, first_next, second_next = tie(
        (across, new_master, first_next, second_next))
    last = swap(across, "zero", 1)
    new_master = put(new_master, across, 2)
    last, new_master = tie((last, new_master))
    new_master = put(new_master, last, 3)
    back_grad, new_master = tie((back_grad, new_master))
    grad_tokens = jnp.where(
        live, back_grad.at[restore].get(mode="promise_in_bounds"), jnp.zeros((), BF16))
    return (
        tokens_out, grad_tokens, new_master.reshape(-1), grad_shard.reshape(-1),
        first_next.reshape(-1), second_next.reshape(-1))


def solution(mesh):
    return jax.shard_map(
        on_device,
        mesh=mesh,
        in_specs=(
            P("zero", "dp", None), P(("dp", "zero"), None, None), P(), P(),
            P("zero"), P("zero"), P("zero"), P(), P(),
        ),
        out_specs=(
            P("zero", "dp", None), P("zero", "dp", None), P(), P("zero"), P("zero"), P("zero"),
        ),
        check_vma=False,
    )
```

```python
import jax
import jax.numpy as jnp
from jax import lax
from jax.experimental import pallas as pl
from jax.experimental.pallas import tpu as pltpu
from jax.sharding import PartitionSpec as P

D = 768
HEADS = 24
HEADDIM = 64
STATE = 128
CONV = 4
INNER = 1536
XBC = 1792
PROJ = 3352
Q = 128
LATE = PROJ - INNER
WINDOW = 1024
PAIRS = HEADS // 2
EPS_NORM = 1e-05
NEG = -1e30
F16_TOP = 30000.0
LOG2E = 1.4426950408889634
F32 = jnp.float32
BF16 = jnp.bfloat16


def dot(a, b):
    return lax.dot_general(a, b, (((1,), (0,)), ((), ())), preferred_element_type=F32)


def dot_nt(a, b):
    return lax.dot_general(a, b, (((1,), (1,)), ((), ())), preferred_element_type=F32)


def split2(v):
    hi = v.astype(BF16)
    return hi, (v - hi.astype(F32)).astype(BF16)


def split3(v):
    hi = v.astype(BF16)
    rest = v - hi.astype(F32)
    mid = rest.astype(BF16)
    return hi, mid, (rest - mid.astype(F32)).astype(BF16)


def wide_left(v):
    hi, lo = split2(v)
    return jnp.concatenate([hi, lo, hi], axis=1)


def tall_right(v):
    hi, lo = split2(v)
    return jnp.concatenate([hi, hi, lo], axis=0)


def split_pair(v, masks):
    hi, lo = split2(v)
    return jnp.concatenate([
        jnp.concatenate([hi * masks[0], lo * masks[0]], axis=1),
        jnp.concatenate([hi * masks[1], lo * masks[1]], axis=1)], axis=0)


def sigmoid(v):
    return lax.logistic(v)


def softplus(v):
    return jnp.maximum(v, 0.0) + jnp.log1p(jnp.exp(-jnp.abs(v)))


def iota(shape, dim):
    return lax.broadcasted_iota(jnp.int32, shape, dim)


def expand(v, e_ref):
    hi, lo = split2(v)
    return dot(jnp.concatenate([hi, lo], axis=1), e_ref[...])


def head_sum(v, et_ref):
    hi, lo = split2(v)
    return dot(hi, et_ref[...]) + dot(lo, et_ref[...])


def quarters(out):
    return out[:Q, :Q] + (out[:Q, Q:] + out[Q:, :Q])


def power_for(bound):
    scale = jnp.log(0.9 * F16_TOP / jnp.maximum(bound, 1e-30)) * LOG2E
    return jnp.clip(jnp.floor(scale), -126.0, 120.0)


def chunk_masks(t0, bound):
    rows = t0 + iota((Q, 1), 0)
    rr = t0 + iota((Q, Q), 0)
    cc = t0 + iota((Q, Q), 1)
    return rows, rr, cc


def conv_rows(ext_ref, w_ref, b_ref, rows, bound):
    total = b_ref[...] + w_ref[3:4, :] * ext_ref[8 : 8 + Q, :]
    for back in (1, 2, 3):
        ok = jnp.logical_or(rows - back >= bound, rows < bound).astype(F32)
        total = total + w_ref[3 - back : 4 - back, :] * (ext_ref[8 - back : 8 - back + Q, :] * ok)
    return total


def decay_parts(dt_raw, dtb_ref, alog_ref, rr, cc):
    dt_in = dt_raw + dtb_ref[...]
    dt_pos = softplus(dt_in)
    rate = -jnp.exp(alog_ref[...])
    step = dt_pos * rate
    tri = (cc <= rr).astype(F32).astype(BF16)
    s_hi, s_mid, s_lo = split3(step)
    cum = dot(tri, s_hi) + dot(tri, s_mid) + dot(tri, s_lo)
    return dt_in, dt_pos, rate, cum


def forward_kernel(
    bound_ref, cot_ref, z_ref, proj_ref, gm_ref, norm_ref, e_ref, et_ref, convw_ref, convb_ref, dtb_ref, alog_ref,
    skip_ref, gain_ref,
    pair_ref, dy_ref, through_ref, state_ref, ggain_ref, power_ref,
    zmax_ref, ext_ref, dt_ref, carry_ref, xd_ref, acc_ref, cumt_ref,
):
    step = pl.program_id(0)
    bound = bound_ref[0]
    t0 = step * Q

    @pl.when(step == 0)
    def _():
        ext_ref[0:8, :] = jnp.zeros((8, XBC), F32)
        carry_ref[...] = jnp.zeros_like(carry_ref)
        dt_ref[...] = jnp.zeros_like(dt_ref)
        ggain_ref[...] = jnp.zeros_like(ggain_ref)
        zmax_ref[...] = jnp.zeros_like(zmax_ref)

    rows, rr, cc = chunk_masks(t0, bound)
    ext_ref[8 : 8 + Q, :] = proj_ref[:, :XBC]
    pre = conv_rows(ext_ref, convw_ref, convb_ref, rows, bound)
    ext_ref[0:8, :] = ext_ref[Q : Q + 8, :]
    conv_out = pre * sigmoid(pre)
    x = conv_out[:, :INNER]
    b_rows = conv_out[:, INNER : INNER + STATE]
    c_rows = conv_out[:, INNER + STATE :]
    dt_ref[:, 0:HEADS] = proj_ref[:, XBC:LATE]
    _, dt_pos, _, cum = decay_parts(dt_ref[...], dtb_ref, alog_ref, rr, cc)
    cum_end = cum[Q - 1 : Q, :]
    keep = jnp.logical_or(rows < bound, bound < t0).astype(F32)
    in_last = jnp.logical_or(rows >= bound, bound > t0 + Q - 1).astype(F32)
    whole = jnp.logical_or(bound < t0, bound > t0 + Q - 1).astype(F32)
    from_start = jnp.exp(cum) * keep
    to_end = jnp.exp(cum_end - cum) * in_last
    carry_scale = jnp.exp(cum_end) * whole
    allowed = jnp.logical_and(cc <= rr, (cc >= bound) == (rr >= bound))
    cum2 = cum * LOG2E
    cumt_ref[...] = cum2.T

    state = carry_ref[...]
    state_ref[0] = state
    spread = expand(jnp.concatenate(
        [dt_pos, to_end, from_start, jnp.broadcast_to(carry_scale, (16, 128))], axis=0), e_ref)
    xd = x * spread[:Q]
    xd_ref[...] = xd
    acc = dot(wide_left(c_rows), tall_right(state)) * spread[2 * Q : 3 * Q]
    acc_ref[...] = acc + skip_ref[...] * x
    b_t = b_rows.T
    carry_ref[...] = state * spread[3 * Q : 3 * Q + 1] + dot(
        wide_left(b_t), tall_right(xd * spread[Q : 2 * Q]))
    gram = dot(wide_left(c_rows), tall_right(b_t))
    first = iota((Q, Q), 1) < HEADDIM
    first_b = (first.astype(F32).astype(BF16), 1.0 - first.astype(F32).astype(BF16))
    for pair in range(PAIRS):
        parts = []
        for head in (2 * pair, 2 * pair + 1):
            differ = cum2[:, head : head + 1] - cumt_ref[head : head + 1, :]
            parts.append(gram * jnp.exp2(jnp.where(allowed, differ, NEG)))
        left = jnp.concatenate(split2(jnp.concatenate(parts, axis=1)), axis=0)
        lanes = slice(pair * 128, pair * 128 + 128)
        xp = xd_ref[:, lanes]
        out = dot(left, split_pair(xp, first_b))
        acc_ref[:, lanes] += out[:Q, :128] + (out[:Q, 128:] + out[Q:, :128])
    scanned = acc_ref[...]
    z = z_ref[...]
    sig_z = sigmoid(z)
    silu_z = z * sig_z
    gated = scanned * silu_z
    ginv = lax.rsqrt(jnp.mean(gated * gated, axis=1, keepdims=True) + EPS_NORM)
    mhat = gated * ginv
    pair_ref[1] = (mhat * gain_ref[...]).astype(BF16)
    gm = gm_ref[...]
    ggain_ref[...] += jnp.sum(mhat * gm, axis=0, keepdims=True)
    gmg = gm * gain_ref[...]
    ggated = ginv * (gmg - mhat * jnp.mean(mhat * gmg, axis=1, keepdims=True))
    dy = ggated * silu_z
    dy_ref[...] = dy
    grad_z = ggated * scanned * (sig_z * (1.0 + z * (1.0 - sig_z)))
    zmax_ref[...] = jnp.maximum(zmax_ref[...], jnp.max(jnp.abs(grad_z), axis=0, keepdims=True))
    pair_ref[0] = grad_z.astype(BF16)
    through_ref[...] = head_sum(dy * (scanned - skip_ref[...] * x), et_ref)

    @pl.when(step == pl.num_programs(0) - 1)
    def _():
        count = float(Q * pl.num_programs(0))
        largest = jnp.max(zmax_ref[...], axis=1, keepdims=True)
        normed = jnp.max(jnp.abs(norm_ref[...]), axis=1, keepdims=True) * (D ** 0.5)
        mixed = jnp.max(jnp.abs(gain_ref[...]), axis=1, keepdims=True) * (INNER ** 0.5)
        power_ref[...] = jnp.broadcast_to(power_for(
            1.05 * count * jnp.maximum(largest * normed, cot_ref[0] * mixed)), (8, 128))


def const_spec(shape):
    return pl.BlockSpec(shape, lambda *_: (0,) * len(shape))


def run_forward(z, proj, gm, bound, cot_top, norm_gain, e2, et, params):
    n = proj.shape[0]
    steps = n // Q
    return pl.pallas_call(
        forward_kernel,
        grid=(steps,),
        in_specs=[
            pl.BlockSpec(memory_space=pltpu.SMEM), pl.BlockSpec(memory_space=pltpu.SMEM),
            pl.BlockSpec((Q, INNER), lambda i: (i, 0)),
            pl.BlockSpec((Q, LATE), lambda i: (i, 0)),
            pl.BlockSpec((Q, INNER), lambda i: (i, 0)),
            const_spec((1, D)),
            const_spec((256, INNER)), const_spec((INNER, 128)),
            const_spec((8, XBC)), const_spec((1, XBC)), const_spec((1, 128)),
            const_spec((1, 128)), const_spec((1, INNER)), const_spec((1, INNER)),
        ],
        out_specs=[
            pl.BlockSpec((2, Q, INNER), lambda i: (0, i, 0)),
            pl.BlockSpec((Q, INNER), lambda i: (i, 0)),
            pl.BlockSpec((Q, 128), lambda i: (i, 0)),
            pl.BlockSpec((1, STATE, INNER), lambda i: (i, 0, 0)),
            const_spec((1, INNER)), const_spec((8, 128)),
        ],
        out_shape=[
            jax.ShapeDtypeStruct((2, n, INNER), BF16),
            jax.ShapeDtypeStruct((n, INNER), F32),
            jax.ShapeDtypeStruct((n, 128), F32),
            jax.ShapeDtypeStruct((steps, STATE, INNER), F32),
            jax.ShapeDtypeStruct((1, INNER), F32),
            jax.ShapeDtypeStruct((8, 128), F32),
        ],
        scratch_shapes=[
            pltpu.VMEM((1, INNER), F32),
            pltpu.VMEM((Q + 8, XBC), F32),
            pltpu.VMEM((Q, 128), F32),
            pltpu.VMEM((STATE, INNER), F32),
            pltpu.VMEM((Q, INNER), F32),
            pltpu.VMEM((Q, INNER), F32),
            pltpu.VMEM((128, Q), F32),
        ],
        compiler_params=pltpu.CompilerParams(
            dimension_semantics=("arbitrary",), vmem_limit_bytes=48 * 2**20),
        cost_estimate=pl.CostEstimate(
            flops=30 * 10**9, bytes_accessed=40 * 2**20, transcendentals=10**7),
    )(bound, cot_top, z, proj, gm, norm_gain, e2, et, *params)


def backward_kernel(
    bound_ref, proj_ref, before_ref, dy_ref, through_ref, state_ref, gz_ref, tok_ref, cot_ref,
    in_ref, norm_ref, ggain_ref,
    e_ref, et_ref, convw_ref, convb_ref, dtb_ref, alog_ref, skip_ref,
    window_ref, gtok_ref, small_ref, power_ref,
    total_ref, gskip_ref, gsmall_ref, dtw_ref, gp_ref, ext_ref, dt_ref, lam_ref, dsum_ref, xd_ref, g_ref, gnext_ref, cumt_ref,
):
    step = pl.program_id(0)
    steps = pl.num_programs(0)
    bound = bound_ref[0]
    t0 = (steps - 1 - step) * Q

    @pl.when(step == 0)
    def _():
        lam_ref[...] = jnp.zeros_like(lam_ref)
        dsum_ref[...] = jnp.zeros_like(dsum_ref)
        dt_ref[...] = jnp.zeros_like(dt_ref)
        gnext_ref[Q : Q + 8, :] = jnp.zeros((8, XBC), F32)
        gskip_ref[...] = jnp.zeros_like(gskip_ref)
        total_ref[...] = jnp.zeros_like(total_ref)
        dtw_ref[...] = jnp.zeros_like(dtw_ref)
        gsmall_ref[...] = jnp.zeros_like(gsmall_ref)

    rows, rr, cc = chunk_masks(t0, bound)
    dy = dy_ref[...]
    first_chunk = (t0 > 0).astype(F32)
    ext_ref[0:8, :] = before_ref[:, :XBC] * first_chunk
    ext_ref[8 : 8 + Q, :] = proj_ref[:, :XBC]
    pre = conv_rows(ext_ref, convw_ref, convb_ref, rows, bound)
    sig_pre = sigmoid(pre)
    conv_out = pre * sig_pre
    x = conv_out[:, :INNER]
    b_rows = conv_out[:, INNER : INNER + STATE]
    c_rows = conv_out[:, INNER + STATE :]
    dt_ref[:, 0:HEADS] = proj_ref[:, XBC:LATE]
    dt_in, dt_pos, rate, cum = decay_parts(dt_ref[...], dtb_ref, alog_ref, rr, cc)
    cum_end = cum[Q - 1 : Q, :]
    keep = jnp.logical_or(rows < bound, bound < t0).astype(F32)
    in_last = jnp.logical_or(rows >= bound, bound > t0 + Q - 1).astype(F32)
    whole = jnp.logical_or(bound < t0, bound > t0 + Q - 1).astype(F32)
    from_start = jnp.exp(cum) * keep
    to_end = jnp.exp(cum_end - cum) * in_last
    carry_scale = jnp.exp(cum_end) * whole
    allowed_t = jnp.logical_and(rr <= cc, (cc >= bound) == (rr >= bound))
    cum2 = cum * LOG2E
    cumt_ref[...] = cum2.T
    c_t = c_rows.T
    gram_t = dot(wide_left(b_rows), tall_right(c_t))
    spread = expand(jnp.concatenate(
        [dt_pos, to_end, from_start, jnp.broadcast_to(carry_scale, (16, 128))], axis=0), e_ref)
    dt_all = spread[:Q]
    end_all = spread[Q : 2 * Q]
    xd = x * dt_all
    xd_ref[...] = xd
    skip = skip_ref[...]
    gskip_ref[...] += jnp.sum(dy * x, axis=0, keepdims=True)
    lam = lam_ref[...]
    lam_hi, lam_lo = split2(lam)
    g_ref[...] = (
        dot(wide_left(b_rows), jnp.concatenate([lam_hi, lam_hi, lam_lo], axis=0)) * end_all
    )
    grad_b = quarters(dot_nt(
        jnp.concatenate(split2(xd * end_all), axis=0), jnp.concatenate([lam_hi, lam_lo], axis=0)))
    state = state_ref[0]
    dye_hi, dye_lo = split2(dy * spread[2 * Q : 3 * Q])
    grad_c = quarters(dot_nt(
        jnp.concatenate([dye_hi, dye_lo], axis=0), jnp.concatenate(split2(state), axis=0)))
    lam_new = lam * spread[3 * Q : 3 * Q + 1] + dot(
        wide_left(c_t), jnp.concatenate([dye_hi, dye_hi, dye_lo], axis=0)
    )
    lam_ref[...] = lam_new
    ended = dsum_ref[0:1, :]
    first = iota((Q, Q), 1) < HEADDIM
    first_b = (first.astype(F32).astype(BF16), 1.0 - first.astype(F32).astype(BF16))
    first_row = (iota((Q, Q), 0) < HEADDIM).astype(F32).astype(BF16)
    first_row = (first_row, 1.0 - first_row)
    gram_grad = jnp.zeros((Q, Q), F32)
    for pair in range(PAIRS):
        lanes = slice(pair * 128, pair * 128 + 128)
        weights = []
        for head in (2 * pair, 2 * pair + 1):
            differ = cumt_ref[head : head + 1, :] - cum2[:, head : head + 1]
            weights.append(jnp.exp2(jnp.where(allowed_t, differ, NEG)))
        left = jnp.concatenate([gram_t * weights[0], gram_t * weights[1]], axis=1)
        left = jnp.concatenate(split2(left), axis=0)
        dyp = dy_ref[:, lanes]
        out = dot(left, split_pair(dyp, first_b))
        g_ref[:, lanes] += out[:Q, :128] + (out[:Q, 128:] + out[Q:, :128])
        dyt_hi, dyt_lo = split2(dyp.T)
        right_hi = jnp.concatenate([dyt_hi * first_row[0], dyt_hi * first_row[1]], axis=1)
        right_lo = jnp.concatenate([dyt_lo * first_row[0], dyt_lo * first_row[1]], axis=1)
        outer = dot(
            wide_left(xd_ref[:, lanes]), jnp.concatenate([right_hi, right_hi, right_lo], axis=0))
        gram_grad = gram_grad + (outer[:, :128] * weights[0] + outer[:, 128:] * weights[1])
    g = g_ref[...]
    grad_x = dt_all * g + skip * dy
    sums = dot(jnp.concatenate(
        split2(x * g) + split2(jnp.broadcast_to(
            jnp.sum(lam_new * state, axis=0, keepdims=True), (16, INNER))), axis=0), et_ref[...])
    direct = sums[:Q] + sums[Q : 2 * Q]
    balance = through_ref[...] - dt_pos * direct
    keep_t = allowed_t.astype(F32).astype(BF16)
    b_hi, b_mid, b_lo = split3(balance)
    grad_step = dot(keep_t, b_hi) + dot(keep_t, b_mid) + dot(keep_t, b_lo) + in_last * ended
    dsum_ref[...] = sums[2 * Q : 2 * Q + 8] + sums[2 * Q + 16 : 2 * Q + 24]
    grad_dt = (direct + rate * grad_step) * sigmoid(dt_in)
    gsmall_ref[0:1, :] += jnp.sum(grad_dt, axis=0, keepdims=True)
    gsmall_ref[1:2, :] += rate * jnp.sum(dt_pos * grad_step, axis=0, keepdims=True)
    grad_c = grad_c + dot(wide_left(gram_grad.T), tall_right(b_rows))
    grad_b = grad_b + dot(wide_left(gram_grad), tall_right(c_rows))
    slope = sig_pre * (1.0 + pre * (1.0 - sig_pre))
    gnext_ref[0:Q, :INNER] = grad_x * slope[:, :INNER]
    gnext_ref[0:Q, INNER : INNER + STATE] = grad_b * slope[:, INNER : INNER + STATE]
    gnext_ref[0:Q, INNER + STATE :] = grad_c * slope[:, INNER + STATE :]
    gcp = gnext_ref[0:Q, :]
    total_ref[4:5, :] += jnp.sum(gcp, axis=0, keepdims=True)
    total_ref[3:4, :] += jnp.sum(gcp * ext_ref[8 : 8 + Q, :], axis=0, keepdims=True)
    total = convw_ref[3:4, :] * gcp
    for back in (1, 2, 3):
        ok = jnp.logical_or(rows - back >= bound, rows < bound).astype(F32)
        total_ref[3 - back : 4 - back, :] += jnp.sum(
            gcp * (ext_ref[8 - back : 8 - back + Q, :] * ok), axis=0, keepdims=True)
        okn = jnp.logical_or(rows >= bound, rows + back < bound).astype(F32)
        total = total + convw_ref[3 - back : 4 - back, :] * (gnext_ref[back : back + Q, :] * okn)
    total_ref[7:8, :] = jnp.maximum(
        total_ref[7:8, :], jnp.max(jnp.abs(total), axis=0, keepdims=True))
    total = total.astype(BF16)
    window_ref[0] = total[:, :WINDOW]
    window_ref[1] = total[:, XBC - WINDOW :]
    gnext_ref[Q : Q + 8, :] = gnext_ref[0:8, :]
    half = (steps - 1 - step) % 2
    at = pl.multiple_of(half * Q, Q)
    gp_ref[pl.ds(at, Q), :INNER] = gz_ref[0]
    gp_ref[pl.ds(at, Q), INNER : INNER + XBC] = total
    gp_ref[pl.ds(at, Q), INNER + XBC :] = grad_dt.astype(BF16)

    @pl.when(half == 0)
    def _():
        grad_normed = dot(gp_ref[...], in_ref[: INNER + XBC + 128, :])
        tok = tok_ref[...].astype(F32)
        rinv = lax.rsqrt(jnp.mean(tok * tok, axis=1, keepdims=True) + EPS_NORM)
        nhat = tok * rinv
        gain = norm_ref[...]
        gng = grad_normed * gain
        gtok_ref[...] = (cot_ref[...].astype(F32) + rinv * (
            gng - nhat * jnp.mean(nhat * gng, axis=1, keepdims=True))).astype(BF16)
        total_ref[6:7, :D] += jnp.sum(nhat * grad_normed, axis=0, keepdims=True)
        normed = (nhat * gain).astype(BF16)
        gdt = gp_ref[:, INNER + XBC :].astype(F32)
        dtw_ref[...] += dot(jnp.concatenate(
            [gdt[:Q].T, gdt[Q:].T], axis=1).astype(BF16), normed)

    @pl.when(step == steps - 1)
    def _():
        skips = head_sum(jnp.broadcast_to(gskip_ref[...], (8, INNER)), et_ref)
        small_ref[...] = jnp.zeros_like(small_ref)
        small_ref[0:HEADS, :] = dtw_ref[0:HEADS, :]
        pieces = [
            total_ref[k : k + 1, j * 128 : j * 128 + 128]
            for k in range(CONV + 1) for j in range(XBC // 128)]
        pieces += [gsmall_ref[0:1, :], gsmall_ref[1:2, :], skips[0:1, :]]
        pieces += [ggain_ref[:, j * 128 : j * 128 + 128] for j in range(INNER // 128)]
        lines = D // 128
        for number, piece in enumerate(pieces):
            line = HEADS + number // lines
            at = number % lines * 128
            small_ref[line : line + 1, at : at + 128] = piece
        small_ref[40:41, :] = total_ref[6:7, :D]
        count = float(Q * steps)
        largest = jnp.max(total_ref[7:8, :], axis=1, keepdims=True)
        normed = jnp.max(jnp.abs(norm_ref[...]), axis=1, keepdims=True) * (D ** 0.5)
        others = jnp.max(jnp.max(jnp.abs(small_ref[...]), axis=1, keepdims=True), axis=0, keepdims=True)
        power_ref[...] = jnp.broadcast_to(power_for(
            jnp.maximum(1.05 * count * largest * normed, others)), (8, 128))


def run_backward(
    proj, dy, through, states, pair, tok, cot, in_w, norm_gain, ggain, bound, e2, et, params
):
    n = proj.shape[0]
    steps = n // Q

    def rev(i):
        return (steps - 1 - i, 0)

    def rev_two(i):
        return ((steps - 1 - i) // 2, 0)

    return pl.pallas_call(
        backward_kernel,
        grid=(steps,),
        in_specs=[
            pl.BlockSpec(memory_space=pltpu.SMEM),
            pl.BlockSpec((Q, LATE), rev),
            pl.BlockSpec((8, LATE), lambda i: (jnp.maximum((steps - 1 - i) * (Q // 8) - 1, 0), 0)),
            pl.BlockSpec((Q, INNER), rev),
            pl.BlockSpec((Q, 128), rev),
            pl.BlockSpec((1, STATE, INNER), lambda i: (steps - 1 - i, 0, 0)),
            pl.BlockSpec((1, Q, INNER), lambda i: (0, steps - 1 - i, 0)),
            pl.BlockSpec((2 * Q, D), rev_two), pl.BlockSpec((2 * Q, D), rev_two),
            const_spec(in_w.shape), const_spec((1, D)), const_spec((1, INNER)),
            const_spec((256, INNER)), const_spec((INNER, 128)),
            const_spec((8, XBC)), const_spec((1, XBC)), const_spec((1, 128)),
            const_spec((1, 128)), const_spec((1, INNER)),
        ],
        out_specs=[
            pl.BlockSpec((2, Q, WINDOW), lambda i: (0, steps - 1 - i, 0)),
            pl.BlockSpec((2 * Q, D), rev_two),
            const_spec((48, D)), const_spec((8, 128)),
        ],
        out_shape=[
            jax.ShapeDtypeStruct((2, n, WINDOW), BF16),
            jax.ShapeDtypeStruct((n, D), BF16),
            jax.ShapeDtypeStruct((48, D), F32),
            jax.ShapeDtypeStruct((8, 128), F32),
        ],
        scratch_shapes=[
            pltpu.VMEM((8, XBC), F32),
            pltpu.VMEM((1, INNER), F32),
            pltpu.VMEM((8, 128), F32),
            pltpu.VMEM((128, D), F32),
            pltpu.VMEM((2 * Q, INNER + XBC + 128), BF16),
            pltpu.VMEM((Q + 8, XBC), F32),
            pltpu.VMEM((Q, 128), F32),
            pltpu.VMEM((STATE, INNER), F32),
            pltpu.VMEM((8, 128), F32),
            pltpu.VMEM((Q, INNER), F32),
            pltpu.VMEM((Q, INNER), F32),
            pltpu.VMEM((Q + 8, XBC), F32),
            pltpu.VMEM((128, Q), F32),
        ],
        compiler_params=pltpu.CompilerParams(
            dimension_semantics=("arbitrary",), vmem_limit_bytes=48 * 2**20),
        cost_estimate=pl.CostEstimate(
            flops=50 * 10**9, bytes_accessed=50 * 2**20, transcendentals=2 * 10**7),
    )(bound, proj, proj, dy, through, states, pair, tok, cot, in_w, norm_gain, ggain,
      e2, et, *params[:5])


BETA_ONE = 0.9
BETA_TWO = 0.95
EPS_ADAM = 1e-08
LANES = 128
NORM_ROWS = D // LANES
IN_ROWS = PROJ * D // LANES
CONVW_ROWS = CONV * XBC // LANES
CONVB_ROWS = XBC // LANES
GAIN_ROWS = INNER // LANES
OUT_ROWS = INNER * D // LANES
DT_ROWS = HEADS * D // LANES
SMALL_ROWS = DT_ROWS + CONVW_ROWS + CONVB_ROWS + 3 + GAIN_ROWS
OUT_START = NORM_ROWS + IN_ROWS + SMALL_ROWS - DT_ROWS
LATE_START = NORM_ROWS + INNER * NORM_ROWS
LEAD = 896
STAGE_ROWS = 16264
STAGE_BLOCKS = 5
MARK = 16


PREP_STEPS = 7
IN_BLOCK = 512
OUT_BLOCK = 256
SMALL_START = NORM_ROWS + IN_ROWS


def prepare_kernel(
    flat_ref,
    in_ref, out_ref, norm_ref, convw_ref, convb_ref, dtb_ref, alog_ref, skip_ref, gain_ref,
    e_ref, et_ref,
    stage_ref,
):
    step = pl.program_id(0)

    @pl.when(step == 0)
    def _():
        rows = flat_ref[0:16, :].astype(F32)
        for lane in range(NORM_ROWS):
            norm_ref[:, lane * LANES : lane * LANES + LANES] = rows[lane : lane + 1, :]
        low = SMALL_START // 16 * 16
        stage_ref[0:112, :] = flat_ref[low : low + 112, :].astype(F32)
        at = SMALL_START - low
        convw_ref[...] = jnp.zeros_like(convw_ref)
        for tap in range(CONV):
            for lane in range(CONVB_ROWS):
                convw_ref[tap : tap + 1, lane * LANES : lane * LANES + LANES] = stage_ref[
                    at : at + 1, :]
                at += 1
        for lane in range(CONVB_ROWS):
            convb_ref[:, lane * LANES : lane * LANES + LANES] = stage_ref[at : at + 1, :]
            at += 1
        heads = iota((1, LANES), 1) < HEADS
        dtb_ref[...] = jnp.where(heads, stage_ref[at : at + 1, :], 0.0)
        alog_ref[...] = jnp.where(heads, stage_ref[at + 1 : at + 2, :], 0.0)
        skips = jnp.where(heads, stage_ref[at + 2 : at + 3, :], 0.0)
        at += 3
        for lane in range(GAIN_ROWS):
            gain_ref[:, lane * LANES : lane * LANES + LANES] = stage_ref[at : at + 1, :]
            at += 1
        one = (iota((128, INNER), 1) // HEADDIM == iota((128, INNER), 0)).astype(F32).astype(BF16)
        e_ref[0:128, :] = one
        e_ref[128:256, :] = one
        et_ref[...] = (
            iota((INNER, 128), 0) // HEADDIM == iota((INNER, 128), 1)).astype(F32).astype(BF16)
        skip_ref[...] = dot(jnp.broadcast_to(skips, (16, LANES)).astype(BF16), one)[0:1, :]

    def block(start, offset, rows, dest_ref):
        size = rows * NORM_ROWS + 16
        at = pl.multiple_of(start + step * (rows * NORM_ROWS), 16)
        stage_ref[0:size, :] = flat_ref[pl.ds(at, size), :].astype(F32)
        for lane in range(NORM_ROWS):
            dest_ref[:, lane * LANES : lane * LANES + LANES] = stage_ref[
                pl.ds(offset + lane, rows, stride=NORM_ROWS), :].astype(BF16)

    block(0, NORM_ROWS, IN_BLOCK, in_ref)

    @pl.when(step == PREP_STEPS - 1)
    def _():
        used = PROJ - (PREP_STEPS - 1) * IN_BLOCK
        in_ref[used:, :] = jnp.zeros((IN_BLOCK - used, D), BF16)

    @pl.when(step < INNER // OUT_BLOCK)
    def _():
        low = OUT_START // 16 * 16
        block(low, OUT_START - low, OUT_BLOCK, out_ref)


def run_prepare(flat):
    vector = lambda n: jax.ShapeDtypeStruct((1, n), F32)
    return pl.pallas_call(
        prepare_kernel,
        grid=(PREP_STEPS,),
        in_specs=[const_spec(flat.shape)],
        out_specs=[
            pl.BlockSpec((IN_BLOCK, D), lambda i: (i, 0)),
            pl.BlockSpec((OUT_BLOCK, D), lambda i: (jnp.minimum(i, INNER // OUT_BLOCK - 1), 0)),
            const_spec((1, D)), const_spec((8, XBC)), const_spec((1, XBC)), const_spec((1, 128)),
            const_spec((1, 128)), const_spec((1, INNER)), const_spec((1, INNER)),
            const_spec((256, INNER)), const_spec((INNER, 128)),
        ],
        out_shape=[
            jax.ShapeDtypeStruct((PREP_STEPS * IN_BLOCK, D), BF16),
            jax.ShapeDtypeStruct((INNER, D), BF16),
            vector(D), jax.ShapeDtypeStruct((8, XBC), F32), vector(XBC), vector(128), vector(128),
            vector(INNER), vector(INNER),
            jax.ShapeDtypeStruct((256, INNER), BF16), jax.ShapeDtypeStruct((INNER, 128), BF16),
        ],
        scratch_shapes=[pltpu.VMEM((IN_BLOCK * NORM_ROWS + 16, LANES), F32)],
        compiler_params=pltpu.CompilerParams(
            dimension_semantics=("arbitrary",), vmem_limit_bytes=40 * 2**20),
        cost_estimate=pl.CostEstimate(
            flops=10**9, bytes_accessed=16 * 2**20, transcendentals=0),
    )(flat)


def stage_kernel(
    who_ref, early_ref, early_other_ref, late_ref, late_other_ref, small_ref,
    grad_ref,
    stage_ref,
):
    step = pl.program_id(0)
    upper = who_ref[0]
    mine = who_ref[1]
    block = grad_ref.shape[0]
    half = 2 * block * STAGE_BLOCKS

    @pl.when(step == 0)
    def _():
        early_at = LEAD + jnp.where(upper == 1, OUT_START - half, NORM_ROWS)
        window = LATE_START + (XBC - WINDOW) * NORM_ROWS
        late_at = LEAD + jnp.where(upper == 1, window - half, LATE_START)
        def lay(source_ref, start, size):
            for lane in range(NORM_ROWS):
                stage_ref[pl.ds(start + lane, size, stride=NORM_ROWS), :] = source_ref[
                    0:size, lane * LANES : lane * LANES + LANES]

        lines = late_ref.shape[0]
        lay(late_ref, late_at + mine * (lines * NORM_ROWS), lines)
        lay(late_other_ref, late_at + (1 - mine) * (lines * NORM_ROWS), lines)

        @pl.when(upper == 1)
        def _():
            lay(small_ref, LEAD + OUT_START - half - SMALL_ROWS, -(-SMALL_ROWS // NORM_ROWS))

        lines = early_ref.shape[0]
        lay(early_ref, early_at + mine * (lines * NORM_ROWS), lines)
        lay(early_other_ref, early_at + (1 - mine) * (lines * NORM_ROWS), lines)

        @pl.when(upper == 0)
        def _():
            for lane in range(NORM_ROWS):
                stage_ref[LEAD + lane : LEAD + lane + 1, :] = small_ref[
                    40:41, lane * LANES : lane * LANES + LANES]

        @pl.when(upper == 1)
        def _():
            at = LEAD + OUT_START + OUT_ROWS - half
            stage_ref[at : LEAD + half, :] = jnp.zeros((LEAD + half - at, LANES), F32)

    @pl.when(step > 0)
    def _():
        at = LEAD + mine * (half // 2) + (step - 1) * block
        grad_ref[...] = stage_ref[pl.ds(pl.multiple_of(at, 8), block), :]


def run_stage(who, rows, early, early_other, late, late_other, small):
    block = rows // STAGE_BLOCKS
    return pl.pallas_call(
        stage_kernel,
        grid=(STAGE_BLOCKS + 1,),
        in_specs=[
            pl.BlockSpec(memory_space=pltpu.SMEM),
            const_spec(early.shape), const_spec(early.shape),
            const_spec(late.shape), const_spec(late.shape), const_spec(small.shape),
        ],
        out_specs=pl.BlockSpec((block, LANES), lambda i: (jnp.maximum(i - 1, 0), 0)),
        out_shape=jax.ShapeDtypeStruct((rows, LANES), F32),
        scratch_shapes=[pltpu.VMEM((STAGE_ROWS, LANES), F32)],
        compiler_params=pltpu.CompilerParams(
            dimension_semantics=("arbitrary",), vmem_limit_bytes=48 * 2**20),
        cost_estimate=pl.CostEstimate(
            flops=10**6, bytes_accessed=12 * 2**20, transcendentals=0),
    )(who, early, early_other, late, late_other, small)


def swap(values, axis, bit):
    size = lax.axis_size(axis)
    return lax.ppermute(values, axis, [(i, i ^ bit) for i in range(size)])


def to_wire(values, power):
    return (values * jnp.exp2(power)).astype(jnp.float16)


def from_wire(values, power):
    return values.astype(F32) * jnp.exp2(-power)


def scatter(values, power, axis, bit=1, count=2, after=None, sent=None):
    place = (lax.axis_index(axis) // bit) % count
    rows = values.shape[-2] // count
    mark = min(MARK, rows)
    dim = values.ndim - 2
    total = lax.dynamic_slice_in_dim(values, place * rows, rows, dim)
    least = power
    arrived = []
    for offset in range(1, count):
        to = place ^ offset
        last = to == count - 1
        start = to * rows - jnp.where(last, mark, 0)
        send = lax.dynamic_slice_in_dim(values, start, rows + mark, dim)
        line = lax.broadcasted_iota(jnp.int32, send.shape, dim)
        marked = jnp.where(last, line < mark, line >= rows)
        wire = jnp.where(marked, power, send * jnp.exp2(power)).astype(jnp.float16)
        arrived.append(swap(wire, axis, bit * offset))
        if sent is not None:
            sent.append(wire)
    if after is not None:
        arrived, _ = lax.optimization_barrier((arrived, after))
    last = place == count - 1
    for got in arrived:
        got_power = lax.dynamic_slice_in_dim(
            got, jnp.where(last, 0, rows), 1, dim).reshape(1, D).astype(F32)
        body = lax.dynamic_slice_in_dim(got, jnp.where(last, mark, 0), rows, dim)
        total = total + from_wire(body, got_power)
        least = jnp.minimum(least, got_power)
    return total, least - float(count.bit_length() - 1)


def scatter_product(left, right, power, axis, bit):
    def product(part):
        return lax.dot_general(
            part, right, (((1,), (1,)), ((0,), (0,))), preferred_element_type=F32)

    side = (lax.axis_index(axis) // bit) % 2
    rows = left.shape[2] // 2
    send = product(jnp.where(side == 1, left[:, :, : rows + LANES], left[:, :, rows - LANES :]))
    line = lax.broadcasted_iota(jnp.int32, send.shape, 1)
    marked = jnp.where(side == 1, line >= rows, line < LANES)
    wire = jnp.where(marked, power, send * jnp.exp2(power)).astype(jnp.float16)
    got = swap(wire, axis, bit)
    left, _ = lax.optimization_barrier((left, wire))
    keep = product(jnp.where(side == 0, left[:, :, :rows], left[:, :, rows:]))
    keep, got = lax.optimization_barrier((keep, got))
    got_power = lax.dynamic_slice(
        got, (0, (1 - side) * rows, 0), (1, 1, D))[0].astype(F32)
    body = lax.dynamic_slice_in_dim(got, side * LANES, rows, 1)
    return keep + from_wire(body, got_power), jnp.minimum(power, got_power) - 1.0


def everyones(values, axis, bit=1, count=2):
    place = (lax.axis_index(axis) // bit) % count
    pieces = [values] + [swap(values, axis, bit * offset) for offset in range(1, count)]
    step = 1
    while step < count:
        flip = (place // step) % 2 == 1
        pieces = [
            jnp.where(flip, pieces[i ^ step], pieces[i]) for i in range(count)]
        step *= 2
    return pieces


def gather(values, axis, bit=1, count=2):
    return jnp.concatenate(everyones(values, axis, bit, count))


def add_pair(values, axis, bit, after=None):
    got = swap(values, axis, bit)
    if after is not None:
        got, _ = lax.optimization_barrier((got, after))
    return values + got


def data_groups():
    size = lax.axis_size("dp")
    groups = [(1, 2)]
    bit = 2
    while bit < size:
        count = 4 if bit * 4 <= size else 2
        groups.append((bit, count))
        bit *= count
    return groups


def dot_tn(a, b):
    return lax.dot_general(a, b, (((0,), (0,)), ((), ())), preferred_element_type=F32)


def pick_rows(index, rows):
    chosen = index[:, None] == jnp.arange(rows.shape[0], dtype=jnp.int32)[None, :]
    return dot(chosen.astype(BF16), rows).astype(BF16)


def on_device(
    tokens, loss_sensitivity, lengths, holder_sequence_list, master, moment_one, moment_two,
    adam_rates, iteration_tally,
):
    group_devices = lax.axis_size("zero")
    data_devices = lax.axis_size("dp")
    zero_index = lax.axis_index("zero")
    dp_index = lax.axis_index("dp")
    seq_len = loss_sensitivity.shape[1]
    group_seqs = tokens.shape[0]
    span = tokens.shape[1]
    slots = group_seqs // data_devices
    shard_rows = master.shape[0] // LANES
    tie = lax.optimization_barrier

    own = master.reshape(shard_rows, LANES)
    arranged = holder_sequence_list.reshape(data_devices, group_devices, slots)
    group_order = lax.dynamic_index_in_dim(arranged, zero_index, 1, keepdims=False).reshape(-1)
    local_ids = group_order - zero_index * group_seqs
    dealt = tokens.at[local_ids].get(mode="promise_in_bounds")
    flat = lax.all_gather(own.astype(BF16), "zero", axis=0, tiled=True)

    local_tok = lax.all_to_all(dealt, "dp", split_axis=0, concat_axis=0, tiled=True)
    my_seqs = lax.dynamic_slice_in_dim(group_order, dp_index * slots, slots)
    bound = lengths[my_seqs[0]]
    positions = jnp.arange(seq_len, dtype=jnp.int32)

    in_w, out_w, norm_gain, *params, e2, et = run_prepare(flat)
    cot = loss_sensitivity[0]
    gm = dot_nt(cot, out_w)
    cot_top = jnp.max(jnp.abs(cot)).astype(F32).reshape(1)
    local_tok, in_w, gm, cot_top = tie((local_tok, in_w, gm, cot_top))
    own_late, _ = tie((own, flat[:8]))
    whole_master = lax.all_gather(own_late, "zero", axis=0, tiled=True)

    def place(slot, at):
        return (at // span) * (slots * span) + slot * span + at % span

    source = jnp.where(positions < bound, place(0, positions), place(1, positions - bound))
    packed = pick_rows(source, local_tok.reshape(slots * seq_len, D))
    blocks = jnp.arange(data_devices, dtype=jnp.int32)[:, None, None] * span
    within = blocks + jnp.arange(span, dtype=jnp.int32)[None, None, :]
    within = within + jnp.arange(slots, dtype=jnp.int32)[None, :, None] * bound
    unpack_rows = jnp.minimum(within, seq_len - 1).reshape(-1)

    def spread(rows):
        return pick_rows(unpack_rows, rows).reshape(data_devices * slots, span, D)

    def send_back(picked):
        return lax.all_to_all(picked, "dp", split_axis=0, concat_axis=0, tiled=True)

    restore = jnp.zeros_like(local_ids).at[local_ids].set(
        jnp.arange(group_seqs, dtype=jnp.int32))
    mine = lax.dynamic_slice_in_dim(lengths, zero_index * group_seqs, group_seqs)
    at = dp_index * span + jnp.arange(span, dtype=jnp.int32)
    live = (at[None, :] < mine[:, None])[:, :, None]

    bound_arr = bound.reshape(1)
    tok = packed.astype(F32)
    nhat = tok * lax.rsqrt(jnp.mean(tok * tok, axis=1, keepdims=True) + EPS_NORM)
    normed = (nhat * norm_gain).astype(BF16)
    proj_z = dot_nt(normed, in_w[:INNER])
    proj = dot_nt(normed, in_w[INNER:PROJ])
    pair, dy, through, states, ggain, early_power = run_forward(
        proj_z, proj, gm, bound_arr, cot_top, norm_gain, e2, et, params)
    result = (tok + dot(pair[1], out_w)).astype(BF16)
    picked = spread(result)
    picked, pair = tie((picked, pair))
    back_out = send_back(picked)
    early_power = early_power[0:1, 0:1]
    early, early_power = scatter_product(
        pair, jnp.stack([normed, cot]), early_power, "zero", 1)
    early, early_power, dy = tie((early.reshape(INNER, D), early_power, dy))
    early, early_power = scatter(early, early_power, "zero", 2)
    window, grad_tok, small, late_power = run_backward(
        proj, dy, through, states, pair, packed, cot, in_w, norm_gain, ggain,
        bound_arr, e2, et, params)
    window, small, late_power, early, early_power, whole_master = tie(
        (window, small, late_power, early, early_power, whole_master))

    groups = data_groups()
    late_power = late_power[0:1, 0:1]
    late, late_power = scatter_product(
        window, jnp.stack([normed, normed]), late_power, "zero", 1)
    late = late.reshape(WINDOW, D)
    small = add_pair(small, "zero", 1)
    early, early_power, grad_tok, _ = tie((early, early_power, grad_tok, late))
    late, late_power = scatter(late, late_power, "zero", 2)
    early, early_power = scatter(early, early_power, "dp", *groups[0])
    small = add_pair(small, "zero", 2, late)
    early_before, power_before = early, early_power
    picked_grad = spread(grad_tok)
    tokens, back_out, _ = tie((tokens, back_out, grad_tok))
    back_rows = back_out.at[restore].get(mode="promise_in_bounds")
    tokens_out = jnp.where(live, back_rows, tokens)
    new_master = jnp.zeros((group_devices, shard_rows, LANES), F32)
    late, tokens_out, new_master, picked_grad = tie((late, tokens_out, new_master, picked_grad))
    lines = small.shape[0]
    late = jnp.concatenate([late, small, jnp.zeros((WINDOW // 8 - lines, D), F32)])
    late, late_power = scatter(late, late_power, "dp", *groups[0])
    sent = []
    for group in groups[1:]:
        late, late_power = scatter(late, late_power, "dp", *group, sent=sent)
    early, early_power = early_before, power_before
    for group in groups[1:]:
        early, early_power = scatter(early, early_power, "dp", *group, after=sent)
    early = to_wire(early, early_power)
    for group in reversed(groups[1:]):
        early = gather(early, "dp", *group)
    early, _ = tie((early, late))
    late = to_wire(late, late_power)
    early = from_wire(gather(early, "dp", *groups[0]), early_power)
    early, picked_grad, _ = tie((early, picked_grad, late))
    for group in reversed(groups[1:]):
        late = gather(late, "dp", *group)
    early_other = swap(early, "zero", 1)
    back_grad = send_back(picked_grad)
    wire = gather(late, "dp", *groups[0])
    late = from_wire(wire[: WINDOW // 2], late_power)
    small = from_wire(wire[WINDOW // 2 : WINDOW // 2 + lines], late_power)
    late_other = swap(late, "zero", 1)

    steps_f = iteration_tally[0].astype(F32)
    who = jnp.stack([zero_index // 2, zero_index % 2]).astype(jnp.int32)
    first = moment_one.reshape(shard_rows, LANES)
    second = moment_two.reshape(shard_rows, LANES)
    grad_shard = run_stage(who, shard_rows, early, early_other, late, late_other, small)
    first_scale = 1.0 / (1.0 - jnp.power(BETA_ONE, steps_f))
    second_scale = 1.0 / (1.0 - jnp.power(BETA_TWO, steps_f))

    def moments(grad, first, second):
        return (
            BETA_ONE * first + (1.0 - BETA_ONE) * grad,
            BETA_TWO * second + (1.0 - BETA_TWO) * grad * grad)

    def quotient(rows):
        first_next, second_next = moments(grad_shard[rows], first[rows], second[rows])
        return ((first_next * first_scale) / (
            jnp.sqrt(second_next * second_scale) + EPS_ADAM)).astype(jnp.float16)

    whole_master = whole_master.reshape(group_devices, shard_rows, LANES)

    def put(new_master, piece, offset):
        shard = zero_index ^ offset
        old = lax.dynamic_index_in_dim(whole_master, shard, 0, keepdims=False)
        new = old - adam_rates[0] * (piece.astype(F32) + adam_rates[1] * old)
        return lax.dynamic_update_index_in_dim(new_master, new, shard, 0)

    own_part, first, second = tie((quotient(slice(0, shard_rows)), first, second))
    across = swap(own_part, "zero", 2)
    core = swap(own_part, "zero", 1)
    first_next, second_next = moments(grad_shard, first, second)
    new_master = put(put(new_master, own_part, 0), core, 1)
    across, new_master, first_next, second_next = tie(
        (across, new_master, first_next, second_next))
    last = swap(across, "zero", 1)
    new_master = put(new_master, across, 2)
    last, new_master = tie((last, new_master))
    new_master = put(new_master, last, 3)
    back_grad, new_master = tie((back_grad, new_master))
    grad_tokens = jnp.where(
        live, back_grad.at[restore].get(mode="promise_in_bounds"), jnp.zeros((), BF16))
    return (
        tokens_out, grad_tokens, new_master.reshape(-1), grad_shard.reshape(-1),
        first_next.reshape(-1), second_next.reshape(-1))


def solution(mesh):
    return jax.shard_map(
        on_device,
        mesh=mesh,
        in_specs=(
            P("zero", "dp", None), P(("dp", "zero"), None, None), P(), P(),
            P("zero"), P("zero"), P("zero"), P(), P(),
        ),
        out_specs=(
            P("zero", "dp", None), P("zero", "dp", None), P(), P("zero"), P("zero"), P("zero"),
        ),
        check_vma=False,
    )
```

```python
import jax
import jax.numpy as jnp
from jax import lax
from jax.experimental import pallas as pl
from jax.experimental.pallas import tpu as pltpu
from jax.sharding import PartitionSpec as P

D = 768
HEADS = 24
HEADDIM = 64
STATE = 128
CONV = 4
INNER = 1536
XBC = 1792
PROJ = 3352
Q = 128
LATE = PROJ - INNER
WINDOW = 1024
PAIRS = HEADS // 2
EPS_NORM = 1e-05
NEG = -1e30
F16_TOP = 30000.0
LOG2E = 1.4426950408889634
F32 = jnp.float32
BF16 = jnp.bfloat16


def dot(a, b):
    return lax.dot_general(a, b, (((1,), (0,)), ((), ())), preferred_element_type=F32)


def dot_nt(a, b):
    return lax.dot_general(a, b, (((1,), (1,)), ((), ())), preferred_element_type=F32)


def split2(v):
    hi = v.astype(BF16)
    return hi, (v - hi.astype(F32)).astype(BF16)


def split3(v):
    hi = v.astype(BF16)
    rest = v - hi.astype(F32)
    mid = rest.astype(BF16)
    return hi, mid, (rest - mid.astype(F32)).astype(BF16)


def wide_left(v):
    hi, lo = split2(v)
    return jnp.concatenate([hi, lo, hi], axis=1)


def tall_right(v):
    hi, lo = split2(v)
    return jnp.concatenate([hi, hi, lo], axis=0)


def split_pair(v, masks):
    hi, lo = split2(v)
    return jnp.concatenate([
        jnp.concatenate([hi * masks[0], lo * masks[0]], axis=1),
        jnp.concatenate([hi * masks[1], lo * masks[1]], axis=1)], axis=0)


def sigmoid(v):
    return lax.logistic(v)


def softplus(v):
    return jnp.maximum(v, 0.0) + jnp.log1p(jnp.exp(-jnp.abs(v)))


def iota(shape, dim):
    return lax.broadcasted_iota(jnp.int32, shape, dim)


def expand(v, e_ref):
    hi, lo = split2(v)
    return dot(jnp.concatenate([hi, lo], axis=1), e_ref[...])


def head_sum(v, et_ref):
    hi, lo = split2(v)
    return dot(hi, et_ref[...]) + dot(lo, et_ref[...])


def quarters(out):
    return out[:Q, :Q] + (out[:Q, Q:] + out[Q:, :Q])


def power_for(bound):
    scale = jnp.log(0.9 * F16_TOP / jnp.maximum(bound, 1e-30)) * LOG2E
    return jnp.clip(jnp.floor(scale), -126.0, 120.0)


def chunk_masks(t0, bound):
    rows = t0 + iota((Q, 1), 0)
    rr = t0 + iota((Q, Q), 0)
    cc = t0 + iota((Q, Q), 1)
    return rows, rr, cc


def conv_rows(ext_ref, w_ref, b_ref, rows, bound):
    total = b_ref[...] + w_ref[3:4, :] * ext_ref[8 : 8 + Q, :]
    for back in (1, 2, 3):
        ok = jnp.logical_or(rows - back >= bound, rows < bound).astype(F32)
        total = total + w_ref[3 - back : 4 - back, :] * (ext_ref[8 - back : 8 - back + Q, :] * ok)
    return total


def decay_parts(dt_raw, dtb_ref, alog_ref, rr, cc):
    dt_in = dt_raw + dtb_ref[...]
    dt_pos = softplus(dt_in)
    rate = -jnp.exp(alog_ref[...])
    step = dt_pos * rate
    tri = (cc <= rr).astype(F32).astype(BF16)
    s_hi, s_mid, s_lo = split3(step)
    cum = dot(tri, s_hi) + dot(tri, s_mid) + dot(tri, s_lo)
    return dt_in, dt_pos, rate, cum


def forward_kernel(
    bound_ref, cot_ref, z_ref, proj_ref, gm_ref, norm_ref, e_ref, et_ref, convw_ref, convb_ref, dtb_ref, alog_ref,
    skip_ref, gain_ref,
    pair_ref, dy_ref, through_ref, state_ref, ggain_ref, power_ref,
    zmax_ref, ext_ref, dt_ref, carry_ref, xd_ref, acc_ref, cumt_ref,
):
    step = pl.program_id(0)
    bound = bound_ref[0]
    t0 = step * Q

    @pl.when(step == 0)
    def _():
        ext_ref[0:8, :] = jnp.zeros((8, XBC), F32)
        carry_ref[...] = jnp.zeros_like(carry_ref)
        dt_ref[...] = jnp.zeros_like(dt_ref)
        ggain_ref[...] = jnp.zeros_like(ggain_ref)
        zmax_ref[...] = jnp.zeros_like(zmax_ref)

    rows, rr, cc = chunk_masks(t0, bound)
    ext_ref[8 : 8 + Q, :] = proj_ref[:, :XBC]
    pre = conv_rows(ext_ref, convw_ref, convb_ref, rows, bound)
    ext_ref[0:8, :] = ext_ref[Q : Q + 8, :]
    conv_out = pre * sigmoid(pre)
    x = conv_out[:, :INNER]
    b_rows = conv_out[:, INNER : INNER + STATE]
    c_rows = conv_out[:, INNER + STATE :]
    dt_ref[:, 0:HEADS] = proj_ref[:, XBC:LATE]
    _, dt_pos, _, cum = decay_parts(dt_ref[...], dtb_ref, alog_ref, rr, cc)
    cum_end = cum[Q - 1 : Q, :]
    keep = jnp.logical_or(rows < bound, bound < t0).astype(F32)
    in_last = jnp.logical_or(rows >= bound, bound > t0 + Q - 1).astype(F32)
    whole = jnp.logical_or(bound < t0, bound > t0 + Q - 1).astype(F32)
    from_start = jnp.exp(cum) * keep
    to_end = jnp.exp(cum_end - cum) * in_last
    carry_scale = jnp.exp(cum_end) * whole
    allowed = jnp.logical_and(cc <= rr, (cc >= bound) == (rr >= bound))
    cum2 = cum * LOG2E
    cumt_ref[...] = cum2.T

    state = carry_ref[...]
    state_ref[0] = state
    spread = expand(jnp.concatenate(
        [dt_pos, to_end, from_start, jnp.broadcast_to(carry_scale, (16, 128))], axis=0), e_ref)
    xd = x * spread[:Q]
    xd_ref[...] = xd
    acc = dot(wide_left(c_rows), tall_right(state)) * spread[2 * Q : 3 * Q]
    acc_ref[...] = acc + skip_ref[...] * x
    b_t = b_rows.T
    carry_ref[...] = state * spread[3 * Q : 3 * Q + 1] + dot(
        wide_left(b_t), tall_right(xd * spread[Q : 2 * Q]))
    gram = dot(wide_left(c_rows), tall_right(b_t))
    first = iota((Q, Q), 1) < HEADDIM
    first_b = (first.astype(F32).astype(BF16), 1.0 - first.astype(F32).astype(BF16))
    for pair in range(PAIRS):
        parts = []
        for head in (2 * pair, 2 * pair + 1):
            differ = cum2[:, head : head + 1] - cumt_ref[head : head + 1, :]
            parts.append(gram * jnp.exp2(jnp.where(allowed, differ, NEG)))
        left = jnp.concatenate(split2(jnp.concatenate(parts, axis=1)), axis=0)
        lanes = slice(pair * 128, pair * 128 + 128)
        xp = xd_ref[:, lanes]
        out = dot(left, split_pair(xp, first_b))
        acc_ref[:, lanes] += out[:Q, :128] + (out[:Q, 128:] + out[Q:, :128])
    scanned = acc_ref[...]
    z = z_ref[...]
    sig_z = sigmoid(z)
    silu_z = z * sig_z
    gated = scanned * silu_z
    ginv = lax.rsqrt(jnp.mean(gated * gated, axis=1, keepdims=True) + EPS_NORM)
    mhat = gated * ginv
    pair_ref[1] = (mhat * gain_ref[...]).astype(BF16)
    gm = gm_ref[...]
    ggain_ref[...] += jnp.sum(mhat * gm, axis=0, keepdims=True)
    gmg = gm * gain_ref[...]
    ggated = ginv * (gmg - mhat * jnp.mean(mhat * gmg, axis=1, keepdims=True))
    dy = ggated * silu_z
    dy_ref[...] = dy
    grad_z = ggated * scanned * (sig_z * (1.0 + z * (1.0 - sig_z)))
    zmax_ref[...] = jnp.maximum(zmax_ref[...], jnp.max(jnp.abs(grad_z), axis=0, keepdims=True))
    pair_ref[0] = grad_z.astype(BF16)
    through_ref[...] = head_sum(dy * (scanned - skip_ref[...] * x), et_ref)

    @pl.when(step == pl.num_programs(0) - 1)
    def _():
        count = float(Q * pl.num_programs(0))
        largest = jnp.max(zmax_ref[...], axis=1, keepdims=True)
        normed = jnp.max(jnp.abs(norm_ref[...]), axis=1, keepdims=True) * (D ** 0.5)
        mixed = jnp.max(jnp.abs(gain_ref[...]), axis=1, keepdims=True) * (INNER ** 0.5)
        power_ref[...] = jnp.broadcast_to(power_for(
            1.05 * count * jnp.maximum(largest * normed, cot_ref[0] * mixed)), (8, 128))


def const_spec(shape):
    return pl.BlockSpec(shape, lambda *_: (0,) * len(shape))


def run_forward(z, proj, gm, bound, cot_top, norm_gain, e2, et, params):
    n = proj.shape[0]
    steps = n // Q
    return pl.pallas_call(
        forward_kernel,
        grid=(steps,),
        in_specs=[
            pl.BlockSpec(memory_space=pltpu.SMEM), pl.BlockSpec(memory_space=pltpu.SMEM),
            pl.BlockSpec((Q, INNER), lambda i: (i, 0)),
            pl.BlockSpec((Q, LATE), lambda i: (i, 0)),
            pl.BlockSpec((Q, INNER), lambda i: (i, 0)),
            const_spec((1, D)),
            const_spec((256, INNER)), const_spec((INNER, 128)),
            const_spec((8, XBC)), const_spec((1, XBC)), const_spec((1, 128)),
            const_spec((1, 128)), const_spec((1, INNER)), const_spec((1, INNER)),
        ],
        out_specs=[
            pl.BlockSpec((2, Q, INNER), lambda i: (0, i, 0)),
            pl.BlockSpec((Q, INNER), lambda i: (i, 0)),
            pl.BlockSpec((Q, 128), lambda i: (i, 0)),
            pl.BlockSpec((1, STATE, INNER), lambda i: (i, 0, 0)),
            const_spec((1, INNER)), const_spec((8, 128)),
        ],
        out_shape=[
            jax.ShapeDtypeStruct((2, n, INNER), BF16),
            jax.ShapeDtypeStruct((n, INNER), F32),
            jax.ShapeDtypeStruct((n, 128), F32),
            jax.ShapeDtypeStruct((steps, STATE, INNER), F32),
            jax.ShapeDtypeStruct((1, INNER), F32),
            jax.ShapeDtypeStruct((8, 128), F32),
        ],
        scratch_shapes=[
            pltpu.VMEM((1, INNER), F32),
            pltpu.VMEM((Q + 8, XBC), F32),
            pltpu.VMEM((Q, 128), F32),
            pltpu.VMEM((STATE, INNER), F32),
            pltpu.VMEM((Q, INNER), F32),
            pltpu.VMEM((Q, INNER), F32),
            pltpu.VMEM((128, Q), F32),
        ],
        compiler_params=pltpu.CompilerParams(
            dimension_semantics=("arbitrary",), vmem_limit_bytes=48 * 2**20),
        cost_estimate=pl.CostEstimate(
            flops=30 * 10**9, bytes_accessed=40 * 2**20, transcendentals=10**7),
    )(bound, cot_top, z, proj, gm, norm_gain, e2, et, *params)


def backward_kernel(
    bound_ref, proj_ref, before_ref, dy_ref, through_ref, state_ref, gz_ref, tok_ref, cot_ref,
    in_ref, norm_ref, ggain_ref,
    e_ref, et_ref, convw_ref, convb_ref, dtb_ref, alog_ref, skip_ref,
    window_ref, gtok_ref, small_ref, power_ref,
    total_ref, gskip_ref, gsmall_ref, dtw_ref, gp_ref, ext_ref, dt_ref, lam_ref, dsum_ref, xd_ref, g_ref, gnext_ref, cumt_ref,
):
    step = pl.program_id(0)
    steps = pl.num_programs(0)
    bound = bound_ref[0]
    t0 = (steps - 1 - step) * Q

    @pl.when(step == 0)
    def _():
        lam_ref[...] = jnp.zeros_like(lam_ref)
        dsum_ref[...] = jnp.zeros_like(dsum_ref)
        dt_ref[...] = jnp.zeros_like(dt_ref)
        gnext_ref[Q : Q + 8, :] = jnp.zeros((8, XBC), F32)
        gskip_ref[...] = jnp.zeros_like(gskip_ref)
        total_ref[...] = jnp.zeros_like(total_ref)
        dtw_ref[...] = jnp.zeros_like(dtw_ref)
        gsmall_ref[...] = jnp.zeros_like(gsmall_ref)

    rows, rr, cc = chunk_masks(t0, bound)
    dy = dy_ref[...]
    first_chunk = (t0 > 0).astype(F32)
    ext_ref[0:8, :] = before_ref[:, :XBC] * first_chunk
    ext_ref[8 : 8 + Q, :] = proj_ref[:, :XBC]
    pre = conv_rows(ext_ref, convw_ref, convb_ref, rows, bound)
    sig_pre = sigmoid(pre)
    conv_out = pre * sig_pre
    x = conv_out[:, :INNER]
    b_rows = conv_out[:, INNER : INNER + STATE]
    c_rows = conv_out[:, INNER + STATE :]
    dt_ref[:, 0:HEADS] = proj_ref[:, XBC:LATE]
    dt_in, dt_pos, rate, cum = decay_parts(dt_ref[...], dtb_ref, alog_ref, rr, cc)
    cum_end = cum[Q - 1 : Q, :]
    keep = jnp.logical_or(rows < bound, bound < t0).astype(F32)
    in_last = jnp.logical_or(rows >= bound, bound > t0 + Q - 1).astype(F32)
    whole = jnp.logical_or(bound < t0, bound > t0 + Q - 1).astype(F32)
    from_start = jnp.exp(cum) * keep
    to_end = jnp.exp(cum_end - cum) * in_last
    carry_scale = jnp.exp(cum_end) * whole
    allowed_t = jnp.logical_and(rr <= cc, (cc >= bound) == (rr >= bound))
    cum2 = cum * LOG2E
    cumt_ref[...] = cum2.T
    c_t = c_rows.T
    gram_t = dot(wide_left(b_rows), tall_right(c_t))
    spread = expand(jnp.concatenate(
        [dt_pos, to_end, from_start, jnp.broadcast_to(carry_scale, (16, 128))], axis=0), e_ref)
    dt_all = spread[:Q]
    end_all = spread[Q : 2 * Q]
    xd = x * dt_all
    xd_ref[...] = xd
    skip = skip_ref[...]
    gskip_ref[...] += jnp.sum(dy * x, axis=0, keepdims=True)
    lam = lam_ref[...]
    lam_hi, lam_lo = split2(lam)
    g_ref[...] = (
        dot(wide_left(b_rows), jnp.concatenate([lam_hi, lam_hi, lam_lo], axis=0)) * end_all
    )
    grad_b = quarters(dot_nt(
        jnp.concatenate(split2(xd * end_all), axis=0), jnp.concatenate([lam_hi, lam_lo], axis=0)))
    state = state_ref[0]
    dye_hi, dye_lo = split2(dy * spread[2 * Q : 3 * Q])
    grad_c = quarters(dot_nt(
        jnp.concatenate([dye_hi, dye_lo], axis=0), jnp.concatenate(split2(state), axis=0)))
    lam_new = lam * spread[3 * Q : 3 * Q + 1] + dot(
        wide_left(c_t), jnp.concatenate([dye_hi, dye_hi, dye_lo], axis=0)
    )
    lam_ref[...] = lam_new
    ended = dsum_ref[0:1, :]
    first = iota((Q, Q), 1) < HEADDIM
    first_b = (first.astype(F32).astype(BF16), 1.0 - first.astype(F32).astype(BF16))
    first_row = (iota((Q, Q), 0) < HEADDIM).astype(F32).astype(BF16)
    first_row = (first_row, 1.0 - first_row)
    gram_grad = jnp.zeros((Q, Q), F32)
    for pair in range(PAIRS):
        lanes = slice(pair * 128, pair * 128 + 128)
        weights = []
        for head in (2 * pair, 2 * pair + 1):
            differ = cumt_ref[head : head + 1, :] - cum2[:, head : head + 1]
            weights.append(jnp.exp2(jnp.where(allowed_t, differ, NEG)))
        left = jnp.concatenate([gram_t * weights[0], gram_t * weights[1]], axis=1)
        left = jnp.concatenate(split2(left), axis=0)
        dyp = dy_ref[:, lanes]
        out = dot(left, split_pair(dyp, first_b))
        g_ref[:, lanes] += out[:Q, :128] + (out[:Q, 128:] + out[Q:, :128])
        dyt_hi, dyt_lo = split2(dyp.T)
        right_hi = jnp.concatenate([dyt_hi * first_row[0], dyt_hi * first_row[1]], axis=1)
        right_lo = jnp.concatenate([dyt_lo * first_row[0], dyt_lo * first_row[1]], axis=1)
        outer = dot(
            wide_left(xd_ref[:, lanes]), jnp.concatenate([right_hi, right_hi, right_lo], axis=0))
        gram_grad = gram_grad + (outer[:, :128] * weights[0] + outer[:, 128:] * weights[1])
    g = g_ref[...]
    grad_x = dt_all * g + skip * dy
    sums = dot(jnp.concatenate(
        split2(x * g) + split2(jnp.broadcast_to(
            jnp.sum(lam_new * state, axis=0, keepdims=True), (16, INNER))), axis=0), et_ref[...])
    direct = sums[:Q] + sums[Q : 2 * Q]
    balance = through_ref[...] - dt_pos * direct
    keep_t = allowed_t.astype(F32).astype(BF16)
    b_hi, b_mid, b_lo = split3(balance)
    grad_step = dot(keep_t, b_hi) + dot(keep_t, b_mid) + dot(keep_t, b_lo) + in_last * ended
    dsum_ref[...] = sums[2 * Q : 2 * Q + 8] + sums[2 * Q + 16 : 2 * Q + 24]
    grad_dt = (direct + rate * grad_step) * sigmoid(dt_in)
    gsmall_ref[0:1, :] += jnp.sum(grad_dt, axis=0, keepdims=True)
    gsmall_ref[1:2, :] += rate * jnp.sum(dt_pos * grad_step, axis=0, keepdims=True)
    grad_c = grad_c + dot(wide_left(gram_grad.T), tall_right(b_rows))
    grad_b = grad_b + dot(wide_left(gram_grad), tall_right(c_rows))
    slope = sig_pre * (1.0 + pre * (1.0 - sig_pre))
    gnext_ref[0:Q, :INNER] = grad_x * slope[:, :INNER]
    gnext_ref[0:Q, INNER : INNER + STATE] = grad_b * slope[:, INNER : INNER + STATE]
    gnext_ref[0:Q, INNER + STATE :] = grad_c * slope[:, INNER + STATE :]
    gcp = gnext_ref[0:Q, :]
    total_ref[4:5, :] += jnp.sum(gcp, axis=0, keepdims=True)
    total_ref[3:4, :] += jnp.sum(gcp * ext_ref[8 : 8 + Q, :], axis=0, keepdims=True)
    total = convw_ref[3:4, :] * gcp
    for back in (1, 2, 3):
        ok = jnp.logical_or(rows - back >= bound, rows < bound).astype(F32)
        total_ref[3 - back : 4 - back, :] += jnp.sum(
            gcp * (ext_ref[8 - back : 8 - back + Q, :] * ok), axis=0, keepdims=True)
        okn = jnp.logical_or(rows >= bound, rows + back < bound).astype(F32)
        total = total + convw_ref[3 - back : 4 - back, :] * (gnext_ref[back : back + Q, :] * okn)
    total_ref[7:8, :] = jnp.maximum(
        total_ref[7:8, :], jnp.max(jnp.abs(total), axis=0, keepdims=True))
    total = total.astype(BF16)
    window_ref[0] = total[:, :WINDOW]
    window_ref[1] = total[:, XBC - WINDOW :]
    gnext_ref[Q : Q + 8, :] = gnext_ref[0:8, :]
    half = (steps - 1 - step) % 2
    at = pl.multiple_of(half * Q, Q)
    gp_ref[pl.ds(at, Q), :INNER] = gz_ref[0]
    gp_ref[pl.ds(at, Q), INNER : INNER + XBC] = total
    gp_ref[pl.ds(at, Q), INNER + XBC :] = grad_dt.astype(BF16)

    @pl.when(half == 0)
    def _():
        grad_normed = dot(gp_ref[...], in_ref[: INNER + XBC + 128, :])
        tok = tok_ref[...].astype(F32)
        rinv = lax.rsqrt(jnp.mean(tok * tok, axis=1, keepdims=True) + EPS_NORM)
        nhat = tok * rinv
        gain = norm_ref[...]
        gng = grad_normed * gain
        gtok_ref[...] = (cot_ref[...].astype(F32) + rinv * (
            gng - nhat * jnp.mean(nhat * gng, axis=1, keepdims=True))).astype(BF16)
        total_ref[6:7, :D] += jnp.sum(nhat * grad_normed, axis=0, keepdims=True)
        normed = (nhat * gain).astype(BF16)
        gdt = gp_ref[:, INNER + XBC :].astype(F32)
        dtw_ref[...] += dot(jnp.concatenate(
            [gdt[:Q].T, gdt[Q:].T], axis=1).astype(BF16), normed)

    @pl.when(step == steps - 1)
    def _():
        skips = head_sum(jnp.broadcast_to(gskip_ref[...], (8, INNER)), et_ref)
        small_ref[...] = jnp.zeros_like(small_ref)
        small_ref[0:HEADS, :] = dtw_ref[0:HEADS, :]
        pieces = [
            total_ref[k : k + 1, j * 128 : j * 128 + 128]
            for k in range(CONV + 1) for j in range(XBC // 128)]
        pieces += [gsmall_ref[0:1, :], gsmall_ref[1:2, :], skips[0:1, :]]
        pieces += [ggain_ref[:, j * 128 : j * 128 + 128] for j in range(INNER // 128)]
        lines = D // 128
        for number, piece in enumerate(pieces):
            line = HEADS + number // lines
            at = number % lines * 128
            small_ref[line : line + 1, at : at + 128] = piece
        small_ref[40:41, :] = total_ref[6:7, :D]
        count = float(Q * steps)
        largest = jnp.max(total_ref[7:8, :], axis=1, keepdims=True)
        normed = jnp.max(jnp.abs(norm_ref[...]), axis=1, keepdims=True) * (D ** 0.5)
        others = jnp.max(jnp.max(jnp.abs(small_ref[...]), axis=1, keepdims=True), axis=0, keepdims=True)
        power_ref[...] = jnp.broadcast_to(power_for(
            jnp.maximum(1.05 * count * largest * normed, others)), (8, 128))


def run_backward(
    proj, dy, through, states, pair, tok, cot, in_w, norm_gain, ggain, bound, e2, et, params
):
    n = proj.shape[0]
    steps = n // Q

    def rev(i):
        return (steps - 1 - i, 0)

    def rev_two(i):
        return ((steps - 1 - i) // 2, 0)

    return pl.pallas_call(
        backward_kernel,
        grid=(steps,),
        in_specs=[
            pl.BlockSpec(memory_space=pltpu.SMEM),
            pl.BlockSpec((Q, LATE), rev),
            pl.BlockSpec((8, LATE), lambda i: (jnp.maximum((steps - 1 - i) * (Q // 8) - 1, 0), 0)),
            pl.BlockSpec((Q, INNER), rev),
            pl.BlockSpec((Q, 128), rev),
            pl.BlockSpec((1, STATE, INNER), lambda i: (steps - 1 - i, 0, 0)),
            pl.BlockSpec((1, Q, INNER), lambda i: (0, steps - 1 - i, 0)),
            pl.BlockSpec((2 * Q, D), rev_two), pl.BlockSpec((2 * Q, D), rev_two),
            const_spec(in_w.shape), const_spec((1, D)), const_spec((1, INNER)),
            const_spec((256, INNER)), const_spec((INNER, 128)),
            const_spec((8, XBC)), const_spec((1, XBC)), const_spec((1, 128)),
            const_spec((1, 128)), const_spec((1, INNER)),
        ],
        out_specs=[
            pl.BlockSpec((2, Q, WINDOW), lambda i: (0, steps - 1 - i, 0)),
            pl.BlockSpec((2 * Q, D), rev_two),
            const_spec((48, D)), const_spec((8, 128)),
        ],
        out_shape=[
            jax.ShapeDtypeStruct((2, n, WINDOW), BF16),
            jax.ShapeDtypeStruct((n, D), BF16),
            jax.ShapeDtypeStruct((48, D), F32),
            jax.ShapeDtypeStruct((8, 128), F32),
        ],
        scratch_shapes=[
            pltpu.VMEM((8, XBC), F32),
            pltpu.VMEM((1, INNER), F32),
            pltpu.VMEM((8, 128), F32),
            pltpu.VMEM((128, D), F32),
            pltpu.VMEM((2 * Q, INNER + XBC + 128), BF16),
            pltpu.VMEM((Q + 8, XBC), F32),
            pltpu.VMEM((Q, 128), F32),
            pltpu.VMEM((STATE, INNER), F32),
            pltpu.VMEM((8, 128), F32),
            pltpu.VMEM((Q, INNER), F32),
            pltpu.VMEM((Q, INNER), F32),
            pltpu.VMEM((Q + 8, XBC), F32),
            pltpu.VMEM((128, Q), F32),
        ],
        compiler_params=pltpu.CompilerParams(
            dimension_semantics=("arbitrary",), vmem_limit_bytes=48 * 2**20),
        cost_estimate=pl.CostEstimate(
            flops=50 * 10**9, bytes_accessed=50 * 2**20, transcendentals=2 * 10**7),
    )(bound, proj, proj, dy, through, states, pair, tok, cot, in_w, norm_gain, ggain,
      e2, et, *params[:5])


BETA_ONE = 0.9
BETA_TWO = 0.95
EPS_ADAM = 1e-08
LANES = 128
NORM_ROWS = D // LANES
IN_ROWS = PROJ * D // LANES
CONVW_ROWS = CONV * XBC // LANES
CONVB_ROWS = XBC // LANES
GAIN_ROWS = INNER // LANES
OUT_ROWS = INNER * D // LANES
DT_ROWS = HEADS * D // LANES
SMALL_ROWS = DT_ROWS + CONVW_ROWS + CONVB_ROWS + 3 + GAIN_ROWS
OUT_START = NORM_ROWS + IN_ROWS + SMALL_ROWS - DT_ROWS
LATE_START = NORM_ROWS + INNER * NORM_ROWS
LEAD = 896
STAGE_ROWS = 16264
STAGE_BLOCKS = 5
MARK = 16


PREP_STEPS = 7
IN_BLOCK = 512
OUT_BLOCK = 256
SMALL_START = NORM_ROWS + IN_ROWS


def prepare_kernel(
    flat_ref,
    in_ref, out_ref, norm_ref, convw_ref, convb_ref, dtb_ref, alog_ref, skip_ref, gain_ref,
    e_ref, et_ref,
    stage_ref,
):
    step = pl.program_id(0)

    @pl.when(step == 0)
    def _():
        rows = flat_ref[0:16, :].astype(F32)
        for lane in range(NORM_ROWS):
            norm_ref[:, lane * LANES : lane * LANES + LANES] = rows[lane : lane + 1, :]
        low = SMALL_START // 16 * 16
        stage_ref[0:112, :] = flat_ref[low : low + 112, :].astype(F32)
        at = SMALL_START - low
        convw_ref[...] = jnp.zeros_like(convw_ref)
        for tap in range(CONV):
            for lane in range(CONVB_ROWS):
                convw_ref[tap : tap + 1, lane * LANES : lane * LANES + LANES] = stage_ref[
                    at : at + 1, :]
                at += 1
        for lane in range(CONVB_ROWS):
            convb_ref[:, lane * LANES : lane * LANES + LANES] = stage_ref[at : at + 1, :]
            at += 1
        heads = iota((1, LANES), 1) < HEADS
        dtb_ref[...] = jnp.where(heads, stage_ref[at : at + 1, :], 0.0)
        alog_ref[...] = jnp.where(heads, stage_ref[at + 1 : at + 2, :], 0.0)
        skips = jnp.where(heads, stage_ref[at + 2 : at + 3, :], 0.0)
        at += 3
        for lane in range(GAIN_ROWS):
            gain_ref[:, lane * LANES : lane * LANES + LANES] = stage_ref[at : at + 1, :]
            at += 1
        one = (iota((128, INNER), 1) // HEADDIM == iota((128, INNER), 0)).astype(F32).astype(BF16)
        e_ref[0:128, :] = one
        e_ref[128:256, :] = one
        et_ref[...] = (
            iota((INNER, 128), 0) // HEADDIM == iota((INNER, 128), 1)).astype(F32).astype(BF16)
        skip_ref[...] = dot(jnp.broadcast_to(skips, (16, LANES)).astype(BF16), one)[0:1, :]

    def block(start, offset, rows, dest_ref):
        size = rows * NORM_ROWS + 16
        at = pl.multiple_of(start + step * (rows * NORM_ROWS), 16)
        stage_ref[0:size, :] = flat_ref[pl.ds(at, size), :].astype(F32)
        for lane in range(NORM_ROWS):
            dest_ref[:, lane * LANES : lane * LANES + LANES] = stage_ref[
                pl.ds(offset + lane, rows, stride=NORM_ROWS), :].astype(BF16)

    block(0, NORM_ROWS, IN_BLOCK, in_ref)

    @pl.when(step == PREP_STEPS - 1)
    def _():
        used = PROJ - (PREP_STEPS - 1) * IN_BLOCK
        in_ref[used:, :] = jnp.zeros((IN_BLOCK - used, D), BF16)

    @pl.when(step < INNER // OUT_BLOCK)
    def _():
        low = OUT_START // 16 * 16
        block(low, OUT_START - low, OUT_BLOCK, out_ref)


def run_prepare(flat):
    vector = lambda n: jax.ShapeDtypeStruct((1, n), F32)
    return pl.pallas_call(
        prepare_kernel,
        grid=(PREP_STEPS,),
        in_specs=[const_spec(flat.shape)],
        out_specs=[
            pl.BlockSpec((IN_BLOCK, D), lambda i: (i, 0)),
            pl.BlockSpec((OUT_BLOCK, D), lambda i: (jnp.minimum(i, INNER // OUT_BLOCK - 1), 0)),
            const_spec((1, D)), const_spec((8, XBC)), const_spec((1, XBC)), const_spec((1, 128)),
            const_spec((1, 128)), const_spec((1, INNER)), const_spec((1, INNER)),
            const_spec((256, INNER)), const_spec((INNER, 128)),
        ],
        out_shape=[
            jax.ShapeDtypeStruct((PREP_STEPS * IN_BLOCK, D), BF16),
            jax.ShapeDtypeStruct((INNER, D), BF16),
            vector(D), jax.ShapeDtypeStruct((8, XBC), F32), vector(XBC), vector(128), vector(128),
            vector(INNER), vector(INNER),
            jax.ShapeDtypeStruct((256, INNER), BF16), jax.ShapeDtypeStruct((INNER, 128), BF16),
        ],
        scratch_shapes=[pltpu.VMEM((IN_BLOCK * NORM_ROWS + 16, LANES), F32)],
        compiler_params=pltpu.CompilerParams(
            dimension_semantics=("arbitrary",), vmem_limit_bytes=40 * 2**20),
        cost_estimate=pl.CostEstimate(
            flops=10**9, bytes_accessed=16 * 2**20, transcendentals=0),
    )(flat)


def stage_kernel(
    who_ref, early_ref, early_other_ref, late_ref, late_other_ref, small_ref,
    grad_ref,
    stage_ref,
):
    step = pl.program_id(0)
    upper = who_ref[0]
    mine = who_ref[1]
    block = grad_ref.shape[0]
    half = 2 * block * STAGE_BLOCKS

    @pl.when(step == 0)
    def _():
        early_at = LEAD + jnp.where(upper == 1, OUT_START - half, NORM_ROWS)
        window = LATE_START + (XBC - WINDOW) * NORM_ROWS
        late_at = LEAD + jnp.where(upper == 1, window - half, LATE_START)
        def lay(source_ref, start, size):
            for lane in range(NORM_ROWS):
                stage_ref[pl.ds(start + lane, size, stride=NORM_ROWS), :] = source_ref[
                    0:size, lane * LANES : lane * LANES + LANES]

        lines = late_ref.shape[0]
        lay(late_ref, late_at + mine * (lines * NORM_ROWS), lines)
        lay(late_other_ref, late_at + (1 - mine) * (lines * NORM_ROWS), lines)

        @pl.when(upper == 1)
        def _():
            lay(small_ref, LEAD + OUT_START - half - SMALL_ROWS, -(-SMALL_ROWS // NORM_ROWS))

        lines = early_ref.shape[0]
        lay(early_ref, early_at + mine * (lines * NORM_ROWS), lines)
        lay(early_other_ref, early_at + (1 - mine) * (lines * NORM_ROWS), lines)

        @pl.when(upper == 0)
        def _():
            for lane in range(NORM_ROWS):
                stage_ref[LEAD + lane : LEAD + lane + 1, :] = small_ref[
                    40:41, lane * LANES : lane * LANES + LANES]

        @pl.when(upper == 1)
        def _():
            at = LEAD + OUT_START + OUT_ROWS - half
            stage_ref[at : LEAD + half, :] = jnp.zeros((LEAD + half - at, LANES), F32)

    @pl.when(step > 0)
    def _():
        at = LEAD + mine * (half // 2) + (step - 1) * block
        grad_ref[...] = stage_ref[pl.ds(pl.multiple_of(at, 8), block), :]


def run_stage(who, rows, early, early_other, late, late_other, small):
    block = rows // STAGE_BLOCKS
    return pl.pallas_call(
        stage_kernel,
        grid=(STAGE_BLOCKS + 1,),
        in_specs=[
            pl.BlockSpec(memory_space=pltpu.SMEM),
            const_spec(early.shape), const_spec(early.shape),
            const_spec(late.shape), const_spec(late.shape), const_spec(small.shape),
        ],
        out_specs=pl.BlockSpec((block, LANES), lambda i: (jnp.maximum(i - 1, 0), 0)),
        out_shape=jax.ShapeDtypeStruct((rows, LANES), F32),
        scratch_shapes=[pltpu.VMEM((STAGE_ROWS, LANES), F32)],
        compiler_params=pltpu.CompilerParams(
            dimension_semantics=("arbitrary",), vmem_limit_bytes=48 * 2**20),
        cost_estimate=pl.CostEstimate(
            flops=10**6, bytes_accessed=12 * 2**20, transcendentals=0),
    )(who, early, early_other, late, late_other, small)


def swap(values, axis, bit):
    size = lax.axis_size(axis)
    return lax.ppermute(values, axis, [(i, i ^ bit) for i in range(size)])


def to_wire(values, power):
    return (values * jnp.exp2(power)).astype(jnp.float16)


def from_wire(values, power):
    return values.astype(F32) * jnp.exp2(-power)


def place_of(axis, bit, count):
    return (lax.axis_index(axis) >> (bit.bit_length() - 1)) & (count - 1)


def wire_masks(axis, bit, count, rows, mark):
    place = place_of(axis, bit, count)
    line = jnp.arange(rows + mark, dtype=jnp.int32)
    return [
        jnp.where((place ^ offset) == count - 1, line < mark, line >= rows)
        for offset in range(1, count)]


def hop_plan():
    plan = []
    for rows in (INNER // 2, WINDOW // 2):
        plan += [("zero", 1, 2, rows, LANES), ("zero", 2, 2, rows, MARK)]
    for rows in (INNER // 2, WINDOW // 2 + WINDOW // 8):
        for bit, count in data_groups():
            rows //= count
            plan.append(("dp", bit, count, rows, min(MARK, rows)))
    return plan


def scatter(values, power, masks, axis, bit=1, count=2, after=None, sent=None):
    place = place_of(axis, bit, count)
    rows = values.shape[-2] // count
    mark = min(MARK, rows)
    dim = values.ndim - 2
    total = lax.dynamic_slice_in_dim(values, place * rows, rows, dim)
    least = power
    arrived = []
    for offset in range(1, count):
        to = place ^ offset
        last = to == count - 1
        start = to * rows - jnp.where(last, mark, 0)
        send = lax.dynamic_slice_in_dim(values, start, rows + mark, dim)
        marked = masks[axis, bit, count, rows, mark][offset - 1][:, None]
        wire = jnp.where(marked, power, send * jnp.exp2(power)).astype(jnp.float16)
        arrived.append(swap(wire, axis, bit * offset))
        if sent is not None:
            sent.append(wire)
    if after is not None:
        arrived, _ = lax.optimization_barrier((arrived, after))
    last = place == count - 1
    for got in arrived:
        got_power = lax.dynamic_slice_in_dim(
            got, jnp.where(last, 0, rows), 1, dim).reshape(1, D).astype(F32)
        body = lax.dynamic_slice_in_dim(got, jnp.where(last, mark, 0), rows, dim)
        total = total + from_wire(body, got_power)
        least = jnp.minimum(least, got_power)
    return total, least - float(count.bit_length() - 1)


def scatter_product(left, right, power, masks, axis, bit):
    def product(part):
        return lax.dot_general(
            part, right, (((1,), (1,)), ((0,), (0,))), preferred_element_type=F32)

    side = place_of(axis, bit, 2)
    rows = left.shape[2] // 2
    send = product(jnp.where(side == 1, left[:, :, : rows + LANES], left[:, :, rows - LANES :]))
    marked = masks[axis, bit, 2, rows, LANES][0][None, :, None]
    wire = jnp.where(marked, power, send * jnp.exp2(power)).astype(jnp.float16)
    got = swap(wire, axis, bit)
    left, _ = lax.optimization_barrier((left, wire))
    keep = product(jnp.where(side == 0, left[:, :, :rows], left[:, :, rows:]))
    keep, got = lax.optimization_barrier((keep, got))
    got_power = lax.dynamic_slice(
        got, (0, (1 - side) * rows, 0), (1, 1, D))[0].astype(F32)
    body = lax.dynamic_slice_in_dim(got, side * LANES, rows, 1)
    return keep + from_wire(body, got_power), jnp.minimum(power, got_power) - 1.0


def everyones(values, axis, bit=1, count=2):
    place = place_of(axis, bit, count)
    pieces = [values] + [swap(values, axis, bit * offset) for offset in range(1, count)]
    step = 1
    while step < count:
        flip = (place & step) != 0
        pieces = [
            jnp.where(flip, pieces[i ^ step], pieces[i]) for i in range(count)]
        step *= 2
    return pieces


def gather(values, axis, bit=1, count=2):
    return jnp.concatenate(everyones(values, axis, bit, count))


def add_pair(values, axis, bit, after=None):
    got = swap(values, axis, bit)
    if after is not None:
        got, _ = lax.optimization_barrier((got, after))
    return values + got


def data_groups():
    size = lax.axis_size("dp")
    groups = [(1, 2)]
    bit = 2
    while bit < size:
        count = 4 if bit * 4 <= size else 2
        groups.append((bit, count))
        bit *= count
    return groups


def dot_tn(a, b):
    return lax.dot_general(a, b, (((0,), (0,)), ((), ())), preferred_element_type=F32)


def pick_rows(index, rows):
    chosen = index[:, None] == jnp.arange(rows.shape[0], dtype=jnp.int32)[None, :]
    return dot(chosen.astype(BF16), rows).astype(BF16)


def on_device(
    tokens, loss_sensitivity, lengths, holder_sequence_list, master, moment_one, moment_two,
    adam_rates, iteration_tally,
):
    group_devices = lax.axis_size("zero")
    data_devices = lax.axis_size("dp")
    zero_index = lax.axis_index("zero")
    dp_index = lax.axis_index("dp")
    seq_len = loss_sensitivity.shape[1]
    group_seqs = tokens.shape[0]
    span = tokens.shape[1]
    slots = group_seqs // data_devices
    shard_rows = master.shape[0] // LANES
    tie = lax.optimization_barrier

    own = master.reshape(shard_rows, LANES)
    arranged = holder_sequence_list.reshape(data_devices, group_devices, slots)
    group_order = lax.dynamic_index_in_dim(arranged, zero_index, 1, keepdims=False).reshape(-1)
    local_ids = group_order - zero_index * group_seqs
    dealt = tokens.at[local_ids].get(mode="promise_in_bounds")
    flat = lax.all_gather(own.astype(BF16), "zero", axis=0, tiled=True)

    local_tok = lax.all_to_all(dealt, "dp", split_axis=0, concat_axis=0, tiled=True)
    my_seqs = lax.dynamic_slice_in_dim(group_order, dp_index * slots, slots)
    bound = lengths[my_seqs[0]]
    positions = jnp.arange(seq_len, dtype=jnp.int32)

    in_w, out_w, norm_gain, *params, e2, et = run_prepare(flat)
    cot = loss_sensitivity[0]
    gm = dot_nt(cot, out_w)
    cot_top = jnp.max(jnp.abs(cot)).astype(F32).reshape(1)
    blocks = jnp.arange(data_devices, dtype=jnp.int32)[:, None, None] * span
    within = blocks + jnp.arange(span, dtype=jnp.int32)[None, None, :]
    within = within + jnp.arange(slots, dtype=jnp.int32)[None, :, None] * bound
    unpack_rows = jnp.minimum(within, seq_len - 1).reshape(-1)

    restore = jnp.zeros_like(local_ids).at[local_ids].set(
        jnp.arange(group_seqs, dtype=jnp.int32))
    mine = lax.dynamic_slice_in_dim(lengths, zero_index * group_seqs, group_seqs)
    at = dp_index * span + jnp.arange(span, dtype=jnp.int32)
    live = (at[None, :] < mine[:, None])[:, :, None]

    masks = {hop: wire_masks(*hop) for hop in hop_plan()}
    flags = list(masks.values())
    local_tok, in_w, gm, cot_top, unpack_rows, restore, live, flags = tie(
        (local_tok, in_w, gm, cot_top, unpack_rows, restore, live, flags))
    masks = dict(zip(masks, flags))
    own_late, _ = tie((own, flat[:8]))
    whole_master = lax.all_gather(own_late, "zero", axis=0, tiled=True)

    def place(slot, at):
        return (at // span) * (slots * span) + slot * span + at % span

    source = jnp.where(positions < bound, place(0, positions), place(1, positions - bound))
    packed = pick_rows(source, local_tok.reshape(slots * seq_len, D))
    def spread(rows):
        return pick_rows(unpack_rows, rows).reshape(data_devices * slots, span, D)

    def send_back(picked):
        return lax.all_to_all(picked, "dp", split_axis=0, concat_axis=0, tiled=True)

    bound_arr = bound.reshape(1)
    tok = packed.astype(F32)
    nhat = tok * lax.rsqrt(jnp.mean(tok * tok, axis=1, keepdims=True) + EPS_NORM)
    normed = (nhat * norm_gain).astype(BF16)
    proj_z = dot_nt(normed, in_w[:INNER])
    proj = dot_nt(normed, in_w[INNER:PROJ])
    pair, dy, through, states, ggain, early_power = run_forward(
        proj_z, proj, gm, bound_arr, cot_top, norm_gain, e2, et, params)
    result = (tok + dot(pair[1], out_w)).astype(BF16)
    picked = spread(result)
    picked, pair = tie((picked, pair))
    back_out = send_back(picked)
    early_power = early_power[0:1, 0:1]
    early, early_power = scatter_product(
        pair, jnp.stack([normed, cot]), early_power, masks, "zero", 1)
    early, early_power, dy = tie((early.reshape(INNER, D), early_power, dy))
    early, early_power = scatter(early, early_power, masks, "zero", 2)
    window, grad_tok, small, late_power = run_backward(
        proj, dy, through, states, pair, packed, cot, in_w, norm_gain, ggain,
        bound_arr, e2, et, params)
    window, small, late_power, early, early_power, whole_master = tie(
        (window, small, late_power, early, early_power, whole_master))

    groups = data_groups()
    late_power = late_power[0:1, 0:1]
    late, late_power = scatter_product(
        window, jnp.stack([normed, normed]), late_power, masks, "zero", 1)
    late = late.reshape(WINDOW, D)
    small = add_pair(small, "zero", 1)
    early, early_power, grad_tok, _ = tie((early, early_power, grad_tok, late))
    late, late_power = scatter(late, late_power, masks, "zero", 2)
    early, early_power = scatter(early, early_power, masks, "dp", *groups[0])
    small = add_pair(small, "zero", 2, late)
    early_before, power_before = early, early_power
    picked_grad = spread(grad_tok)
    tokens, back_out, _ = tie((tokens, back_out, grad_tok))
    back_rows = back_out.at[restore].get(mode="promise_in_bounds")
    tokens_out = jnp.where(live, back_rows, tokens)
    new_master = jnp.zeros((group_devices, shard_rows, LANES), F32)
    late, tokens_out, new_master, picked_grad = tie((late, tokens_out, new_master, picked_grad))
    lines = small.shape[0]
    late = jnp.concatenate([late, small, jnp.zeros((WINDOW // 8 - lines, D), F32)])
    late, late_power = scatter(late, late_power, masks, "dp", *groups[0])
    sent = []
    for group in groups[1:]:
        late, late_power = scatter(late, late_power, masks, "dp", *group, sent=sent)
    early, early_power = early_before, power_before
    for group in groups[1:]:
        early, early_power = scatter(early, early_power, masks, "dp", *group, after=sent)
    early = to_wire(early, early_power)
    for group in reversed(groups[1:]):
        early = gather(early, "dp", *group)
    early, _ = tie((early, late))
    late = to_wire(late, late_power)
    early = from_wire(gather(early, "dp", *groups[0]), early_power)
    early, picked_grad, _ = tie((early, picked_grad, late))
    for group in reversed(groups[1:]):
        late = gather(late, "dp", *group)
    early_other = swap(early, "zero", 1)
    back_grad = send_back(picked_grad)
    wire = gather(late, "dp", *groups[0])
    late = from_wire(wire[: WINDOW // 2], late_power)
    small = from_wire(wire[WINDOW // 2 : WINDOW // 2 + lines], late_power)
    late_other = swap(late, "zero", 1)

    steps_f = iteration_tally[0].astype(F32)
    who = jnp.stack([zero_index >> 1, zero_index & 1]).astype(jnp.int32)
    first = moment_one.reshape(shard_rows, LANES)
    second = moment_two.reshape(shard_rows, LANES)
    grad_shard = run_stage(who, shard_rows, early, early_other, late, late_other, small)
    first_scale = 1.0 / (1.0 - jnp.power(BETA_ONE, steps_f))
    second_scale = 1.0 / (1.0 - jnp.power(BETA_TWO, steps_f))

    def moments(grad, first, second):
        return (
            BETA_ONE * first + (1.0 - BETA_ONE) * grad,
            BETA_TWO * second + (1.0 - BETA_TWO) * grad * grad)

    def quotient(rows):
        first_next, second_next = moments(grad_shard[rows], first[rows], second[rows])
        return ((first_next * first_scale) / (
            jnp.sqrt(second_next * second_scale) + EPS_ADAM)).astype(jnp.float16)

    whole_master = whole_master.reshape(group_devices, shard_rows, LANES)

    def put(new_master, piece, offset):
        shard = zero_index ^ offset
        old = lax.dynamic_index_in_dim(whole_master, shard, 0, keepdims=False)
        new = old - adam_rates[0] * (piece.astype(F32) + adam_rates[1] * old)
        return lax.dynamic_update_index_in_dim(new_master, new, shard, 0)

    own_part, first, second = tie((quotient(slice(0, shard_rows)), first, second))
    across = swap(own_part, "zero", 2)
    core = swap(own_part, "zero", 1)
    first_next, second_next = moments(grad_shard, first, second)
    new_master = put(put(new_master, own_part, 0), core, 1)
    across, new_master, first_next, second_next = tie(
        (across, new_master, first_next, second_next))
    last = swap(across, "zero", 1)
    new_master = put(new_master, across, 2)
    last, new_master = tie((last, new_master))
    new_master = put(new_master, last, 3)
    back_grad, new_master = tie((back_grad, new_master))
    grad_tokens = jnp.where(
        live, back_grad.at[restore].get(mode="promise_in_bounds"), jnp.zeros((), BF16))
    return (
        tokens_out, grad_tokens, new_master.reshape(-1), grad_shard.reshape(-1),
        first_next.reshape(-1), second_next.reshape(-1))


def solution(mesh):
    return jax.shard_map(
        on_device,
        mesh=mesh,
        in_specs=(
            P("zero", "dp", None), P(("dp", "zero"), None, None), P(), P(),
            P("zero"), P("zero"), P("zero"), P(), P(),
        ),
        out_specs=(
            P("zero", "dp", None), P("zero", "dp", None), P(), P("zero"), P("zero"), P("zero"),
        ),
        check_vma=False,
    )
```

```python
import jax
import jax.numpy as jnp
from jax import lax
from jax.experimental import pallas as pl
from jax.experimental.pallas import tpu as pltpu
from jax.sharding import PartitionSpec as P

D = 768
HEADS = 24
HEADDIM = 64
STATE = 128
CONV = 4
INNER = 1536
XBC = 1792
PROJ = 3352
Q = 128
LATE = PROJ - INNER
WINDOW = 1024
PAIRS = HEADS // 2
EPS_NORM = 1e-05
NEG = -1e30
F16_TOP = 30000.0
LOG2E = 1.4426950408889634
F32 = jnp.float32
BF16 = jnp.bfloat16


def dot(a, b):
    return lax.dot_general(a, b, (((1,), (0,)), ((), ())), preferred_element_type=F32)


def dot_nt(a, b):
    return lax.dot_general(a, b, (((1,), (1,)), ((), ())), preferred_element_type=F32)


def split2(v):
    hi = v.astype(BF16)
    return hi, (v - hi.astype(F32)).astype(BF16)


def split3(v):
    hi = v.astype(BF16)
    rest = v - hi.astype(F32)
    mid = rest.astype(BF16)
    return hi, mid, (rest - mid.astype(F32)).astype(BF16)


def wide_left(v):
    hi, lo = split2(v)
    return jnp.concatenate([hi, lo, hi], axis=1)


def tall_right(v):
    hi, lo = split2(v)
    return jnp.concatenate([hi, hi, lo], axis=0)


def split_pair(v, masks):
    hi, lo = split2(v)
    return jnp.concatenate([
        jnp.concatenate([hi * masks[0], lo * masks[0]], axis=1),
        jnp.concatenate([hi * masks[1], lo * masks[1]], axis=1)], axis=0)


def sigmoid(v):
    return lax.logistic(v)


def softplus(v):
    return jnp.maximum(v, 0.0) + jnp.log1p(jnp.exp(-jnp.abs(v)))


def iota(shape, dim):
    return lax.broadcasted_iota(jnp.int32, shape, dim)


def expand(v, e_ref):
    hi, lo = split2(v)
    return dot(jnp.concatenate([hi, lo], axis=1), e_ref[...])


def head_sum(v, et_ref):
    hi, lo = split2(v)
    return dot(hi, et_ref[...]) + dot(lo, et_ref[...])


def quarters(out):
    return out[:Q, :Q] + (out[:Q, Q:] + out[Q:, :Q])


def power_for(bound):
    scale = jnp.log(0.9 * F16_TOP / jnp.maximum(bound, 1e-30)) * LOG2E
    return jnp.clip(jnp.floor(scale), -126.0, 120.0)


def chunk_masks(t0, bound):
    rows = t0 + iota((Q, 1), 0)
    rr = t0 + iota((Q, Q), 0)
    cc = t0 + iota((Q, Q), 1)
    return rows, rr, cc


def conv_rows(ext_ref, w_ref, b_ref, rows, bound):
    total = b_ref[...] + w_ref[3:4, :] * ext_ref[8 : 8 + Q, :]
    for back in (1, 2, 3):
        ok = jnp.logical_or(rows - back >= bound, rows < bound).astype(F32)
        total = total + w_ref[3 - back : 4 - back, :] * (ext_ref[8 - back : 8 - back + Q, :] * ok)
    return total


def decay_parts(dt_raw, dtb_ref, alog_ref, rr, cc):
    dt_in = dt_raw + dtb_ref[...]
    dt_pos = softplus(dt_in)
    rate = -jnp.exp(alog_ref[...])
    step = dt_pos * rate
    tri = (cc <= rr).astype(F32).astype(BF16)
    s_hi, s_mid, s_lo = split3(step)
    cum = dot(tri, s_hi) + dot(tri, s_mid) + dot(tri, s_lo)
    return dt_in, dt_pos, rate, cum


def forward_kernel(
    bound_ref, cot_ref, z_ref, proj_ref, gm_ref, norm_ref, e_ref, et_ref, convw_ref, convb_ref, dtb_ref, alog_ref,
    skip_ref, gain_ref,
    pair_ref, dy_ref, through_ref, state_ref, ggain_ref, power_ref,
    zmax_ref, ext_ref, dt_ref, carry_ref, xd_ref, acc_ref, cumt_ref,
):
    step = pl.program_id(0)
    bound = bound_ref[0]
    t0 = step * Q

    @pl.when(step == 0)
    def _():
        ext_ref[0:8, :] = jnp.zeros((8, XBC), F32)
        carry_ref[...] = jnp.zeros_like(carry_ref)
        dt_ref[...] = jnp.zeros_like(dt_ref)
        ggain_ref[...] = jnp.zeros_like(ggain_ref)
        zmax_ref[...] = jnp.zeros_like(zmax_ref)

    rows, rr, cc = chunk_masks(t0, bound)
    ext_ref[8 : 8 + Q, :] = proj_ref[:, :XBC]
    pre = conv_rows(ext_ref, convw_ref, convb_ref, rows, bound)
    ext_ref[0:8, :] = ext_ref[Q : Q + 8, :]
    conv_out = pre * sigmoid(pre)
    x = conv_out[:, :INNER]
    b_rows = conv_out[:, INNER : INNER + STATE]
    c_rows = conv_out[:, INNER + STATE :]
    dt_ref[:, 0:HEADS] = proj_ref[:, XBC:LATE]
    _, dt_pos, _, cum = decay_parts(dt_ref[...], dtb_ref, alog_ref, rr, cc)
    cum_end = cum[Q - 1 : Q, :]
    keep = jnp.logical_or(rows < bound, bound < t0).astype(F32)
    in_last = jnp.logical_or(rows >= bound, bound > t0 + Q - 1).astype(F32)
    whole = jnp.logical_or(bound < t0, bound > t0 + Q - 1).astype(F32)
    from_start = jnp.exp(cum) * keep
    to_end = jnp.exp(cum_end - cum) * in_last
    carry_scale = jnp.exp(cum_end) * whole
    allowed = jnp.logical_and(cc <= rr, (cc >= bound) == (rr >= bound))
    cum2 = cum * LOG2E
    cumt_ref[...] = cum2.T

    state = carry_ref[...]
    state_ref[0] = state
    spread = expand(jnp.concatenate(
        [dt_pos, to_end, from_start, jnp.broadcast_to(carry_scale, (16, 128))], axis=0), e_ref)
    xd = x * spread[:Q]
    xd_ref[...] = xd
    acc = dot(wide_left(c_rows), tall_right(state)) * spread[2 * Q : 3 * Q]
    acc_ref[...] = acc + skip_ref[...] * x
    b_t = b_rows.T
    carry_ref[...] = state * spread[3 * Q : 3 * Q + 1] + dot(
        wide_left(b_t), tall_right(xd * spread[Q : 2 * Q]))
    gram = dot(wide_left(c_rows), tall_right(b_t))
    first = iota((Q, Q), 1) < HEADDIM
    first_b = (first.astype(F32).astype(BF16), 1.0 - first.astype(F32).astype(BF16))
    for pair in range(PAIRS):
        parts = []
        for head in (2 * pair, 2 * pair + 1):
            differ = cum2[:, head : head + 1] - cumt_ref[head : head + 1, :]
            parts.append(gram * jnp.exp2(jnp.where(allowed, differ, NEG)))
        left = jnp.concatenate(split2(jnp.concatenate(parts, axis=1)), axis=0)
        lanes = slice(pair * 128, pair * 128 + 128)
        xp = xd_ref[:, lanes]
        out = dot(left, split_pair(xp, first_b))
        acc_ref[:, lanes] += out[:Q, :128] + (out[:Q, 128:] + out[Q:, :128])
    scanned = acc_ref[...]
    z = z_ref[...]
    sig_z = sigmoid(z)
    silu_z = z * sig_z
    gated = scanned * silu_z
    ginv = lax.rsqrt(jnp.mean(gated * gated, axis=1, keepdims=True) + EPS_NORM)
    mhat = gated * ginv
    pair_ref[1] = (mhat * gain_ref[...]).astype(BF16)
    gm = gm_ref[...]
    ggain_ref[...] += jnp.sum(mhat * gm, axis=0, keepdims=True)
    gmg = gm * gain_ref[...]
    ggated = ginv * (gmg - mhat * jnp.mean(mhat * gmg, axis=1, keepdims=True))
    dy = ggated * silu_z
    dy_ref[...] = dy
    grad_z = ggated * scanned * (sig_z * (1.0 + z * (1.0 - sig_z)))
    zmax_ref[...] = jnp.maximum(zmax_ref[...], jnp.max(jnp.abs(grad_z), axis=0, keepdims=True))
    pair_ref[0] = grad_z.astype(BF16)
    through_ref[...] = head_sum(dy * (scanned - skip_ref[...] * x), et_ref)

    @pl.when(step == pl.num_programs(0) - 1)
    def _():
        count = float(Q * pl.num_programs(0))
        largest = jnp.max(zmax_ref[...], axis=1, keepdims=True)
        normed = jnp.max(jnp.abs(norm_ref[...]), axis=1, keepdims=True) * (D ** 0.5)
        mixed = jnp.max(jnp.abs(gain_ref[...]), axis=1, keepdims=True) * (INNER ** 0.5)
        power_ref[...] = jnp.broadcast_to(power_for(
            1.05 * count * jnp.maximum(largest * normed, cot_ref[0] * mixed)), (8, 128))


def const_spec(shape):
    return pl.BlockSpec(shape, lambda *_: (0,) * len(shape))


def run_forward(z, proj, gm, bound, cot_top, norm_gain, e2, et, params):
    n = proj.shape[0]
    steps = n // Q
    return pl.pallas_call(
        forward_kernel,
        grid=(steps,),
        in_specs=[
            pl.BlockSpec(memory_space=pltpu.SMEM), pl.BlockSpec(memory_space=pltpu.SMEM),
            pl.BlockSpec((Q, INNER), lambda i: (i, 0)),
            pl.BlockSpec((Q, LATE), lambda i: (i, 0)),
            pl.BlockSpec((Q, INNER), lambda i: (i, 0)),
            const_spec((1, D)),
            const_spec((256, INNER)), const_spec((INNER, 128)),
            const_spec((8, XBC)), const_spec((1, XBC)), const_spec((1, 128)),
            const_spec((1, 128)), const_spec((1, INNER)), const_spec((1, INNER)),
        ],
        out_specs=[
            pl.BlockSpec((2, Q, INNER), lambda i: (0, i, 0)),
            pl.BlockSpec((Q, INNER), lambda i: (i, 0)),
            pl.BlockSpec((Q, 128), lambda i: (i, 0)),
            pl.BlockSpec((1, STATE, INNER), lambda i: (i, 0, 0)),
            const_spec((1, INNER)), const_spec((8, 128)),
        ],
        out_shape=[
            jax.ShapeDtypeStruct((2, n, INNER), BF16),
            jax.ShapeDtypeStruct((n, INNER), F32),
            jax.ShapeDtypeStruct((n, 128), F32),
            jax.ShapeDtypeStruct((steps, STATE, INNER), F32),
            jax.ShapeDtypeStruct((1, INNER), F32),
            jax.ShapeDtypeStruct((8, 128), F32),
        ],
        scratch_shapes=[
            pltpu.VMEM((1, INNER), F32),
            pltpu.VMEM((Q + 8, XBC), F32),
            pltpu.VMEM((Q, 128), F32),
            pltpu.VMEM((STATE, INNER), F32),
            pltpu.VMEM((Q, INNER), F32),
            pltpu.VMEM((Q, INNER), F32),
            pltpu.VMEM((128, Q), F32),
        ],
        compiler_params=pltpu.CompilerParams(
            dimension_semantics=("arbitrary",), vmem_limit_bytes=48 * 2**20),
        cost_estimate=pl.CostEstimate(
            flops=30 * 10**9, bytes_accessed=40 * 2**20, transcendentals=10**7),
    )(bound, cot_top, z, proj, gm, norm_gain, e2, et, *params)


def backward_kernel(
    bound_ref, proj_ref, before_ref, dy_ref, through_ref, state_ref, gz_ref, tok_ref, cot_ref,
    in_ref, norm_ref, ggain_ref,
    e_ref, et_ref, convw_ref, convb_ref, dtb_ref, alog_ref, skip_ref,
    window_ref, gtok_ref, small_ref, power_ref,
    total_ref, gskip_ref, gsmall_ref, dtw_ref, gp_ref, ext_ref, dt_ref, lam_ref, dsum_ref, xd_ref, g_ref, gnext_ref, cumt_ref,
):
    step = pl.program_id(0)
    steps = pl.num_programs(0)
    bound = bound_ref[0]
    t0 = (steps - 1 - step) * Q

    @pl.when(step == 0)
    def _():
        lam_ref[...] = jnp.zeros_like(lam_ref)
        dsum_ref[...] = jnp.zeros_like(dsum_ref)
        dt_ref[...] = jnp.zeros_like(dt_ref)
        gnext_ref[Q : Q + 8, :] = jnp.zeros((8, XBC), F32)
        gskip_ref[...] = jnp.zeros_like(gskip_ref)
        total_ref[...] = jnp.zeros_like(total_ref)
        dtw_ref[...] = jnp.zeros_like(dtw_ref)
        gsmall_ref[...] = jnp.zeros_like(gsmall_ref)

    rows, rr, cc = chunk_masks(t0, bound)
    dy = dy_ref[...]
    first_chunk = (t0 > 0).astype(F32)
    ext_ref[0:8, :] = before_ref[:, :XBC] * first_chunk
    ext_ref[8 : 8 + Q, :] = proj_ref[:, :XBC]
    pre = conv_rows(ext_ref, convw_ref, convb_ref, rows, bound)
    sig_pre = sigmoid(pre)
    conv_out = pre * sig_pre
    x = conv_out[:, :INNER]
    b_rows = conv_out[:, INNER : INNER + STATE]
    c_rows = conv_out[:, INNER + STATE :]
    dt_ref[:, 0:HEADS] = proj_ref[:, XBC:LATE]
    dt_in, dt_pos, rate, cum = decay_parts(dt_ref[...], dtb_ref, alog_ref, rr, cc)
    cum_end = cum[Q - 1 : Q, :]
    keep = jnp.logical_or(rows < bound, bound < t0).astype(F32)
    in_last = jnp.logical_or(rows >= bound, bound > t0 + Q - 1).astype(F32)
    whole = jnp.logical_or(bound < t0, bound > t0 + Q - 1).astype(F32)
    from_start = jnp.exp(cum) * keep
    to_end = jnp.exp(cum_end - cum) * in_last
    carry_scale = jnp.exp(cum_end) * whole
    allowed_t = jnp.logical_and(rr <= cc, (cc >= bound) == (rr >= bound))
    cum2 = cum * LOG2E
    cumt_ref[...] = cum2.T
    c_t = c_rows.T
    gram_t = dot(wide_left(b_rows), tall_right(c_t))
    spread = expand(jnp.concatenate(
        [dt_pos, to_end, from_start, jnp.broadcast_to(carry_scale, (16, 128))], axis=0), e_ref)
    dt_all = spread[:Q]
    end_all = spread[Q : 2 * Q]
    xd = x * dt_all
    xd_ref[...] = xd
    skip = skip_ref[...]
    gskip_ref[...] += jnp.sum(dy * x, axis=0, keepdims=True)
    lam = lam_ref[...]
    lam_hi, lam_lo = split2(lam)
    g_ref[...] = (
        dot(wide_left(b_rows), jnp.concatenate([lam_hi, lam_hi, lam_lo], axis=0)) * end_all
    )
    grad_b = quarters(dot_nt(
        jnp.concatenate(split2(xd * end_all), axis=0), jnp.concatenate([lam_hi, lam_lo], axis=0)))
    state = state_ref[0]
    dye_hi, dye_lo = split2(dy * spread[2 * Q : 3 * Q])
    grad_c = quarters(dot_nt(
        jnp.concatenate([dye_hi, dye_lo], axis=0), jnp.concatenate(split2(state), axis=0)))
    lam_new = lam * spread[3 * Q : 3 * Q + 1] + dot(
        wide_left(c_t), jnp.concatenate([dye_hi, dye_hi, dye_lo], axis=0)
    )
    lam_ref[...] = lam_new
    ended = dsum_ref[0:1, :]
    first = iota((Q, Q), 1) < HEADDIM
    first_b = (first.astype(F32).astype(BF16), 1.0 - first.astype(F32).astype(BF16))
    first_row = (iota((Q, Q), 0) < HEADDIM).astype(F32).astype(BF16)
    first_row = (first_row, 1.0 - first_row)
    gram_grad = jnp.zeros((Q, Q), F32)
    for pair in range(PAIRS):
        lanes = slice(pair * 128, pair * 128 + 128)
        weights = []
        for head in (2 * pair, 2 * pair + 1):
            differ = cumt_ref[head : head + 1, :] - cum2[:, head : head + 1]
            weights.append(jnp.exp2(jnp.where(allowed_t, differ, NEG)))
        left = jnp.concatenate([gram_t * weights[0], gram_t * weights[1]], axis=1)
        left = jnp.concatenate(split2(left), axis=0)
        dyp = dy_ref[:, lanes]
        out = dot(left, split_pair(dyp, first_b))
        g_ref[:, lanes] += out[:Q, :128] + (out[:Q, 128:] + out[Q:, :128])
        dyt_hi, dyt_lo = split2(dyp.T)
        right_hi = jnp.concatenate([dyt_hi * first_row[0], dyt_hi * first_row[1]], axis=1)
        right_lo = jnp.concatenate([dyt_lo * first_row[0], dyt_lo * first_row[1]], axis=1)
        outer = dot(
            wide_left(xd_ref[:, lanes]), jnp.concatenate([right_hi, right_hi, right_lo], axis=0))
        gram_grad = gram_grad + (outer[:, :128] * weights[0] + outer[:, 128:] * weights[1])
    g = g_ref[...]
    grad_x = dt_all * g + skip * dy
    sums = dot(jnp.concatenate(
        split2(x * g) + split2(jnp.broadcast_to(
            jnp.sum(lam_new * state, axis=0, keepdims=True), (16, INNER))), axis=0), et_ref[...])
    direct = sums[:Q] + sums[Q : 2 * Q]
    balance = through_ref[...] - dt_pos * direct
    keep_t = allowed_t.astype(F32).astype(BF16)
    b_hi, b_mid, b_lo = split3(balance)
    grad_step = dot(keep_t, b_hi) + dot(keep_t, b_mid) + dot(keep_t, b_lo) + in_last * ended
    dsum_ref[...] = sums[2 * Q : 2 * Q + 8] + sums[2 * Q + 16 : 2 * Q + 24]
    grad_dt = (direct + rate * grad_step) * sigmoid(dt_in)
    gsmall_ref[0:1, :] += jnp.sum(grad_dt, axis=0, keepdims=True)
    gsmall_ref[1:2, :] += rate * jnp.sum(dt_pos * grad_step, axis=0, keepdims=True)
    grad_c = grad_c + dot(wide_left(gram_grad.T), tall_right(b_rows))
    grad_b = grad_b + dot(wide_left(gram_grad), tall_right(c_rows))
    slope = sig_pre * (1.0 + pre * (1.0 - sig_pre))
    gnext_ref[0:Q, :INNER] = grad_x * slope[:, :INNER]
    gnext_ref[0:Q, INNER : INNER + STATE] = grad_b * slope[:, INNER : INNER + STATE]
    gnext_ref[0:Q, INNER + STATE :] = grad_c * slope[:, INNER + STATE :]
    gcp = gnext_ref[0:Q, :]
    total_ref[4:5, :] += jnp.sum(gcp, axis=0, keepdims=True)
    total_ref[3:4, :] += jnp.sum(gcp * ext_ref[8 : 8 + Q, :], axis=0, keepdims=True)
    total = convw_ref[3:4, :] * gcp
    for back in (1, 2, 3):
        ok = jnp.logical_or(rows - back >= bound, rows < bound).astype(F32)
        total_ref[3 - back : 4 - back, :] += jnp.sum(
            gcp * (ext_ref[8 - back : 8 - back + Q, :] * ok), axis=0, keepdims=True)
        okn = jnp.logical_or(rows >= bound, rows + back < bound).astype(F32)
        total = total + convw_ref[3 - back : 4 - back, :] * (gnext_ref[back : back + Q, :] * okn)
    total_ref[7:8, :] = jnp.maximum(
        total_ref[7:8, :], jnp.max(jnp.abs(total), axis=0, keepdims=True))
    total = total.astype(BF16)
    window_ref[0] = total[:, :WINDOW]
    window_ref[1] = total[:, XBC - WINDOW :]
    gnext_ref[Q : Q + 8, :] = gnext_ref[0:8, :]
    half = (steps - 1 - step) % 2
    at = pl.multiple_of(half * Q, Q)
    gp_ref[pl.ds(at, Q), :INNER] = gz_ref[0]
    gp_ref[pl.ds(at, Q), INNER : INNER + XBC] = total
    gp_ref[pl.ds(at, Q), INNER + XBC :] = grad_dt.astype(BF16)

    @pl.when(half == 0)
    def _():
        grad_normed = dot(gp_ref[...], in_ref[: INNER + XBC + 128, :])
        tok = tok_ref[...].astype(F32)
        rinv = lax.rsqrt(jnp.mean(tok * tok, axis=1, keepdims=True) + EPS_NORM)
        nhat = tok * rinv
        gain = norm_ref[...]
        gng = grad_normed * gain
        gtok_ref[...] = (cot_ref[...].astype(F32) + rinv * (
            gng - nhat * jnp.mean(nhat * gng, axis=1, keepdims=True))).astype(BF16)
        total_ref[6:7, :D] += jnp.sum(nhat * grad_normed, axis=0, keepdims=True)
        normed = (nhat * gain).astype(BF16)
        gdt = gp_ref[:, INNER + XBC :].astype(F32)
        dtw_ref[...] += dot(jnp.concatenate(
            [gdt[:Q].T, gdt[Q:].T], axis=1).astype(BF16), normed)

    @pl.when(step == steps - 1)
    def _():
        skips = head_sum(jnp.broadcast_to(gskip_ref[...], (8, INNER)), et_ref)
        small_ref[...] = jnp.zeros_like(small_ref)
        small_ref[0:HEADS, :] = dtw_ref[0:HEADS, :]
        pieces = [
            total_ref[k : k + 1, j * 128 : j * 128 + 128]
            for k in range(CONV + 1) for j in range(XBC // 128)]
        pieces += [gsmall_ref[0:1, :], gsmall_ref[1:2, :], skips[0:1, :]]
        pieces += [ggain_ref[:, j * 128 : j * 128 + 128] for j in range(INNER // 128)]
        lines = D // 128
        for number, piece in enumerate(pieces):
            line = HEADS + number // lines
            at = number % lines * 128
            small_ref[line : line + 1, at : at + 128] = piece
        small_ref[40:41, :] = total_ref[6:7, :D]
        count = float(Q * steps)
        largest = jnp.max(total_ref[7:8, :], axis=1, keepdims=True)
        normed = jnp.max(jnp.abs(norm_ref[...]), axis=1, keepdims=True) * (D ** 0.5)
        others = jnp.max(jnp.max(jnp.abs(small_ref[...]), axis=1, keepdims=True), axis=0, keepdims=True)
        power_ref[...] = jnp.broadcast_to(power_for(
            jnp.maximum(1.05 * count * largest * normed, others)), (8, 128))


def run_backward(
    proj, dy, through, states, pair, tok, cot, in_w, norm_gain, ggain, bound, e2, et, params
):
    n = proj.shape[0]
    steps = n // Q

    def rev(i):
        return (steps - 1 - i, 0)

    def rev_two(i):
        return ((steps - 1 - i) // 2, 0)

    return pl.pallas_call(
        backward_kernel,
        grid=(steps,),
        in_specs=[
            pl.BlockSpec(memory_space=pltpu.SMEM),
            pl.BlockSpec((Q, LATE), rev),
            pl.BlockSpec((8, LATE), lambda i: (jnp.maximum((steps - 1 - i) * (Q // 8) - 1, 0), 0)),
            pl.BlockSpec((Q, INNER), rev),
            pl.BlockSpec((Q, 128), rev),
            pl.BlockSpec((1, STATE, INNER), lambda i: (steps - 1 - i, 0, 0)),
            pl.BlockSpec((1, Q, INNER), lambda i: (0, steps - 1 - i, 0)),
            pl.BlockSpec((2 * Q, D), rev_two), pl.BlockSpec((2 * Q, D), rev_two),
            const_spec(in_w.shape), const_spec((1, D)), const_spec((1, INNER)),
            const_spec((256, INNER)), const_spec((INNER, 128)),
            const_spec((8, XBC)), const_spec((1, XBC)), const_spec((1, 128)),
            const_spec((1, 128)), const_spec((1, INNER)),
        ],
        out_specs=[
            pl.BlockSpec((2, Q, WINDOW), lambda i: (0, steps - 1 - i, 0)),
            pl.BlockSpec((2 * Q, D), rev_two),
            const_spec((48, D)), const_spec((8, 128)),
        ],
        out_shape=[
            jax.ShapeDtypeStruct((2, n, WINDOW), BF16),
            jax.ShapeDtypeStruct((n, D), BF16),
            jax.ShapeDtypeStruct((48, D), F32),
            jax.ShapeDtypeStruct((8, 128), F32),
        ],
        scratch_shapes=[
            pltpu.VMEM((8, XBC), F32),
            pltpu.VMEM((1, INNER), F32),
            pltpu.VMEM((8, 128), F32),
            pltpu.VMEM((128, D), F32),
            pltpu.VMEM((2 * Q, INNER + XBC + 128), BF16),
            pltpu.VMEM((Q + 8, XBC), F32),
            pltpu.VMEM((Q, 128), F32),
            pltpu.VMEM((STATE, INNER), F32),
            pltpu.VMEM((8, 128), F32),
            pltpu.VMEM((Q, INNER), F32),
            pltpu.VMEM((Q, INNER), F32),
            pltpu.VMEM((Q + 8, XBC), F32),
            pltpu.VMEM((128, Q), F32),
        ],
        compiler_params=pltpu.CompilerParams(
            dimension_semantics=("arbitrary",), vmem_limit_bytes=48 * 2**20),
        cost_estimate=pl.CostEstimate(
            flops=50 * 10**9, bytes_accessed=50 * 2**20, transcendentals=2 * 10**7),
    )(bound, proj, proj, dy, through, states, pair, tok, cot, in_w, norm_gain, ggain,
      e2, et, *params[:5])


BETA_ONE = 0.9
BETA_TWO = 0.95
EPS_ADAM = 1e-08
LANES = 128
NORM_ROWS = D // LANES
IN_ROWS = PROJ * D // LANES
CONVW_ROWS = CONV * XBC // LANES
CONVB_ROWS = XBC // LANES
GAIN_ROWS = INNER // LANES
OUT_ROWS = INNER * D // LANES
DT_ROWS = HEADS * D // LANES
SMALL_ROWS = DT_ROWS + CONVW_ROWS + CONVB_ROWS + 3 + GAIN_ROWS
OUT_START = NORM_ROWS + IN_ROWS + SMALL_ROWS - DT_ROWS
LATE_START = NORM_ROWS + INNER * NORM_ROWS
LEAD = 896
STAGE_ROWS = 16264
STAGE_BLOCKS = 5
MARK = 16


PREP_STEPS = 7
IN_BLOCK = 512
OUT_BLOCK = 256
SMALL_START = NORM_ROWS + IN_ROWS


def prepare_kernel(
    flat_ref,
    in_ref, out_ref, norm_ref, convw_ref, convb_ref, dtb_ref, alog_ref, skip_ref, gain_ref,
    e_ref, et_ref,
    stage_ref,
):
    step = pl.program_id(0)

    @pl.when(step == 0)
    def _():
        rows = flat_ref[0:16, :].astype(F32)
        for lane in range(NORM_ROWS):
            norm_ref[:, lane * LANES : lane * LANES + LANES] = rows[lane : lane + 1, :]
        low = SMALL_START // 16 * 16
        stage_ref[0:112, :] = flat_ref[low : low + 112, :].astype(F32)
        at = SMALL_START - low
        convw_ref[...] = jnp.zeros_like(convw_ref)
        for tap in range(CONV):
            for lane in range(CONVB_ROWS):
                convw_ref[tap : tap + 1, lane * LANES : lane * LANES + LANES] = stage_ref[
                    at : at + 1, :]
                at += 1
        for lane in range(CONVB_ROWS):
            convb_ref[:, lane * LANES : lane * LANES + LANES] = stage_ref[at : at + 1, :]
            at += 1
        heads = iota((1, LANES), 1) < HEADS
        dtb_ref[...] = jnp.where(heads, stage_ref[at : at + 1, :], 0.0)
        alog_ref[...] = jnp.where(heads, stage_ref[at + 1 : at + 2, :], 0.0)
        skips = jnp.where(heads, stage_ref[at + 2 : at + 3, :], 0.0)
        at += 3
        for lane in range(GAIN_ROWS):
            gain_ref[:, lane * LANES : lane * LANES + LANES] = stage_ref[at : at + 1, :]
            at += 1
        one = (iota((128, INNER), 1) // HEADDIM == iota((128, INNER), 0)).astype(F32).astype(BF16)
        e_ref[0:128, :] = one
        e_ref[128:256, :] = one
        et_ref[...] = (
            iota((INNER, 128), 0) // HEADDIM == iota((INNER, 128), 1)).astype(F32).astype(BF16)
        skip_ref[...] = dot(jnp.broadcast_to(skips, (16, LANES)).astype(BF16), one)[0:1, :]

    def block(start, offset, rows, dest_ref):
        size = rows * NORM_ROWS + 16
        at = pl.multiple_of(start + step * (rows * NORM_ROWS), 16)
        stage_ref[0:size, :] = flat_ref[pl.ds(at, size), :].astype(F32)
        for lane in range(NORM_ROWS):
            dest_ref[:, lane * LANES : lane * LANES + LANES] = stage_ref[
                pl.ds(offset + lane, rows, stride=NORM_ROWS), :].astype(BF16)

    block(0, NORM_ROWS, IN_BLOCK, in_ref)

    @pl.when(step == PREP_STEPS - 1)
    def _():
        used = PROJ - (PREP_STEPS - 1) * IN_BLOCK
        in_ref[used:, :] = jnp.zeros((IN_BLOCK - used, D), BF16)

    @pl.when(step < INNER // OUT_BLOCK)
    def _():
        low = OUT_START // 16 * 16
        block(low, OUT_START - low, OUT_BLOCK, out_ref)


def run_prepare(flat):
    vector = lambda n: jax.ShapeDtypeStruct((1, n), F32)
    return pl.pallas_call(
        prepare_kernel,
        grid=(PREP_STEPS,),
        in_specs=[const_spec(flat.shape)],
        out_specs=[
            pl.BlockSpec((IN_BLOCK, D), lambda i: (i, 0)),
            pl.BlockSpec((OUT_BLOCK, D), lambda i: (jnp.minimum(i, INNER // OUT_BLOCK - 1), 0)),
            const_spec((1, D)), const_spec((8, XBC)), const_spec((1, XBC)), const_spec((1, 128)),
            const_spec((1, 128)), const_spec((1, INNER)), const_spec((1, INNER)),
            const_spec((256, INNER)), const_spec((INNER, 128)),
        ],
        out_shape=[
            jax.ShapeDtypeStruct((PREP_STEPS * IN_BLOCK, D), BF16),
            jax.ShapeDtypeStruct((INNER, D), BF16),
            vector(D), jax.ShapeDtypeStruct((8, XBC), F32), vector(XBC), vector(128), vector(128),
            vector(INNER), vector(INNER),
            jax.ShapeDtypeStruct((256, INNER), BF16), jax.ShapeDtypeStruct((INNER, 128), BF16),
        ],
        scratch_shapes=[pltpu.VMEM((IN_BLOCK * NORM_ROWS + 16, LANES), F32)],
        compiler_params=pltpu.CompilerParams(
            dimension_semantics=("arbitrary",), vmem_limit_bytes=40 * 2**20),
        cost_estimate=pl.CostEstimate(
            flops=10**9, bytes_accessed=16 * 2**20, transcendentals=0),
    )(flat)


def stage_kernel(
    who_ref, early_ref, early_other_ref, late_ref, late_other_ref, small_ref,
    grad_ref,
    stage_ref,
):
    step = pl.program_id(0)
    upper = who_ref[0]
    mine = who_ref[1]
    block = grad_ref.shape[0]
    half = 2 * block * STAGE_BLOCKS

    @pl.when(step == 0)
    def _():
        early_at = LEAD + jnp.where(upper == 1, OUT_START - half, NORM_ROWS)
        window = LATE_START + (XBC - WINDOW) * NORM_ROWS
        late_at = LEAD + jnp.where(upper == 1, window - half, LATE_START)
        def lay(source_ref, start, size):
            for lane in range(NORM_ROWS):
                stage_ref[pl.ds(start + lane, size, stride=NORM_ROWS), :] = source_ref[
                    0:size, lane * LANES : lane * LANES + LANES]

        lines = late_ref.shape[0]
        lay(late_ref, late_at + mine * (lines * NORM_ROWS), lines)
        lay(late_other_ref, late_at + (1 - mine) * (lines * NORM_ROWS), lines)

        @pl.when(upper == 1)
        def _():
            lay(small_ref, LEAD + OUT_START - half - SMALL_ROWS, -(-SMALL_ROWS // NORM_ROWS))

        lines = early_ref.shape[0]
        lay(early_ref, early_at + mine * (lines * NORM_ROWS), lines)
        lay(early_other_ref, early_at + (1 - mine) * (lines * NORM_ROWS), lines)

        @pl.when(upper == 0)
        def _():
            for lane in range(NORM_ROWS):
                stage_ref[LEAD + lane : LEAD + lane + 1, :] = small_ref[
                    40:41, lane * LANES : lane * LANES + LANES]

        @pl.when(upper == 1)
        def _():
            at = LEAD + OUT_START + OUT_ROWS - half
            stage_ref[at : LEAD + half, :] = jnp.zeros((LEAD + half - at, LANES), F32)

    @pl.when(step > 0)
    def _():
        at = LEAD + mine * (half // 2) + (step - 1) * block
        grad_ref[...] = stage_ref[pl.ds(pl.multiple_of(at, 8), block), :]


def run_stage(who, rows, early, early_other, late, late_other, small):
    block = rows // STAGE_BLOCKS
    return pl.pallas_call(
        stage_kernel,
        grid=(STAGE_BLOCKS + 1,),
        in_specs=[
            pl.BlockSpec(memory_space=pltpu.SMEM),
            const_spec(early.shape), const_spec(early.shape),
            const_spec(late.shape), const_spec(late.shape), const_spec(small.shape),
        ],
        out_specs=pl.BlockSpec((block, LANES), lambda i: (jnp.maximum(i - 1, 0), 0)),
        out_shape=jax.ShapeDtypeStruct((rows, LANES), F32),
        scratch_shapes=[pltpu.VMEM((STAGE_ROWS, LANES), F32)],
        compiler_params=pltpu.CompilerParams(
            dimension_semantics=("arbitrary",), vmem_limit_bytes=48 * 2**20),
        cost_estimate=pl.CostEstimate(
            flops=10**6, bytes_accessed=12 * 2**20, transcendentals=0),
    )(who, early, early_other, late, late_other, small)


def swap(values, axis, bit):
    size = lax.axis_size(axis)
    return lax.ppermute(values, axis, [(i, i ^ bit) for i in range(size)])


def to_wire(values, power):
    return (values * jnp.exp2(power)).astype(jnp.float16)


def from_wire(values, power):
    return values.astype(F32) * jnp.exp2(-power)


def scatter(values, power, axis, bit=1, count=2, after=None, sent=None):
    place = (lax.axis_index(axis) // bit) % count
    rows = values.shape[-2] // count
    mark = min(MARK, rows)
    dim = values.ndim - 2
    total = lax.dynamic_slice_in_dim(values, place * rows, rows, dim)
    least = power
    arrived = []
    for offset in range(1, count):
        to = place ^ offset
        last = to == count - 1
        start = to * rows - jnp.where(last, mark, 0)
        send = lax.dynamic_slice_in_dim(values, start, rows + mark, dim)
        line = lax.broadcasted_iota(jnp.int32, send.shape, dim)
        marked = jnp.where(last, line < mark, line >= rows)
        wire = jnp.where(marked, power, send * jnp.exp2(power)).astype(jnp.float16)
        arrived.append(swap(wire, axis, bit * offset))
        if sent is not None:
            sent.append(wire)
    if after is not None:
        arrived, _ = lax.optimization_barrier((arrived, after))
    last = place == count - 1
    for got in arrived:
        got_power = lax.dynamic_slice_in_dim(
            got, jnp.where(last, 0, rows), 1, dim).reshape(1, D).astype(F32)
        body = lax.dynamic_slice_in_dim(got, jnp.where(last, mark, 0), rows, dim)
        total = total + from_wire(body, got_power)
        least = jnp.minimum(least, got_power)
    return total, least - float(count.bit_length() - 1)


def scatter_product(left, right, power, axis, bit):
    def product(part):
        return lax.dot_general(
            part, right, (((1,), (1,)), ((0,), (0,))), preferred_element_type=F32)

    side = (lax.axis_index(axis) // bit) % 2
    rows = left.shape[2] // 2
    send = product(jnp.where(side == 1, left[:, :, : rows + LANES], left[:, :, rows - LANES :]))
    line = lax.broadcasted_iota(jnp.int32, send.shape, 1)
    marked = jnp.where(side == 1, line >= rows, line < LANES)
    wire = jnp.where(marked, power, send * jnp.exp2(power)).astype(jnp.float16)
    got = swap(wire, axis, bit)
    left, _ = lax.optimization_barrier((left, wire))
    keep = product(jnp.where(side == 0, left[:, :, :rows], left[:, :, rows:]))
    keep, got = lax.optimization_barrier((keep, got))
    got_power = lax.dynamic_slice(
        got, (0, (1 - side) * rows, 0), (1, 1, D))[0].astype(F32)
    body = lax.dynamic_slice_in_dim(got, side * LANES, rows, 1)
    return keep + from_wire(body, got_power), jnp.minimum(power, got_power) - 1.0


def everyones(values, axis, bit=1, count=2):
    place = (lax.axis_index(axis) // bit) % count
    pieces = [values] + [swap(values, axis, bit * offset) for offset in range(1, count)]
    step = 1
    while step < count:
        flip = (place // step) % 2 == 1
        pieces = [
            jnp.where(flip, pieces[i ^ step], pieces[i]) for i in range(count)]
        step *= 2
    return pieces


def gather(values, axis, bit=1, count=2):
    return jnp.concatenate(everyones(values, axis, bit, count))


def add_pair(values, axis, bit, after=None):
    got = swap(values, axis, bit)
    if after is not None:
        got, _ = lax.optimization_barrier((got, after))
    return values + got


def data_groups():
    size = lax.axis_size("dp")
    groups = [(1, 2)]
    bit = 2
    while bit < size:
        count = 4 if bit * 4 <= size else 2
        groups.append((bit, count))
        bit *= count
    return groups


def dot_tn(a, b):
    return lax.dot_general(a, b, (((0,), (0,)), ((), ())), preferred_element_type=F32)


def pick_rows(index, rows):
    chosen = index[:, None] == jnp.arange(rows.shape[0], dtype=jnp.int32)[None, :]
    return dot(chosen.astype(BF16), rows).astype(BF16)


def on_device(
    tokens, loss_sensitivity, lengths, holder_sequence_list, master, moment_one, moment_two,
    adam_rates, iteration_tally,
):
    group_devices = lax.axis_size("zero")
    data_devices = lax.axis_size("dp")
    zero_index = lax.axis_index("zero")
    dp_index = lax.axis_index("dp")
    seq_len = loss_sensitivity.shape[1]
    group_seqs = tokens.shape[0]
    span = tokens.shape[1]
    slots = group_seqs // data_devices
    shard_rows = master.shape[0] // LANES
    tie = lax.optimization_barrier

    own = master.reshape(shard_rows, LANES)
    arranged = holder_sequence_list.reshape(data_devices, group_devices, slots)
    group_order = lax.dynamic_index_in_dim(arranged, zero_index, 1, keepdims=False).reshape(-1)
    local_ids = group_order - zero_index * group_seqs
    dealt = tokens.at[local_ids].get(mode="promise_in_bounds")
    flat = lax.all_gather(own.astype(BF16), "zero", axis=0, tiled=True)

    local_tok = lax.all_to_all(dealt, "dp", split_axis=0, concat_axis=0, tiled=True)
    my_seqs = lax.dynamic_slice_in_dim(group_order, dp_index * slots, slots)
    bound = lengths[my_seqs[0]]
    positions = jnp.arange(seq_len, dtype=jnp.int32)

    in_w, out_w, norm_gain, *params, e2, et = run_prepare(flat)
    cot = loss_sensitivity[0]
    gm = dot_nt(cot, out_w)
    cot_top = jnp.max(jnp.abs(cot)).astype(F32).reshape(1)
    local_tok, in_w, gm, cot_top = tie((local_tok, in_w, gm, cot_top))
    own_late, _ = tie((own, flat[:8]))
    whole_master = lax.all_gather(own_late, "zero", axis=0, tiled=True)

    def place(slot, at):
        return (at // span) * (slots * span) + slot * span + at % span

    source = jnp.where(positions < bound, place(0, positions), place(1, positions - bound))
    packed = pick_rows(source, local_tok.reshape(slots * seq_len, D))
    blocks = jnp.arange(data_devices, dtype=jnp.int32)[:, None, None] * span
    within = blocks + jnp.arange(span, dtype=jnp.int32)[None, None, :]
    within = within + jnp.arange(slots, dtype=jnp.int32)[None, :, None] * bound
    unpack_rows = jnp.minimum(within, seq_len - 1).reshape(-1)

    def spread(rows):
        return pick_rows(unpack_rows, rows).reshape(data_devices * slots, span, D)

    def send_back(picked):
        return lax.all_to_all(picked, "dp", split_axis=0, concat_axis=0, tiled=True)

    restore = jnp.zeros_like(local_ids).at[local_ids].set(
        jnp.arange(group_seqs, dtype=jnp.int32))
    mine = lax.dynamic_slice_in_dim(lengths, zero_index * group_seqs, group_seqs)
    at = dp_index * span + jnp.arange(span, dtype=jnp.int32)
    live = (at[None, :] < mine[:, None])[:, :, None]

    bound_arr = bound.reshape(1)
    tok = packed.astype(F32)
    nhat = tok * lax.rsqrt(jnp.mean(tok * tok, axis=1, keepdims=True) + EPS_NORM)
    normed = (nhat * norm_gain).astype(BF16)
    proj_z = dot_nt(normed, in_w[:INNER])
    proj = dot_nt(normed, in_w[INNER:PROJ])
    pair, dy, through, states, ggain, early_power = run_forward(
        proj_z, proj, gm, bound_arr, cot_top, norm_gain, e2, et, params)
    result = (tok + dot(pair[1], out_w)).astype(BF16)
    picked = spread(result)
    picked, pair = tie((picked, pair))
    back_out = send_back(picked)
    early_power = early_power[0:1, 0:1]
    early, early_power = scatter_product(
        pair, jnp.stack([normed, cot]), early_power, "zero", 1)
    early, early_power, dy = tie((early.reshape(INNER, D), early_power, dy))
    early, early_power = scatter(early, early_power, "zero", 2)
    window, grad_tok, small, late_power = run_backward(
        proj, dy, through, states, pair, packed, cot, in_w, norm_gain, ggain,
        bound_arr, e2, et, params)
    window, small, late_power, early, early_power, whole_master = tie(
        (window, small, late_power, early, early_power, whole_master))

    groups = data_groups()
    late_power = late_power[0:1, 0:1]
    late, late_power = scatter_product(
        window, jnp.stack([normed, normed]), late_power, "zero", 1)
    late = late.reshape(WINDOW, D)
    small = add_pair(small, "zero", 1)
    early, early_power, grad_tok, _ = tie((early, early_power, grad_tok, late))
    late, late_power = scatter(late, late_power, "zero", 2)
    pairs = [(1 << k, 2) for k in range(data_devices.bit_length() - 1)]
    early, early_power = scatter(early, early_power, "dp", *pairs[0])
    small = add_pair(small, "zero", 2, late)
    early_before, power_before = early, early_power
    picked_grad = spread(grad_tok)
    tokens, back_out, _ = tie((tokens, back_out, grad_tok))
    back_rows = back_out.at[restore].get(mode="promise_in_bounds")
    tokens_out = jnp.where(live, back_rows, tokens)
    new_master = jnp.zeros((group_devices, shard_rows, LANES), F32)
    late, tokens_out, new_master, picked_grad = tie((late, tokens_out, new_master, picked_grad))
    lines = small.shape[0]
    late = jnp.concatenate([late, small, jnp.zeros((WINDOW // 8 - lines, D), F32)])
    late, late_power = scatter(late, late_power, "dp", *groups[0])
    sent = []
    for group in groups[1:]:
        late, late_power = scatter(late, late_power, "dp", *group, sent=sent)
    early, early_power = early_before, power_before
    for pair_of in pairs[1:]:
        early, early_power = scatter(early, early_power, "dp", *pair_of, after=sent)
    early = to_wire(early, early_power)
    late = to_wire(late, late_power)
    for pair_of in reversed(pairs[2:]):
        early = gather(early, "dp", *pair_of)
    early, picked_grad, _ = tie((early, picked_grad, late))
    early = gather(early, "dp", *pairs[1])
    for group in reversed(groups[1:]):
        late = gather(late, "dp", *group)
    early, _ = tie((early, late))
    early = from_wire(gather(early, "dp", *pairs[0]), early_power)
    early_other = swap(early, "zero", 1)
    back_grad = send_back(picked_grad)
    wire = gather(late, "dp", *groups[0])
    late = from_wire(wire[: WINDOW // 2], late_power)
    small = from_wire(wire[WINDOW // 2 : WINDOW // 2 + lines], late_power)
    late_other = swap(late, "zero", 1)

    steps_f = iteration_tally[0].astype(F32)
    who = jnp.stack([zero_index // 2, zero_index % 2]).astype(jnp.int32)
    first = moment_one.reshape(shard_rows, LANES)
    second = moment_two.reshape(shard_rows, LANES)
    grad_shard = run_stage(who, shard_rows, early, early_other, late, late_other, small)
    first_scale = 1.0 / (1.0 - jnp.power(BETA_ONE, steps_f))
    second_scale = 1.0 / (1.0 - jnp.power(BETA_TWO, steps_f))

    def moments(grad, first, second):
        return (
            BETA_ONE * first + (1.0 - BETA_ONE) * grad,
            BETA_TWO * second + (1.0 - BETA_TWO) * grad * grad)

    def quotient(rows):
        first_next, second_next = moments(grad_shard[rows], first[rows], second[rows])
        return ((first_next * first_scale) / (
            jnp.sqrt(second_next * second_scale) + EPS_ADAM)).astype(jnp.float16)

    whole_master = whole_master.reshape(group_devices, shard_rows, LANES)

    def put(new_master, piece, offset):
        shard = zero_index ^ offset
        old = lax.dynamic_index_in_dim(whole_master, shard, 0, keepdims=False)
        new = old - adam_rates[0] * (piece.astype(F32) + adam_rates[1] * old)
        return lax.dynamic_update_index_in_dim(new_master, new, shard, 0)

    own_part, first, second = tie((quotient(slice(0, shard_rows)), first, second))
    across = swap(own_part, "zero", 2)
    core = swap(own_part, "zero", 1)
    first_next, second_next = moments(grad_shard, first, second)
    new_master = put(put(new_master, own_part, 0), core, 1)
    across, new_master, first_next, second_next = tie(
        (across, new_master, first_next, second_next))
    last = swap(across, "zero", 1)
    new_master = put(new_master, across, 2)
    last, new_master = tie((last, new_master))
    new_master = put(new_master, last, 3)
    back_grad, new_master = tie((back_grad, new_master))
    grad_tokens = jnp.where(
        live, back_grad.at[restore].get(mode="promise_in_bounds"), jnp.zeros((), BF16))
    return (
        tokens_out, grad_tokens, new_master.reshape(-1), grad_shard.reshape(-1),
        first_next.reshape(-1), second_next.reshape(-1))


def solution(mesh):
    return jax.shard_map(
        on_device,
        mesh=mesh,
        in_specs=(
            P("zero", "dp", None), P(("dp", "zero"), None, None), P(), P(),
            P("zero"), P("zero"), P("zero"), P(), P(),
        ),
        out_specs=(
            P("zero", "dp", None), P("zero", "dp", None), P(), P("zero"), P("zero"), P("zero"),
        ),
        check_vma=False,
    )
```

```python
import jax
import jax.numpy as jnp
from jax import lax
from jax.experimental import pallas as pl
from jax.experimental.pallas import tpu as pltpu
from jax.sharding import PartitionSpec as P

D = 768
HEADS = 24
HEADDIM = 64
STATE = 128
CONV = 4
INNER = 1536
XBC = 1792
PROJ = 3352
Q = 128
LATE = PROJ - INNER
WINDOW = 1024
PAIRS = HEADS // 2
EPS_NORM = 1e-05
NEG = -1e30
F16_TOP = 30000.0
LOG2E = 1.4426950408889634
F32 = jnp.float32
BF16 = jnp.bfloat16


def dot(a, b):
    return lax.dot_general(a, b, (((1,), (0,)), ((), ())), preferred_element_type=F32)


def dot_nt(a, b):
    return lax.dot_general(a, b, (((1,), (1,)), ((), ())), preferred_element_type=F32)


def split2(v):
    hi = v.astype(BF16)
    return hi, (v - hi.astype(F32)).astype(BF16)


def split3(v):
    hi = v.astype(BF16)
    rest = v - hi.astype(F32)
    mid = rest.astype(BF16)
    return hi, mid, (rest - mid.astype(F32)).astype(BF16)


def wide_left(v):
    hi, lo = split2(v)
    return jnp.concatenate([hi, lo, hi], axis=1)


def tall_right(v):
    hi, lo = split2(v)
    return jnp.concatenate([hi, hi, lo], axis=0)


def split_pair(v, masks):
    hi, lo = split2(v)
    return jnp.concatenate([
        jnp.concatenate([hi * masks[0], lo * masks[0]], axis=1),
        jnp.concatenate([hi * masks[1], lo * masks[1]], axis=1)], axis=0)


def sigmoid(v):
    return lax.logistic(v)


def softplus(v):
    return jnp.maximum(v, 0.0) + jnp.log1p(jnp.exp(-jnp.abs(v)))


def iota(shape, dim):
    return lax.broadcasted_iota(jnp.int32, shape, dim)


def expand(v, e_ref):
    hi, lo = split2(v)
    return dot(jnp.concatenate([hi, lo], axis=1), e_ref[...])


def head_sum(v, et_ref):
    hi, lo = split2(v)
    return dot(hi, et_ref[...]) + dot(lo, et_ref[...])


def quarters(out):
    return out[:Q, :Q] + (out[:Q, Q:] + out[Q:, :Q])


def power_for(bound):
    scale = jnp.log(0.9 * F16_TOP / jnp.maximum(bound, 1e-30)) * LOG2E
    return jnp.clip(jnp.floor(scale), -126.0, 120.0)


def chunk_masks(t0, bound):
    rows = t0 + iota((Q, 1), 0)
    rr = t0 + iota((Q, Q), 0)
    cc = t0 + iota((Q, Q), 1)
    return rows, rr, cc


def conv_rows(ext_ref, w_ref, b_ref, rows, bound):
    total = b_ref[...] + w_ref[3:4, :] * ext_ref[8 : 8 + Q, :]
    for back in (1, 2, 3):
        ok = jnp.logical_or(rows - back >= bound, rows < bound).astype(F32)
        total = total + w_ref[3 - back : 4 - back, :] * (ext_ref[8 - back : 8 - back + Q, :] * ok)
    return total


def decay_parts(dt_raw, dtb_ref, alog_ref, rr, cc):
    dt_in = dt_raw + dtb_ref[...]
    dt_pos = softplus(dt_in)
    rate = -jnp.exp(alog_ref[...])
    step = dt_pos * rate
    tri = (cc <= rr).astype(F32).astype(BF16)
    s_hi, s_mid, s_lo = split3(step)
    cum = dot(tri, s_hi) + dot(tri, s_mid) + dot(tri, s_lo)
    return dt_in, dt_pos, rate, cum


def forward_kernel(
    bound_ref, cot_ref, z_ref, proj_ref, gm_ref, norm_ref, e_ref, et_ref, convw_ref, convb_ref, dtb_ref, alog_ref,
    skip_ref, gain_ref,
    pair_ref, dy_ref, through_ref, state_ref, ggain_ref, power_ref,
    zmax_ref, ext_ref, dt_ref, carry_ref, xd_ref, acc_ref, cumt_ref,
):
    step = pl.program_id(0)
    bound = bound_ref[0]
    t0 = step * Q

    @pl.when(step == 0)
    def _():
        ext_ref[0:8, :] = jnp.zeros((8, XBC), F32)
        carry_ref[...] = jnp.zeros_like(carry_ref)
        dt_ref[...] = jnp.zeros_like(dt_ref)
        ggain_ref[...] = jnp.zeros_like(ggain_ref)
        zmax_ref[...] = jnp.zeros_like(zmax_ref)

    rows, rr, cc = chunk_masks(t0, bound)
    ext_ref[8 : 8 + Q, :] = proj_ref[:, :XBC]
    pre = conv_rows(ext_ref, convw_ref, convb_ref, rows, bound)
    ext_ref[0:8, :] = ext_ref[Q : Q + 8, :]
    conv_out = pre * sigmoid(pre)
    x = conv_out[:, :INNER]
    b_rows = conv_out[:, INNER : INNER + STATE]
    c_rows = conv_out[:, INNER + STATE :]
    dt_ref[:, 0:HEADS] = proj_ref[:, XBC:LATE]
    _, dt_pos, _, cum = decay_parts(dt_ref[...], dtb_ref, alog_ref, rr, cc)
    cum_end = cum[Q - 1 : Q, :]
    keep = jnp.logical_or(rows < bound, bound < t0).astype(F32)
    in_last = jnp.logical_or(rows >= bound, bound > t0 + Q - 1).astype(F32)
    whole = jnp.logical_or(bound < t0, bound > t0 + Q - 1).astype(F32)
    from_start = jnp.exp(cum) * keep
    to_end = jnp.exp(cum_end - cum) * in_last
    carry_scale = jnp.exp(cum_end) * whole
    allowed = jnp.logical_and(cc <= rr, (cc >= bound) == (rr >= bound))
    cum2 = cum * LOG2E
    cumt_ref[...] = cum2.T

    state = carry_ref[...]
    state_ref[0] = state
    spread = expand(jnp.concatenate(
        [dt_pos, to_end, from_start, jnp.broadcast_to(carry_scale, (16, 128))], axis=0), e_ref)
    xd = x * spread[:Q]
    xd_ref[...] = xd
    acc = dot(wide_left(c_rows), tall_right(state)) * spread[2 * Q : 3 * Q]
    acc_ref[...] = acc + skip_ref[...] * x
    b_t = b_rows.T
    carry_ref[...] = state * spread[3 * Q : 3 * Q + 1] + dot(
        wide_left(b_t), tall_right(xd * spread[Q : 2 * Q]))
    gram = dot(wide_left(c_rows), tall_right(b_t))
    first = iota((Q, Q), 1) < HEADDIM
    first_b = (first.astype(F32).astype(BF16), 1.0 - first.astype(F32).astype(BF16))
    for pair in range(PAIRS):
        parts = []
        for head in (2 * pair, 2 * pair + 1):
            differ = cum2[:, head : head + 1] - cumt_ref[head : head + 1, :]
            parts.append(gram * jnp.exp2(jnp.where(allowed, differ, NEG)))
        left = jnp.concatenate(split2(jnp.concatenate(parts, axis=1)), axis=0)
        lanes = slice(pair * 128, pair * 128 + 128)
        xp = xd_ref[:, lanes]
        out = dot(left, split_pair(xp, first_b))
        acc_ref[:, lanes] += out[:Q, :128] + (out[:Q, 128:] + out[Q:, :128])
    scanned = acc_ref[...]
    z = z_ref[...]
    sig_z = sigmoid(z)
    silu_z = z * sig_z
    gated = scanned * silu_z
    ginv = lax.rsqrt(jnp.mean(gated * gated, axis=1, keepdims=True) + EPS_NORM)
    mhat = gated * ginv
    pair_ref[1] = (mhat * gain_ref[...]).astype(BF16)
    gm = gm_ref[...]
    ggain_ref[...] += jnp.sum(mhat * gm, axis=0, keepdims=True)
    gmg = gm * gain_ref[...]
    ggated = ginv * (gmg - mhat * jnp.mean(mhat * gmg, axis=1, keepdims=True))
    dy = ggated * silu_z
    dy_ref[...] = dy
    grad_z = ggated * scanned * (sig_z * (1.0 + z * (1.0 - sig_z)))
    zmax_ref[...] = jnp.maximum(zmax_ref[...], jnp.max(jnp.abs(grad_z), axis=0, keepdims=True))
    pair_ref[0] = grad_z.astype(BF16)
    through_ref[...] = head_sum(dy * (scanned - skip_ref[...] * x), et_ref)

    @pl.when(step == pl.num_programs(0) - 1)
    def _():
        count = float(Q * pl.num_programs(0))
        largest = jnp.max(zmax_ref[...], axis=1, keepdims=True)
        normed = jnp.max(jnp.abs(norm_ref[...]), axis=1, keepdims=True) * (D ** 0.5)
        mixed = jnp.max(jnp.abs(gain_ref[...]), axis=1, keepdims=True) * (INNER ** 0.5)
        power_ref[...] = jnp.broadcast_to(power_for(
            1.05 * count * jnp.maximum(largest * normed, cot_ref[0] * mixed)), (8, 128))


def const_spec(shape):
    return pl.BlockSpec(shape, lambda *_: (0,) * len(shape))


def run_forward(z, proj, gm, bound, cot_top, norm_gain, e2, et, params):
    n = proj.shape[0]
    steps = n // Q
    return pl.pallas_call(
        forward_kernel,
        grid=(steps,),
        in_specs=[
            pl.BlockSpec(memory_space=pltpu.SMEM), pl.BlockSpec(memory_space=pltpu.SMEM),
            pl.BlockSpec((Q, INNER), lambda i: (i, 0)),
            pl.BlockSpec((Q, LATE), lambda i: (i, 0)),
            pl.BlockSpec((Q, INNER), lambda i: (i, 0)),
            const_spec((1, D)),
            const_spec((256, INNER)), const_spec((INNER, 128)),
            const_spec((8, XBC)), const_spec((1, XBC)), const_spec((1, 128)),
            const_spec((1, 128)), const_spec((1, INNER)), const_spec((1, INNER)),
        ],
        out_specs=[
            pl.BlockSpec((2, Q, INNER), lambda i: (0, i, 0)),
            pl.BlockSpec((Q, INNER), lambda i: (i, 0)),
            pl.BlockSpec((Q, 128), lambda i: (i, 0)),
            pl.BlockSpec((1, STATE, INNER), lambda i: (i, 0, 0)),
            const_spec((1, INNER)), const_spec((8, 128)),
        ],
        out_shape=[
            jax.ShapeDtypeStruct((2, n, INNER), BF16),
            jax.ShapeDtypeStruct((n, INNER), F32),
            jax.ShapeDtypeStruct((n, 128), F32),
            jax.ShapeDtypeStruct((steps, STATE, INNER), F32),
            jax.ShapeDtypeStruct((1, INNER), F32),
            jax.ShapeDtypeStruct((8, 128), F32),
        ],
        scratch_shapes=[
            pltpu.VMEM((1, INNER), F32),
            pltpu.VMEM((Q + 8, XBC), F32),
            pltpu.VMEM((Q, 128), F32),
            pltpu.VMEM((STATE, INNER), F32),
            pltpu.VMEM((Q, INNER), F32),
            pltpu.VMEM((Q, INNER), F32),
            pltpu.VMEM((128, Q), F32),
        ],
        compiler_params=pltpu.CompilerParams(
            dimension_semantics=("arbitrary",), vmem_limit_bytes=48 * 2**20),
        cost_estimate=pl.CostEstimate(
            flops=30 * 10**9, bytes_accessed=40 * 2**20, transcendentals=10**7),
    )(bound, cot_top, z, proj, gm, norm_gain, e2, et, *params)


def backward_kernel(
    bound_ref, proj_ref, before_ref, dy_ref, through_ref, state_ref, gz_ref, tok_ref, cot_ref,
    in_ref, norm_ref, ggain_ref,
    e_ref, et_ref, convw_ref, convb_ref, dtb_ref, alog_ref, skip_ref,
    window_ref, gtok_ref, small_ref, power_ref,
    total_ref, gskip_ref, gsmall_ref, dtw_ref, gp_ref, ext_ref, dt_ref, lam_ref, dsum_ref, xd_ref, g_ref, gnext_ref, cumt_ref,
):
    step = pl.program_id(0)
    steps = pl.num_programs(0)
    bound = bound_ref[0]
    t0 = (steps - 1 - step) * Q

    @pl.when(step == 0)
    def _():
        lam_ref[...] = jnp.zeros_like(lam_ref)
        dsum_ref[...] = jnp.zeros_like(dsum_ref)
        dt_ref[...] = jnp.zeros_like(dt_ref)
        gnext_ref[Q : Q + 8, :] = jnp.zeros((8, XBC), F32)
        gskip_ref[...] = jnp.zeros_like(gskip_ref)
        total_ref[...] = jnp.zeros_like(total_ref)
        dtw_ref[...] = jnp.zeros_like(dtw_ref)
        gsmall_ref[...] = jnp.zeros_like(gsmall_ref)

    rows, rr, cc = chunk_masks(t0, bound)
    dy = dy_ref[...]
    first_chunk = (t0 > 0).astype(F32)
    ext_ref[0:8, :] = before_ref[:, :XBC] * first_chunk
    ext_ref[8 : 8 + Q, :] = proj_ref[:, :XBC]
    pre = conv_rows(ext_ref, convw_ref, convb_ref, rows, bound)
    sig_pre = sigmoid(pre)
    conv_out = pre * sig_pre
    x = conv_out[:, :INNER]
    b_rows = conv_out[:, INNER : INNER + STATE]
    c_rows = conv_out[:, INNER + STATE :]
    dt_ref[:, 0:HEADS] = proj_ref[:, XBC:LATE]
    dt_in, dt_pos, rate, cum = decay_parts(dt_ref[...], dtb_ref, alog_ref, rr, cc)
    cum_end = cum[Q - 1 : Q, :]
    keep = jnp.logical_or(rows < bound, bound < t0).astype(F32)
    in_last = jnp.logical_or(rows >= bound, bound > t0 + Q - 1).astype(F32)
    whole = jnp.logical_or(bound < t0, bound > t0 + Q - 1).astype(F32)
    from_start = jnp.exp(cum) * keep
    to_end = jnp.exp(cum_end - cum) * in_last
    carry_scale = jnp.exp(cum_end) * whole
    allowed_t = jnp.logical_and(rr <= cc, (cc >= bound) == (rr >= bound))
    cum2 = cum * LOG2E
    cumt_ref[...] = cum2.T
    c_t = c_rows.T
    gram_t = dot(wide_left(b_rows), tall_right(c_t))
    spread = expand(jnp.concatenate(
        [dt_pos, to_end, from_start, jnp.broadcast_to(carry_scale, (16, 128))], axis=0), e_ref)
    dt_all = spread[:Q]
    end_all = spread[Q : 2 * Q]
    xd = x * dt_all
    xd_ref[...] = xd
    skip = skip_ref[...]
    gskip_ref[...] += jnp.sum(dy * x, axis=0, keepdims=True)
    lam = lam_ref[...]
    lam_hi, lam_lo = split2(lam)
    g_ref[...] = (
        dot(wide_left(b_rows), jnp.concatenate([lam_hi, lam_hi, lam_lo], axis=0)) * end_all
    )
    grad_b = quarters(dot_nt(
        jnp.concatenate(split2(xd * end_all), axis=0), jnp.concatenate([lam_hi, lam_lo], axis=0)))
    state = state_ref[0]
    dye_hi, dye_lo = split2(dy * spread[2 * Q : 3 * Q])
    grad_c = quarters(dot_nt(
        jnp.concatenate([dye_hi, dye_lo], axis=0), jnp.concatenate(split2(state), axis=0)))
    lam_new = lam * spread[3 * Q : 3 * Q + 1] + dot(
        wide_left(c_t), jnp.concatenate([dye_hi, dye_hi, dye_lo], axis=0)
    )
    lam_ref[...] = lam_new
    ended = dsum_ref[0:1, :]
    first = iota((Q, Q), 1) < HEADDIM
    first_b = (first.astype(F32).astype(BF16), 1.0 - first.astype(F32).astype(BF16))
    first_row = (iota((Q, Q), 0) < HEADDIM).astype(F32).astype(BF16)
    first_row = (first_row, 1.0 - first_row)
    gram_grad = jnp.zeros((Q, Q), F32)
    for pair in range(PAIRS):
        lanes = slice(pair * 128, pair * 128 + 128)
        weights = []
        for head in (2 * pair, 2 * pair + 1):
            differ = cumt_ref[head : head + 1, :] - cum2[:, head : head + 1]
            weights.append(jnp.exp2(jnp.where(allowed_t, differ, NEG)))
        left = jnp.concatenate([gram_t * weights[0], gram_t * weights[1]], axis=1)
        left = jnp.concatenate(split2(left), axis=0)
        dyp = dy_ref[:, lanes]
        out = dot(left, split_pair(dyp, first_b))
        g_ref[:, lanes] += out[:Q, :128] + (out[:Q, 128:] + out[Q:, :128])
        dyt_hi, dyt_lo = split2(dyp.T)
        right_hi = jnp.concatenate([dyt_hi * first_row[0], dyt_hi * first_row[1]], axis=1)
        right_lo = jnp.concatenate([dyt_lo * first_row[0], dyt_lo * first_row[1]], axis=1)
        outer = dot(
            wide_left(xd_ref[:, lanes]), jnp.concatenate([right_hi, right_hi, right_lo], axis=0))
        gram_grad = gram_grad + (outer[:, :128] * weights[0] + outer[:, 128:] * weights[1])
    g = g_ref[...]
    grad_x = dt_all * g + skip * dy
    sums = dot(jnp.concatenate(
        split2(x * g) + split2(jnp.broadcast_to(
            jnp.sum(lam_new * state, axis=0, keepdims=True), (16, INNER))), axis=0), et_ref[...])
    direct = sums[:Q] + sums[Q : 2 * Q]
    balance = through_ref[...] - dt_pos * direct
    keep_t = allowed_t.astype(F32).astype(BF16)
    b_hi, b_mid, b_lo = split3(balance)
    grad_step = dot(keep_t, b_hi) + dot(keep_t, b_mid) + dot(keep_t, b_lo) + in_last * ended
    dsum_ref[...] = sums[2 * Q : 2 * Q + 8] + sums[2 * Q + 16 : 2 * Q + 24]
    grad_dt = (direct + rate * grad_step) * sigmoid(dt_in)
    gsmall_ref[0:1, :] += jnp.sum(grad_dt, axis=0, keepdims=True)
    gsmall_ref[1:2, :] += rate * jnp.sum(dt_pos * grad_step, axis=0, keepdims=True)
    grad_c = grad_c + dot(wide_left(gram_grad.T), tall_right(b_rows))
    grad_b = grad_b + dot(wide_left(gram_grad), tall_right(c_rows))
    slope = sig_pre * (1.0 + pre * (1.0 - sig_pre))
    gnext_ref[0:Q, :INNER] = grad_x * slope[:, :INNER]
    gnext_ref[0:Q, INNER : INNER + STATE] = grad_b * slope[:, INNER : INNER + STATE]
    gnext_ref[0:Q, INNER + STATE :] = grad_c * slope[:, INNER + STATE :]
    gcp = gnext_ref[0:Q, :]
    total_ref[4:5, :] += jnp.sum(gcp, axis=0, keepdims=True)
    total_ref[3:4, :] += jnp.sum(gcp * ext_ref[8 : 8 + Q, :], axis=0, keepdims=True)
    total = convw_ref[3:4, :] * gcp
    for back in (1, 2, 3):
        ok = jnp.logical_or(rows - back >= bound, rows < bound).astype(F32)
        total_ref[3 - back : 4 - back, :] += jnp.sum(
            gcp * (ext_ref[8 - back : 8 - back + Q, :] * ok), axis=0, keepdims=True)
        okn = jnp.logical_or(rows >= bound, rows + back < bound).astype(F32)
        total = total + convw_ref[3 - back : 4 - back, :] * (gnext_ref[back : back + Q, :] * okn)
    total_ref[7:8, :] = jnp.maximum(
        total_ref[7:8, :], jnp.max(jnp.abs(total), axis=0, keepdims=True))
    total = total.astype(BF16)
    window_ref[0] = total[:, :WINDOW]
    window_ref[1] = total[:, XBC - WINDOW :]
    gnext_ref[Q : Q + 8, :] = gnext_ref[0:8, :]
    half = (steps - 1 - step) % 2
    at = pl.multiple_of(half * Q, Q)
    gp_ref[pl.ds(at, Q), :INNER] = gz_ref[0]
    gp_ref[pl.ds(at, Q), INNER : INNER + XBC] = total
    gp_ref[pl.ds(at, Q), INNER + XBC :] = grad_dt.astype(BF16)

    @pl.when(half == 0)
    def _():
        grad_normed = dot(gp_ref[...], in_ref[: INNER + XBC + 128, :])
        tok = tok_ref[...].astype(F32)
        rinv = lax.rsqrt(jnp.mean(tok * tok, axis=1, keepdims=True) + EPS_NORM)
        nhat = tok * rinv
        gain = norm_ref[...]
        gng = grad_normed * gain
        gtok_ref[...] = (cot_ref[...].astype(F32) + rinv * (
            gng - nhat * jnp.mean(nhat * gng, axis=1, keepdims=True))).astype(BF16)
        total_ref[6:7, :D] += jnp.sum(nhat * grad_normed, axis=0, keepdims=True)
        normed = (nhat * gain).astype(BF16)
        gdt = gp_ref[:, INNER + XBC :].astype(F32)
        dtw_ref[...] += dot(jnp.concatenate(
            [gdt[:Q].T, gdt[Q:].T], axis=1).astype(BF16), normed)

    @pl.when(step == steps - 1)
    def _():
        skips = head_sum(jnp.broadcast_to(gskip_ref[...], (8, INNER)), et_ref)
        small_ref[...] = jnp.zeros_like(small_ref)
        small_ref[0:HEADS, :] = dtw_ref[0:HEADS, :]
        pieces = [
            total_ref[k : k + 1, j * 128 : j * 128 + 128]
            for k in range(CONV + 1) for j in range(XBC // 128)]
        pieces += [gsmall_ref[0:1, :], gsmall_ref[1:2, :], skips[0:1, :]]
        pieces += [ggain_ref[:, j * 128 : j * 128 + 128] for j in range(INNER // 128)]
        lines = D // 128
        for number, piece in enumerate(pieces):
            line = HEADS + number // lines
            at = number % lines * 128
            small_ref[line : line + 1, at : at + 128] = piece
        small_ref[40:41, :] = total_ref[6:7, :D]
        count = float(Q * steps)
        largest = jnp.max(total_ref[7:8, :], axis=1, keepdims=True)
        normed = jnp.max(jnp.abs(norm_ref[...]), axis=1, keepdims=True) * (D ** 0.5)
        others = jnp.max(jnp.max(jnp.abs(small_ref[...]), axis=1, keepdims=True), axis=0, keepdims=True)
        power_ref[...] = jnp.broadcast_to(power_for(
            jnp.maximum(1.05 * count * largest * normed, others)), (8, 128))


def run_backward(
    proj, dy, through, states, pair, tok, cot, in_w, norm_gain, ggain, bound, e2, et, params
):
    n = proj.shape[0]
    steps = n // Q

    def rev(i):
        return (steps - 1 - i, 0)

    def rev_two(i):
        return ((steps - 1 - i) // 2, 0)

    return pl.pallas_call(
        backward_kernel,
        grid=(steps,),
        in_specs=[
            pl.BlockSpec(memory_space=pltpu.SMEM),
            pl.BlockSpec((Q, LATE), rev),
            pl.BlockSpec((8, LATE), lambda i: (jnp.maximum((steps - 1 - i) * (Q // 8) - 1, 0), 0)),
            pl.BlockSpec((Q, INNER), rev),
            pl.BlockSpec((Q, 128), rev),
            pl.BlockSpec((1, STATE, INNER), lambda i: (steps - 1 - i, 0, 0)),
            pl.BlockSpec((1, Q, INNER), lambda i: (0, steps - 1 - i, 0)),
            pl.BlockSpec((2 * Q, D), rev_two), pl.BlockSpec((2 * Q, D), rev_two),
            const_spec(in_w.shape), const_spec((1, D)), const_spec((1, INNER)),
            const_spec((256, INNER)), const_spec((INNER, 128)),
            const_spec((8, XBC)), const_spec((1, XBC)), const_spec((1, 128)),
            const_spec((1, 128)), const_spec((1, INNER)),
        ],
        out_specs=[
            pl.BlockSpec((2, Q, WINDOW), lambda i: (0, steps - 1 - i, 0)),
            pl.BlockSpec((2 * Q, D), rev_two),
            const_spec((48, D)), const_spec((8, 128)),
        ],
        out_shape=[
            jax.ShapeDtypeStruct((2, n, WINDOW), BF16),
            jax.ShapeDtypeStruct((n, D), BF16),
            jax.ShapeDtypeStruct((48, D), F32),
            jax.ShapeDtypeStruct((8, 128), F32),
        ],
        scratch_shapes=[
            pltpu.VMEM((8, XBC), F32),
            pltpu.VMEM((1, INNER), F32),
            pltpu.VMEM((8, 128), F32),
            pltpu.VMEM((128, D), F32),
            pltpu.VMEM((2 * Q, INNER + XBC + 128), BF16),
            pltpu.VMEM((Q + 8, XBC), F32),
            pltpu.VMEM((Q, 128), F32),
            pltpu.VMEM((STATE, INNER), F32),
            pltpu.VMEM((8, 128), F32),
            pltpu.VMEM((Q, INNER), F32),
            pltpu.VMEM((Q, INNER), F32),
            pltpu.VMEM((Q + 8, XBC), F32),
            pltpu.VMEM((128, Q), F32),
        ],
        compiler_params=pltpu.CompilerParams(
            dimension_semantics=("arbitrary",), vmem_limit_bytes=48 * 2**20),
        cost_estimate=pl.CostEstimate(
            flops=50 * 10**9, bytes_accessed=50 * 2**20, transcendentals=2 * 10**7),
    )(bound, proj, proj, dy, through, states, pair, tok, cot, in_w, norm_gain, ggain,
      e2, et, *params[:5])


BETA_ONE = 0.9
BETA_TWO = 0.95
EPS_ADAM = 1e-08
LANES = 128
NORM_ROWS = D // LANES
IN_ROWS = PROJ * D // LANES
CONVW_ROWS = CONV * XBC // LANES
CONVB_ROWS = XBC // LANES
GAIN_ROWS = INNER // LANES
OUT_ROWS = INNER * D // LANES
DT_ROWS = HEADS * D // LANES
SMALL_ROWS = DT_ROWS + CONVW_ROWS + CONVB_ROWS + 3 + GAIN_ROWS
OUT_START = NORM_ROWS + IN_ROWS + SMALL_ROWS - DT_ROWS
LATE_START = NORM_ROWS + INNER * NORM_ROWS
LEAD = 896
STAGE_ROWS = 16264
STAGE_BLOCKS = 5
MARK = 16


PREP_STEPS = 7
IN_BLOCK = 512
OUT_BLOCK = 256
SMALL_START = NORM_ROWS + IN_ROWS


def prepare_kernel(
    flat_ref,
    in_ref, out_ref, norm_ref, convw_ref, convb_ref, dtb_ref, alog_ref, skip_ref, gain_ref,
    e_ref, et_ref,
    stage_ref,
):
    step = pl.program_id(0)

    @pl.when(step == 0)
    def _():
        rows = flat_ref[0:16, :].astype(F32)
        for lane in range(NORM_ROWS):
            norm_ref[:, lane * LANES : lane * LANES + LANES] = rows[lane : lane + 1, :]
        low = SMALL_START // 16 * 16
        stage_ref[0:112, :] = flat_ref[low : low + 112, :].astype(F32)
        at = SMALL_START - low
        convw_ref[...] = jnp.zeros_like(convw_ref)
        for tap in range(CONV):
            for lane in range(CONVB_ROWS):
                convw_ref[tap : tap + 1, lane * LANES : lane * LANES + LANES] = stage_ref[
                    at : at + 1, :]
                at += 1
        for lane in range(CONVB_ROWS):
            convb_ref[:, lane * LANES : lane * LANES + LANES] = stage_ref[at : at + 1, :]
            at += 1
        heads = iota((1, LANES), 1) < HEADS
        dtb_ref[...] = jnp.where(heads, stage_ref[at : at + 1, :], 0.0)
        alog_ref[...] = jnp.where(heads, stage_ref[at + 1 : at + 2, :], 0.0)
        skips = jnp.where(heads, stage_ref[at + 2 : at + 3, :], 0.0)
        at += 3
        for lane in range(GAIN_ROWS):
            gain_ref[:, lane * LANES : lane * LANES + LANES] = stage_ref[at : at + 1, :]
            at += 1
        one = (iota((128, INNER), 1) // HEADDIM == iota((128, INNER), 0)).astype(F32).astype(BF16)
        e_ref[0:128, :] = one
        e_ref[128:256, :] = one
        et_ref[...] = (
            iota((INNER, 128), 0) // HEADDIM == iota((INNER, 128), 1)).astype(F32).astype(BF16)
        skip_ref[...] = dot(jnp.broadcast_to(skips, (16, LANES)).astype(BF16), one)[0:1, :]

    def block(start, offset, rows, dest_ref):
        size = rows * NORM_ROWS + 16
        at = pl.multiple_of(start + step * (rows * NORM_ROWS), 16)
        stage_ref[0:size, :] = flat_ref[pl.ds(at, size), :].astype(F32)
        for lane in range(NORM_ROWS):
            dest_ref[:, lane * LANES : lane * LANES + LANES] = stage_ref[
                pl.ds(offset + lane, rows, stride=NORM_ROWS), :].astype(BF16)

    block(0, NORM_ROWS, IN_BLOCK, in_ref)

    @pl.when(step == PREP_STEPS - 1)
    def _():
        used = PROJ - (PREP_STEPS - 1) * IN_BLOCK
        in_ref[used:, :] = jnp.zeros((IN_BLOCK - used, D), BF16)

    @pl.when(step < INNER // OUT_BLOCK)
    def _():
        low = OUT_START // 16 * 16
        block(low, OUT_START - low, OUT_BLOCK, out_ref)


def run_prepare(flat):
    vector = lambda n: jax.ShapeDtypeStruct((1, n), F32)
    return pl.pallas_call(
        prepare_kernel,
        grid=(PREP_STEPS,),
        in_specs=[const_spec(flat.shape)],
        out_specs=[
            pl.BlockSpec((IN_BLOCK, D), lambda i: (i, 0)),
            pl.BlockSpec((OUT_BLOCK, D), lambda i: (jnp.minimum(i, INNER // OUT_BLOCK - 1), 0)),
            const_spec((1, D)), const_spec((8, XBC)), const_spec((1, XBC)), const_spec((1, 128)),
            const_spec((1, 128)), const_spec((1, INNER)), const_spec((1, INNER)),
            const_spec((256, INNER)), const_spec((INNER, 128)),
        ],
        out_shape=[
            jax.ShapeDtypeStruct((PREP_STEPS * IN_BLOCK, D), BF16),
            jax.ShapeDtypeStruct((INNER, D), BF16),
            vector(D), jax.ShapeDtypeStruct((8, XBC), F32), vector(XBC), vector(128), vector(128),
            vector(INNER), vector(INNER),
            jax.ShapeDtypeStruct((256, INNER), BF16), jax.ShapeDtypeStruct((INNER, 128), BF16),
        ],
        scratch_shapes=[pltpu.VMEM((IN_BLOCK * NORM_ROWS + 16, LANES), F32)],
        compiler_params=pltpu.CompilerParams(
            dimension_semantics=("arbitrary",), vmem_limit_bytes=40 * 2**20),
        cost_estimate=pl.CostEstimate(
            flops=10**9, bytes_accessed=16 * 2**20, transcendentals=0),
    )(flat)


def stage_kernel(
    who_ref, early_ref, early_other_ref, late_ref, late_other_ref, small_ref,
    grad_ref,
    stage_ref,
):
    step = pl.program_id(0)
    upper = who_ref[0]
    mine = who_ref[1]
    block = grad_ref.shape[0]
    half = 2 * block * STAGE_BLOCKS

    @pl.when(step == 0)
    def _():
        early_at = LEAD + jnp.where(upper == 1, OUT_START - half, NORM_ROWS)
        window = LATE_START + (XBC - WINDOW) * NORM_ROWS
        late_at = LEAD + jnp.where(upper == 1, window - half, LATE_START)
        def lay(source_ref, start, size):
            for lane in range(NORM_ROWS):
                stage_ref[pl.ds(start + lane, size, stride=NORM_ROWS), :] = source_ref[
                    0:size, lane * LANES : lane * LANES + LANES]

        lines = late_ref.shape[0]
        lay(late_ref, late_at + mine * (lines * NORM_ROWS), lines)
        lay(late_other_ref, late_at + (1 - mine) * (lines * NORM_ROWS), lines)

        @pl.when(upper == 1)
        def _():
            lay(small_ref, LEAD + OUT_START - half - SMALL_ROWS, -(-SMALL_ROWS // NORM_ROWS))

        lines = early_ref.shape[0]
        lay(early_ref, early_at + mine * (lines * NORM_ROWS), lines)
        lay(early_other_ref, early_at + (1 - mine) * (lines * NORM_ROWS), lines)

        @pl.when(upper == 0)
        def _():
            for lane in range(NORM_ROWS):
                stage_ref[LEAD + lane : LEAD + lane + 1, :] = small_ref[
                    40:41, lane * LANES : lane * LANES + LANES]

        @pl.when(upper == 1)
        def _():
            at = LEAD + OUT_START + OUT_ROWS - half
            stage_ref[at : LEAD + half, :] = jnp.zeros((LEAD + half - at, LANES), F32)

    @pl.when(step > 0)
    def _():
        at = LEAD + mine * (half // 2) + (step - 1) * block
        grad_ref[...] = stage_ref[pl.ds(pl.multiple_of(at, 8), block), :]


def run_stage(who, rows, early, early_other, late, late_other, small):
    block = rows // STAGE_BLOCKS
    return pl.pallas_call(
        stage_kernel,
        grid=(STAGE_BLOCKS + 1,),
        in_specs=[
            pl.BlockSpec(memory_space=pltpu.SMEM),
            const_spec(early.shape), const_spec(early.shape),
            const_spec(late.shape), const_spec(late.shape), const_spec(small.shape),
        ],
        out_specs=pl.BlockSpec((block, LANES), lambda i: (jnp.maximum(i - 1, 0), 0)),
        out_shape=jax.ShapeDtypeStruct((rows, LANES), F32),
        scratch_shapes=[pltpu.VMEM((STAGE_ROWS, LANES), F32)],
        compiler_params=pltpu.CompilerParams(
            dimension_semantics=("arbitrary",), vmem_limit_bytes=48 * 2**20),
        cost_estimate=pl.CostEstimate(
            flops=10**6, bytes_accessed=12 * 2**20, transcendentals=0),
    )(who, early, early_other, late, late_other, small)


def swap(values, axis, bit):
    size = lax.axis_size(axis)
    return lax.ppermute(values, axis, [(i, i ^ bit) for i in range(size)])


def to_wire(values, power):
    return (values * jnp.exp2(power)).astype(jnp.float16)


def from_wire(values, power):
    return values.astype(F32) * jnp.exp2(-power)


def scatter(values, power, axis, bit=1, count=2, after=None, sent=None):
    place = (lax.axis_index(axis) // bit) % count
    rows = values.shape[-2] // count
    mark = min(MARK, rows)
    dim = values.ndim - 2
    total = lax.dynamic_slice_in_dim(values, place * rows, rows, dim)
    least = power
    arrived = []
    for offset in range(1, count):
        to = place ^ offset
        last = to == count - 1
        start = to * rows - jnp.where(last, mark, 0)
        send = lax.dynamic_slice_in_dim(values, start, rows + mark, dim)
        line = lax.broadcasted_iota(jnp.int32, send.shape, dim)
        marked = jnp.where(last, line < mark, line >= rows)
        wire = jnp.where(marked, power, send * jnp.exp2(power)).astype(jnp.float16)
        arrived.append(swap(wire, axis, bit * offset))
        if sent is not None:
            sent.append(wire)
    if after is not None:
        arrived, _ = lax.optimization_barrier((arrived, after))
    last = place == count - 1
    for got in arrived:
        got_power = lax.dynamic_slice_in_dim(
            got, jnp.where(last, 0, rows), 1, dim).reshape(1, D).astype(F32)
        body = lax.dynamic_slice_in_dim(got, jnp.where(last, mark, 0), rows, dim)
        total = total + from_wire(body, got_power)
        least = jnp.minimum(least, got_power)
    return total, least - float(count.bit_length() - 1)


def scatter_product(left, right, power, axis, bit):
    def product(part):
        return lax.dot_general(
            part, right, (((1,), (1,)), ((0,), (0,))), preferred_element_type=F32)

    side = (lax.axis_index(axis) // bit) % 2
    rows = left.shape[2] // 2
    send = product(jnp.where(side == 1, left[:, :, : rows + LANES], left[:, :, rows - LANES :]))
    line = lax.broadcasted_iota(jnp.int32, send.shape, 1)
    marked = jnp.where(side == 1, line >= rows, line < LANES)
    wire = jnp.where(marked, power, send * jnp.exp2(power)).astype(jnp.float16)
    got = swap(wire, axis, bit)
    left, _ = lax.optimization_barrier((left, wire))
    keep = product(jnp.where(side == 0, left[:, :, :rows], left[:, :, rows:]))
    keep, got = lax.optimization_barrier((keep, got))
    got_power = lax.dynamic_slice(
        got, (0, (1 - side) * rows, 0), (1, 1, D))[0].astype(F32)
    body = lax.dynamic_slice_in_dim(got, side * LANES, rows, 1)
    return keep + from_wire(body, got_power), jnp.minimum(power, got_power) - 1.0


def everyones(values, axis, bit=1, count=2):
    place = (lax.axis_index(axis) // bit) % count
    pieces = [values] + [swap(values, axis, bit * offset) for offset in range(1, count)]
    step = 1
    while step < count:
        flip = (place // step) % 2 == 1
        pieces = [
            jnp.where(flip, pieces[i ^ step], pieces[i]) for i in range(count)]
        step *= 2
    return pieces


def gather(values, axis, bit=1, count=2):
    return jnp.concatenate(everyones(values, axis, bit, count))


def add_pair(values, axis, bit, after=None):
    got = swap(values, axis, bit)
    if after is not None:
        got, _ = lax.optimization_barrier((got, after))
    return values + got


def data_groups():
    size = lax.axis_size("dp")
    groups = [(1, 2)]
    bit = 2
    while bit < size:
        count = 4 if bit * 4 <= size else 2
        groups.append((bit, count))
        bit *= count
    return groups


def dot_tn(a, b):
    return lax.dot_general(a, b, (((0,), (0,)), ((), ())), preferred_element_type=F32)


def pick_rows(index, rows):
    chosen = index[:, None] == jnp.arange(rows.shape[0], dtype=jnp.int32)[None, :]
    return dot(chosen.astype(BF16), rows).astype(BF16)


def on_device(
    tokens, loss_sensitivity, lengths, holder_sequence_list, master, moment_one, moment_two,
    adam_rates, iteration_tally,
):
    group_devices = lax.axis_size("zero")
    data_devices = lax.axis_size("dp")
    zero_index = lax.axis_index("zero")
    dp_index = lax.axis_index("dp")
    seq_len = loss_sensitivity.shape[1]
    group_seqs = tokens.shape[0]
    span = tokens.shape[1]
    slots = group_seqs // data_devices
    shard_rows = master.shape[0] // LANES
    tie = lax.optimization_barrier

    own = master.reshape(shard_rows, LANES)
    arranged = holder_sequence_list.reshape(data_devices, group_devices, slots)
    group_order = lax.dynamic_index_in_dim(arranged, zero_index, 1, keepdims=False).reshape(-1)
    local_ids = group_order - zero_index * group_seqs
    dealt = tokens.at[local_ids].get(mode="promise_in_bounds")
    flat = lax.all_gather(own.astype(BF16), "zero", axis=0, tiled=True)

    local_tok = lax.all_to_all(dealt, "dp", split_axis=0, concat_axis=0, tiled=True)
    my_seqs = lax.dynamic_slice_in_dim(group_order, dp_index * slots, slots)
    bound = lengths[my_seqs[0]]
    positions = jnp.arange(seq_len, dtype=jnp.int32)

    in_w, out_w, norm_gain, *params, e2, et = run_prepare(flat)
    cot = loss_sensitivity[0]
    gm = dot_nt(cot, out_w)
    cot_top = jnp.max(jnp.abs(cot)).astype(F32).reshape(1)
    local_tok, in_w, gm, cot_top = tie((local_tok, in_w, gm, cot_top))
    own_late, _ = tie((own, flat[:8]))
    whole_master = lax.all_gather(own_late, "zero", axis=0, tiled=True)

    def place(slot, at):
        return (at // span) * (slots * span) + slot * span + at % span

    source = jnp.where(positions < bound, place(0, positions), place(1, positions - bound))
    packed = pick_rows(source, local_tok.reshape(slots * seq_len, D))
    blocks = jnp.arange(data_devices, dtype=jnp.int32)[:, None, None] * span
    within = blocks + jnp.arange(span, dtype=jnp.int32)[None, None, :]
    within = within + jnp.arange(slots, dtype=jnp.int32)[None, :, None] * bound
    unpack_rows = jnp.minimum(within, seq_len - 1).reshape(-1)
    ends = jnp.stack([bound, jnp.int32(seq_len)])[None, :, None]
    live_rows = jnp.where(within < ends, within, -1).reshape(-1)

    def spread(rows, index):
        return pick_rows(index, rows).reshape(data_devices * slots, span, D)

    def send_back(picked):
        return lax.all_to_all(picked, "dp", split_axis=0, concat_axis=0, tiled=True)

    restore = jnp.zeros_like(local_ids).at[local_ids].set(
        jnp.arange(group_seqs, dtype=jnp.int32))
    mine = lax.dynamic_slice_in_dim(lengths, zero_index * group_seqs, group_seqs)
    at = dp_index * span + jnp.arange(span, dtype=jnp.int32)
    live = (at[None, :] < mine[:, None])[:, :, None]

    bound_arr = bound.reshape(1)
    tok = packed.astype(F32)
    nhat = tok * lax.rsqrt(jnp.mean(tok * tok, axis=1, keepdims=True) + EPS_NORM)
    normed = (nhat * norm_gain).astype(BF16)
    proj_z = dot_nt(normed, in_w[:INNER])
    proj = dot_nt(normed, in_w[INNER:PROJ])
    pair, dy, through, states, ggain, early_power = run_forward(
        proj_z, proj, gm, bound_arr, cot_top, norm_gain, e2, et, params)
    result = (tok + dot(pair[1], out_w)).astype(BF16)
    picked = spread(result, unpack_rows)
    picked, pair = tie((picked, pair))
    back_out = send_back(picked)
    early_power = early_power[0:1, 0:1]
    early, early_power = scatter_product(
        pair, jnp.stack([normed, cot]), early_power, "zero", 1)
    early, early_power, dy = tie((early.reshape(INNER, D), early_power, dy))
    early, early_power = scatter(early, early_power, "zero", 2)
    window, grad_tok, small, late_power = run_backward(
        proj, dy, through, states, pair, packed, cot, in_w, norm_gain, ggain,
        bound_arr, e2, et, params)
    window, small, late_power, early, early_power, whole_master = tie(
        (window, small, late_power, early, early_power, whole_master))

    groups = data_groups()
    late_power = late_power[0:1, 0:1]
    late, late_power = scatter_product(
        window, jnp.stack([normed, normed]), late_power, "zero", 1)
    late = late.reshape(WINDOW, D)
    small = add_pair(small, "zero", 1)
    early, early_power, grad_tok, _ = tie((early, early_power, grad_tok, late))
    late, late_power = scatter(late, late_power, "zero", 2)
    early, early_power = scatter(early, early_power, "dp", *groups[0])
    small = add_pair(small, "zero", 2, late)
    early_before, power_before = early, early_power
    picked_grad = spread(grad_tok, live_rows)
    tokens, back_out, _ = tie((tokens, back_out, grad_tok))
    back_rows = back_out.at[restore].get(mode="promise_in_bounds")
    tokens_out = jnp.where(live, back_rows, tokens)
    new_master = jnp.zeros((group_devices, shard_rows, LANES), F32)
    late, tokens_out, new_master, picked_grad = tie((late, tokens_out, new_master, picked_grad))
    lines = small.shape[0]
    late = jnp.concatenate([late, small, jnp.zeros((WINDOW // 8 - lines, D), F32)])
    late, late_power = scatter(late, late_power, "dp", *groups[0])
    sent = []
    for group in groups[1:]:
        late, late_power = scatter(late, late_power, "dp", *group, sent=sent)
    early, early_power = early_before, power_before
    for group in groups[1:]:
        early, early_power = scatter(early, early_power, "dp", *group, after=sent)
    early = to_wire(early, early_power)
    for group in reversed(groups[1:]):
        early = gather(early, "dp", *group)
    early, _ = tie((early, late))
    late = to_wire(late, late_power)
    early = from_wire(gather(early, "dp", *groups[0]), early_power)
    early, picked_grad, _ = tie((early, picked_grad, late))
    for group in reversed(groups[1:]):
        late = gather(late, "dp", *group)
    early_other = swap(early, "zero", 1)
    back_grad = send_back(picked_grad)
    wire = gather(late, "dp", *groups[0])
    late = from_wire(wire[: WINDOW // 2], late_power)
    small = from_wire(wire[WINDOW // 2 : WINDOW // 2 + lines], late_power)
    late_other = swap(late, "zero", 1)

    steps_f = iteration_tally[0].astype(F32)
    who = jnp.stack([zero_index // 2, zero_index % 2]).astype(jnp.int32)
    first = moment_one.reshape(shard_rows, LANES)
    second = moment_two.reshape(shard_rows, LANES)
    grad_shard = run_stage(who, shard_rows, early, early_other, late, late_other, small)
    first_scale = 1.0 / (1.0 - jnp.power(BETA_ONE, steps_f))
    second_scale = 1.0 / (1.0 - jnp.power(BETA_TWO, steps_f))

    def moments(grad, first, second):
        return (
            BETA_ONE * first + (1.0 - BETA_ONE) * grad,
            BETA_TWO * second + (1.0 - BETA_TWO) * grad * grad)

    def quotient(rows):
        first_next, second_next = moments(grad_shard[rows], first[rows], second[rows])
        return ((first_next * first_scale) / (
            jnp.sqrt(second_next * second_scale) + EPS_ADAM)).astype(jnp.float16)

    whole_master = whole_master.reshape(group_devices, shard_rows, LANES)

    def put(new_master, piece, offset):
        shard = zero_index ^ offset
        old = lax.dynamic_index_in_dim(whole_master, shard, 0, keepdims=False)
        new = old - adam_rates[0] * (piece.astype(F32) + adam_rates[1] * old)
        return lax.dynamic_update_index_in_dim(new_master, new, shard, 0)

    own_part, first, second = tie((quotient(slice(0, shard_rows)), first, second))
    across = swap(own_part, "zero", 2)
    core = swap(own_part, "zero", 1)
    first_next, second_next = moments(grad_shard, first, second)
    new_master = put(put(new_master, own_part, 0), core, 1)
    across, new_master, first_next, second_next = tie(
        (across, new_master, first_next, second_next))
    last = swap(across, "zero", 1)
    new_master = put(new_master, across, 2)
    last, new_master = tie((last, new_master))
    new_master = put(new_master, last, 3)
    back_grad, new_master = tie((back_grad, new_master))
    grad_tokens = back_grad.at[restore].get(mode="promise_in_bounds")
    return (
        tokens_out, grad_tokens, new_master.reshape(-1), grad_shard.reshape(-1),
        first_next.reshape(-1), second_next.reshape(-1))


def solution(mesh):
    return jax.shard_map(
        on_device,
        mesh=mesh,
        in_specs=(
            P("zero", "dp", None), P(("dp", "zero"), None, None), P(), P(),
            P("zero"), P("zero"), P("zero"), P(), P(),
        ),
        out_specs=(
            P("zero", "dp", None), P("zero", "dp", None), P(), P("zero"), P("zero"), P("zero"),
        ),
        check_vma=False,
    )
```

```python
import jax
import jax.numpy as jnp
from jax import lax
from jax.experimental import pallas as pl
from jax.experimental.pallas import tpu as pltpu
from jax.sharding import PartitionSpec as P

D = 768
HEADS = 24
HEADDIM = 64
STATE = 128
CONV = 4
INNER = 1536
XBC = 1792
PROJ = 3352
Q = 128
LATE = PROJ - INNER
WINDOW = 1024
PAIRS = HEADS // 2
EPS_NORM = 1e-05
NEG = -1e30
F16_TOP = 30000.0
LOG2E = 1.4426950408889634
F32 = jnp.float32
BF16 = jnp.bfloat16


def dot(a, b):
    return lax.dot_general(a, b, (((1,), (0,)), ((), ())), preferred_element_type=F32)


def dot_nt(a, b):
    return lax.dot_general(a, b, (((1,), (1,)), ((), ())), preferred_element_type=F32)


def split2(v):
    hi = v.astype(BF16)
    return hi, (v - hi.astype(F32)).astype(BF16)


def split3(v):
    hi = v.astype(BF16)
    rest = v - hi.astype(F32)
    mid = rest.astype(BF16)
    return hi, mid, (rest - mid.astype(F32)).astype(BF16)


def wide_left(v):
    hi, lo = split2(v)
    return jnp.concatenate([hi, lo, hi], axis=1)


def tall_right(v):
    hi, lo = split2(v)
    return jnp.concatenate([hi, hi, lo], axis=0)


def split_pair(v, masks):
    hi, lo = split2(v)
    return jnp.concatenate([
        jnp.concatenate([hi * masks[0], lo * masks[0]], axis=1),
        jnp.concatenate([hi * masks[1], lo * masks[1]], axis=1)], axis=0)


def sigmoid(v):
    return lax.logistic(v)


def softplus(v):
    return jnp.maximum(v, 0.0) + jnp.log1p(jnp.exp(-jnp.abs(v)))


def iota(shape, dim):
    return lax.broadcasted_iota(jnp.int32, shape, dim)


def expand(v, e_ref):
    hi, lo = split2(v)
    return dot(jnp.concatenate([hi, lo], axis=1), e_ref[...])


def head_sum(v, et_ref):
    hi, lo = split2(v)
    return dot(hi, et_ref[...]) + dot(lo, et_ref[...])


def quarters(out):
    return out[:Q, :Q] + (out[:Q, Q:] + out[Q:, :Q])


def power_for(bound):
    scale = jnp.log(0.9 * F16_TOP / jnp.maximum(bound, 1e-30)) * LOG2E
    return jnp.clip(jnp.floor(scale), -126.0, 120.0)


def chunk_masks(t0, bound):
    rows = t0 + iota((Q, 1), 0)
    rr = t0 + iota((Q, Q), 0)
    cc = t0 + iota((Q, Q), 1)
    return rows, rr, cc


def conv_rows(ext_ref, w_ref, b_ref, rows, bound):
    total = b_ref[...] + w_ref[3:4, :] * ext_ref[8 : 8 + Q, :]
    for back in (1, 2, 3):
        ok = jnp.logical_or(rows - back >= bound, rows < bound).astype(F32)
        total = total + w_ref[3 - back : 4 - back, :] * (ext_ref[8 - back : 8 - back + Q, :] * ok)
    return total


def decay_parts(dt_raw, dtb_ref, alog_ref, rr, cc):
    dt_in = dt_raw + dtb_ref[...]
    dt_pos = softplus(dt_in)
    rate = -jnp.exp(alog_ref[...])
    step = dt_pos * rate
    tri = (cc <= rr).astype(F32).astype(BF16)
    s_hi, s_mid, s_lo = split3(step)
    cum = dot(tri, s_hi) + dot(tri, s_mid) + dot(tri, s_lo)
    return dt_in, dt_pos, rate, cum


def forward_kernel(
    bound_ref, cot_ref, z_ref, proj_ref, gm_ref, norm_ref, e_ref, et_ref, convw_ref, convb_ref, dtb_ref, alog_ref,
    skip_ref, gain_ref,
    pair_ref, dy_ref, through_ref, state_ref, ggain_ref, power_ref,
    zmax_ref, ext_ref, dt_ref, carry_ref, xd_ref, acc_ref, cumt_ref,
):
    step = pl.program_id(0)
    bound = bound_ref[0]
    t0 = step * Q

    @pl.when(step == 0)
    def _():
        ext_ref[0:8, :] = jnp.zeros((8, XBC), F32)
        carry_ref[...] = jnp.zeros_like(carry_ref)
        dt_ref[...] = jnp.zeros_like(dt_ref)
        ggain_ref[...] = jnp.zeros_like(ggain_ref)
        zmax_ref[...] = jnp.zeros_like(zmax_ref)

    rows, rr, cc = chunk_masks(t0, bound)
    ext_ref[8 : 8 + Q, :] = proj_ref[:, :XBC]
    pre = conv_rows(ext_ref, convw_ref, convb_ref, rows, bound)
    ext_ref[0:8, :] = ext_ref[Q : Q + 8, :]
    conv_out = pre * sigmoid(pre)
    x = conv_out[:, :INNER]
    b_rows = conv_out[:, INNER : INNER + STATE]
    c_rows = conv_out[:, INNER + STATE :]
    dt_ref[:, 0:HEADS] = proj_ref[:, XBC:LATE]
    _, dt_pos, _, cum = decay_parts(dt_ref[...], dtb_ref, alog_ref, rr, cc)
    cum_end = cum[Q - 1 : Q, :]
    keep = jnp.logical_or(rows < bound, bound < t0).astype(F32)
    in_last = jnp.logical_or(rows >= bound, bound > t0 + Q - 1).astype(F32)
    whole = jnp.logical_or(bound < t0, bound > t0 + Q - 1).astype(F32)
    from_start = jnp.exp(cum) * keep
    to_end = jnp.exp(cum_end - cum) * in_last
    carry_scale = jnp.exp(cum_end) * whole
    allowed = jnp.logical_and(cc <= rr, (cc >= bound) == (rr >= bound))
    cum2 = cum * LOG2E
    cumt_ref[...] = cum2.T

    state = carry_ref[...]
    state_ref[0] = state
    spread = expand(jnp.concatenate(
        [dt_pos, to_end, from_start, jnp.broadcast_to(carry_scale, (16, 128))], axis=0), e_ref)
    xd = x * spread[:Q]
    xd_ref[...] = xd
    acc = dot(wide_left(c_rows), tall_right(state)) * spread[2 * Q : 3 * Q]
    acc_ref[...] = acc + skip_ref[...] * x
    b_t = b_rows.T
    carry_ref[...] = state * spread[3 * Q : 3 * Q + 1] + dot(
        wide_left(b_t), tall_right(xd * spread[Q : 2 * Q]))
    gram = dot(wide_left(c_rows), tall_right(b_t))
    first = iota((Q, Q), 1) < HEADDIM
    first_b = (first.astype(F32).astype(BF16), 1.0 - first.astype(F32).astype(BF16))
    for pair in range(PAIRS):
        parts = []
        for head in (2 * pair, 2 * pair + 1):
            differ = cum2[:, head : head + 1] - cumt_ref[head : head + 1, :]
            parts.append(gram * jnp.exp2(jnp.where(allowed, differ, NEG)))
        left = jnp.concatenate(split2(jnp.concatenate(parts, axis=1)), axis=0)
        lanes = slice(pair * 128, pair * 128 + 128)
        xp = xd_ref[:, lanes]
        out = dot(left, split_pair(xp, first_b))
        acc_ref[:, lanes] += out[:Q, :128] + (out[:Q, 128:] + out[Q:, :128])
    scanned = acc_ref[...]
    z = z_ref[...]
    sig_z = sigmoid(z)
    silu_z = z * sig_z
    gated = scanned * silu_z
    ginv = lax.rsqrt(jnp.mean(gated * gated, axis=1, keepdims=True) + EPS_NORM)
    mhat = gated * ginv
    pair_ref[1] = (mhat * gain_ref[...]).astype(BF16)
    gm = gm_ref[...]
    ggain_ref[...] += jnp.sum(mhat * gm, axis=0, keepdims=True)
    gmg = gm * gain_ref[...]
    ggated = ginv * (gmg - mhat * jnp.mean(mhat * gmg, axis=1, keepdims=True))
    dy = ggated * silu_z
    dy_ref[...] = dy
    grad_z = ggated * scanned * (sig_z * (1.0 + z * (1.0 - sig_z)))
    zmax_ref[...] = jnp.maximum(zmax_ref[...], jnp.max(jnp.abs(grad_z), axis=0, keepdims=True))
    pair_ref[0] = grad_z.astype(BF16)
    through_ref[...] = head_sum(dy * (scanned - skip_ref[...] * x), et_ref)

    @pl.when(step == pl.num_programs(0) - 1)
    def _():
        count = float(Q * pl.num_programs(0))
        largest = jnp.max(zmax_ref[...], axis=1, keepdims=True)
        normed = jnp.max(jnp.abs(norm_ref[...]), axis=1, keepdims=True) * (D ** 0.5)
        mixed = jnp.max(jnp.abs(gain_ref[...]), axis=1, keepdims=True) * (INNER ** 0.5)
        power_ref[...] = jnp.broadcast_to(power_for(
            1.05 * count * jnp.maximum(largest * normed, cot_ref[0] * mixed)), (8, 128))


def const_spec(shape):
    return pl.BlockSpec(shape, lambda *_: (0,) * len(shape))


def run_forward(z, proj, gm, bound, cot_top, norm_gain, e2, et, params):
    n = proj.shape[0]
    steps = n // Q
    return pl.pallas_call(
        forward_kernel,
        grid=(steps,),
        in_specs=[
            pl.BlockSpec(memory_space=pltpu.SMEM), pl.BlockSpec(memory_space=pltpu.SMEM),
            pl.BlockSpec((Q, INNER), lambda i: (i, 0)),
            pl.BlockSpec((Q, LATE), lambda i: (i, 0)),
            pl.BlockSpec((Q, INNER), lambda i: (i, 0)),
            const_spec((1, D)),
            const_spec((256, INNER)), const_spec((INNER, 128)),
            const_spec((8, XBC)), const_spec((1, XBC)), const_spec((1, 128)),
            const_spec((1, 128)), const_spec((1, INNER)), const_spec((1, INNER)),
        ],
        out_specs=[
            pl.BlockSpec((2, Q, INNER), lambda i: (0, i, 0)),
            pl.BlockSpec((Q, INNER), lambda i: (i, 0)),
            pl.BlockSpec((Q, 128), lambda i: (i, 0)),
            pl.BlockSpec((1, STATE, INNER), lambda i: (i, 0, 0)),
            const_spec((1, INNER)), const_spec((8, 128)),
        ],
        out_shape=[
            jax.ShapeDtypeStruct((2, n, INNER), BF16),
            jax.ShapeDtypeStruct((n, INNER), F32),
            jax.ShapeDtypeStruct((n, 128), F32),
            jax.ShapeDtypeStruct((steps, STATE, INNER), F32),
            jax.ShapeDtypeStruct((1, INNER), F32),
            jax.ShapeDtypeStruct((8, 128), F32),
        ],
        scratch_shapes=[
            pltpu.VMEM((1, INNER), F32),
            pltpu.VMEM((Q + 8, XBC), F32),
            pltpu.VMEM((Q, 128), F32),
            pltpu.VMEM((STATE, INNER), F32),
            pltpu.VMEM((Q, INNER), F32),
            pltpu.VMEM((Q, INNER), F32),
            pltpu.VMEM((128, Q), F32),
        ],
        compiler_params=pltpu.CompilerParams(
            dimension_semantics=("arbitrary",), vmem_limit_bytes=26 * 2**20),
        cost_estimate=pl.CostEstimate(
            flops=30 * 10**9, bytes_accessed=40 * 2**20, transcendentals=10**7),
    )(bound, cot_top, z, proj, gm, norm_gain, e2, et, *params)


def backward_kernel(
    bound_ref, proj_ref, before_ref, dy_ref, through_ref, state_ref, gz_ref, tok_ref, cot_ref,
    in_ref, norm_ref, ggain_ref,
    e_ref, et_ref, convw_ref, convb_ref, dtb_ref, alog_ref, skip_ref,
    window_ref, gtok_ref, small_ref, power_ref,
    total_ref, gskip_ref, gsmall_ref, dtw_ref, gp_ref, ext_ref, dt_ref, lam_ref, dsum_ref, xd_ref, g_ref, gnext_ref, cumt_ref,
):
    step = pl.program_id(0)
    steps = pl.num_programs(0)
    bound = bound_ref[0]
    t0 = (steps - 1 - step) * Q

    @pl.when(step == 0)
    def _():
        lam_ref[...] = jnp.zeros_like(lam_ref)
        dsum_ref[...] = jnp.zeros_like(dsum_ref)
        dt_ref[...] = jnp.zeros_like(dt_ref)
        gnext_ref[Q : Q + 8, :] = jnp.zeros((8, XBC), F32)
        gskip_ref[...] = jnp.zeros_like(gskip_ref)
        total_ref[...] = jnp.zeros_like(total_ref)
        dtw_ref[...] = jnp.zeros_like(dtw_ref)
        gsmall_ref[...] = jnp.zeros_like(gsmall_ref)

    rows, rr, cc = chunk_masks(t0, bound)
    dy = dy_ref[...]
    first_chunk = (t0 > 0).astype(F32)
    ext_ref[0:8, :] = before_ref[:, :XBC] * first_chunk
    ext_ref[8 : 8 + Q, :] = proj_ref[:, :XBC]
    pre = conv_rows(ext_ref, convw_ref, convb_ref, rows, bound)
    sig_pre = sigmoid(pre)
    conv_out = pre * sig_pre
    x = conv_out[:, :INNER]
    b_rows = conv_out[:, INNER : INNER + STATE]
    c_rows = conv_out[:, INNER + STATE :]
    dt_ref[:, 0:HEADS] = proj_ref[:, XBC:LATE]
    dt_in, dt_pos, rate, cum = decay_parts(dt_ref[...], dtb_ref, alog_ref, rr, cc)
    cum_end = cum[Q - 1 : Q, :]
    keep = jnp.logical_or(rows < bound, bound < t0).astype(F32)
    in_last = jnp.logical_or(rows >= bound, bound > t0 + Q - 1).astype(F32)
    whole = jnp.logical_or(bound < t0, bound > t0 + Q - 1).astype(F32)
    from_start = jnp.exp(cum) * keep
    to_end = jnp.exp(cum_end - cum) * in_last
    carry_scale = jnp.exp(cum_end) * whole
    allowed_t = jnp.logical_and(rr <= cc, (cc >= bound) == (rr >= bound))
    cum2 = cum * LOG2E
    cumt_ref[...] = cum2.T
    c_t = c_rows.T
    gram_t = dot(wide_left(b_rows), tall_right(c_t))
    spread = expand(jnp.concatenate(
        [dt_pos, to_end, from_start, jnp.broadcast_to(carry_scale, (16, 128))], axis=0), e_ref)
    dt_all = spread[:Q]
    end_all = spread[Q : 2 * Q]
    xd = x * dt_all
    xd_ref[...] = xd
    skip = skip_ref[...]
    gskip_ref[...] += jnp.sum(dy * x, axis=0, keepdims=True)
    lam = lam_ref[...]
    lam_hi, lam_lo = split2(lam)
    g_ref[...] = (
        dot(wide_left(b_rows), jnp.concatenate([lam_hi, lam_hi, lam_lo], axis=0)) * end_all
    )
    grad_b = quarters(dot_nt(
        jnp.concatenate(split2(xd * end_all), axis=0), jnp.concatenate([lam_hi, lam_lo], axis=0)))
    state = state_ref[0]
    dye_hi, dye_lo = split2(dy * spread[2 * Q : 3 * Q])
    grad_c = quarters(dot_nt(
        jnp.concatenate([dye_hi, dye_lo], axis=0), jnp.concatenate(split2(state), axis=0)))
    lam_new = lam * spread[3 * Q : 3 * Q + 1] + dot(
        wide_left(c_t), jnp.concatenate([dye_hi, dye_hi, dye_lo], axis=0)
    )
    lam_ref[...] = lam_new
    ended = dsum_ref[0:1, :]
    first = iota((Q, Q), 1) < HEADDIM
    first_b = (first.astype(F32).astype(BF16), 1.0 - first.astype(F32).astype(BF16))
    first_row = (iota((Q, Q), 0) < HEADDIM).astype(F32).astype(BF16)
    first_row = (first_row, 1.0 - first_row)
    gram_grad = jnp.zeros((Q, Q), F32)
    for pair in range(PAIRS):
        lanes = slice(pair * 128, pair * 128 + 128)
        weights = []
        for head in (2 * pair, 2 * pair + 1):
            differ = cumt_ref[head : head + 1, :] - cum2[:, head : head + 1]
            weights.append(jnp.exp2(jnp.where(allowed_t, differ, NEG)))
        left = jnp.concatenate([gram_t * weights[0], gram_t * weights[1]], axis=1)
        left = jnp.concatenate(split2(left), axis=0)
        dyp = dy_ref[:, lanes]
        out = dot(left, split_pair(dyp, first_b))
        g_ref[:, lanes] += out[:Q, :128] + (out[:Q, 128:] + out[Q:, :128])
        dyt_hi, dyt_lo = split2(dyp.T)
        right_hi = jnp.concatenate([dyt_hi * first_row[0], dyt_hi * first_row[1]], axis=1)
        right_lo = jnp.concatenate([dyt_lo * first_row[0], dyt_lo * first_row[1]], axis=1)
        outer = dot(
            wide_left(xd_ref[:, lanes]), jnp.concatenate([right_hi, right_hi, right_lo], axis=0))
        gram_grad = gram_grad + (outer[:, :128] * weights[0] + outer[:, 128:] * weights[1])
    g = g_ref[...]
    grad_x = dt_all * g + skip * dy
    sums = dot(jnp.concatenate(
        split2(x * g) + split2(jnp.broadcast_to(
            jnp.sum(lam_new * state, axis=0, keepdims=True), (16, INNER))), axis=0), et_ref[...])
    direct = sums[:Q] + sums[Q : 2 * Q]
    balance = through_ref[...] - dt_pos * direct
    keep_t = allowed_t.astype(F32).astype(BF16)
    b_hi, b_mid, b_lo = split3(balance)
    grad_step = dot(keep_t, b_hi) + dot(keep_t, b_mid) + dot(keep_t, b_lo) + in_last * ended
    dsum_ref[...] = sums[2 * Q : 2 * Q + 8] + sums[2 * Q + 16 : 2 * Q + 24]
    grad_dt = (direct + rate * grad_step) * sigmoid(dt_in)
    gsmall_ref[0:1, :] += jnp.sum(grad_dt, axis=0, keepdims=True)
    gsmall_ref[1:2, :] += rate * jnp.sum(dt_pos * grad_step, axis=0, keepdims=True)
    grad_c = grad_c + dot(wide_left(gram_grad.T), tall_right(b_rows))
    grad_b = grad_b + dot(wide_left(gram_grad), tall_right(c_rows))
    slope = sig_pre * (1.0 + pre * (1.0 - sig_pre))
    gnext_ref[0:Q, :INNER] = grad_x * slope[:, :INNER]
    gnext_ref[0:Q, INNER : INNER + STATE] = grad_b * slope[:, INNER : INNER + STATE]
    gnext_ref[0:Q, INNER + STATE :] = grad_c * slope[:, INNER + STATE :]
    gcp = gnext_ref[0:Q, :]
    total_ref[4:5, :] += jnp.sum(gcp, axis=0, keepdims=True)
    total_ref[3:4, :] += jnp.sum(gcp * ext_ref[8 : 8 + Q, :], axis=0, keepdims=True)
    total = convw_ref[3:4, :] * gcp
    for back in (1, 2, 3):
        ok = jnp.logical_or(rows - back >= bound, rows < bound).astype(F32)
        total_ref[3 - back : 4 - back, :] += jnp.sum(
            gcp * (ext_ref[8 - back : 8 - back + Q, :] * ok), axis=0, keepdims=True)
        okn = jnp.logical_or(rows >= bound, rows + back < bound).astype(F32)
        total = total + convw_ref[3 - back : 4 - back, :] * (gnext_ref[back : back + Q, :] * okn)
    total_ref[7:8, :] = jnp.maximum(
        total_ref[7:8, :], jnp.max(jnp.abs(total), axis=0, keepdims=True))
    total = total.astype(BF16)
    window_ref[0] = total[:, :WINDOW]
    window_ref[1] = total[:, XBC - WINDOW :]
    gnext_ref[Q : Q + 8, :] = gnext_ref[0:8, :]
    half = (steps - 1 - step) % 2
    at = pl.multiple_of(half * Q, Q)
    gp_ref[pl.ds(at, Q), :INNER] = gz_ref[0]
    gp_ref[pl.ds(at, Q), INNER : INNER + XBC] = total
    gp_ref[pl.ds(at, Q), INNER + XBC :] = grad_dt.astype(BF16)

    @pl.when(half == 0)
    def _():
        grad_normed = dot(gp_ref[...], in_ref[: INNER + XBC + 128, :])
        tok = tok_ref[...].astype(F32)
        rinv = lax.rsqrt(jnp.mean(tok * tok, axis=1, keepdims=True) + EPS_NORM)
        nhat = tok * rinv
        gain = norm_ref[...]
        gng = grad_normed * gain
        gtok_ref[...] = (cot_ref[...].astype(F32) + rinv * (
            gng - nhat * jnp.mean(nhat * gng, axis=1, keepdims=True))).astype(BF16)
        total_ref[6:7, :D] += jnp.sum(nhat * grad_normed, axis=0, keepdims=True)
        normed = (nhat * gain).astype(BF16)
        gdt = gp_ref[:, INNER + XBC :].astype(F32)
        dtw_ref[...] += dot(jnp.concatenate(
            [gdt[:Q].T, gdt[Q:].T], axis=1).astype(BF16), normed)

    @pl.when(step == steps - 1)
    def _():
        skips = head_sum(jnp.broadcast_to(gskip_ref[...], (8, INNER)), et_ref)
        small_ref[...] = jnp.zeros_like(small_ref)
        small_ref[0:HEADS, :] = dtw_ref[0:HEADS, :]
        pieces = [
            total_ref[k : k + 1, j * 128 : j * 128 + 128]
            for k in range(CONV + 1) for j in range(XBC // 128)]
        pieces += [gsmall_ref[0:1, :], gsmall_ref[1:2, :], skips[0:1, :]]
        pieces += [ggain_ref[:, j * 128 : j * 128 + 128] for j in range(INNER // 128)]
        lines = D // 128
        for number, piece in enumerate(pieces):
            line = HEADS + number // lines
            at = number % lines * 128
            small_ref[line : line + 1, at : at + 128] = piece
        small_ref[40:41, :] = total_ref[6:7, :D]
        count = float(Q * steps)
        largest = jnp.max(total_ref[7:8, :], axis=1, keepdims=True)
        normed = jnp.max(jnp.abs(norm_ref[...]), axis=1, keepdims=True) * (D ** 0.5)
        others = jnp.max(jnp.max(jnp.abs(small_ref[...]), axis=1, keepdims=True), axis=0, keepdims=True)
        power_ref[...] = jnp.broadcast_to(power_for(
            jnp.maximum(1.05 * count * largest * normed, others)), (8, 128))


def run_backward(
    proj, dy, through, states, pair, tok, cot, in_w, norm_gain, ggain, bound, e2, et, params
):
    n = proj.shape[0]
    steps = n // Q

    def rev(i):
        return (steps - 1 - i, 0)

    def rev_two(i):
        return ((steps - 1 - i) // 2, 0)

    return pl.pallas_call(
        backward_kernel,
        grid=(steps,),
        in_specs=[
            pl.BlockSpec(memory_space=pltpu.SMEM),
            pl.BlockSpec((Q, LATE), rev),
            pl.BlockSpec((8, LATE), lambda i: (jnp.maximum((steps - 1 - i) * (Q // 8) - 1, 0), 0)),
            pl.BlockSpec((Q, INNER), rev),
            pl.BlockSpec((Q, 128), rev),
            pl.BlockSpec((1, STATE, INNER), lambda i: (steps - 1 - i, 0, 0)),
            pl.BlockSpec((1, Q, INNER), lambda i: (0, steps - 1 - i, 0)),
            pl.BlockSpec((2 * Q, D), rev_two), pl.BlockSpec((2 * Q, D), rev_two),
            const_spec(in_w.shape), const_spec((1, D)), const_spec((1, INNER)),
            const_spec((256, INNER)), const_spec((INNER, 128)),
            const_spec((8, XBC)), const_spec((1, XBC)), const_spec((1, 128)),
            const_spec((1, 128)), const_spec((1, INNER)),
        ],
        out_specs=[
            pl.BlockSpec((2, Q, WINDOW), lambda i: (0, steps - 1 - i, 0)),
            pl.BlockSpec((2 * Q, D), rev_two),
            const_spec((48, D)), const_spec((8, 128)),
        ],
        out_shape=[
            jax.ShapeDtypeStruct((2, n, WINDOW), BF16),
            jax.ShapeDtypeStruct((n, D), BF16),
            jax.ShapeDtypeStruct((48, D), F32),
            jax.ShapeDtypeStruct((8, 128), F32),
        ],
        scratch_shapes=[
            pltpu.VMEM((8, XBC), F32),
            pltpu.VMEM((1, INNER), F32),
            pltpu.VMEM((8, 128), F32),
            pltpu.VMEM((128, D), F32),
            pltpu.VMEM((2 * Q, INNER + XBC + 128), BF16),
            pltpu.VMEM((Q + 8, XBC), F32),
            pltpu.VMEM((Q, 128), F32),
            pltpu.VMEM((STATE, INNER), F32),
            pltpu.VMEM((8, 128), F32),
            pltpu.VMEM((Q, INNER), F32),
            pltpu.VMEM((Q, INNER), F32),
            pltpu.VMEM((Q + 8, XBC), F32),
            pltpu.VMEM((128, Q), F32),
        ],
        compiler_params=pltpu.CompilerParams(
            dimension_semantics=("arbitrary",), vmem_limit_bytes=36 * 2**20),
        cost_estimate=pl.CostEstimate(
            flops=50 * 10**9, bytes_accessed=50 * 2**20, transcendentals=2 * 10**7),
    )(bound, proj, proj, dy, through, states, pair, tok, cot, in_w, norm_gain, ggain,
      e2, et, *params[:5])


BETA_ONE = 0.9
BETA_TWO = 0.95
EPS_ADAM = 1e-08
LANES = 128
NORM_ROWS = D // LANES
IN_ROWS = PROJ * D // LANES
CONVW_ROWS = CONV * XBC // LANES
CONVB_ROWS = XBC // LANES
GAIN_ROWS = INNER // LANES
OUT_ROWS = INNER * D // LANES
DT_ROWS = HEADS * D // LANES
SMALL_ROWS = DT_ROWS + CONVW_ROWS + CONVB_ROWS + 3 + GAIN_ROWS
OUT_START = NORM_ROWS + IN_ROWS + SMALL_ROWS - DT_ROWS
LATE_START = NORM_ROWS + INNER * NORM_ROWS
LEAD = 896
STAGE_ROWS = 16264
STAGE_BLOCKS = 5
MARK = 16


PREP_STEPS = 7
IN_BLOCK = 512
OUT_BLOCK = 256
SMALL_START = NORM_ROWS + IN_ROWS


def prepare_kernel(
    flat_ref,
    in_ref, out_ref, norm_ref, convw_ref, convb_ref, dtb_ref, alog_ref, skip_ref, gain_ref,
    e_ref, et_ref,
    stage_ref,
):
    step = pl.program_id(0)

    @pl.when(step == 0)
    def _():
        rows = flat_ref[0:16, :].astype(F32)
        for lane in range(NORM_ROWS):
            norm_ref[:, lane * LANES : lane * LANES + LANES] = rows[lane : lane + 1, :]
        low = SMALL_START // 16 * 16
        stage_ref[0:112, :] = flat_ref[low : low + 112, :].astype(F32)
        at = SMALL_START - low
        convw_ref[...] = jnp.zeros_like(convw_ref)
        for tap in range(CONV):
            for lane in range(CONVB_ROWS):
                convw_ref[tap : tap + 1, lane * LANES : lane * LANES + LANES] = stage_ref[
                    at : at + 1, :]
                at += 1
        for lane in range(CONVB_ROWS):
            convb_ref[:, lane * LANES : lane * LANES + LANES] = stage_ref[at : at + 1, :]
            at += 1
        heads = iota((1, LANES), 1) < HEADS
        dtb_ref[...] = jnp.where(heads, stage_ref[at : at + 1, :], 0.0)
        alog_ref[...] = jnp.where(heads, stage_ref[at + 1 : at + 2, :], 0.0)
        skips = jnp.where(heads, stage_ref[at + 2 : at + 3, :], 0.0)
        at += 3
        for lane in range(GAIN_ROWS):
            gain_ref[:, lane * LANES : lane * LANES + LANES] = stage_ref[at : at + 1, :]
            at += 1
        one = (iota((128, INNER), 1) // HEADDIM == iota((128, INNER), 0)).astype(F32).astype(BF16)
        e_ref[0:128, :] = one
        e_ref[128:256, :] = one
        et_ref[...] = (
            iota((INNER, 128), 0) // HEADDIM == iota((INNER, 128), 1)).astype(F32).astype(BF16)
        skip_ref[...] = dot(jnp.broadcast_to(skips, (16, LANES)).astype(BF16), one)[0:1, :]

    def block(start, offset, rows, dest_ref):
        size = rows * NORM_ROWS + 16
        at = pl.multiple_of(start + step * (rows * NORM_ROWS), 16)
        stage_ref[0:size, :] = flat_ref[pl.ds(at, size), :].astype(F32)
        for lane in range(NORM_ROWS):
            dest_ref[:, lane * LANES : lane * LANES + LANES] = stage_ref[
                pl.ds(offset + lane, rows, stride=NORM_ROWS), :].astype(BF16)

    block(0, NORM_ROWS, IN_BLOCK, in_ref)

    @pl.when(step == PREP_STEPS - 1)
    def _():
        used = PROJ - (PREP_STEPS - 1) * IN_BLOCK
        in_ref[used:, :] = jnp.zeros((IN_BLOCK - used, D), BF16)

    @pl.when(step < INNER // OUT_BLOCK)
    def _():
        low = OUT_START // 16 * 16
        block(low, OUT_START - low, OUT_BLOCK, out_ref)


def run_prepare(flat):
    vector = lambda n: jax.ShapeDtypeStruct((1, n), F32)
    return pl.pallas_call(
        prepare_kernel,
        grid=(PREP_STEPS,),
        in_specs=[const_spec(flat.shape)],
        out_specs=[
            pl.BlockSpec((IN_BLOCK, D), lambda i: (i, 0)),
            pl.BlockSpec((OUT_BLOCK, D), lambda i: (jnp.minimum(i, INNER // OUT_BLOCK - 1), 0)),
            const_spec((1, D)), const_spec((8, XBC)), const_spec((1, XBC)), const_spec((1, 128)),
            const_spec((1, 128)), const_spec((1, INNER)), const_spec((1, INNER)),
            const_spec((256, INNER)), const_spec((INNER, 128)),
        ],
        out_shape=[
            jax.ShapeDtypeStruct((PREP_STEPS * IN_BLOCK, D), BF16),
            jax.ShapeDtypeStruct((INNER, D), BF16),
            vector(D), jax.ShapeDtypeStruct((8, XBC), F32), vector(XBC), vector(128), vector(128),
            vector(INNER), vector(INNER),
            jax.ShapeDtypeStruct((256, INNER), BF16), jax.ShapeDtypeStruct((INNER, 128), BF16),
        ],
        scratch_shapes=[pltpu.VMEM((IN_BLOCK * NORM_ROWS + 16, LANES), F32)],
        compiler_params=pltpu.CompilerParams(
            dimension_semantics=("arbitrary",), vmem_limit_bytes=40 * 2**20),
        cost_estimate=pl.CostEstimate(
            flops=10**9, bytes_accessed=16 * 2**20, transcendentals=0),
    )(flat)


def stage_kernel(
    who_ref, early_ref, early_other_ref, late_ref, late_other_ref, small_ref,
    grad_ref,
    stage_ref,
):
    step = pl.program_id(0)
    upper = who_ref[0]
    mine = who_ref[1]
    block = grad_ref.shape[0]
    half = 2 * block * STAGE_BLOCKS

    @pl.when(step == 0)
    def _():
        early_at = LEAD + jnp.where(upper == 1, OUT_START - half, NORM_ROWS)
        window = LATE_START + (XBC - WINDOW) * NORM_ROWS
        late_at = LEAD + jnp.where(upper == 1, window - half, LATE_START)
        def lay(source_ref, start, size):
            for lane in range(NORM_ROWS):
                stage_ref[pl.ds(start + lane, size, stride=NORM_ROWS), :] = source_ref[
                    0:size, lane * LANES : lane * LANES + LANES]

        lines = late_ref.shape[0]
        lay(late_ref, late_at + mine * (lines * NORM_ROWS), lines)
        lay(late_other_ref, late_at + (1 - mine) * (lines * NORM_ROWS), lines)

        @pl.when(upper == 1)
        def _():
            lay(small_ref, LEAD + OUT_START - half - SMALL_ROWS, -(-SMALL_ROWS // NORM_ROWS))

        lines = early_ref.shape[0]
        lay(early_ref, early_at + mine * (lines * NORM_ROWS), lines)
        lay(early_other_ref, early_at + (1 - mine) * (lines * NORM_ROWS), lines)

        @pl.when(upper == 0)
        def _():
            for lane in range(NORM_ROWS):
                stage_ref[LEAD + lane : LEAD + lane + 1, :] = small_ref[
                    40:41, lane * LANES : lane * LANES + LANES]

        @pl.when(upper == 1)
        def _():
            at = LEAD + OUT_START + OUT_ROWS - half
            stage_ref[at : LEAD + half, :] = jnp.zeros((LEAD + half - at, LANES), F32)

    @pl.when(step > 0)
    def _():
        at = LEAD + mine * (half // 2) + (step - 1) * block
        grad_ref[...] = stage_ref[pl.ds(pl.multiple_of(at, 8), block), :]


def run_stage(who, rows, early, early_other, late, late_other, small):
    block = rows // STAGE_BLOCKS
    return pl.pallas_call(
        stage_kernel,
        grid=(STAGE_BLOCKS + 1,),
        in_specs=[
            pl.BlockSpec(memory_space=pltpu.SMEM),
            const_spec(early.shape), const_spec(early.shape),
            const_spec(late.shape), const_spec(late.shape), const_spec(small.shape),
        ],
        out_specs=pl.BlockSpec((block, LANES), lambda i: (jnp.maximum(i - 1, 0), 0)),
        out_shape=jax.ShapeDtypeStruct((rows, LANES), F32),
        scratch_shapes=[pltpu.VMEM((STAGE_ROWS, LANES), F32)],
        compiler_params=pltpu.CompilerParams(
            dimension_semantics=("arbitrary",), vmem_limit_bytes=48 * 2**20),
        cost_estimate=pl.CostEstimate(
            flops=10**6, bytes_accessed=12 * 2**20, transcendentals=0),
    )(who, early, early_other, late, late_other, small)


def swap(values, axis, bit):
    size = lax.axis_size(axis)
    return lax.ppermute(values, axis, [(i, i ^ bit) for i in range(size)])


def to_wire(values, power):
    return (values * jnp.exp2(power)).astype(jnp.float16)


def from_wire(values, power):
    return values.astype(F32) * jnp.exp2(-power)


def scatter(values, power, axis, bit=1, count=2, after=None, sent=None):
    place = (lax.axis_index(axis) // bit) % count
    rows = values.shape[-2] // count
    mark = min(MARK, rows)
    dim = values.ndim - 2
    total = lax.dynamic_slice_in_dim(values, place * rows, rows, dim)
    least = power
    arrived = []
    for offset in range(1, count):
        to = place ^ offset
        last = to == count - 1
        start = to * rows - jnp.where(last, mark, 0)
        send = lax.dynamic_slice_in_dim(values, start, rows + mark, dim)
        line = lax.broadcasted_iota(jnp.int32, send.shape, dim)
        marked = jnp.where(last, line < mark, line >= rows)
        wire = jnp.where(marked, power, send * jnp.exp2(power)).astype(jnp.float16)
        arrived.append(swap(wire, axis, bit * offset))
        if sent is not None:
            sent.append(wire)
    if after is not None:
        arrived, _ = lax.optimization_barrier((arrived, after))
    last = place == count - 1
    for got in arrived:
        got_power = lax.dynamic_slice_in_dim(
            got, jnp.where(last, 0, rows), 1, dim).reshape(1, D).astype(F32)
        body = lax.dynamic_slice_in_dim(got, jnp.where(last, mark, 0), rows, dim)
        total = total + from_wire(body, got_power)
        least = jnp.minimum(least, got_power)
    return total, least - float(count.bit_length() - 1)


def scatter_product(left, right, power, axis, bit):
    def product(part):
        return lax.dot_general(
            part, right, (((1,), (1,)), ((0,), (0,))), preferred_element_type=F32)

    side = (lax.axis_index(axis) // bit) % 2
    rows = left.shape[2] // 2
    send = product(jnp.where(side == 1, left[:, :, : rows + LANES], left[:, :, rows - LANES :]))
    line = lax.broadcasted_iota(jnp.int32, send.shape, 1)
    marked = jnp.where(side == 1, line >= rows, line < LANES)
    wire = jnp.where(marked, power, send * jnp.exp2(power)).astype(jnp.float16)
    got = swap(wire, axis, bit)
    left, _ = lax.optimization_barrier((left, wire))
    keep = product(jnp.where(side == 0, left[:, :, :rows], left[:, :, rows:]))
    keep, got = lax.optimization_barrier((keep, got))
    got_power = lax.dynamic_slice(
        got, (0, (1 - side) * rows, 0), (1, 1, D))[0].astype(F32)
    body = lax.dynamic_slice_in_dim(got, side * LANES, rows, 1)
    return keep + from_wire(body, got_power), jnp.minimum(power, got_power) - 1.0


def everyones(values, axis, bit=1, count=2):
    place = (lax.axis_index(axis) // bit) % count
    pieces = [values] + [swap(values, axis, bit * offset) for offset in range(1, count)]
    step = 1
    while step < count:
        flip = (place // step) % 2 == 1
        pieces = [
            jnp.where(flip, pieces[i ^ step], pieces[i]) for i in range(count)]
        step *= 2
    return pieces


def gather(values, axis, bit=1, count=2):
    return jnp.concatenate(everyones(values, axis, bit, count))


def add_pair(values, axis, bit, after=None):
    got = swap(values, axis, bit)
    if after is not None:
        got, _ = lax.optimization_barrier((got, after))
    return values + got


def data_groups():
    size = lax.axis_size("dp")
    groups = [(1, 2)]
    bit = 2
    while bit < size:
        count = 4 if bit * 4 <= size else 2
        groups.append((bit, count))
        bit *= count
    return groups


def dot_tn(a, b):
    return lax.dot_general(a, b, (((0,), (0,)), ((), ())), preferred_element_type=F32)


def pick_rows(index, rows):
    chosen = index[:, None] == jnp.arange(rows.shape[0], dtype=jnp.int32)[None, :]
    return dot(chosen.astype(BF16), rows).astype(BF16)


def on_device(
    tokens, loss_sensitivity, lengths, holder_sequence_list, master, moment_one, moment_two,
    adam_rates, iteration_tally,
):
    group_devices = lax.axis_size("zero")
    data_devices = lax.axis_size("dp")
    zero_index = lax.axis_index("zero")
    dp_index = lax.axis_index("dp")
    seq_len = loss_sensitivity.shape[1]
    group_seqs = tokens.shape[0]
    span = tokens.shape[1]
    slots = group_seqs // data_devices
    shard_rows = master.shape[0] // LANES
    tie = lax.optimization_barrier

    own = master.reshape(shard_rows, LANES)
    arranged = holder_sequence_list.reshape(data_devices, group_devices, slots)
    group_order = lax.dynamic_index_in_dim(arranged, zero_index, 1, keepdims=False).reshape(-1)
    local_ids = group_order - zero_index * group_seqs
    dealt = tokens.at[local_ids].get(mode="promise_in_bounds")
    flat = lax.all_gather(own.astype(BF16), "zero", axis=0, tiled=True)

    local_tok = lax.all_to_all(dealt, "dp", split_axis=0, concat_axis=0, tiled=True)
    my_seqs = lax.dynamic_slice_in_dim(group_order, dp_index * slots, slots)
    bound = lengths[my_seqs[0]]
    positions = jnp.arange(seq_len, dtype=jnp.int32)

    in_w, out_w, norm_gain, *params, e2, et = run_prepare(flat)
    cot = loss_sensitivity[0]
    gm = dot_nt(cot, out_w)
    cot_top = jnp.max(jnp.abs(cot)).astype(F32).reshape(1)
    local_tok, in_w, gm, cot_top = tie((local_tok, in_w, gm, cot_top))
    own_late, _ = tie((own, flat[:8]))
    whole_master = lax.all_gather(own_late, "zero", axis=0, tiled=True)

    def place(slot, at):
        return (at // span) * (slots * span) + slot * span + at % span

    source = jnp.where(positions < bound, place(0, positions), place(1, positions - bound))
    packed = pick_rows(source, local_tok.reshape(slots * seq_len, D))
    blocks = jnp.arange(data_devices, dtype=jnp.int32)[:, None, None] * span
    within = blocks + jnp.arange(span, dtype=jnp.int32)[None, None, :]
    within = within + jnp.arange(slots, dtype=jnp.int32)[None, :, None] * bound
    unpack_rows = jnp.minimum(within, seq_len - 1).reshape(-1)
    ends = jnp.stack([bound, jnp.int32(seq_len)])[None, :, None]
    live_rows = jnp.where(within < ends, within, -1).reshape(-1)

    def spread(rows, index):
        return pick_rows(index, rows).reshape(data_devices * slots, span, D)

    def send_back(picked):
        return lax.all_to_all(picked, "dp", split_axis=0, concat_axis=0, tiled=True)

    restore = jnp.zeros_like(local_ids).at[local_ids].set(
        jnp.arange(group_seqs, dtype=jnp.int32))
    mine = lax.dynamic_slice_in_dim(lengths, zero_index * group_seqs, group_seqs)
    at = dp_index * span + jnp.arange(span, dtype=jnp.int32)
    live = (at[None, :] < mine[:, None])[:, :, None]

    bound_arr = bound.reshape(1)
    tok = packed.astype(F32)
    nhat = tok * lax.rsqrt(jnp.mean(tok * tok, axis=1, keepdims=True) + EPS_NORM)
    normed = (nhat * norm_gain).astype(BF16)
    proj_z = dot_nt(normed, in_w[:INNER])
    proj = dot_nt(normed, in_w[INNER:PROJ])
    pair, dy, through, states, ggain, early_power = run_forward(
        proj_z, proj, gm, bound_arr, cot_top, norm_gain, e2, et, params)
    result = (tok + dot(pair[1], out_w)).astype(BF16)
    picked = spread(result, unpack_rows)
    picked, pair = tie((picked, pair))
    back_out = send_back(picked)
    early_power = early_power[0:1, 0:1]
    early, early_power = scatter_product(
        pair, jnp.stack([normed, cot]), early_power, "zero", 1)
    early, early_power, dy = tie((early.reshape(INNER, D), early_power, dy))
    early, early_power = scatter(early, early_power, "zero", 2)
    window, grad_tok, small, late_power = run_backward(
        proj, dy, through, states, pair, packed, cot, in_w, norm_gain, ggain,
        bound_arr, e2, et, params)
    window, small, late_power, early, early_power, whole_master = tie(
        (window, small, late_power, early, early_power, whole_master))

    groups = data_groups()
    late_power = late_power[0:1, 0:1]
    late, late_power = scatter_product(
        window, jnp.stack([normed, normed]), late_power, "zero", 1)
    late = late.reshape(WINDOW, D)
    small = add_pair(small, "zero", 1)
    early, early_power, grad_tok, _ = tie((early, early_power, grad_tok, late))
    late, late_power = scatter(late, late_power, "zero", 2)
    early, early_power = scatter(early, early_power, "dp", *groups[0])
    small = add_pair(small, "zero", 2, late)
    early_before, power_before = early, early_power
    picked_grad = spread(grad_tok, live_rows)
    tokens, back_out, _ = tie((tokens, back_out, grad_tok))
    back_rows = back_out.at[restore].get(mode="promise_in_bounds")
    tokens_out = jnp.where(live, back_rows, tokens)
    new_master = jnp.zeros((group_devices, shard_rows, LANES), F32)
    late, tokens_out, new_master, picked_grad = tie((late, tokens_out, new_master, picked_grad))
    lines = small.shape[0]
    late = jnp.concatenate([late, small, jnp.zeros((WINDOW // 8 - lines, D), F32)])
    late, late_power = scatter(late, late_power, "dp", *groups[0])
    sent = []
    for group in groups[1:]:
        late, late_power = scatter(late, late_power, "dp", *group, sent=sent)
    early, early_power = early_before, power_before
    for group in groups[1:]:
        early, early_power = scatter(early, early_power, "dp", *group, after=sent)
    early = to_wire(early, early_power)
    for group in reversed(groups[1:]):
        early = gather(early, "dp", *group)
    early, _ = tie((early, late))
    late = to_wire(late, late_power)
    early = from_wire(gather(early, "dp", *groups[0]), early_power)
    early, picked_grad, _ = tie((early, picked_grad, late))
    for group in reversed(groups[1:]):
        late = gather(late, "dp", *group)
    early_other = swap(early, "zero", 1)
    back_grad = send_back(picked_grad)
    wire = gather(late, "dp", *groups[0])
    late = from_wire(wire[: WINDOW // 2], late_power)
    small = from_wire(wire[WINDOW // 2 : WINDOW // 2 + lines], late_power)
    late_other = swap(late, "zero", 1)

    steps_f = iteration_tally[0].astype(F32)
    who = jnp.stack([zero_index // 2, zero_index % 2]).astype(jnp.int32)
    first = moment_one.reshape(shard_rows, LANES)
    second = moment_two.reshape(shard_rows, LANES)
    grad_shard = run_stage(who, shard_rows, early, early_other, late, late_other, small)
    first_scale = 1.0 / (1.0 - jnp.power(BETA_ONE, steps_f))
    second_scale = 1.0 / (1.0 - jnp.power(BETA_TWO, steps_f))

    def moments(grad, first, second):
        return (
            BETA_ONE * first + (1.0 - BETA_ONE) * grad,
            BETA_TWO * second + (1.0 - BETA_TWO) * grad * grad)

    def quotient(rows):
        first_next, second_next = moments(grad_shard[rows], first[rows], second[rows])
        return ((first_next * first_scale) / (
            jnp.sqrt(second_next * second_scale) + EPS_ADAM)).astype(jnp.float16)

    whole_master = whole_master.reshape(group_devices, shard_rows, LANES)

    def put(new_master, piece, offset):
        shard = zero_index ^ offset
        old = lax.dynamic_index_in_dim(whole_master, shard, 0, keepdims=False)
        new = old - adam_rates[0] * (piece.astype(F32) + adam_rates[1] * old)
        return lax.dynamic_update_index_in_dim(new_master, new, shard, 0)

    own_part, first, second = tie((quotient(slice(0, shard_rows)), first, second))
    across = swap(own_part, "zero", 2)
    core = swap(own_part, "zero", 1)
    first_next, second_next = moments(grad_shard, first, second)
    new_master = put(put(new_master, own_part, 0), core, 1)
    across, new_master, first_next, second_next = tie(
        (across, new_master, first_next, second_next))
    last = swap(across, "zero", 1)
    new_master = put(new_master, across, 2)
    last, new_master = tie((last, new_master))
    new_master = put(new_master, last, 3)
    back_grad, new_master = tie((back_grad, new_master))
    grad_tokens = back_grad.at[restore].get(mode="promise_in_bounds")
    return (
        tokens_out, grad_tokens, new_master.reshape(-1), grad_shard.reshape(-1),
        first_next.reshape(-1), second_next.reshape(-1))


def solution(mesh):
    return jax.shard_map(
        on_device,
        mesh=mesh,
        in_specs=(
            P("zero", "dp", None), P(("dp", "zero"), None, None), P(), P(),
            P("zero"), P("zero"), P("zero"), P(), P(),
        ),
        out_specs=(
            P("zero", "dp", None), P("zero", "dp", None), P(), P("zero"), P("zero"), P("zero"),
        ),
        check_vma=False,
    )
```

```python
import jax
import jax.numpy as jnp
from jax import lax
from jax.experimental import pallas as pl
from jax.experimental.pallas import tpu as pltpu
from jax.sharding import PartitionSpec as P

D = 768
HEADS = 24
HEADDIM = 64
STATE = 128
CONV = 4
INNER = 1536
XBC = 1792
PROJ = 3352
Q = 128
LATE = PROJ - INNER
WINDOW = 1024
PAIRS = HEADS // 2
EPS_NORM = 1e-05
NEG = -1e30
F16_TOP = 30000.0
LOG2E = 1.4426950408889634
F32 = jnp.float32
BF16 = jnp.bfloat16


def dot(a, b):
    return lax.dot_general(a, b, (((1,), (0,)), ((), ())), preferred_element_type=F32)


def dot_nt(a, b):
    return lax.dot_general(a, b, (((1,), (1,)), ((), ())), preferred_element_type=F32)


def split2(v):
    hi = v.astype(BF16)
    return hi, (v - hi.astype(F32)).astype(BF16)


def split3(v):
    hi = v.astype(BF16)
    rest = v - hi.astype(F32)
    mid = rest.astype(BF16)
    return hi, mid, (rest - mid.astype(F32)).astype(BF16)


def wide_left(v):
    hi, lo = split2(v)
    return jnp.concatenate([hi, lo, hi], axis=1)


def tall_right(v):
    hi, lo = split2(v)
    return jnp.concatenate([hi, hi, lo], axis=0)


def split_pair(v, masks):
    hi, lo = split2(v)
    return jnp.concatenate([
        jnp.concatenate([hi * masks[0], lo * masks[0]], axis=1),
        jnp.concatenate([hi * masks[1], lo * masks[1]], axis=1)], axis=0)


def sigmoid(v):
    return lax.logistic(v)


def softplus(v):
    return jnp.maximum(v, 0.0) + jnp.log1p(jnp.exp(-jnp.abs(v)))


def iota(shape, dim):
    return lax.broadcasted_iota(jnp.int32, shape, dim)


def expand(v, e_ref):
    hi, lo = split2(v)
    return dot(jnp.concatenate([hi, lo], axis=1), e_ref[...])


def head_sum(v, et_ref):
    hi, lo = split2(v)
    return dot(hi, et_ref[...]) + dot(lo, et_ref[...])


def quarters(out):
    return out[:Q, :Q] + (out[:Q, Q:] + out[Q:, :Q])


def power_for(bound):
    scale = jnp.log(0.9 * F16_TOP / jnp.maximum(bound, 1e-30)) * LOG2E
    return jnp.clip(jnp.floor(scale), -126.0, 120.0)


def chunk_masks(t0, bound):
    rows = t0 + iota((Q, 1), 0)
    rr = t0 + iota((Q, Q), 0)
    cc = t0 + iota((Q, Q), 1)
    return rows, rr, cc


def conv_rows(ext_ref, w_ref, b_ref, rows, bound):
    total = b_ref[...] + w_ref[3:4, :] * ext_ref[8 : 8 + Q, :]
    for back in (1, 2, 3):
        ok = jnp.logical_or(rows - back >= bound, rows < bound).astype(F32)
        total = total + w_ref[3 - back : 4 - back, :] * (ext_ref[8 - back : 8 - back + Q, :] * ok)
    return total


def decay_parts(dt_raw, dtb_ref, alog_ref, rr, cc):
    dt_in = dt_raw + dtb_ref[...]
    dt_pos = softplus(dt_in)
    rate = -jnp.exp(alog_ref[...])
    step = dt_pos * rate
    tri = (cc <= rr).astype(F32).astype(BF16)
    s_hi, s_mid, s_lo = split3(step)
    cum = dot(tri, s_hi) + dot(tri, s_mid) + dot(tri, s_lo)
    return dt_in, dt_pos, rate, cum


def forward_kernel(
    bound_ref, cot_ref, z_ref, proj_ref, gm_ref, norm_ref, e_ref, et_ref, convw_ref, convb_ref, dtb_ref, alog_ref,
    skip_ref, gain_ref,
    pair_ref, dy_ref, through_ref, state_ref, ggain_ref, power_ref,
    zmax_ref, ext_ref, dt_ref, carry_ref, xd_ref, acc_ref, cumt_ref,
):
    step = pl.program_id(0)
    bound = bound_ref[0]
    t0 = step * Q

    @pl.when(step == 0)
    def _():
        ext_ref[0:8, :] = jnp.zeros((8, XBC), F32)
        carry_ref[...] = jnp.zeros_like(carry_ref)
        dt_ref[...] = jnp.zeros_like(dt_ref)
        ggain_ref[...] = jnp.zeros_like(ggain_ref)
        zmax_ref[...] = jnp.zeros_like(zmax_ref)

    rows, rr, cc = chunk_masks(t0, bound)
    ext_ref[8 : 8 + Q, :] = proj_ref[:, :XBC]
    pre = conv_rows(ext_ref, convw_ref, convb_ref, rows, bound)
    ext_ref[0:8, :] = ext_ref[Q : Q + 8, :]
    conv_out = pre * sigmoid(pre)
    x = conv_out[:, :INNER]
    b_rows = conv_out[:, INNER : INNER + STATE]
    c_rows = conv_out[:, INNER + STATE :]
    dt_ref[:, 0:HEADS] = proj_ref[:, XBC:LATE]
    _, dt_pos, _, cum = decay_parts(dt_ref[...], dtb_ref, alog_ref, rr, cc)
    cum_end = cum[Q - 1 : Q, :]
    keep = jnp.logical_or(rows < bound, bound < t0).astype(F32)
    in_last = jnp.logical_or(rows >= bound, bound > t0 + Q - 1).astype(F32)
    whole = jnp.logical_or(bound < t0, bound > t0 + Q - 1).astype(F32)
    from_start = jnp.exp(cum) * keep
    to_end = jnp.exp(cum_end - cum) * in_last
    carry_scale = jnp.exp(cum_end) * whole
    allowed = jnp.logical_and(cc <= rr, (cc >= bound) == (rr >= bound))
    cum2 = cum * LOG2E
    cumt_ref[...] = cum2.T

    state = carry_ref[...]
    state_ref[0] = state
    spread = expand(jnp.concatenate(
        [dt_pos, to_end, from_start, jnp.broadcast_to(carry_scale, (16, 128))], axis=0), e_ref)
    xd = x * spread[:Q]
    xd_ref[...] = xd
    acc = dot(wide_left(c_rows), tall_right(state)) * spread[2 * Q : 3 * Q]
    acc_ref[...] = acc + skip_ref[...] * x
    b_t = b_rows.T
    carry_ref[...] = state * spread[3 * Q : 3 * Q + 1] + dot(
        wide_left(b_t), tall_right(xd * spread[Q : 2 * Q]))
    gram = dot(wide_left(c_rows), tall_right(b_t))
    first = iota((Q, Q), 1) < HEADDIM
    first_b = (first.astype(F32).astype(BF16), 1.0 - first.astype(F32).astype(BF16))
    for pair in range(PAIRS):
        parts = []
        for head in (2 * pair, 2 * pair + 1):
            differ = cum2[:, head : head + 1] - cumt_ref[head : head + 1, :]
            parts.append(gram * jnp.exp2(jnp.where(allowed, differ, NEG)))
        left = jnp.concatenate(split2(jnp.concatenate(parts, axis=1)), axis=0)
        lanes = slice(pair * 128, pair * 128 + 128)
        xp = xd_ref[:, lanes]
        out = dot(left, split_pair(xp, first_b))
        acc_ref[:, lanes] += out[:Q, :128] + (out[:Q, 128:] + out[Q:, :128])
    scanned = acc_ref[...]
    z = z_ref[...]
    sig_z = sigmoid(z)
    silu_z = z * sig_z
    gated = scanned * silu_z
    ginv = lax.rsqrt(jnp.mean(gated * gated, axis=1, keepdims=True) + EPS_NORM)
    mhat = gated * ginv
    pair_ref[1] = (mhat * gain_ref[...]).astype(BF16)
    gm = gm_ref[...]
    ggain_ref[...] += jnp.sum(mhat * gm, axis=0, keepdims=True)
    gmg = gm * gain_ref[...]
    ggated = ginv * (gmg - mhat * jnp.mean(mhat * gmg, axis=1, keepdims=True))
    dy = ggated * silu_z
    dy_ref[...] = dy
    grad_z = ggated * scanned * (sig_z * (1.0 + z * (1.0 - sig_z)))
    zmax_ref[...] = jnp.maximum(zmax_ref[...], jnp.max(jnp.abs(grad_z), axis=0, keepdims=True))
    pair_ref[0] = grad_z.astype(BF16)
    through_ref[...] = head_sum(dy * (scanned - skip_ref[...] * x), et_ref)

    @pl.when(step == pl.num_programs(0) - 1)
    def _():
        count = float(Q * pl.num_programs(0))
        largest = jnp.max(zmax_ref[...], axis=1, keepdims=True)
        normed = jnp.max(jnp.abs(norm_ref[...]), axis=1, keepdims=True) * (D ** 0.5)
        mixed = jnp.max(jnp.abs(gain_ref[...]), axis=1, keepdims=True) * (INNER ** 0.5)
        power_ref[...] = jnp.broadcast_to(power_for(
            1.05 * count * jnp.maximum(largest * normed, cot_ref[0] * mixed)), (8, 128))


def const_spec(shape):
    return pl.BlockSpec(shape, lambda *_: (0,) * len(shape))


def run_forward(z, proj, gm, bound, cot_top, norm_gain, e2, et, params):
    n = proj.shape[0]
    steps = n // Q
    return pl.pallas_call(
        forward_kernel,
        grid=(steps,),
        in_specs=[
            pl.BlockSpec(memory_space=pltpu.SMEM), pl.BlockSpec(memory_space=pltpu.SMEM),
            pl.BlockSpec((Q, INNER), lambda i: (i, 0)),
            pl.BlockSpec((Q, LATE), lambda i: (i, 0)),
            pl.BlockSpec((Q, INNER), lambda i: (i, 0)),
            const_spec((1, D)),
            const_spec((256, INNER)), const_spec((INNER, 128)),
            const_spec((8, XBC)), const_spec((1, XBC)), const_spec((1, 128)),
            const_spec((1, 128)), const_spec((1, INNER)), const_spec((1, INNER)),
        ],
        out_specs=[
            pl.BlockSpec((2, Q, INNER), lambda i: (0, i, 0)),
            pl.BlockSpec((Q, INNER), lambda i: (i, 0)),
            pl.BlockSpec((Q, 128), lambda i: (i, 0)),
            pl.BlockSpec((1, STATE, INNER), lambda i: (i, 0, 0)),
            const_spec((1, INNER)), const_spec((8, 128)),
        ],
        out_shape=[
            jax.ShapeDtypeStruct((2, n, INNER), BF16),
            jax.ShapeDtypeStruct((n, INNER), F32),
            jax.ShapeDtypeStruct((n, 128), F32),
            jax.ShapeDtypeStruct((steps, STATE, INNER), F32),
            jax.ShapeDtypeStruct((1, INNER), F32),
            jax.ShapeDtypeStruct((8, 128), F32),
        ],
        scratch_shapes=[
            pltpu.VMEM((1, INNER), F32),
            pltpu.VMEM((Q + 8, XBC), F32),
            pltpu.VMEM((Q, 128), F32),
            pltpu.VMEM((STATE, INNER), F32),
            pltpu.VMEM((Q, INNER), F32),
            pltpu.VMEM((Q, INNER), F32),
            pltpu.VMEM((128, Q), F32),
        ],
        compiler_params=pltpu.CompilerParams(
            dimension_semantics=("arbitrary",), vmem_limit_bytes=48 * 2**20),
        cost_estimate=pl.CostEstimate(
            flops=30 * 10**9, bytes_accessed=40 * 2**20, transcendentals=10**7),
    )(bound, cot_top, z, proj, gm, norm_gain, e2, et, *params)


def backward_kernel(
    bound_ref, proj_ref, before_ref, dy_ref, through_ref, state_ref, gz_ref, tok_ref, cot_ref,
    in_ref, norm_ref, ggain_ref,
    e_ref, et_ref, convw_ref, convb_ref, dtb_ref, alog_ref, skip_ref,
    window_ref, gtok_ref, small_ref, power_ref,
    total_ref, gskip_ref, gsmall_ref, dtw_ref, gp_ref, ext_ref, dt_ref, lam_ref, dsum_ref, xd_ref, g_ref, gnext_ref, cumt_ref,
):
    step = pl.program_id(0)
    steps = pl.num_programs(0)
    bound = bound_ref[0]
    t0 = (steps - 1 - step) * Q

    @pl.when(step == 0)
    def _():
        lam_ref[...] = jnp.zeros_like(lam_ref)
        dsum_ref[...] = jnp.zeros_like(dsum_ref)
        dt_ref[...] = jnp.zeros_like(dt_ref)
        gnext_ref[Q : Q + 8, :] = jnp.zeros((8, XBC), F32)
        gskip_ref[...] = jnp.zeros_like(gskip_ref)
        total_ref[...] = jnp.zeros_like(total_ref)
        dtw_ref[...] = jnp.zeros_like(dtw_ref)
        gsmall_ref[...] = jnp.zeros_like(gsmall_ref)

    rows, rr, cc = chunk_masks(t0, bound)
    dy = dy_ref[...]
    first_chunk = (t0 > 0).astype(F32)
    ext_ref[0:8, :] = before_ref[:, :XBC] * first_chunk
    ext_ref[8 : 8 + Q, :] = proj_ref[:, :XBC]
    pre = conv_rows(ext_ref, convw_ref, convb_ref, rows, bound)
    sig_pre = sigmoid(pre)
    conv_out = pre * sig_pre
    x = conv_out[:, :INNER]
    b_rows = conv_out[:, INNER : INNER + STATE]
    c_rows = conv_out[:, INNER + STATE :]
    dt_ref[:, 0:HEADS] = proj_ref[:, XBC:LATE]
    dt_in, dt_pos, rate, cum = decay_parts(dt_ref[...], dtb_ref, alog_ref, rr, cc)
    cum_end = cum[Q - 1 : Q, :]
    keep = jnp.logical_or(rows < bound, bound < t0).astype(F32)
    in_last = jnp.logical_or(rows >= bound, bound > t0 + Q - 1).astype(F32)
    whole = jnp.logical_or(bound < t0, bound > t0 + Q - 1).astype(F32)
    from_start = jnp.exp(cum) * keep
    to_end = jnp.exp(cum_end - cum) * in_last
    carry_scale = jnp.exp(cum_end) * whole
    allowed_t = jnp.logical_and(rr <= cc, (cc >= bound) == (rr >= bound))
    cum2 = cum * LOG2E
    cumt_ref[...] = cum2.T
    c_t = c_rows.T
    gram_t = dot(wide_left(b_rows), tall_right(c_t))
    spread = expand(jnp.concatenate(
        [dt_pos, to_end, from_start, jnp.broadcast_to(carry_scale, (16, 128))], axis=0), e_ref)
    dt_all = spread[:Q]
    end_all = spread[Q : 2 * Q]
    xd = x * dt_all
    xd_ref[...] = xd
    skip = skip_ref[...]
    gskip_ref[...] += jnp.sum(dy * x, axis=0, keepdims=True)
    lam = lam_ref[...]
    lam_hi, lam_lo = split2(lam)
    g_ref[...] = (
        dot(wide_left(b_rows), jnp.concatenate([lam_hi, lam_hi, lam_lo], axis=0)) * end_all
    )
    grad_b = quarters(dot_nt(
        jnp.concatenate(split2(xd * end_all), axis=0), jnp.concatenate([lam_hi, lam_lo], axis=0)))
    state = state_ref[0]
    dye_hi, dye_lo = split2(dy * spread[2 * Q : 3 * Q])
    grad_c = quarters(dot_nt(
        jnp.concatenate([dye_hi, dye_lo], axis=0), jnp.concatenate(split2(state), axis=0)))
    lam_new = lam * spread[3 * Q : 3 * Q + 1] + dot(
        wide_left(c_t), jnp.concatenate([dye_hi, dye_hi, dye_lo], axis=0)
    )
    lam_ref[...] = lam_new
    ended = dsum_ref[0:1, :]
    first = iota((Q, Q), 1) < HEADDIM
    first_b = (first.astype(F32).astype(BF16), 1.0 - first.astype(F32).astype(BF16))
    first_row = (iota((Q, Q), 0) < HEADDIM).astype(F32).astype(BF16)
    first_row = (first_row, 1.0 - first_row)
    gram_grad = jnp.zeros((Q, Q), F32)
    for pair in range(PAIRS):
        lanes = slice(pair * 128, pair * 128 + 128)
        weights = []
        for head in (2 * pair, 2 * pair + 1):
            differ = cumt_ref[head : head + 1, :] - cum2[:, head : head + 1]
            weights.append(jnp.exp2(jnp.where(allowed_t, differ, NEG)))
        left = jnp.concatenate([gram_t * weights[0], gram_t * weights[1]], axis=1)
        left = jnp.concatenate(split2(left), axis=0)
        dyp = dy_ref[:, lanes]
        out = dot(left, split_pair(dyp, first_b))
        g_ref[:, lanes] += out[:Q, :128] + (out[:Q, 128:] + out[Q:, :128])
        dyt_hi, dyt_lo = split2(dyp.T)
        right_hi = jnp.concatenate([dyt_hi * first_row[0], dyt_hi * first_row[1]], axis=1)
        right_lo = jnp.concatenate([dyt_lo * first_row[0], dyt_lo * first_row[1]], axis=1)
        outer = dot(
            wide_left(xd_ref[:, lanes]), jnp.concatenate([right_hi, right_hi, right_lo], axis=0))
        gram_grad = gram_grad + (outer[:, :128] * weights[0] + outer[:, 128:] * weights[1])
    g = g_ref[...]
    grad_x = dt_all * g + skip * dy
    sums = dot(jnp.concatenate(
        split2(x * g) + split2(jnp.broadcast_to(
            jnp.sum(lam_new * state, axis=0, keepdims=True), (16, INNER))), axis=0), et_ref[...])
    direct = sums[:Q] + sums[Q : 2 * Q]
    balance = through_ref[...] - dt_pos * direct
    keep_t = allowed_t.astype(F32).astype(BF16)
    b_hi, b_mid, b_lo = split3(balance)
    grad_step = dot(keep_t, b_hi) + dot(keep_t, b_mid) + dot(keep_t, b_lo) + in_last * ended
    dsum_ref[...] = sums[2 * Q : 2 * Q + 8] + sums[2 * Q + 16 : 2 * Q + 24]
    grad_dt = (direct + rate * grad_step) * sigmoid(dt_in)
    gsmall_ref[0:1, :] += jnp.sum(grad_dt, axis=0, keepdims=True)
    gsmall_ref[1:2, :] += rate * jnp.sum(dt_pos * grad_step, axis=0, keepdims=True)
    grad_c = grad_c + dot(wide_left(gram_grad.T), tall_right(b_rows))
    grad_b = grad_b + dot(wide_left(gram_grad), tall_right(c_rows))
    slope = sig_pre * (1.0 + pre * (1.0 - sig_pre))
    gnext_ref[0:Q, :INNER] = grad_x * slope[:, :INNER]
    gnext_ref[0:Q, INNER : INNER + STATE] = grad_b * slope[:, INNER : INNER + STATE]
    gnext_ref[0:Q, INNER + STATE :] = grad_c * slope[:, INNER + STATE :]
    gcp = gnext_ref[0:Q, :]
    total_ref[4:5, :] += jnp.sum(gcp, axis=0, keepdims=True)
    total_ref[3:4, :] += jnp.sum(gcp * ext_ref[8 : 8 + Q, :], axis=0, keepdims=True)
    total = convw_ref[3:4, :] * gcp
    for back in (1, 2, 3):
        ok = jnp.logical_or(rows - back >= bound, rows < bound).astype(F32)
        total_ref[3 - back : 4 - back, :] += jnp.sum(
            gcp * (ext_ref[8 - back : 8 - back + Q, :] * ok), axis=0, keepdims=True)
        okn = jnp.logical_or(rows >= bound, rows + back < bound).astype(F32)
        total = total + convw_ref[3 - back : 4 - back, :] * (gnext_ref[back : back + Q, :] * okn)
    total_ref[7:8, :] = jnp.maximum(
        total_ref[7:8, :], jnp.max(jnp.abs(total), axis=0, keepdims=True))
    total = total.astype(BF16)
    window_ref[0] = total[:, :WINDOW]
    window_ref[1] = total[:, XBC - WINDOW :]
    gnext_ref[Q : Q + 8, :] = gnext_ref[0:8, :]
    half = (steps - 1 - step) % 2
    at = pl.multiple_of(half * Q, Q)
    gp_ref[pl.ds(at, Q), :INNER] = gz_ref[0]
    gp_ref[pl.ds(at, Q), INNER : INNER + XBC] = total
    gp_ref[pl.ds(at, Q), INNER + XBC :] = grad_dt.astype(BF16)

    @pl.when(half == 0)
    def _():
        grad_normed = dot(gp_ref[...], in_ref[: INNER + XBC + 128, :])
        tok = tok_ref[...].astype(F32)
        rinv = lax.rsqrt(jnp.mean(tok * tok, axis=1, keepdims=True) + EPS_NORM)
        nhat = tok * rinv
        gain = norm_ref[...]
        gng = grad_normed * gain
        gtok_ref[...] = (cot_ref[...].astype(F32) + rinv * (
            gng - nhat * jnp.mean(nhat * gng, axis=1, keepdims=True))).astype(BF16)
        total_ref[6:7, :D] += jnp.sum(nhat * grad_normed, axis=0, keepdims=True)
        normed = (nhat * gain).astype(BF16)
        gdt = gp_ref[:, INNER + XBC :].astype(F32)
        dtw_ref[...] += dot(jnp.concatenate(
            [gdt[:Q].T, gdt[Q:].T], axis=1).astype(BF16), normed)

    @pl.when(step == steps - 1)
    def _():
        skips = head_sum(jnp.broadcast_to(gskip_ref[...], (8, INNER)), et_ref)
        small_ref[...] = jnp.zeros_like(small_ref)
        small_ref[0:HEADS, :] = dtw_ref[0:HEADS, :]
        pieces = [
            total_ref[k : k + 1, j * 128 : j * 128 + 128]
            for k in range(CONV + 1) for j in range(XBC // 128)]
        pieces += [gsmall_ref[0:1, :], gsmall_ref[1:2, :], skips[0:1, :]]
        pieces += [ggain_ref[:, j * 128 : j * 128 + 128] for j in range(INNER // 128)]
        lines = D // 128
        for number, piece in enumerate(pieces):
            line = HEADS + number // lines
            at = number % lines * 128
            small_ref[line : line + 1, at : at + 128] = piece
        small_ref[40:41, :] = total_ref[6:7, :D]
        count = float(Q * steps)
        largest = jnp.max(total_ref[7:8, :], axis=1, keepdims=True)
        normed = jnp.max(jnp.abs(norm_ref[...]), axis=1, keepdims=True) * (D ** 0.5)
        others = jnp.max(jnp.max(jnp.abs(small_ref[...]), axis=1, keepdims=True), axis=0, keepdims=True)
        power_ref[...] = jnp.broadcast_to(power_for(
            jnp.maximum(1.05 * count * largest * normed, others)), (8, 128))


def run_backward(
    proj, dy, through, states, pair, tok, cot, in_w, norm_gain, ggain, bound, e2, et, params
):
    n = proj.shape[0]
    steps = n // Q

    def rev(i):
        return (steps - 1 - i, 0)

    def rev_two(i):
        return ((steps - 1 - i) // 2, 0)

    return pl.pallas_call(
        backward_kernel,
        grid=(steps,),
        in_specs=[
            pl.BlockSpec(memory_space=pltpu.SMEM),
            pl.BlockSpec((Q, LATE), rev),
            pl.BlockSpec((8, LATE), lambda i: (jnp.maximum((steps - 1 - i) * (Q // 8) - 1, 0), 0)),
            pl.BlockSpec((Q, INNER), rev),
            pl.BlockSpec((Q, 128), rev),
            pl.BlockSpec((1, STATE, INNER), lambda i: (steps - 1 - i, 0, 0)),
            pl.BlockSpec((1, Q, INNER), lambda i: (0, steps - 1 - i, 0)),
            pl.BlockSpec((2 * Q, D), rev_two), pl.BlockSpec((2 * Q, D), rev_two),
            const_spec(in_w.shape), const_spec((1, D)), const_spec((1, INNER)),
            const_spec((256, INNER)), const_spec((INNER, 128)),
            const_spec((8, XBC)), const_spec((1, XBC)), const_spec((1, 128)),
            const_spec((1, 128)), const_spec((1, INNER)),
        ],
        out_specs=[
            pl.BlockSpec((2, Q, WINDOW), lambda i: (0, steps - 1 - i, 0)),
            pl.BlockSpec((2 * Q, D), rev_two),
            const_spec((48, D)), const_spec((8, 128)),
        ],
        out_shape=[
            jax.ShapeDtypeStruct((2, n, WINDOW), BF16),
            jax.ShapeDtypeStruct((n, D), BF16),
            jax.ShapeDtypeStruct((48, D), F32),
            jax.ShapeDtypeStruct((8, 128), F32),
        ],
        scratch_shapes=[
            pltpu.VMEM((8, XBC), F32),
            pltpu.VMEM((1, INNER), F32),
            pltpu.VMEM((8, 128), F32),
            pltpu.VMEM((128, D), F32),
            pltpu.VMEM((2 * Q, INNER + XBC + 128), BF16),
            pltpu.VMEM((Q + 8, XBC), F32),
            pltpu.VMEM((Q, 128), F32),
            pltpu.VMEM((STATE, INNER), F32),
            pltpu.VMEM((8, 128), F32),
            pltpu.VMEM((Q, INNER), F32),
            pltpu.VMEM((Q, INNER), F32),
            pltpu.VMEM((Q + 8, XBC), F32),
            pltpu.VMEM((128, Q), F32),
        ],
        compiler_params=pltpu.CompilerParams(
            dimension_semantics=("arbitrary",), vmem_limit_bytes=40 * 2**20),
        cost_estimate=pl.CostEstimate(
            flops=50 * 10**9, bytes_accessed=50 * 2**20, transcendentals=2 * 10**7),
    )(bound, proj, proj, dy, through, states, pair, tok, cot, in_w, norm_gain, ggain,
      e2, et, *params[:5])


BETA_ONE = 0.9
BETA_TWO = 0.95
EPS_ADAM = 1e-08
LANES = 128
NORM_ROWS = D // LANES
IN_ROWS = PROJ * D // LANES
CONVW_ROWS = CONV * XBC // LANES
CONVB_ROWS = XBC // LANES
GAIN_ROWS = INNER // LANES
OUT_ROWS = INNER * D // LANES
DT_ROWS = HEADS * D // LANES
SMALL_ROWS = DT_ROWS + CONVW_ROWS + CONVB_ROWS + 3 + GAIN_ROWS
OUT_START = NORM_ROWS + IN_ROWS + SMALL_ROWS - DT_ROWS
LATE_START = NORM_ROWS + INNER * NORM_ROWS
LEAD = 896
STAGE_ROWS = 16264
STAGE_BLOCKS = 5
MARK = 16


PREP_STEPS = 7
IN_BLOCK = 512
OUT_BLOCK = 256
SMALL_START = NORM_ROWS + IN_ROWS


def prepare_kernel(
    flat_ref,
    in_ref, out_ref, norm_ref, convw_ref, convb_ref, dtb_ref, alog_ref, skip_ref, gain_ref,
    e_ref, et_ref,
    stage_ref,
):
    step = pl.program_id(0)

    @pl.when(step == 0)
    def _():
        rows = flat_ref[0:16, :].astype(F32)
        for lane in range(NORM_ROWS):
            norm_ref[:, lane * LANES : lane * LANES + LANES] = rows[lane : lane + 1, :]
        low = SMALL_START // 16 * 16
        stage_ref[0:112, :] = flat_ref[low : low + 112, :].astype(F32)
        at = SMALL_START - low
        convw_ref[...] = jnp.zeros_like(convw_ref)
        for tap in range(CONV):
            for lane in range(CONVB_ROWS):
                convw_ref[tap : tap + 1, lane * LANES : lane * LANES + LANES] = stage_ref[
                    at : at + 1, :]
                at += 1
        for lane in range(CONVB_ROWS):
            convb_ref[:, lane * LANES : lane * LANES + LANES] = stage_ref[at : at + 1, :]
            at += 1
        heads = iota((1, LANES), 1) < HEADS
        dtb_ref[...] = jnp.where(heads, stage_ref[at : at + 1, :], 0.0)
        alog_ref[...] = jnp.where(heads, stage_ref[at + 1 : at + 2, :], 0.0)
        skips = jnp.where(heads, stage_ref[at + 2 : at + 3, :], 0.0)
        at += 3
        for lane in range(GAIN_ROWS):
            gain_ref[:, lane * LANES : lane * LANES + LANES] = stage_ref[at : at + 1, :]
            at += 1
        one = (iota((128, INNER), 1) // HEADDIM == iota((128, INNER), 0)).astype(F32).astype(BF16)
        e_ref[0:128, :] = one
        e_ref[128:256, :] = one
        et_ref[...] = (
            iota((INNER, 128), 0) // HEADDIM == iota((INNER, 128), 1)).astype(F32).astype(BF16)
        skip_ref[...] = dot(jnp.broadcast_to(skips, (16, LANES)).astype(BF16), one)[0:1, :]

    def block(start, offset, rows, dest_ref):
        size = rows * NORM_ROWS + 16
        at = pl.multiple_of(start + step * (rows * NORM_ROWS), 16)
        stage_ref[0:size, :] = flat_ref[pl.ds(at, size), :].astype(F32)
        for lane in range(NORM_ROWS):
            dest_ref[:, lane * LANES : lane * LANES + LANES] = stage_ref[
                pl.ds(offset + lane, rows, stride=NORM_ROWS), :].astype(BF16)

    block(0, NORM_ROWS, IN_BLOCK, in_ref)

    @pl.when(step == PREP_STEPS - 1)
    def _():
        used = PROJ - (PREP_STEPS - 1) * IN_BLOCK
        in_ref[used:, :] = jnp.zeros((IN_BLOCK - used, D), BF16)

    @pl.when(step < INNER // OUT_BLOCK)
    def _():
        low = OUT_START // 16 * 16
        block(low, OUT_START - low, OUT_BLOCK, out_ref)


def run_prepare(flat):
    vector = lambda n: jax.ShapeDtypeStruct((1, n), F32)
    return pl.pallas_call(
        prepare_kernel,
        grid=(PREP_STEPS,),
        in_specs=[const_spec(flat.shape)],
        out_specs=[
            pl.BlockSpec((IN_BLOCK, D), lambda i: (i, 0)),
            pl.BlockSpec((OUT_BLOCK, D), lambda i: (jnp.minimum(i, INNER // OUT_BLOCK - 1), 0)),
            const_spec((1, D)), const_spec((8, XBC)), const_spec((1, XBC)), const_spec((1, 128)),
            const_spec((1, 128)), const_spec((1, INNER)), const_spec((1, INNER)),
            const_spec((256, INNER)), const_spec((INNER, 128)),
        ],
        out_shape=[
            jax.ShapeDtypeStruct((PREP_STEPS * IN_BLOCK, D), BF16),
            jax.ShapeDtypeStruct((INNER, D), BF16),
            vector(D), jax.ShapeDtypeStruct((8, XBC), F32), vector(XBC), vector(128), vector(128),
            vector(INNER), vector(INNER),
            jax.ShapeDtypeStruct((256, INNER), BF16), jax.ShapeDtypeStruct((INNER, 128), BF16),
        ],
        scratch_shapes=[pltpu.VMEM((IN_BLOCK * NORM_ROWS + 16, LANES), F32)],
        compiler_params=pltpu.CompilerParams(
            dimension_semantics=("arbitrary",), vmem_limit_bytes=40 * 2**20),
        cost_estimate=pl.CostEstimate(
            flops=10**9, bytes_accessed=16 * 2**20, transcendentals=0),
    )(flat)


def stage_kernel(
    who_ref, early_ref, early_other_ref, late_ref, late_other_ref, small_ref,
    grad_ref,
    stage_ref,
):
    step = pl.program_id(0)
    upper = who_ref[0]
    mine = who_ref[1]
    block = grad_ref.shape[0]
    half = 2 * block * STAGE_BLOCKS

    @pl.when(step == 0)
    def _():
        early_at = LEAD + jnp.where(upper == 1, OUT_START - half, NORM_ROWS)
        window = LATE_START + (XBC - WINDOW) * NORM_ROWS
        late_at = LEAD + jnp.where(upper == 1, window - half, LATE_START)
        def lay(source_ref, start, size):
            for lane in range(NORM_ROWS):
                stage_ref[pl.ds(start + lane, size, stride=NORM_ROWS), :] = source_ref[
                    0:size, lane * LANES : lane * LANES + LANES]

        lines = late_ref.shape[0]
        lay(late_ref, late_at + mine * (lines * NORM_ROWS), lines)
        lay(late_other_ref, late_at + (1 - mine) * (lines * NORM_ROWS), lines)

        @pl.when(upper == 1)
        def _():
            lay(small_ref, LEAD + OUT_START - half - SMALL_ROWS, -(-SMALL_ROWS // NORM_ROWS))

        lines = early_ref.shape[0]
        lay(early_ref, early_at + mine * (lines * NORM_ROWS), lines)
        lay(early_other_ref, early_at + (1 - mine) * (lines * NORM_ROWS), lines)

        @pl.when(upper == 0)
        def _():
            for lane in range(NORM_ROWS):
                stage_ref[LEAD + lane : LEAD + lane + 1, :] = small_ref[
                    40:41, lane * LANES : lane * LANES + LANES]

        @pl.when(upper == 1)
        def _():
            at = LEAD + OUT_START + OUT_ROWS - half
            stage_ref[at : LEAD + half, :] = jnp.zeros((LEAD + half - at, LANES), F32)

    @pl.when(step > 0)
    def _():
        at = LEAD + mine * (half // 2) + (step - 1) * block
        grad_ref[...] = stage_ref[pl.ds(pl.multiple_of(at, 8), block), :]


def run_stage(who, rows, early, early_other, late, late_other, small):
    block = rows // STAGE_BLOCKS
    return pl.pallas_call(
        stage_kernel,
        grid=(STAGE_BLOCKS + 1,),
        in_specs=[
            pl.BlockSpec(memory_space=pltpu.SMEM),
            const_spec(early.shape), const_spec(early.shape),
            const_spec(late.shape), const_spec(late.shape), const_spec(small.shape),
        ],
        out_specs=pl.BlockSpec((block, LANES), lambda i: (jnp.maximum(i - 1, 0), 0)),
        out_shape=jax.ShapeDtypeStruct((rows, LANES), F32),
        scratch_shapes=[pltpu.VMEM((STAGE_ROWS, LANES), F32)],
        compiler_params=pltpu.CompilerParams(
            dimension_semantics=("arbitrary",), vmem_limit_bytes=48 * 2**20),
        cost_estimate=pl.CostEstimate(
            flops=10**6, bytes_accessed=12 * 2**20, transcendentals=0),
    )(who, early, early_other, late, late_other, small)


def swap(values, axis, bit):
    size = lax.axis_size(axis)
    return lax.ppermute(values, axis, [(i, i ^ bit) for i in range(size)])


def to_wire(values, power):
    return (values * jnp.exp2(power)).astype(jnp.float16)


def from_wire(values, power):
    return values.astype(F32) * jnp.exp2(-power)


def scatter(values, power, axis, bit=1, count=2, after=None, sent=None):
    place = (lax.axis_index(axis) // bit) % count
    rows = values.shape[-2] // count
    mark = min(MARK, rows)
    dim = values.ndim - 2
    total = lax.dynamic_slice_in_dim(values, place * rows, rows, dim)
    least = power
    arrived = []
    for offset in range(1, count):
        to = place ^ offset
        last = to == count - 1
        start = to * rows - jnp.where(last, mark, 0)
        send = lax.dynamic_slice_in_dim(values, start, rows + mark, dim)
        line = lax.broadcasted_iota(jnp.int32, send.shape, dim)
        marked = jnp.where(last, line < mark, line >= rows)
        wire = jnp.where(marked, power, send * jnp.exp2(power)).astype(jnp.float16)
        arrived.append(swap(wire, axis, bit * offset))
        if sent is not None:
            sent.append(wire)
    if after is not None:
        arrived, _ = lax.optimization_barrier((arrived, after))
    last = place == count - 1
    for got in arrived:
        got_power = lax.dynamic_slice_in_dim(
            got, jnp.where(last, 0, rows), 1, dim).reshape(1, D).astype(F32)
        body = lax.dynamic_slice_in_dim(got, jnp.where(last, mark, 0), rows, dim)
        total = total + from_wire(body, got_power)
        least = jnp.minimum(least, got_power)
    return total, least - float(count.bit_length() - 1)


def scatter_product(left, right, power, axis, bit):
    def product(part):
        return lax.dot_general(
            part, right, (((1,), (1,)), ((0,), (0,))), preferred_element_type=F32)

    side = (lax.axis_index(axis) // bit) % 2
    rows = left.shape[2] // 2
    send = product(jnp.where(side == 1, left[:, :, : rows + LANES], left[:, :, rows - LANES :]))
    line = lax.broadcasted_iota(jnp.int32, send.shape, 1)
    marked = jnp.where(side == 1, line >= rows, line < LANES)
    wire = jnp.where(marked, power, send * jnp.exp2(power)).astype(jnp.float16)
    got = swap(wire, axis, bit)
    left, _ = lax.optimization_barrier((left, wire))
    keep = product(jnp.where(side == 0, left[:, :, :rows], left[:, :, rows:]))
    keep, got = lax.optimization_barrier((keep, got))
    got_power = lax.dynamic_slice(
        got, (0, (1 - side) * rows, 0), (1, 1, D))[0].astype(F32)
    body = lax.dynamic_slice_in_dim(got, side * LANES, rows, 1)
    return keep + from_wire(body, got_power), jnp.minimum(power, got_power) - 1.0


def everyones(values, axis, bit=1, count=2):
    place = (lax.axis_index(axis) // bit) % count
    pieces = [values] + [swap(values, axis, bit * offset) for offset in range(1, count)]
    step = 1
    while step < count:
        flip = (place // step) % 2 == 1
        pieces = [
            jnp.where(flip, pieces[i ^ step], pieces[i]) for i in range(count)]
        step *= 2
    return pieces


def gather(values, axis, bit=1, count=2):
    return jnp.concatenate(everyones(values, axis, bit, count))


def add_pair(values, axis, bit, after=None):
    got = swap(values, axis, bit)
    if after is not None:
        got, _ = lax.optimization_barrier((got, after))
    return values + got


def data_groups():
    size = lax.axis_size("dp")
    groups = [(1, 2)]
    bit = 2
    while bit < size:
        count = 4 if bit * 4 <= size else 2
        groups.append((bit, count))
        bit *= count
    return groups


def dot_tn(a, b):
    return lax.dot_general(a, b, (((0,), (0,)), ((), ())), preferred_element_type=F32)


def pick_rows(index, rows):
    chosen = index[:, None] == jnp.arange(rows.shape[0], dtype=jnp.int32)[None, :]
    return dot(chosen.astype(BF16), rows).astype(BF16)


def on_device(
    tokens, loss_sensitivity, lengths, holder_sequence_list, master, moment_one, moment_two,
    adam_rates, iteration_tally,
):
    group_devices = lax.axis_size("zero")
    data_devices = lax.axis_size("dp")
    zero_index = lax.axis_index("zero")
    dp_index = lax.axis_index("dp")
    seq_len = loss_sensitivity.shape[1]
    group_seqs = tokens.shape[0]
    span = tokens.shape[1]
    slots = group_seqs // data_devices
    shard_rows = master.shape[0] // LANES
    tie = lax.optimization_barrier

    own = master.reshape(shard_rows, LANES)
    arranged = holder_sequence_list.reshape(data_devices, group_devices, slots)
    group_order = lax.dynamic_index_in_dim(arranged, zero_index, 1, keepdims=False).reshape(-1)
    local_ids = group_order - zero_index * group_seqs
    dealt = tokens.at[local_ids].get(mode="promise_in_bounds")
    flat = lax.all_gather(own.astype(BF16), "zero", axis=0, tiled=True)

    local_tok = lax.all_to_all(dealt, "dp", split_axis=0, concat_axis=0, tiled=True)
    my_seqs = lax.dynamic_slice_in_dim(group_order, dp_index * slots, slots)
    bound = lengths[my_seqs[0]]
    positions = jnp.arange(seq_len, dtype=jnp.int32)

    in_w, out_w, norm_gain, *params, e2, et = run_prepare(flat)
    cot = loss_sensitivity[0]
    gm = dot_nt(cot, out_w)
    cot_top = jnp.max(jnp.abs(cot)).astype(F32).reshape(1)
    local_tok, in_w, gm, cot_top = tie((local_tok, in_w, gm, cot_top))
    own_late, _ = tie((own, flat[:8]))
    whole_master = lax.all_gather(own_late, "zero", axis=0, tiled=True)

    def place(slot, at):
        return (at // span) * (slots * span) + slot * span + at % span

    source = jnp.where(positions < bound, place(0, positions), place(1, positions - bound))
    packed = pick_rows(source, local_tok.reshape(slots * seq_len, D))
    blocks = jnp.arange(data_devices, dtype=jnp.int32)[:, None, None] * span
    within = blocks + jnp.arange(span, dtype=jnp.int32)[None, None, :]
    within = within + jnp.arange(slots, dtype=jnp.int32)[None, :, None] * bound
    unpack_rows = jnp.minimum(within, seq_len - 1).reshape(-1)
    ends = jnp.stack([bound, jnp.int32(seq_len)])[None, :, None]
    live_rows = jnp.where(within < ends, within, -1).reshape(-1)

    def spread(rows, index):
        return pick_rows(index, rows).reshape(data_devices * slots, span, D)

    def send_back(picked):
        return lax.all_to_all(picked, "dp", split_axis=0, concat_axis=0, tiled=True)

    restore = jnp.zeros_like(local_ids).at[local_ids].set(
        jnp.arange(group_seqs, dtype=jnp.int32))
    mine = lax.dynamic_slice_in_dim(lengths, zero_index * group_seqs, group_seqs)
    at = dp_index * span + jnp.arange(span, dtype=jnp.int32)
    live = (at[None, :] < mine[:, None])[:, :, None]

    bound_arr = bound.reshape(1)
    tok = packed.astype(F32)
    nhat = tok * lax.rsqrt(jnp.mean(tok * tok, axis=1, keepdims=True) + EPS_NORM)
    normed = (nhat * norm_gain).astype(BF16)
    proj_z = dot_nt(normed, in_w[:INNER])
    proj = dot_nt(normed, in_w[INNER:PROJ])
    pair, dy, through, states, ggain, early_power = run_forward(
        proj_z, proj, gm, bound_arr, cot_top, norm_gain, e2, et, params)
    result = (tok + dot(pair[1], out_w)).astype(BF16)
    picked = spread(result, unpack_rows)
    picked, pair = tie((picked, pair))
    back_out = send_back(picked)
    early_power = early_power[0:1, 0:1]
    early, early_power = scatter_product(
        pair, jnp.stack([normed, cot]), early_power, "zero", 1)
    early, early_power, dy = tie((early.reshape(INNER, D), early_power, dy))
    early, early_power = scatter(early, early_power, "zero", 2)
    window, grad_tok, small, late_power = run_backward(
        proj, dy, through, states, pair, packed, cot, in_w, norm_gain, ggain,
        bound_arr, e2, et, params)
    window, small, late_power, early, early_power, whole_master = tie(
        (window, small, late_power, early, early_power, whole_master))

    groups = data_groups()
    late_power = late_power[0:1, 0:1]
    late, late_power = scatter_product(
        window, jnp.stack([normed, normed]), late_power, "zero", 1)
    late = late.reshape(WINDOW, D)
    small = add_pair(small, "zero", 1)
    early, early_power, grad_tok, _ = tie((early, early_power, grad_tok, late))
    late, late_power = scatter(late, late_power, "zero", 2)
    early, early_power = scatter(early, early_power, "dp", *groups[0])
    small = add_pair(small, "zero", 2, late)
    early_before, power_before = early, early_power
    picked_grad = spread(grad_tok, live_rows)
    tokens, back_out, _ = tie((tokens, back_out, grad_tok))
    back_rows = back_out.at[restore].get(mode="promise_in_bounds")
    tokens_out = jnp.where(live, back_rows, tokens)
    new_master = jnp.zeros((group_devices, shard_rows, LANES), F32)
    late, tokens_out, new_master, picked_grad = tie((late, tokens_out, new_master, picked_grad))
    lines = small.shape[0]
    late = jnp.concatenate([late, small, jnp.zeros((WINDOW // 8 - lines, D), F32)])
    late, late_power = scatter(late, late_power, "dp", *groups[0])
    sent = []
    for group in groups[1:]:
        late, late_power = scatter(late, late_power, "dp", *group, sent=sent)
    early, early_power = early_before, power_before
    for group in groups[1:]:
        early, early_power = scatter(early, early_power, "dp", *group, after=sent)
    early = to_wire(early, early_power)
    for group in reversed(groups[1:]):
        early = gather(early, "dp", *group)
    early, _ = tie((early, late))
    late = to_wire(late, late_power)
    early = from_wire(gather(early, "dp", *groups[0]), early_power)
    early, picked_grad, _ = tie((early, picked_grad, late))
    for group in reversed(groups[1:]):
        late = gather(late, "dp", *group)
    early_other = swap(early, "zero", 1)
    back_grad = send_back(picked_grad)
    wire = gather(late, "dp", *groups[0])
    late = from_wire(wire[: WINDOW // 2], late_power)
    small = from_wire(wire[WINDOW // 2 : WINDOW // 2 + lines], late_power)
    late_other = swap(late, "zero", 1)

    steps_f = iteration_tally[0].astype(F32)
    who = jnp.stack([zero_index // 2, zero_index % 2]).astype(jnp.int32)
    first = moment_one.reshape(shard_rows, LANES)
    second = moment_two.reshape(shard_rows, LANES)
    grad_shard = run_stage(who, shard_rows, early, early_other, late, late_other, small)
    first_scale = 1.0 / (1.0 - jnp.power(BETA_ONE, steps_f))
    second_scale = 1.0 / (1.0 - jnp.power(BETA_TWO, steps_f))

    def moments(grad, first, second):
        return (
            BETA_ONE * first + (1.0 - BETA_ONE) * grad,
            BETA_TWO * second + (1.0 - BETA_TWO) * grad * grad)

    def quotient(rows):
        first_next, second_next = moments(grad_shard[rows], first[rows], second[rows])
        return ((first_next * first_scale) / (
            jnp.sqrt(second_next * second_scale) + EPS_ADAM)).astype(jnp.float16)

    whole_master = whole_master.reshape(group_devices, shard_rows, LANES)

    def put(new_master, piece, offset):
        shard = zero_index ^ offset
        old = lax.dynamic_index_in_dim(whole_master, shard, 0, keepdims=False)
        new = old - adam_rates[0] * (piece.astype(F32) + adam_rates[1] * old)
        return lax.dynamic_update_index_in_dim(new_master, new, shard, 0)

    own_part, first, second = tie((quotient(slice(0, shard_rows)), first, second))
    across = swap(own_part, "zero", 2)
    core = swap(own_part, "zero", 1)
    first_next, second_next = moments(grad_shard, first, second)
    new_master = put(put(new_master, own_part, 0), core, 1)
    across, new_master, first_next, second_next = tie(
        (across, new_master, first_next, second_next))
    last = swap(across, "zero", 1)
    new_master = put(new_master, across, 2)
    last, new_master = tie((last, new_master))
    new_master = put(new_master, last, 3)
    back_grad, new_master = tie((back_grad, new_master))
    grad_tokens = back_grad.at[restore].get(mode="promise_in_bounds")
    return (
        tokens_out, grad_tokens, new_master.reshape(-1), grad_shard.reshape(-1),
        first_next.reshape(-1), second_next.reshape(-1))


def solution(mesh):
    return jax.shard_map(
        on_device,
        mesh=mesh,
        in_specs=(
            P("zero", "dp", None), P(("dp", "zero"), None, None), P(), P(),
            P("zero"), P("zero"), P("zero"), P(), P(),
        ),
        out_specs=(
            P("zero", "dp", None), P("zero", "dp", None), P(), P("zero"), P("zero"), P("zero"),
        ),
        check_vma=False,
    )
```
